32 devices in a mesh: row: 4 (over y, x), col: 8 (over z, core).
Axes of the slice: x: 2, y: 2, z: 4, core: 2. Of those that a mesh axis runs over, the one named last changes fastest.
Arguments:
- inputs: bfloat16 [4096, 2048], P('row', 'col'), may hold values from -6 to 6
- cotangent: bfloat16 [4096, 2048], P('row', 'col'), may hold values from -6 to 6
- norm_first: float32 [2048], replicated, may hold values from 0.1 to 1.9
- norm_second: float32 [2048], replicated, may hold values from 0.1 to 1.9
- query_gain: float32 [2048], replicated, may hold values from 0.1 to 1.9
- key_gain: float32 [2048], replicated, may hold values from 0.1 to 1.9
- w_query: bfloat16 [2048, 2048], P(None, 'col'), may hold values from -0.125 to 0.125
- w_key: bfloat16 [2048, 2048], P(None, 'col'), may hold values from -0.125 to 0.125
- w_value: bfloat16 [2048, 2048], P(None, 'col'), may hold values from -0.125 to 0.125
- w_out: bfloat16 [2048, 2048], P('col'), may hold values from -0.5 to 0.5
- w_router: bfloat16 [2048, 16], replicated, may hold values from -0.0625 to 0.0625
- w_gate: bfloat16 [16, 2048, 1024], P('col', None, 'row'), may hold values from -0.125 to 0.125
- w_up: bfloat16 [16, 2048, 1024], P('col', None, 'row'), may hold values from -0.125 to 0.125
- w_down: bfloat16 [16, 1024, 2048], P('col', 'row'), may hold values from -3 to 3
- adapter_a: bfloat16 [5, 8, 2048, 16], replicated, may hold values from -0.125 to 0.125
- adapter_b: bfloat16 [4, 8, 16, 2048], replicated, may hold values from -0.75 to 0.75
- adapter_router: bfloat16 [8, 16, 16], replicated, may hold values from -0.375 to 0.375
- routes: int32 [4096, 8], P('row'), may hold values from 0 to 15, all different within a row; in each aligned block of 1024 rows (0 to 1023, 1024 to 2047, ...) at most 640 rows name the same one
- prefix: int32 [4], P('row'), may hold values from 1 to 511
- adapter_index: int32 [4], P('row'), may hold values from 0 to 7
Outputs:
- layer_out: bfloat16 [4096, 2048], P('row', 'col')
- grad_inputs: float32 [4096, 2048], P('row', 'col')
- grad_a: float32 [5, 8, 2048, 16], P(None, 'row', 'col')
- grad_b: float32 [4, 8, 16, 2048], P(None, 'row', None, 'col')
- grad_router: float32 [8, 16, 16], P('row')
The draws below stay inside these ranges and needn't reach their ends.
Inputs may be any that keep to these rules, and one draw needn't show every extreme that they name: `routes`: each token names 8 different experts; within one sequence no expert is named by more than 640 tokens, and in every draw some expert is named by exactly 640 tokens of some sequence.
All inputs are finite; a program needn't handle non-finite values.
Results may differ from the reference program's by a relative error of at most 0.023.
Values may be sent and summed in bfloat16 or wider, within the bound.
A program may use at most 256 MiB of HBM per device.

```python
import math
import jax
import jax.numpy as jnp
import numpy as np
from jax import lax

D = 2048
HEADS = 16
HD = 128
FF = 1024
TOP = 8
RANK = 16
ADAPTERS = 8
SEQ_LEN = 1024
EXPERTS = 16
SEQS = 4
TOKENS = 4096
CAP = 640


def touch_ends(drawn, key, low, largest):
    dims = drawn.shape
    spot = [jax.random.randint(jax.random.fold_in(key, axis), (), 0, dims[axis]) for axis in range(len(dims))]
    drawn = drawn.at[tuple(spot)].set(low)
    longest = dims.index(max(dims))
    spot[longest] = (spot[longest] + 1) % dims[longest]
    return drawn.at[tuple(spot)].set(largest)


def steps_of(rng, dims, cuts, low, high):
    def one(dim, parts):
        draws = jax.random.uniform(jax.random.fold_in(jax.random.fold_in(rng, 6), dim), (parts,), jnp.float32, low / len(cuts), high / len(cuts))
        return jnp.repeat(jnp.exp(draws), dims[dim] // parts).reshape((-1,) + (1,) * (len(dims) - dim - 1))

    loudness = one(*cuts[0])
    for cut in cuts[1:]:
        loudness = loudness * one(*cut)
    return loudness


def shared_out(rng, own, number, rows, amount, top, bound, slope):
    sequence = jax.random.permutation(rng, amount)
    crowded, usual = load_shares(amount, rows * top, bound, slope, True), load_shares(amount, rows * top, bound, slope, False)
    places = jnp.arange(amount)

    def named(tallies, turn):
        used = int((tallies > 0).sum())
        fixed = max(1, used // 4)
        moved = fixed + (places - fixed + turn * (used - fixed)) % max(1, amount - fixed)
        return jnp.zeros((amount,), jnp.int32).at[sequence[jnp.where(places < fixed, places, moved)]].set(jnp.asarray(tallies, jnp.int32))

    tallies = jnp.where(number % 4 == 0, named(crowded, number // 4), named(usual, number - number // 4 - 1))
    mixed = jax.random.permutation(jax.random.fold_in(own, 3), amount)
    donor, taker = mixed[0:amount // 2 * 2:2], mixed[1:amount // 2 * 2:2]
    margin = jnp.minimum(tallies[donor] - 1, bound - tallies[taker]) // 2
    margin = jnp.where((donor == sequence[0]) | (taker == sequence[0]) | (tallies[taker] == 0), 0, jnp.maximum(margin, 0))
    moved = jax.random.randint(jax.random.fold_in(own, 4), (amount // 2,), 0, 1 << 20) % (margin + 1)
    tallies = tallies.at[donor].add(-moved).at[taker].add(moved)
    members = jnp.searchsorted(jnp.cumsum(tallies), jnp.arange(rows * top), side="right").astype(jnp.int32)
    grid = members.reshape(top, rows).T
    grid = grid[jax.random.permutation(jax.random.fold_in(own, 1), rows)]
    turn = jax.random.randint(jax.random.fold_in(own, 2), (rows, 1), 0, top)
    return jnp.take_along_axis(grid, (jnp.arange(top)[None, :] + turn) % top, axis=1)


def load_shares(count, total, reach, lean, full):
    portions = [(1 << 20) // math.isqrt(standing ** lean) + 1 for standing in range(1, count + 1)]
    largest = reach if full else min(reach, max(-(-total // count), total * portions[0] // sum(portions)))
    least = 1 if total - largest >= count - 1 else 0
    given, spare = [largest] + [least] * (count - 1), total - largest - least * (count - 1)
    while spare > 0:
        free = [i for i in range(1, count) if given[i] < largest] or [i for i in range(1, count) if given[i] < reach]
        whole, left = sum([portions[i] for i in free]), spare
        for i in free:
            more = min(reach - given[i], max(1, left * portions[i] // whole), spare)
            given[i] = given[i] + more
            spare = spare - more
    return np.array(given)


def scatter_about(stream_key, shape, width, limit, shards=(), held_as=jnp.bfloat16):
    entries = jax.random.normal(stream_key, shape, jnp.float32) * width
    if len(shards) > 0:
        entries = steps_of(stream_key, shape, shards, -0.22, 0.18) * entries
    return jnp.clip(entries, min=-limit, max=limit).astype(held_as)


def setup_inputs(seed: int = 0) -> dict:
    splits = jax.random.split(jax.random.key(seed), 21)
    inputs = scatter_about(splits[0], (TOKENS, D), 1.0, 6.0, ((0, 4), (1, 8)))
    cotangent = scatter_about(splits[1], (TOKENS, D), 1.0, 6.0, ((0, 4), (1, 8)))
    norm_first = jnp.clip(1.0 + 0.18 * jax.random.normal(splits[2], (D,), jnp.float32), 0.1, 1.9)
    norm_second = jnp.clip(1.0 + 0.18 * jax.random.normal(splits[3], (D,), jnp.float32), 0.1, 1.9)
    query_gain = jnp.clip(1.0 + 0.18 * jax.random.normal(splits[4], (D,), jnp.float32), 0.1, 1.9)
    key_gain = jnp.clip(1.0 + 0.18 * jax.random.normal(splits[5], (D,), jnp.float32), 0.1, 1.9)
    w_query = scatter_about(splits[6], (D, D), D ** -0.5, 0.125, ((1, 8),))
    w_key = scatter_about(splits[7], (D, D), D ** -0.5, 0.125, ((1, 8),))
    w_value = scatter_about(splits[8], (D, D), D ** -0.5, 0.125, ((1, 8),))
    w_out = scatter_about(splits[9], (D, D), (D // 16) ** -0.5, 0.5, ((0, 8),))
    w_router = scatter_about(splits[10], (D, EXPERTS), (4 * D) ** -0.5, 0.0625)
    w_gate = scatter_about(splits[11], (EXPERTS, D, FF), D ** -0.5, 0.125, ((0, 8), (2, 4)))
    w_up = scatter_about(splits[12], (EXPERTS, D, FF), D ** -0.5, 0.125, ((0, 8), (2, 4)))
    w_down = scatter_about(splits[13], (EXPERTS, FF, D), (max(FF // 256, 1)) ** -0.5, 3.0, ((0, 8), (1, 4)))
    adapter_a = scatter_about(splits[14], (5, ADAPTERS, D, RANK), D ** -0.5, 0.125)
    adapter_b = scatter_about(splits[15], (4, ADAPTERS, RANK, D), (4 * RANK) ** -0.5, 0.75)
    adapter_router = scatter_about(splits[16], (ADAPTERS, RANK, EXPERTS), (16 * RANK) ** -0.5, 0.375)
    routes_keys = jax.random.split(jax.random.fold_in(splits[17], 1), TOKENS // SEQ_LEN)
    routes_turns = jax.random.permutation(jax.random.fold_in(splits[17], 3), TOKENS // SEQ_LEN)
    routes = jax.vmap(lambda own, number: shared_out(jax.random.fold_in(splits[17], 2), own, number, SEQ_LEN, EXPERTS, TOP, CAP, 1))(routes_keys, routes_turns).reshape((TOKENS, TOP))
    prefix = touch_ends(jax.random.randint(splits[18], (SEQS,), 1, SEQ_LEN // 2), jax.random.fold_in(splits[18], 1), 1, (SEQ_LEN // 2) - 1).astype(jnp.int32)
    adapter_index = touch_ends(jax.random.randint(splits[19], (SEQS,), 0, ADAPTERS), jax.random.fold_in(splits[19], 1), 0, ADAPTERS - 1).astype(jnp.int32)
    return {"inputs": inputs, "cotangent": cotangent, "norm_first": norm_first, "norm_second": norm_second, "query_gain": query_gain, "key_gain": key_gain, "w_query": w_query, "w_key": w_key, "w_value": w_value, "w_out": w_out, "w_router": w_router, "w_gate": w_gate, "w_up": w_up, "w_down": w_down, "adapter_a": adapter_a, "adapter_b": adapter_b, "adapter_router": adapter_router, "routes": routes, "prefix": prefix, "adapter_index": adapter_index}


norm_eps = 1e-05
rope_base = 10000.0
masked_score = -1e+30
highest = lax.Precision.HIGHEST

@jax.custom_vjp
def low(v):
    return lax.optimization_barrier(v.astype(jnp.bfloat16)).astype(jnp.float32)

@jax.custom_vjp
def low_back(v):
    return v

def low_keep(v):
    return (low(v), None)

def low_pass(kept, grad):
    return (grad,)

def back_keep(v):
    return (v, None)

def back_low(kept, grad):
    return (low(grad),)
low.defvjp(low_keep, low_pass)
low_back.defvjp(back_keep, back_low)

def product(left_side, right_side):
    return jnp.dot(left_side.astype(jnp.float32), right_side.astype(jnp.float32), precision=highest, preferred_element_type=jnp.float32)

def rms_scale(values, gain_vector):
    return values * lax.rsqrt(lax.optimization_barrier(jnp.mean(values * values, axis=-1, keepdims=True)) + norm_eps) * gain_vector

def rope_tables(length, head_dim):
    half_dim = head_dim // 2
    frequency = rope_base ** (-(2.0 * jnp.arange(half_dim, dtype=jnp.float32)) / head_dim)
    angles = jnp.arange(length, dtype=jnp.float32)[:, None] * frequency[None, :]
    return (jnp.cos(angles), jnp.sin(angles))

def rotate(values, cosine_table, sine_table):
    half_dim = values.shape[-1] // 2
    first_half = values[..., :half_dim]
    second_half = values[..., half_dim:]
    return jnp.concatenate([first_half * cosine_table - second_half * sine_table, second_half * cosine_table + first_half * sine_table], axis=-1)

def reference(inputs, cotangent, norm_first, norm_second, query_gain, key_gain, w_query, w_key, w_value, w_out, w_router, w_gate, w_up, w_down, adapter_a, adapter_b, adapter_router, routes, prefix, adapter_index):
    cosine_table, sine_table = rope_tables(SEQ_LEN, HD)
    score_scale = HD ** (-0.5)

    def expert(packed):
        slot_rows, gate_weight, up_weight, down_weight = packed
        gate_in = low_back(product(slot_rows, gate_weight))
        up_in = low_back(product(slot_rows, up_weight))
        active = low(jax.nn.silu(gate_in) * up_in)
        return low_back(product(active, down_weight))

    def split_heads(values):
        return values.reshape(SEQ_LEN, HEADS, HD).transpose(1, 0, 2)

    def forward(input_rows, adapters_a, adapters_b, router_adapter):

        def one_sequence(packed):
            tokens, token_routes, prefix_len, adapter_slot = packed
            chosen_a = jnp.take(adapters_a, adapter_slot, axis=1)
            chosen_b = jnp.take(adapters_b, adapter_slot, axis=1)
            chosen_router = jnp.take(router_adapter, adapter_slot, axis=0)
            normed = low(rms_scale(tokens, norm_first))

            def project(which_one, weight):
                middle = low_back(low(product(normed, chosen_a[which_one])))
                return low_back(product(normed, weight) + product(middle, chosen_b[which_one]))
            queries = rms_scale(project(0, w_query), query_gain)
            key_rows = rms_scale(project(1, w_key), key_gain)
            value_rows = low(project(2, w_value))
            queries = low(rotate(split_heads(queries), cosine_table, sine_table))
            key_rows = low(rotate(split_heads(key_rows), cosine_table, sine_table))
            position = jnp.arange(SEQ_LEN, dtype=jnp.int32)
            allowed = (position[None, :] <= position[:, None]) | (position[None, :] < prefix_len)

            def attend_head(head_pack):
                head_query, head_key, head_value = head_pack
                scores = low_back(product(head_query, head_key.T) * score_scale)
                scores = jnp.where(allowed, scores, masked_score)
                weights = jax.nn.softmax(scores, axis=-1)
                return product(low(weights), head_value)
            attended = lax.map(jax.checkpoint(attend_head), (queries, key_rows, split_heads(value_rows)))
            attended = low_back(low(attended.transpose(1, 0, 2).reshape(SEQ_LEN, D)))
            middle_out = low_back(low(product(attended, chosen_a[3])))
            hidden = tokens + low_back(product(attended, w_out) + product(middle_out, chosen_b[3]))
            normed_two = low(rms_scale(hidden, norm_second))
            middle_router = low_back(low(product(normed_two, chosen_a[4])))
            logits = low_back(product(normed_two, w_router) + product(middle_router, chosen_router))
            router_probs = jax.nn.softmax(logits, axis=-1)
            expert_ids = jnp.arange(EXPERTS, dtype=jnp.int32)
            member = lax.optimization_barrier(jnp.sum((token_routes[:, :, None] == expert_ids[None, None, :]).astype(jnp.int32), axis=1))
            slot_rank = jnp.cumsum(member, axis=0) - member
            target = jnp.where(member > 0, expert_ids[None, :] * CAP + slot_rank, EXPERTS * CAP)
            token_ids = jnp.broadcast_to(jnp.arange(SEQ_LEN, dtype=jnp.int32)[:, None], (SEQ_LEN, EXPERTS))
            slot_token = jnp.zeros((EXPERTS * CAP,), jnp.int32).at[target.reshape(-1)].set(token_ids.reshape(-1), mode='drop')
            slot_live = jnp.zeros((EXPERTS * CAP,), jnp.float32).at[target.reshape(-1)].set(1.0, mode='drop')
            slot_expert = jnp.arange(EXPERTS * CAP, dtype=jnp.int32) // CAP
            slot_gate = router_probs[slot_token, slot_expert] * slot_live
            slot_rows = normed_two[slot_token].reshape(EXPERTS, CAP, D)
            outputs = lax.map(jax.checkpoint(expert), (slot_rows, w_gate, w_up, w_down))
            expert_sum = jax.ops.segment_sum(outputs.reshape(EXPERTS * CAP, D) * slot_gate[:, None], slot_token, num_segments=SEQ_LEN)
            return hidden + expert_sum
        results = lax.map(jax.checkpoint(one_sequence), (input_rows.reshape(SEQS, SEQ_LEN, D), routes.reshape(SEQS, SEQ_LEN, TOP), prefix, adapter_index))
        return results.reshape(TOKENS, D)
    layer_out, pullback = jax.vjp(forward, inputs.astype(jnp.float32), adapter_a.astype(jnp.float32), adapter_b.astype(jnp.float32), adapter_router.astype(jnp.float32))
    gradients = pullback(cotangent.astype(jnp.float32))
    return (layer_out.astype(jnp.bfloat16), gradients[0], gradients[1], gradients[2], gradients[3])
```

```python
import functools

import jax
import jax.numpy as jnp
from jax import lax
from jax.experimental import pallas as pl
from jax.experimental.pallas import tpu as pltpu
from jax.sharding import PartitionSpec as P

HD = 128
F32, BF16 = jnp.float32, jnp.bfloat16
MESH_ID = pl.DeviceIdType.MESH
VM = pl.BlockSpec(memory_space=pltpu.VMEM)
ANY = pl.BlockSpec(memory_space=pl.ANY)
VMEM_LIMIT = 60 * 1024 * 1024

norm_eps = 1e-05
rope_base = 10000.0
masked_score = -1e30


def nn(left, right):
    return jnp.dot(left, right, preferred_element_type=F32)


def nt(left, right):
    return lax.dot_general(left, right, (((1,), (1,)), ((), ())), preferred_element_type=F32)


def tn(left, right):
    return lax.dot_general(left, right, (((0,), (0,)), ((), ())), preferred_element_type=F32)


def remote(src, dst, send_sem, recv_sem, device):
    return pltpu.make_async_remote_copy(
        src_ref=src,
        dst_ref=dst,
        send_sem=send_sem,
        recv_sem=recv_sem,
        device_id={"col": device},
        device_id_type=MESH_ID,
    )


def line_place():
    here = lax.axis_index("col")
    core = here % 2
    return here, here // 2, core, here + 1 - 2 * core


def line_barrier(chips):
    here, chip, core, mate = line_place()
    barrier = pltpu.get_barrier_semaphore()
    has_left, has_right = chip > 0, chip < chips - 1
    pl.semaphore_signal(barrier, inc=1, device_id={"col": mate}, device_id_type=MESH_ID)

    @pl.when(has_left)
    def _():
        pl.semaphore_signal(barrier, inc=1, device_id={"col": here - 2}, device_id_type=MESH_ID)

    @pl.when(has_right)
    def _():
        pl.semaphore_signal(barrier, inc=1, device_id={"col": here + 2}, device_id_type=MESH_ID)

    inner = jnp.logical_and(has_left, has_right)

    @pl.when(inner)
    def _():
        pl.semaphore_wait(barrier, 3)

    @pl.when(jnp.logical_not(inner))
    def _():
        pl.semaphore_wait(barrier, 2)


def spot(axis, size, parts, block, part):
    rows, cols = size
    step = rows // parts
    if axis == 0:
        return (pl.ds(pl.multiple_of(block * rows + part * step, 8), step), slice(None))
    return (pl.ds(part * step, step), pl.ds(pl.multiple_of(block * cols, 128), cols))


def gather_body(chips, parts, axis, x_ref, o_ref, right_sem, left_sem, mate_sem, line_recv, mate_recv, own_sem):
    here, chip, core, mate = line_place()
    size = x_ref.shape
    step = size[0] // parts
    line_barrier(chips)

    def at(block, part):
        return o_ref.at[spot(axis, size, parts, block, part)]

    def copy(j, part, sem, recv, device, first=False, block=None):
        block = 2 * j + core if block is None else block
        src = x_ref.at[pl.ds(part * step, step)] if first else at(block, part)
        return remote(src, at(block, part), sem.at[j, part], recv.at[j, part], device)

    def forward(j, part, rightward, leftward, first):
        if rightward:

            @pl.when(chip < chips - 1)
            def _():
                copy(j, part, right_sem, line_recv, here + 2, first).start()

        if leftward:

            @pl.when(chip > 0)
            def _():
                copy(j, part, left_sem, line_recv, here - 2, first).start()

        copy(j, part, mate_sem, mate_recv, mate, first).start()

    for part in range(parts):
        forward(chip, part, True, True, True)
    own = []
    for part in range(parts):
        own.append(
            pltpu.make_async_copy(x_ref.at[pl.ds(part * step, step)], at(here, part), own_sem.at[part])
        )
        own[-1].start()
    for far in range(1, chips):
        for part in range(parts):

            @pl.when(chip - far >= 0)
            def _():
                copy(chip - far, part, right_sem, line_recv, mate).wait_recv()
                forward(chip - far, part, True, False, False)

            @pl.when(chip + far < chips)
            def _():
                copy(chip + far, part, left_sem, line_recv, mate).wait_recv()
                forward(chip + far, part, False, True, False)

    for own_copy in own:
        own_copy.wait()
    for j in range(chips):
        for part in range(parts):
            copy(j, part, mate_sem, mate_recv, mate, block=2 * j + 1 - core).wait_recv()
            copy(j, part, mate_sem, mate_recv, mate).wait_send()

            @pl.when(jnp.logical_and(j <= chip, chip < chips - 1))
            def _():
                copy(j, part, right_sem, line_recv, here + 2).wait_send()

            @pl.when(jnp.logical_and(j >= chip, chip > 0))
            def _():
                copy(j, part, left_sem, line_recv, here - 2).wait_send()


def line_gather(x, chips, axis, ident, parts=2):
    rows, cols = x.shape
    sems = pltpu.SemaphoreType.DMA((chips, parts))
    shape = (2 * chips * rows, cols) if axis == 0 else (rows, 2 * chips * cols)
    return pl.pallas_call(
        functools.partial(gather_body, chips, parts, axis),
        out_shape=jax.ShapeDtypeStruct(shape, x.dtype),
        in_specs=[VM],
        out_specs=VM,
        scratch_shapes=[sems] * 5 + [pltpu.SemaphoreType.DMA((parts,))],
        compiler_params=pltpu.CompilerParams(
            collective_id=ident, has_side_effects=True, vmem_limit_bytes=VMEM_LIMIT
        ),
        name="line_gather",
    )(x)


def reduce_body(
    chips, parts, axis, p_ref, o_ref, pair_buf, line_buf, sums, right_sem, left_sem, mate_sem, line_recv, mate_recv
):
    here, chip, core, mate = line_place()
    size = o_ref.shape
    step = size[0] // parts
    line_barrier(chips)

    def rows(part):
        return pl.ds(part * step, step)

    def at(block, part):
        return spot(axis, size, parts, block, part)

    def mate_copy(j, part):
        return remote(
            p_ref.at[at(2 * j + 1 - core, part)],
            pair_buf.at[j, rows(part)],
            mate_sem.at[j, part],
            mate_recv.at[j, part],
            mate,
        )

    def line_copy(j, slot, part, sem, device):
        return remote(
            sums.at[j, rows(part)], line_buf.at[slot, rows(part)], sem.at[j, part], line_recv.at[slot, part], device
        )

    for far in range(chips - 1, -1, -1):
        for part in range(parts):

            @pl.when(chip + far < chips)
            def _():
                mate_copy(chip + far, part).start()

            if far > 0:

                @pl.when(chip - far >= 0)
                def _():
                    mate_copy(chip - far, part).start()

    def pair_sum(j, part):
        mate_copy(j, part).wait_recv()
        return p_ref[at(2 * j + core, part)].astype(F32) + pair_buf[j, rows(part)].astype(F32)

    def pass_on(j, slot, part, more, sem, device):
        @pl.when(more)
        def _():
            line_copy(j, j, part, sem, mate).wait_recv()
            total = pair_sum(j, part) + line_buf[j, rows(part)].astype(F32)
            sums[j, rows(part)] = total.astype(BF16)

        @pl.when(jnp.logical_not(more))
        def _():
            sums[j, rows(part)] = pair_sum(j, part).astype(BF16)

        line_copy(j, slot, part, sem, device).start()

    for far in range(chips - 1, 0, -1):
        for part in range(parts):

            @pl.when(chip + far < chips)
            def _():
                pass_on(chip + far, chip + far, part, chip > 0, right_sem, here + 2)

            @pl.when(chip - far >= 0)
            def _():
                pass_on(
                    chip - far, chips if far == 1 else chip - far, part, chip < chips - 1, left_sem, here - 2
                )

    for part in range(parts):
        o_ref[rows(part)] = pair_sum(chip, part)

        @pl.when(chip > 0)
        def _():
            line_copy(chip, chip, part, right_sem, mate).wait_recv()
            o_ref[rows(part)] += line_buf[chip, rows(part)].astype(F32)

        @pl.when(chip < chips - 1)
        def _():
            line_copy(chip, chips, part, left_sem, mate).wait_recv()
            o_ref[rows(part)] += line_buf[chips, rows(part)].astype(F32)

    for j in range(chips):
        for part in range(parts):
            mate_copy(j, part).wait_send()

            @pl.when(j > chip)
            def _():
                line_copy(j, j, part, right_sem, mate).wait_send()

            @pl.when(j < chip)
            def _():
                line_copy(j, j, part, left_sem, mate).wait_send()


def line_reduce(p, chips, axis, ident, parts=2):
    rows, cols = p.shape
    if axis == 0:
        rows //= 2 * chips
    else:
        cols //= 2 * chips
    sems = pltpu.SemaphoreType.DMA((chips, parts))
    return pl.pallas_call(
        functools.partial(reduce_body, chips, parts, axis),
        out_shape=jax.ShapeDtypeStruct((rows, cols), F32),
        in_specs=[VM],
        out_specs=VM,
        scratch_shapes=[
            pltpu.VMEM((chips, rows, cols), BF16),
            pltpu.VMEM((chips + 1, rows, cols), BF16),
            pltpu.VMEM((chips, rows, cols), BF16),
            sems,
            sems,
            sems,
            pltpu.SemaphoreType.DMA((chips + 1, parts)),
            sems,
        ],
        compiler_params=pltpu.CompilerParams(
            collective_id=ident, has_side_effects=True, vmem_limit_bytes=VMEM_LIMIT
        ),
        name="line_reduce",
    )(p)


def small_body(count, x_ref, o_ref, send_sem, recv_sem):
    here = lax.axis_index("col")
    barrier = pltpu.get_barrier_semaphore()
    for hop in range(1, count):
        other = lax.rem(here + hop, count)
        pl.semaphore_signal(barrier, inc=1, device_id={"col": other}, device_id_type=MESH_ID)
    o_ref[here] = x_ref[...]
    pl.semaphore_wait(barrier, count - 1)

    def copy(hop, block):
        other = lax.rem(here + hop, count)
        return remote(x_ref, o_ref.at[block], send_sem.at[hop], recv_sem.at[hop], other)

    for hop in range(1, count):
        copy(hop, here).start()
    for hop in range(1, count):
        copy(hop, lax.rem(here + count - hop, count)).wait_recv()
    for hop in range(1, count):
        copy(hop, here).wait_send()


def small_gather(x, count, ident):
    sems = pltpu.SemaphoreType.DMA((count,))
    return pl.pallas_call(
        functools.partial(small_body, count),
        out_shape=jax.ShapeDtypeStruct((count,) + x.shape, x.dtype),
        in_specs=[VM],
        out_specs=VM,
        scratch_shapes=[sems, sems],
        compiler_params=pltpu.CompilerParams(collective_id=ident, has_side_effects=True),
        name="small_gather",
    )(x)


def moe_body(count, pieces, tile, x_ref, g_ref, gates_ref, *refs):
    weights = refs[: 3 * count]
    out_ref, dx_ref, dgate_ref, out_acc, dx_acc, wgu, wd, sems = refs[3 * count :]
    experts = weights[0].shape[0]
    hidden = wd.shape[1]
    tokens = x_ref.shape[0]
    each = experts * pieces
    steps = count * each

    def copies(a, step, slot):
        gate, up, down = weights[3 * a : 3 * a + 3]
        e, piece = step % experts, (step % each) // experts
        units = pl.ds(pl.multiple_of(piece * hidden, 128), hidden)
        return (
            pltpu.make_async_copy(gate.at[e, :, units], wgu.at[slot, :, pl.ds(0, hidden)], sems.at[slot, 0]),
            pltpu.make_async_copy(up.at[e, :, units], wgu.at[slot, :, pl.ds(hidden, hidden)], sems.at[slot, 1]),
            pltpu.make_async_copy(down.at[e, units], wd.at[slot], sems.at[slot, 2]),
        )

    def fetch(step, slot):
        for a in range(count):

            @pl.when(step // each == a)
            def _():
                for copy in copies(a, step, slot):
                    copy.start()

    fetch(0, 0)
    out_acc[...] = jnp.zeros_like(out_acc)
    dx_acc[...] = jnp.zeros_like(dx_acc)
    dgate_ref[...] = jnp.zeros_like(dgate_ref)

    def one_step(step, carry):
        slot = step % 2
        for copy in copies(0, 0, slot):
            copy.wait()

        @pl.when(step + 1 < steps)
        def _():
            fetch(step + 1, 1 - slot)

        e = step % experts

        def one_tile(t, carry):
            rows = pl.ds(pl.multiple_of(t * tile, tile), tile)
            mine = lax.broadcasted_iota(jnp.int32, (tile, experts), 1) == e
            gate = jnp.sum(jnp.where(mine, gates_ref[rows], 0.0), axis=1, keepdims=True)
            both = nn(x_ref[rows], wgu[slot])
            gate_in, up_in = both[:, :hidden], both[:, hidden:]
            sigmoid = jax.nn.sigmoid(gate_in)
            silu = gate_in * sigmoid
            active = silu * up_in
            back = nt(g_ref[rows], wd[slot])
            dgate_ref[rows] += jnp.where(mine, jnp.sum(active * back, axis=1, keepdims=True), 0.0)
            out_acc[rows] += nn((active * gate).astype(BF16), wd[slot])
            d_active = back * gate
            d_gate_in = d_active * up_in * (sigmoid + silu * (1.0 - sigmoid))
            d_up_in = d_active * silu
            d_both = jnp.concatenate([d_gate_in.astype(BF16), d_up_in.astype(BF16)], axis=1)
            dx_acc[rows] += nt(d_both, wgu[slot])
            return carry

        return lax.fori_loop(0, tokens // tile, one_tile, carry)

    lax.fori_loop(0, steps, one_step, 0)
    out_ref[...] = out_acc[...].astype(out_ref.dtype)
    dx_ref[...] = dx_acc[...].astype(dx_ref.dtype)


def moe(x, g, gates, weights, tile=512):
    tokens, width = x.shape
    experts, _, units = weights[0].shape
    hidden = min(256, units)
    count = len(weights) // 3
    return pl.pallas_call(
        functools.partial(moe_body, count, units // hidden, min(tile, tokens)),
        out_shape=(
            jax.ShapeDtypeStruct((tokens, width), BF16),
            jax.ShapeDtypeStruct((tokens, width), BF16),
            jax.ShapeDtypeStruct(gates.shape, F32),
        ),
        in_specs=[VM, VM, VM] + [ANY] * (3 * count),
        out_specs=(VM, VM, VM),
        scratch_shapes=[
            pltpu.VMEM((tokens, width), F32),
            pltpu.VMEM((tokens, width), F32),
            pltpu.VMEM((2, width, 2 * hidden), BF16),
            pltpu.VMEM((2, hidden, width), BF16),
            pltpu.SemaphoreType.DMA((2, 3)),
        ],
        compiler_params=pltpu.CompilerParams(vmem_limit_bytes=VMEM_LIMIT),
        name="moe",
    )(x, g, gates, *weights)


def rope_tables(length, head_dim):
    half_dim = head_dim // 2
    frequency = rope_base ** (-(2.0 * jnp.arange(half_dim, dtype=F32)) / head_dim)
    angles = jnp.arange(length, dtype=F32)[:, None] * frequency[None, :]
    return (jnp.cos(angles), jnp.sin(angles))


def rotate(values, cosine_table, sine_table):
    half_dim = values.shape[-1] // 2
    first_half = values[..., :half_dim]
    second_half = values[..., half_dim:]
    return jnp.concatenate(
        [
            first_half * cosine_table - second_half * sine_table,
            second_half * cosine_table + first_half * sine_table,
        ],
        axis=-1,
    )


def unrotate(values, cosine_table, sine_table):
    return rotate(values, cosine_table, -sine_table)


def shards(
    inputs,
    cotangent,
    norm_first,
    norm_second,
    query_gain,
    key_gain,
    w_query,
    w_key,
    w_value,
    w_out,
    w_router,
    w_gate,
    w_up,
    w_down,
    adapter_a,
    adapter_b,
    adapter_router,
    routes,
    prefix,
    adapter_index,
):
    seq_len, width_part = inputs.shape
    col_count = lax.axis_size("col")
    row_count = lax.axis_size("row")
    col_index = lax.axis_index("col")
    row_index = lax.axis_index("row")
    chips = col_count // 2
    full_width = width_part * col_count
    head_width = w_query.shape[1]
    head_count = head_width // HD
    local_experts = w_gate.shape[0]
    feature_start = col_index * width_part
    head_start = col_index * head_width
    own_rows = seq_len // col_count
    row_start = col_index * own_rows
    score_scale = HD ** (-0.5)

    def columns(array, axis_num):
        return lax.dynamic_slice_in_dim(array, feature_start, width_part, axis_num)

    def head_cols(array):
        return lax.dynamic_slice_in_dim(array, head_start, head_width, 1)

    def held_rows(array):
        return lax.dynamic_slice_in_dim(array, row_start, own_rows, 0)

    def col_sum(pair, ident):
        packed = jnp.stack(pair).reshape(-1, 128)
        return jnp.sum(small_gather(packed, col_count, ident), axis=0).reshape(len(pair), seq_len)

    full_gate, full_up, full_down = (
        lax.all_gather(w_gate, "row", axis=2, tiled=True),
        lax.all_gather(w_up, "row", axis=2, tiled=True),
        lax.all_gather(w_down, "row", axis=1, tiled=True),
    )
    adapter_slot = adapter_index[0]
    chosen_a = lax.dynamic_index_in_dim(adapter_a, adapter_slot, 1, keepdims=False)
    chosen_b = lax.dynamic_index_in_dim(adapter_b, adapter_slot, 1, keepdims=False)
    chosen_router = lax.dynamic_index_in_dim(adapter_router, adapter_slot, 0, keepdims=False)
    rank_count = chosen_a.shape[2]
    a_three = jnp.concatenate([chosen_a[0], chosen_a[1], chosen_a[2]], axis=1)
    b_query = head_cols(chosen_b[0])
    b_key = head_cols(chosen_b[1])
    b_value = head_cols(chosen_b[2])
    a_out_rows = lax.dynamic_slice_in_dim(chosen_a[3], head_start, head_width, 0)
    out_map = (w_out.astype(F32) + nn(a_out_rows, chosen_b[3])).astype(BF16)
    router_map = w_router.astype(F32) + nn(chosen_a[4], chosen_router)

    full_inputs = line_gather(inputs, chips, 1, 0)
    input_f32 = full_inputs.astype(F32)
    inv_first = lax.rsqrt(jnp.mean(input_f32 * input_f32, axis=1, keepdims=True) + norm_eps)
    normed = (input_f32 * inv_first * norm_first).astype(BF16)
    middle = nn(normed, a_three).astype(BF16)
    mid_query = middle[:, :rank_count]
    mid_key = middle[:, rank_count : 2 * rank_count]
    mid_value = middle[:, 2 * rank_count :]
    proj_query = nn(normed, w_query) + nn(mid_query, b_query)
    proj_key = nn(normed, w_key) + nn(mid_key, b_key)
    proj_value = nn(normed, w_value) + nn(mid_value, b_value)
    square_sums = col_sum(
        (jnp.sum(proj_query * proj_query, axis=1), jnp.sum(proj_key * proj_key, axis=1)), 1
    )
    inv_query = lax.rsqrt(square_sums[0] / full_width + norm_eps)[:, None]
    inv_key = lax.rsqrt(square_sums[1] / full_width + norm_eps)[:, None]
    gain_query = lax.dynamic_slice_in_dim(query_gain, head_start, head_width, 0)
    gain_key = lax.dynamic_slice_in_dim(key_gain, head_start, head_width, 0)
    cosine_table, sine_table = rope_tables(seq_len, HD)
    cosine_table = cosine_table[:, None, :]
    sine_table = sine_table[:, None, :]
    rot_query = rotate(
        (proj_query * inv_query * gain_query).reshape(seq_len, head_count, HD),
        cosine_table,
        sine_table,
    ).astype(BF16)
    rot_key = rotate(
        (proj_key * inv_key * gain_key).reshape(seq_len, head_count, HD), cosine_table, sine_table
    ).astype(BF16)
    value_rows = proj_value.astype(BF16).reshape(seq_len, head_count, HD)
    block_rows = min(512, seq_len)
    starts = jnp.arange(seq_len // block_rows, dtype=jnp.int32) * block_rows
    key_pos = jnp.arange(seq_len, dtype=jnp.int32)
    prefix_len = prefix[0]

    def block_scores(start_row):
        block_query = lax.dynamic_slice_in_dim(rot_query, start_row, block_rows, 0)
        query_pos = start_row + jnp.arange(block_rows, dtype=jnp.int32)
        allowed = (key_pos[None, :] <= query_pos[:, None]) | (key_pos[None, :] < prefix_len)
        raw_scores = (
            jnp.einsum("qhd,khd->hqk", block_query, rot_key, preferred_element_type=F32)
            * score_scale
        )
        return (block_query, jnp.where(allowed[None], raw_scores, masked_score))

    def attend_block(start_row):
        block_query, scores = block_scores(start_row)
        row_max = jnp.max(scores, axis=2, keepdims=True)
        exponent = jnp.exp(scores - row_max)
        row_total = jnp.sum(exponent, axis=2, keepdims=True)
        weights = (exponent / row_total).astype(BF16)
        attended_block = jnp.einsum(
            "hqk,khd->qhd", weights, value_rows, preferred_element_type=F32
        )
        return (attended_block.astype(BF16), (row_max + jnp.log(row_total))[:, :, 0])

    attended_blocks, log_totals = lax.map(attend_block, starts)
    attended = attended_blocks.reshape(seq_len, head_width)
    out_rows = line_reduce(nn(attended, out_map).astype(BF16), chips, 0, 2)
    hidden_rows = held_rows(full_inputs).astype(F32) + out_rows
    hidden = line_gather(hidden_rows.astype(BF16), chips, 0, 3)
    full_cot = line_gather(cotangent, chips, 1, 4)
    mid_out = jnp.sum(
        small_gather(nn(attended, a_out_rows).astype(BF16).reshape(-1, 128), col_count, 5).astype(F32), axis=0
    ).reshape(seq_len, rank_count).astype(BF16)

    hidden_f32 = hidden.astype(F32)
    inv_second = lax.rsqrt(jnp.mean(hidden_f32 * hidden_f32, axis=1, keepdims=True) + norm_eps)
    normed_two = (hidden_f32 * inv_second * norm_second).astype(BF16)
    mid_router = nn(normed_two, chosen_a[4]).astype(BF16)
    logits = nn(normed_two, w_router) + nn(mid_router, chosen_router)
    router_probs = jax.nn.softmax(logits, axis=1)
    expert_total = router_probs.shape[1]
    own_ids = col_index * local_experts + jnp.arange(local_experts, dtype=jnp.int32)
    member = jnp.any(routes[:, :, None] == own_ids[None, None, :], axis=1)
    own_probs = lax.dynamic_slice_in_dim(router_probs, col_index * local_experts, local_experts, 1)
    gates = jnp.where(member, own_probs, 0.0)
    moe_out, back_out, d_gate = moe(normed_two, full_cot, gates, (full_gate, full_up, full_down))
    d_gate = jnp.where(member, d_gate, 0.0)
    grad_probs = small_gather(d_gate.T.reshape(-1, 128), col_count, 6).reshape(expert_total, seq_len).T
    grad_logits = (
        router_probs * (grad_probs - jnp.sum(router_probs * grad_probs, axis=1, keepdims=True))
    ).astype(BF16)
    back_rows = line_reduce(back_out, chips, 0, 7)
    grad_normed_two = back_rows + nt(held_rows(grad_logits).astype(F32), router_map)
    hidden_held = held_rows(hidden).astype(F32)
    inv_held = held_rows(inv_second)
    scaled_two = grad_normed_two * norm_second
    grad_hidden_rows = (
        held_rows(full_cot).astype(F32)
        + inv_held * scaled_two
        - hidden_held * inv_held * inv_held * inv_held * jnp.mean(hidden_held * scaled_two, axis=1, keepdims=True)
    )
    grad_attn = line_gather(grad_hidden_rows.astype(BF16), chips, 0, 8)
    layer_out = (columns(hidden, 1).astype(F32) + line_reduce(moe_out, chips, 1, 9)).astype(BF16)

    grad_mid_router = nt(grad_logits, chosen_router).astype(BF16)
    grad_mid_out = nt(grad_attn, chosen_b[3]).astype(BF16)
    grad_attended = nt(grad_attn, out_map).astype(BF16)
    grad_b_out = tn(mid_out, columns(grad_attn, 1))
    grad_a_out = tn(attended, grad_mid_out)
    grad_heads = grad_attended.reshape(seq_len, head_count, HD)

    def back_block(carried, packed):
        key_acc, value_acc = carried
        start_row, log_total = packed
        block_query, scores = block_scores(start_row)
        weights = jnp.exp(scores - log_total[:, :, None])
        block_grad = lax.dynamic_slice_in_dim(grad_heads, start_row, block_rows, 0)
        grad_weights = jnp.einsum("qhd,khd->hqk", block_grad, value_rows, preferred_element_type=F32)
        row_dot = jnp.sum(weights * grad_weights, axis=2, keepdims=True)
        grad_scores = (weights * (grad_weights - row_dot)).astype(BF16)
        query_block = (
            jnp.einsum("hqk,khd->qhd", grad_scores, rot_key, preferred_element_type=F32)
            * score_scale
        )
        key_acc = (
            key_acc
            + jnp.einsum("hqk,qhd->khd", grad_scores, block_query, preferred_element_type=F32)
            * score_scale
        )
        value_acc = value_acc + jnp.einsum(
            "hqk,qhd->khd", weights.astype(BF16), block_grad, preferred_element_type=F32
        )
        return ((key_acc, value_acc), query_block)

    zero_heads = jnp.zeros((seq_len, head_count, HD), F32)
    (grad_key_rot, grad_value_all), query_blocks = lax.scan(
        back_block, (zero_heads, zero_heads), (starts, log_totals)
    )
    grad_query_rot = query_blocks.reshape(seq_len, head_count, HD)
    scaled_query = (
        unrotate(grad_query_rot, cosine_table, sine_table).reshape(seq_len, head_width) * gain_query
    )
    scaled_key = (
        unrotate(grad_key_rot, cosine_table, sine_table).reshape(seq_len, head_width) * gain_key
    )
    norm_stats = col_sum(
        (jnp.sum(proj_query * scaled_query, axis=1), jnp.sum(proj_key * scaled_key, axis=1)), 10
    )
    grad_proj_query = (
        inv_query * scaled_query
        - proj_query * inv_query * inv_query * inv_query * norm_stats[0][:, None] / full_width
    ).astype(BF16)
    grad_proj_key = (
        inv_key * scaled_key
        - proj_key * inv_key * inv_key * inv_key * norm_stats[1][:, None] / full_width
    ).astype(BF16)
    grad_proj_value = grad_value_all.reshape(seq_len, head_width).astype(BF16)
    part_query = nt(grad_proj_query, b_query).astype(BF16)
    part_key = nt(grad_proj_key, b_key).astype(BF16)
    part_value = nt(grad_proj_value, b_value).astype(BF16)
    part_middle = jnp.concatenate([part_query, part_key, part_value], axis=1)
    normed_part = (
        nt(grad_proj_query, w_query) + nt(grad_proj_key, w_key) + nt(grad_proj_value, w_value)
        + nt(part_middle, a_three)
    )
    first_stat = jnp.sum(input_f32 * norm_first * normed_part, axis=1)
    total_stat = col_sum((first_stat,), 11)[0]
    normed_own = line_reduce(normed_part.astype(BF16), chips, 1, 12)
    grad_inputs = (
        columns(grad_attn, 1).astype(F32)
        + inv_first * columns(norm_first, 0) * normed_own
        - inputs.astype(F32) * inv_first * inv_first * inv_first * total_stat[:, None] / full_width
    )
    grad_middle = jnp.sum(
        small_gather(part_middle.reshape(-1, 128), col_count, 13).astype(F32), axis=0
    ).reshape(seq_len, 3 * rank_count).astype(BF16)
    grad_a_three = tn(columns(normed, 1), grad_middle)
    grad_a_router = tn(columns(normed_two, 1), grad_mid_router)
    grad_a_stack = jnp.stack(
        [
            grad_a_three[:, :rank_count],
            grad_a_three[:, rank_count : 2 * rank_count],
            grad_a_three[:, 2 * rank_count :],
            grad_a_out,
            grad_a_router,
        ]
    )
    grad_b_stack = jnp.stack(
        [
            tn(mid_query, grad_proj_query),
            tn(mid_key, grad_proj_key),
            tn(mid_value, grad_proj_value),
            grad_b_out,
        ]
    )
    grad_router_one = tn(mid_router, grad_logits)
    adapter_count = adapter_a.shape[1]
    held_adapters = adapter_count // row_count
    flat = jnp.concatenate(
        [
            grad_a_stack.reshape(-1, 128),
            grad_b_stack.reshape(-1, 128),
            grad_router_one.reshape(-1, 128),
            jnp.broadcast_to(adapter_slot.astype(F32), (8, 128)),
        ]
    ).astype(BF16)
    every = lax.all_gather(flat, "row", axis=0).astype(F32)
    owners = every[:, -1, 0]
    held_ids = (row_index * held_adapters + jnp.arange(held_adapters)).astype(F32)
    pick = (owners[None, :] == held_ids[:, None]).astype(F32)
    summed = jnp.sum(pick[:, :, None, None] * every[None], axis=1)
    a_lines = grad_a_stack.size // 128
    b_lines = grad_b_stack.size // 128
    r_lines = grad_router_one.size // 128
    grad_a = summed[:, :a_lines].reshape((held_adapters,) + grad_a_stack.shape).transpose(1, 0, 2, 3)
    grad_b = summed[:, a_lines : a_lines + b_lines].reshape((held_adapters,) + grad_b_stack.shape)
    grad_b = grad_b.transpose(1, 0, 2, 3)
    grad_router = summed[:, a_lines + b_lines : a_lines + b_lines + r_lines].reshape(
        (held_adapters,) + grad_router_one.shape
    )
    return (layer_out, grad_inputs, grad_a, grad_b, grad_router)


def solution(mesh):
    placed = (
        P("row", "col"),
        P("row", "col"),
        P(),
        P(),
        P(),
        P(),
        P(None, "col"),
        P(None, "col"),
        P(None, "col"),
        P("col", None),
        P(),
        P("col", None, "row"),
        P("col", None, "row"),
        P("col", "row", None),
        P(),
        P(),
        P(),
        P("row", None),
        P("row"),
        P("row"),
    )
    return jax.shard_map(
        shards,
        mesh=mesh,
        in_specs=placed,
        out_specs=(
            P("row", "col"),
            P("row", "col"),
            P(None, "row", "col", None),
            P(None, "row", None, "col"),
            P("row", None, None),
        ),
        check_vma=False,
    )
```

```python
import functools

import jax
import jax.numpy as jnp
from jax import lax
from jax.experimental import pallas as pl
from jax.experimental.pallas import tpu as pltpu
from jax.sharding import PartitionSpec as P

HD = 128
F32, BF16 = jnp.float32, jnp.bfloat16
MESH_ID = pl.DeviceIdType.MESH
VM = pl.BlockSpec(memory_space=pltpu.VMEM)
ANY = pl.BlockSpec(memory_space=pl.ANY)
VMEM_LIMIT = 60 * 1024 * 1024

norm_eps = 1e-05
rope_base = 10000.0
masked_score = -1e30


def nn(left, right):
    return jnp.dot(left, right, preferred_element_type=F32)


def nt(left, right):
    return lax.dot_general(left, right, (((1,), (1,)), ((), ())), preferred_element_type=F32)


def tn(left, right):
    return lax.dot_general(left, right, (((0,), (0,)), ((), ())), preferred_element_type=F32)


def remote(src, dst, send_sem, recv_sem, device):
    return pltpu.make_async_remote_copy(
        src_ref=src,
        dst_ref=dst,
        send_sem=send_sem,
        recv_sem=recv_sem,
        device_id={"col": device},
        device_id_type=MESH_ID,
    )


def line_place():
    here = lax.axis_index("col")
    core = here % 2
    return here, here // 2, core, here + 1 - 2 * core


def line_barrier(chips):
    here, chip, core, mate = line_place()
    barrier = pltpu.get_barrier_semaphore()
    has_left, has_right = chip > 0, chip < chips - 1
    pl.semaphore_signal(barrier, inc=1, device_id={"col": mate}, device_id_type=MESH_ID)

    @pl.when(has_left)
    def _():
        pl.semaphore_signal(barrier, inc=1, device_id={"col": here - 2}, device_id_type=MESH_ID)

    @pl.when(has_right)
    def _():
        pl.semaphore_signal(barrier, inc=1, device_id={"col": here + 2}, device_id_type=MESH_ID)

    inner = jnp.logical_and(has_left, has_right)

    @pl.when(inner)
    def _():
        pl.semaphore_wait(barrier, 3)

    @pl.when(jnp.logical_not(inner))
    def _():
        pl.semaphore_wait(barrier, 2)


def spot(axis, size, parts, block, part):
    rows, cols = size
    step = rows // parts
    if axis == 0:
        return (pl.ds(pl.multiple_of(block * rows + part * step, 8), step), slice(None))
    return (pl.ds(part * step, step), pl.ds(pl.multiple_of(block * cols, 128), cols))


def gather_body(chips, parts, axis, x_ref, o_ref, right_sem, left_sem, mate_sem, line_recv, mate_recv, own_sem):
    here, chip, core, mate = line_place()
    size = x_ref.shape
    step = size[0] // parts
    line_barrier(chips)

    def at(block, part):
        return o_ref.at[spot(axis, size, parts, block, part)]

    def copy(j, part, sem, recv, device, first=False, block=None):
        block = 2 * j + core if block is None else block
        src = x_ref.at[pl.ds(part * step, step)] if first else at(block, part)
        return remote(src, at(block, part), sem.at[j, part], recv.at[j, part], device)

    def forward(j, part, rightward, leftward, first):
        if rightward:

            @pl.when(chip < chips - 1)
            def _():
                copy(j, part, right_sem, line_recv, here + 2, first).start()

        if leftward:

            @pl.when(chip > 0)
            def _():
                copy(j, part, left_sem, line_recv, here - 2, first).start()

        copy(j, part, mate_sem, mate_recv, mate, first).start()

    for part in range(parts):
        forward(chip, part, True, True, True)
    own = []
    for part in range(parts):
        own.append(
            pltpu.make_async_copy(x_ref.at[pl.ds(part * step, step)], at(here, part), own_sem.at[part])
        )
        own[-1].start()
    for far in range(1, chips):
        for part in range(parts):

            @pl.when(chip - far >= 0)
            def _():
                copy(chip - far, part, right_sem, line_recv, mate).wait_recv()
                forward(chip - far, part, True, False, False)

            @pl.when(chip + far < chips)
            def _():
                copy(chip + far, part, left_sem, line_recv, mate).wait_recv()
                forward(chip + far, part, False, True, False)

    for own_copy in own:
        own_copy.wait()
    for j in range(chips):
        for part in range(parts):
            copy(j, part, mate_sem, mate_recv, mate, block=2 * j + 1 - core).wait_recv()
            copy(j, part, mate_sem, mate_recv, mate).wait_send()

            @pl.when(jnp.logical_and(j <= chip, chip < chips - 1))
            def _():
                copy(j, part, right_sem, line_recv, here + 2).wait_send()

            @pl.when(jnp.logical_and(j >= chip, chip > 0))
            def _():
                copy(j, part, left_sem, line_recv, here - 2).wait_send()


def line_gather(x, chips, axis, ident, parts=2):
    rows, cols = x.shape
    sems = pltpu.SemaphoreType.DMA((chips, parts))
    shape = (2 * chips * rows, cols) if axis == 0 else (rows, 2 * chips * cols)
    return pl.pallas_call(
        functools.partial(gather_body, chips, parts, axis),
        out_shape=jax.ShapeDtypeStruct(shape, x.dtype),
        in_specs=[VM],
        out_specs=VM,
        scratch_shapes=[sems] * 5 + [pltpu.SemaphoreType.DMA((parts,))],
        compiler_params=pltpu.CompilerParams(
            collective_id=ident, has_side_effects=True, vmem_limit_bytes=VMEM_LIMIT
        ),
        name="line_gather",
    )(x)


def reduce_body(
    chips, parts, axis, p_ref, o_ref, pair_buf, line_buf, sums, right_sem, left_sem, mate_sem, line_recv, mate_recv
):
    here, chip, core, mate = line_place()
    size = o_ref.shape
    step = size[0] // parts
    line_barrier(chips)

    def rows(part):
        return pl.ds(part * step, step)

    def at(block, part):
        return spot(axis, size, parts, block, part)

    def mate_copy(j, part):
        return remote(
            p_ref.at[at(2 * j + 1 - core, part)],
            pair_buf.at[j, rows(part)],
            mate_sem.at[j, part],
            mate_recv.at[j, part],
            mate,
        )

    def line_copy(j, slot, part, sem, device):
        return remote(
            sums.at[j, rows(part)], line_buf.at[slot, rows(part)], sem.at[j, part], line_recv.at[slot, part], device
        )

    for far in range(chips - 1, -1, -1):
        for part in range(parts):

            @pl.when(chip + far < chips)
            def _():
                mate_copy(chip + far, part).start()

            if far > 0:

                @pl.when(chip - far >= 0)
                def _():
                    mate_copy(chip - far, part).start()

    def pair_sum(j, part):
        mate_copy(j, part).wait_recv()
        return p_ref[at(2 * j + core, part)].astype(F32) + pair_buf[j, rows(part)].astype(F32)

    def pass_on(j, slot, part, more, sem, device):
        @pl.when(more)
        def _():
            line_copy(j, j, part, sem, mate).wait_recv()
            total = pair_sum(j, part) + line_buf[j, rows(part)].astype(F32)
            sums[j, rows(part)] = total.astype(BF16)

        @pl.when(jnp.logical_not(more))
        def _():
            sums[j, rows(part)] = pair_sum(j, part).astype(BF16)

        line_copy(j, slot, part, sem, device).start()

    for far in range(chips - 1, 0, -1):
        for part in range(parts):

            @pl.when(chip + far < chips)
            def _():
                pass_on(chip + far, chip + far, part, chip > 0, right_sem, here + 2)

            @pl.when(chip - far >= 0)
            def _():
                pass_on(
                    chip - far, chips if far == 1 else chip - far, part, chip < chips - 1, left_sem, here - 2
                )

    for part in range(parts):
        o_ref[rows(part)] = pair_sum(chip, part)

        @pl.when(chip > 0)
        def _():
            line_copy(chip, chip, part, right_sem, mate).wait_recv()
            o_ref[rows(part)] += line_buf[chip, rows(part)].astype(F32)

        @pl.when(chip < chips - 1)
        def _():
            line_copy(chip, chips, part, left_sem, mate).wait_recv()
            o_ref[rows(part)] += line_buf[chips, rows(part)].astype(F32)

    for j in range(chips):
        for part in range(parts):
            mate_copy(j, part).wait_send()

            @pl.when(j > chip)
            def _():
                line_copy(j, j, part, right_sem, mate).wait_send()

            @pl.when(j < chip)
            def _():
                line_copy(j, j, part, left_sem, mate).wait_send()


def line_reduce(p, chips, axis, ident, parts=2):
    rows, cols = p.shape
    if axis == 0:
        rows //= 2 * chips
    else:
        cols //= 2 * chips
    sems = pltpu.SemaphoreType.DMA((chips, parts))
    return pl.pallas_call(
        functools.partial(reduce_body, chips, parts, axis),
        out_shape=jax.ShapeDtypeStruct((rows, cols), F32),
        in_specs=[VM],
        out_specs=VM,
        scratch_shapes=[
            pltpu.VMEM((chips, rows, cols), BF16),
            pltpu.VMEM((chips + 1, rows, cols), BF16),
            pltpu.VMEM((chips, rows, cols), BF16),
            sems,
            sems,
            sems,
            pltpu.SemaphoreType.DMA((chips + 1, parts)),
            sems,
        ],
        compiler_params=pltpu.CompilerParams(
            collective_id=ident, has_side_effects=True, vmem_limit_bytes=VMEM_LIMIT
        ),
        name="line_reduce",
    )(p)


def small_body(count, x_ref, o_ref, send_sem, recv_sem):
    here = lax.axis_index("col")
    barrier = pltpu.get_barrier_semaphore()
    for hop in range(1, count):
        other = lax.rem(here + hop, count)
        pl.semaphore_signal(barrier, inc=1, device_id={"col": other}, device_id_type=MESH_ID)
    o_ref[here] = x_ref[...]
    pl.semaphore_wait(barrier, count - 1)

    def copy(hop, block):
        other = lax.rem(here + hop, count)
        return remote(x_ref, o_ref.at[block], send_sem.at[hop], recv_sem.at[hop], other)

    for hop in range(1, count):
        copy(hop, here).start()
    for hop in range(1, count):
        copy(hop, lax.rem(here + count - hop, count)).wait_recv()
    for hop in range(1, count):
        copy(hop, here).wait_send()


def small_gather(x, count, ident):
    sems = pltpu.SemaphoreType.DMA((count,))
    return pl.pallas_call(
        functools.partial(small_body, count),
        out_shape=jax.ShapeDtypeStruct((count,) + x.shape, x.dtype),
        in_specs=[VM],
        out_specs=VM,
        scratch_shapes=[sems, sems],
        compiler_params=pltpu.CompilerParams(collective_id=ident, has_side_effects=True),
        name="small_gather",
    )(x)


def turn_body(chips, parts, first, last, held, late_count, *refs):
    p_ref = refs[0]
    operands = refs[1 : 1 + held]
    o_ref = refs[1 + held]
    results = refs[2 + held : 2 + held + late_count]
    sums_in, pair_buf, line_buf, sums = refs[2 + held + late_count : 6 + held + late_count]
    reduce_sems = refs[6 + held + late_count : 11 + held + late_count]
    gather_sems = refs[11 + held + late_count : 16 + held + late_count]
    reduce_body(chips, parts, 0, p_ref, sums_in, pair_buf, line_buf, sums, *reduce_sems)
    here = lax.axis_index("col")
    own = o_ref.shape[0] // (2 * chips)
    kept = first(sums_in, operands, results, o_ref, pl.ds(pl.multiple_of(here * own, 8), own))
    gather_rows(chips, parts, o_ref, *gather_sems, lambda: last(kept, operands, results))


def gather_rows(chips, parts, o_ref, right_sem, left_sem, mate_sem, line_recv, mate_recv, beside):
    here, chip, core, mate = line_place()
    size = (o_ref.shape[0] // (2 * chips), o_ref.shape[1])

    def copy(j, part, sem, recv, device, block=None):
        block = 2 * j + core if block is None else block
        ref = o_ref.at[spot(0, size, parts, block, part)]
        return remote(ref, ref, sem.at[j, part], recv.at[j, part], device)

    def forward(j, part, rightward, leftward):
        if rightward:

            @pl.when(chip < chips - 1)
            def _():
                copy(j, part, right_sem, line_recv, here + 2).start()

        if leftward:

            @pl.when(chip > 0)
            def _():
                copy(j, part, left_sem, line_recv, here - 2).start()

        copy(j, part, mate_sem, mate_recv, mate).start()

    for part in range(parts):
        forward(chip, part, True, True)
    beside()
    for far in range(1, chips):
        for part in range(parts):

            @pl.when(chip - far >= 0)
            def _():
                copy(chip - far, part, right_sem, line_recv, mate).wait_recv()
                forward(chip - far, part, True, False)

            @pl.when(chip + far < chips)
            def _():
                copy(chip + far, part, left_sem, line_recv, mate).wait_recv()
                forward(chip + far, part, False, True)

    for j in range(chips):
        for part in range(parts):
            copy(j, part, mate_sem, mate_recv, mate, block=2 * j + 1 - core).wait_recv()
            copy(j, part, mate_sem, mate_recv, mate).wait_send()

            @pl.when(jnp.logical_and(j <= chip, chip < chips - 1))
            def _():
                copy(j, part, right_sem, line_recv, here + 2).wait_send()

            @pl.when(jnp.logical_and(j >= chip, chip > 0))
            def _():
                copy(j, part, left_sem, line_recv, here - 2).wait_send()


def line_turn(p, operands, width, results, first, last, chips, ident, parts=2):
    rows, cols = p.shape
    own = rows // (2 * chips)
    sems = pltpu.SemaphoreType.DMA((chips, parts))
    longer = pltpu.SemaphoreType.DMA((chips + 1, parts))
    return pl.pallas_call(
        functools.partial(turn_body, chips, parts, first, last, len(operands), len(results)),
        out_shape=(jax.ShapeDtypeStruct((rows, width), BF16),) + tuple(results),
        in_specs=[VM] * (1 + len(operands)),
        out_specs=(VM,) * (1 + len(results)),
        scratch_shapes=[
            pltpu.VMEM((own, cols), F32),
            pltpu.VMEM((chips, own, cols), BF16),
            pltpu.VMEM((chips + 1, own, cols), BF16),
            pltpu.VMEM((chips, own, cols), BF16),
            sems,
            sems,
            sems,
            longer,
            sems,
        ]
        + [sems] * 5,
        compiler_params=pltpu.CompilerParams(
            collective_id=ident, has_side_effects=True, vmem_limit_bytes=VMEM_LIMIT
        ),
        name="line_turn",
    )(p, *operands)


def inverse_rms(values):
    return lax.rsqrt(jnp.mean(values * values, axis=1, keepdims=True) + norm_eps)


def turn_forward(width, experts, sums, operands, results, o_ref, own):
    x_ref, gain_ref, a_ref, router_ref, up_ref = operands
    hidden_ref, mid_ref, mid_router_ref, probs_ref = results
    hidden = x_ref[...].astype(F32) + sums[:, :width]
    mid_ref[...] = sums[:, width:].astype(BF16)
    hidden_ref[...] = hidden
    normed = (hidden * inverse_rms(hidden) * gain_ref[...]).astype(BF16)
    o_ref[own, :width] = normed
    mid_router = nt(normed, a_ref[...]).astype(BF16)
    mid_router_ref[...] = mid_router
    logits = nt(normed, router_ref[...]) + nn(mid_router, up_ref[...])
    lane = lax.broadcasted_iota(jnp.int32, logits.shape, 1)
    logits = jnp.where(lane < experts, logits, masked_score)
    exponent = jnp.exp(logits - jnp.max(logits, axis=1, keepdims=True))
    probs = exponent / jnp.sum(exponent, axis=1, keepdims=True)
    probs_ref[...] = probs
    high = probs.astype(BF16)
    rest = probs - high.astype(F32)
    o_ref[own, width:] = (high.astype(F32) + pltpu.roll(rest, experts, 1)).astype(BF16)
    return None


def turn_backward(width, experts, sums, operands, results, o_ref, own):
    g_ref, hidden_ref, gain_ref, a_ref, router_ref, up_ref, probs_ref, mid_router_ref, mid_ref = operands
    pair = sums[:, width:]
    lanes = pair.shape[1]
    grad_probs = pair + pltpu.roll(pair, lanes - experts, 1)
    probs = probs_ref[...]
    grad_logits = (probs * (grad_probs - jnp.sum(probs * grad_probs, axis=1, keepdims=True))).astype(BF16)
    grad_mid = nt(grad_logits, up_ref[...]).astype(BF16)
    grad_normed = sums[:, :width] + nn(grad_logits, router_ref[...]) + nn(grad_mid, a_ref[...])
    hidden = hidden_ref[...]
    inv = inverse_rms(hidden)
    scaled = grad_normed * gain_ref[...]
    grad_hidden = (
        g_ref[...].astype(F32)
        + inv * scaled
        - hidden * (inv * inv * inv * jnp.mean(hidden * scaled, axis=1, keepdims=True))
    )
    grad_hidden = grad_hidden.astype(BF16)
    o_ref[own, :] = grad_hidden
    return grad_logits, grad_mid, grad_hidden


def turn_late(kept, operands, results):
    _, hidden_ref, gain_ref, _, _, _, _, mid_router_ref, mid_ref = operands
    grad_logits, grad_mid, grad_hidden = kept
    hidden = hidden_ref[...]
    normed = (hidden * inverse_rms(hidden) * gain_ref[...]).astype(BF16)
    rank = grad_mid.shape[1]
    late_ref, router_ref = results
    late_ref[pl.ds(0, rank)] = tn(grad_mid, normed)
    late_ref[pl.ds(rank, rank)] = tn(mid_ref[:, :rank], grad_hidden)
    router_ref[...] = tn(mid_router_ref[...], grad_logits)


def row_sums(values):
    high = values.astype(BF16)
    rest = (values - high.astype(F32)).astype(BF16)
    ones = jnp.ones((8, values.shape[1]), BF16)
    return nt(ones, high) + nt(ones, rest)


def project_body(tile, x_ref, gain_ref, wq, wk, wv, a_ref, b_ref, proj_ref, mid_ref, inv_ref, sq_ref):
    part = wq.shape[1]
    for t in range(x_ref.shape[0] // tile):
        rows = pl.ds(t * tile, tile)
        x = x_ref[rows].astype(F32)
        inv = inverse_rms(x)
        inv_ref[rows] = inv
        normed = (x * inv * gain_ref[...]).astype(BF16)
        mid = nt(normed, a_ref[...]).astype(BF16)
        mid_ref[rows] = mid
        for m, w in enumerate((wq, wk, wv)):
            cols = pl.ds(m * part, part)
            proj = nn(normed, w[...]) + nn(mid, b_ref[:, cols])
            proj_ref[rows, cols] = proj
            if m < 2:
                sq_ref[pl.ds(m, 1), rows] = row_sums(proj * proj)[0:1]


def project(x, gain, weights, a_rows, b_cols):
    seq_len, width = x.shape
    part = weights[0].shape[1]
    rank = a_rows.shape[0]
    return pl.pallas_call(
        functools.partial(project_body, min(256, seq_len)),
        out_shape=(
            jax.ShapeDtypeStruct((seq_len, 3 * part), F32),
            jax.ShapeDtypeStruct((seq_len, rank), BF16),
            jax.ShapeDtypeStruct((seq_len, 1), F32),
            jax.ShapeDtypeStruct((2, seq_len), F32),
        ),
        in_specs=[VM] * 7,
        out_specs=(VM,) * 4,
        compiler_params=pltpu.CompilerParams(vmem_limit_bytes=VMEM_LIMIT),
        name="project",
    )(x, gain, *weights, a_rows, b_cols)


def key_limit(start, tile, seq_len, reach):
    return min(seq_len, max(start + tile, reach))


def allowed_keys(start, tile, limit, prefix_len):
    query = start + lax.broadcasted_iota(jnp.int32, (tile, limit), 0)
    key = lax.broadcasted_iota(jnp.int32, (tile, limit), 1)
    return jnp.logical_or(key <= query, key < prefix_len)


def attend_body(
    tile, reach, scale, prefix_ref, proj_ref, inv_ref, gains_ref, cos_ref, sin_ref, map_ref,
    p_ref, att_ref, q_ref, k_ref, v_ref, log_ref,
):
    seq_len, part = att_ref.shape
    prefix_len = prefix_ref[0]
    for h in range(part // HD):
        cols = pl.ds(h * HD, HD)
        for m, ref in ((0, q_ref), (1, k_ref)):
            plain = proj_ref[:, pl.ds(m * part + h * HD, HD)] * inv_ref[:, m : m + 1] * gains_ref[m : m + 1, cols]
            ref[:, cols] = (plain * cos_ref[...] + pltpu.roll(plain, HD // 2, 1) * sin_ref[...]).astype(BF16)
        v_ref[:, cols] = proj_ref[:, pl.ds(2 * part + h * HD, HD)].astype(BF16)
    for start in range(0, seq_len, tile):
        rows = pl.ds(start, tile)
        limit = key_limit(start, tile, seq_len, reach)
        allowed = allowed_keys(start, tile, limit, prefix_len)
        for h in range(part // HD):
            cols = pl.ds(h * HD, HD)
            scores = nt(q_ref[rows, cols], k_ref[pl.ds(0, limit), cols]) * scale
            scores = jnp.where(allowed, scores, masked_score)
            top = jnp.max(scores, axis=1, keepdims=True)
            exponent = jnp.exp(scores - top)
            total = jnp.sum(exponent, axis=1, keepdims=True)
            weights = (exponent / total).astype(BF16)
            att_ref[rows, cols] = nn(weights, v_ref[pl.ds(0, limit), cols]).astype(BF16)
            log_ref[rows, h : h + 1] = top + jnp.log(total)
        p_ref[rows] = nn(att_ref[rows], map_ref[...]).astype(BF16)


def attend(prefix, proj, inv, gains, tables, out_map, reach, scale):
    seq_len = proj.shape[0]
    part = proj.shape[1] // 3
    heads = jax.ShapeDtypeStruct((seq_len, part), BF16)
    return pl.pallas_call(
        functools.partial(attend_body, min(256, seq_len), reach, scale),
        out_shape=(
            jax.ShapeDtypeStruct((seq_len, out_map.shape[1]), BF16),
            heads,
            heads,
            heads,
            heads,
            jax.ShapeDtypeStruct((seq_len, part // HD), F32),
        ),
        in_specs=[pl.BlockSpec(memory_space=pltpu.SMEM)] + [VM] * 6,
        out_specs=(VM,) * 6,
        compiler_params=pltpu.CompilerParams(vmem_limit_bytes=VMEM_LIMIT),
        name="attend",
    )(prefix, proj, inv, gains, *tables, out_map)


def attend_back_body(
    tile, reach, scale, prefix_ref, g_ref, map_ref, b_ref, att_ref, q_ref, k_ref, v_ref, log_ref, proj_ref,
    gains_ref, cos_ref, sin_ref, scaled_ref, dv_ref, stat_ref, ga_ref, da_ref, dq_acc, dk_acc, dv_acc,
):
    seq_len, part = att_ref.shape
    prefix_len = prefix_ref[0]
    grad_a = jnp.zeros(ga_ref.shape, F32)
    for start in range(0, seq_len, tile):
        rows = pl.ds(start, tile)
        grads = g_ref[rows]
        da_ref[rows] = nt(grads, map_ref[...]).astype(BF16)
        grad_mid = nt(grads, b_ref[...]).astype(BF16)
        grad_a += tn(grad_mid, att_ref[rows])
    ga_ref[...] = grad_a
    dk_acc[...] = jnp.zeros_like(dk_acc)
    dv_acc[...] = jnp.zeros_like(dv_acc)
    for start in range(0, seq_len, tile):
        rows = pl.ds(start, tile)
        limit = key_limit(start, tile, seq_len, reach)
        keys = pl.ds(0, limit)
        allowed = allowed_keys(start, tile, limit, prefix_len)
        for h in range(part // HD):
            cols = pl.ds(h * HD, HD)
            query, key = q_ref[rows, cols], k_ref[keys, cols]
            grads = da_ref[rows, cols]
            scores = jnp.where(allowed, nt(query, key) * scale, masked_score)
            weights = jnp.exp(scores - log_ref[rows, h : h + 1])
            grad_weights = nt(grads, v_ref[keys, cols])
            dot = jnp.sum(weights * grad_weights, axis=1, keepdims=True)
            grad_scores = (weights * (grad_weights - dot)).astype(BF16)
            dq_acc[rows, cols] = nn(grad_scores, key) * scale
            dk_acc[keys, cols] += tn(grad_scores, query) * scale
            dv_acc[keys, cols] += tn(weights.astype(BF16), grads)
    dv_ref[...] = dv_acc[...].astype(BF16)
    for m, acc in ((0, dq_acc), (1, dk_acc)):
        for start in range(0, seq_len, tile):
            rows = pl.ds(start, tile)
            total = jnp.zeros((8, tile), F32)
            for h in range(part // HD):
                cols = pl.ds(h * HD, HD)
                here = pl.ds(m * part + h * HD, HD)
                plain = acc[rows, cols]
                turned = plain * cos_ref[rows] - pltpu.roll(plain, HD // 2, 1) * sin_ref[rows]
                scaled = turned * gains_ref[m : m + 1, cols]
                scaled_ref[rows, here] = scaled
                total += row_sums(proj_ref[rows, here] * scaled)
            stat_ref[pl.ds(m, 1), rows] = total[0:1]


def attend_back(prefix, grads, out_map, b_out, saved, proj, gains, tables, reach, scale):
    seq_len = proj.shape[0]
    part = proj.shape[1] // 3
    return pl.pallas_call(
        functools.partial(attend_back_body, min(256, seq_len), reach, scale),
        out_shape=(
            jax.ShapeDtypeStruct((seq_len, 2 * part), F32),
            jax.ShapeDtypeStruct((seq_len, part), BF16),
            jax.ShapeDtypeStruct((2, seq_len), F32),
            jax.ShapeDtypeStruct((b_out.shape[0], part), F32),
        ),
        in_specs=[pl.BlockSpec(memory_space=pltpu.SMEM)] + [VM] * 12,
        out_specs=(VM,) * 4,
        scratch_shapes=[pltpu.VMEM((seq_len, part), BF16)] + [pltpu.VMEM((seq_len, part), F32)] * 3,
        compiler_params=pltpu.CompilerParams(vmem_limit_bytes=VMEM_LIMIT),
        name="attend_back",
    )(prefix, grads, out_map, b_out, *saved, proj, gains, *tables)


def inputs_back_body(
    tile, extra, scaled_ref, dv_ref, proj_ref, inv_ref, stat_ref, wq, wk, wv, b_ref, a_ref, x_ref, inv1_ref,
    gain_ref, mid_ref, late_ref, router_ref, p_ref, gb_ref,
):
    seq_len, width = x_ref.shape
    part = dv_ref.shape[1]
    ranks = a_ref.shape[0]
    rank = ranks // 3
    grad_b = [jnp.zeros((rank, part), F32) for _ in range(3)]
    grad_a = jnp.zeros((ranks, width), F32)
    stats = jnp.zeros((8, width), F32)
    line = lax.broadcasted_iota(jnp.int32, (8, width), 0)
    for t in range(seq_len // tile):
        rows = pl.ds(t * tile, tile)
        normed_part = jnp.zeros((tile, width), F32)
        middles = []
        for m, w in enumerate((wq, wk, wv)):
            if m < 2:
                cols = pl.ds(m * part, part)
                inv = inv_ref[rows, m : m + 1]
                shift = inv * inv * inv * stat_ref[rows, m : m + 1]
                grad = (inv * scaled_ref[rows, cols] - proj_ref[rows, cols] * shift).astype(BF16)
            else:
                grad = dv_ref[rows]
            middles.append(nt(grad, b_ref[pl.ds(m * rank, rank)]).astype(BF16))
            normed_part += nt(grad, w[...]) + nn(middles[m], a_ref[pl.ds(m * rank, rank)])
            grad_b[m] += tn(mid_ref[rows, m * rank : (m + 1) * rank], grad)
        p_ref[rows] = normed_part.astype(BF16)
        scaled_x = x_ref[rows].astype(F32) * gain_ref[...]
        normed = (scaled_x * inv1_ref[rows]).astype(BF16)
        grad_a += jnp.concatenate([tn(middle, normed) for middle in middles], axis=0)
        first = row_sums(scaled_x * normed_part)
        for j in range(tile // part):
            wide = jnp.concatenate([first[:, j * part : (j + 1) * part]] * (width // part), axis=1)
            stats = jnp.where(line == (t * tile) // part + j, wide, stats)
    for m in range(3):
        gb_ref[pl.ds(m * rank, rank)] = grad_b[m]
    high = stats.astype(BF16).astype(F32)
    router = router_ref[...]
    if part > router.shape[1]:
        router = jnp.concatenate([router, jnp.zeros((rank, part - router.shape[1]), F32)], axis=1)
    pieces = [
        grad_a,
        late_ref[...],
        jnp.concatenate([router] * (width // part), axis=1),
        high,
        stats - high,
    ]
    used = sum(piece.shape[0] for piece in pieces)
    pieces.append(jnp.zeros((extra - used, width), F32))
    start = seq_len
    p_ref[pl.ds(start, extra)] = jnp.concatenate(pieces, axis=0).astype(BF16)


def inputs_back(extra, *operands):
    x = operands[10]
    seq_len, width = x.shape
    part = operands[1].shape[1]
    ranks = operands[9].shape[0]
    return pl.pallas_call(
        functools.partial(inputs_back_body, min(256, seq_len), extra),
        out_shape=(
            jax.ShapeDtypeStruct((seq_len + extra, width), BF16),
            jax.ShapeDtypeStruct((ranks, part), F32),
        ),
        in_specs=[VM] * len(operands),
        out_specs=(VM,) * 2,
        compiler_params=pltpu.CompilerParams(vmem_limit_bytes=VMEM_LIMIT),
        name="inputs_back",
    )(*operands)


def moe_body(experts, chosen, tile, done, x_ref, g_ref, routes_ref, *refs):
    count = len(chosen)
    weights = refs[: 3 * count]
    refs = refs[3 * count :]
    if done:
        earlier, hidden_ref, refs = refs[:3], refs[3], refs[4:]
    out_ref, dx_ref = refs[:2]
    gate_ref = None if done else refs[2]
    out_acc, dx_acc, gate_acc, wgu, wd, sems = refs[2 if done else 3 :]
    hidden = wd.shape[1]
    tokens, width = g_ref.shape
    lanes = gate_acc.shape[1]
    pieces = weights[0].shape[2] // hidden
    here = lax.axis_index("col")
    local = experts // lax.axis_size("col")

    def copies(a, piece, slot):
        gate, up, down = weights[3 * a : 3 * a + 3]
        which, at_gate, at_down = chosen[a]
        units = pl.ds(pl.multiple_of(piece * hidden, 128), hidden)
        return (
            pltpu.make_async_copy(gate.at[at_gate, :, units], wgu.at[slot, :, pl.ds(0, hidden)], sems.at[slot, 0]),
            pltpu.make_async_copy(up.at[at_gate, :, units], wgu.at[slot, :, pl.ds(hidden, hidden)], sems.at[slot, 1]),
            pltpu.make_async_copy(down.at[at_down, units], wd.at[slot], sems.at[slot, 2]),
        )

    for copy in copies(0, 0, 0):
        copy.start()
    if done:
        out_acc[...] = earlier[0][...].astype(F32)
        dx_acc[...] = earlier[1][...].astype(F32)
        gate_acc[...] = earlier[2][...]
        own = hidden_ref.shape[0]
        out_acc[pl.ds(pl.multiple_of(here * own, 8), own)] += hidden_ref[...]
    else:
        out_acc[...] = jnp.zeros_like(out_acc)
        dx_acc[...] = jnp.zeros_like(dx_acc)
        gate_acc[...] = jnp.zeros_like(gate_acc)

    for a in range(count):
        e = here * local + chosen[a][0]

        def one_step(piece, carry):
            slot = piece % 2
            for copy in copies(a, 0, slot):
                copy.wait()

            @pl.when(piece + 1 < pieces)
            def _():
                for copy in copies(a, piece + 1, 1 - slot):
                    copy.start()

            if a + 1 < count:

                @pl.when(piece + 1 == pieces)
                def _():
                    for copy in copies(a + 1, 0, 1 - slot):
                        copy.start()

            def one_tile(t, carry):
                rows = pl.ds(pl.multiple_of(t * tile, tile), tile)
                lane = lax.broadcasted_iota(jnp.int32, (tile, lanes), 1)
                mine = lane == e
                halves = jnp.logical_or(mine, lane == e + experts)
                named = jnp.sum(jnp.where(routes_ref[rows] == e, 1.0, 0.0), axis=1, keepdims=True)
                gate = jnp.sum(jnp.where(halves, x_ref[rows, width:].astype(F32), 0.0), axis=1, keepdims=True)
                gate = gate * named
                both = nn(x_ref[rows, :width], wgu[slot])
                gate_in, up_in = both[:, :hidden], both[:, hidden:]
                sigmoid = jax.nn.sigmoid(gate_in)
                silu = gate_in * sigmoid
                active = silu * up_in
                back = nt(g_ref[rows], wd[slot])
                d_gate = jnp.sum(active * back, axis=1, keepdims=True) * named
                gate_acc[rows] += jnp.where(mine, d_gate, 0.0)
                out_acc[rows] += nn((active * gate).astype(BF16), wd[slot])
                d_active = back * gate
                d_gate_in = d_active * up_in * (sigmoid + silu * (1.0 - sigmoid))
                d_up_in = d_active * silu
                d_both = jnp.concatenate([d_gate_in.astype(BF16), d_up_in.astype(BF16)], axis=1)
                dx_acc[rows] += nt(d_both, wgu[slot])
                return carry

            return lax.fori_loop(0, tokens // tile, one_tile, carry)

        lax.fori_loop(0, pieces, one_step, 0)
    out_ref[...] = out_acc[...].astype(BF16)
    if done:
        dx_ref[:, :width] = dx_acc[...].astype(BF16)
        high = gate_acc[...].astype(BF16).astype(F32)
        rest = gate_acc[...] - high
        dx_ref[:, width:] = (high + pltpu.roll(rest, experts, 1)).astype(BF16)
    else:
        dx_ref[...] = dx_acc[...].astype(BF16)
        gate_ref[...] = gate_acc[...]


def moe(x, g, routes, experts, chosen, weights, earlier=None, hidden_rows=None, tile=512):
    tokens, width = g.shape
    units = weights[0].shape[2]
    hidden = min(256, units)
    lanes = x.shape[1] - width
    done = earlier is not None
    outs = [jax.ShapeDtypeStruct((tokens, width), BF16)]
    outs.append(jax.ShapeDtypeStruct((tokens, width + (lanes if done else 0)), BF16))
    if not done:
        outs.append(jax.ShapeDtypeStruct((tokens, lanes), F32))
    more = (tuple(earlier) + (hidden_rows,)) if done else ()
    return pl.pallas_call(
        functools.partial(moe_body, experts, chosen, min(tile, tokens), done),
        out_shape=tuple(outs),
        in_specs=[VM] * 3 + [ANY] * len(weights) + [VM] * len(more),
        out_specs=(VM,) * len(outs),
        scratch_shapes=[
            pltpu.VMEM((tokens, width), F32),
            pltpu.VMEM((tokens, width), F32),
            pltpu.VMEM((tokens, lanes), F32),
            pltpu.VMEM((2, width, 2 * hidden), BF16),
            pltpu.VMEM((2, hidden, width), BF16),
            pltpu.SemaphoreType.DMA((2, 3)),
        ],
        compiler_params=pltpu.CompilerParams(vmem_limit_bytes=VMEM_LIMIT),
        name="moe",
    )(x, g, routes, *weights, *more)


def rope_tables(length, head_dim):
    half_dim = head_dim // 2
    frequency = rope_base ** (-(2.0 * jnp.arange(half_dim, dtype=F32)) / head_dim)
    angles = jnp.arange(length, dtype=F32)[:, None] * frequency[None, :]
    cosine, sine = jnp.cos(angles), jnp.sin(angles)
    return jnp.concatenate([cosine, cosine], axis=1), jnp.concatenate([-sine, sine], axis=1)


def shards(
    inputs,
    cotangent,
    norm_first,
    norm_second,
    query_gain,
    key_gain,
    w_query,
    w_key,
    w_value,
    w_out,
    w_router,
    w_gate,
    w_up,
    w_down,
    adapter_a,
    adapter_b,
    adapter_router,
    routes,
    prefix,
    adapter_index,
):
    seq_len, width_part = inputs.shape
    col_count = lax.axis_size("col")
    row_count = lax.axis_size("row")
    col_index = lax.axis_index("col")
    row_index = lax.axis_index("row")
    chips = col_count // 2
    full_width = width_part * col_count
    head_width = w_query.shape[1]
    local_experts = w_gate.shape[0]
    expert_total = w_router.shape[1]
    feature_start = col_index * width_part
    head_start = col_index * head_width
    own_rows = seq_len // col_count
    row_start = col_index * own_rows
    score_scale = HD ** (-0.5)
    reach = seq_len // 2
    lanes = 128

    def columns(array, axis_num):
        return lax.dynamic_slice_in_dim(array, feature_start, width_part, axis_num)

    def head_cols(array, axis_num=1):
        return lax.dynamic_slice_in_dim(array, head_start, head_width, axis_num)

    def held_rows(array):
        return lax.dynamic_slice_in_dim(array, row_start, own_rows, 0)

    def col_sum(pair, ident):
        return jnp.sum(small_gather(pair, col_count, ident), axis=0)

    full_gate = lax.all_gather(w_gate, "row", axis=2, tiled=True)
    full_up = lax.all_gather(w_up, "row", axis=2, tiled=True)
    full_down = [
        lax.all_gather(w_down[e : e + 1], "row", axis=1, tiled=True) for e in range(local_experts)
    ]
    adapter_slot = adapter_index[0]
    chosen_a = lax.dynamic_index_in_dim(adapter_a, adapter_slot, 1, keepdims=False).swapaxes(1, 2)
    chosen_b = lax.dynamic_index_in_dim(adapter_b, adapter_slot, 1, keepdims=False)
    chosen_router = lax.dynamic_index_in_dim(adapter_router, adapter_slot, 0, keepdims=False)
    rank = chosen_a.shape[1]
    a_three = chosen_a[:3].reshape(3 * rank, full_width)
    b_three = head_cols(chosen_b[:3].reshape(3 * rank, full_width))
    blank = jnp.zeros((rank, head_width), BF16)
    b_cols = jnp.concatenate(
        [
            jnp.concatenate([b_three[m * rank : (m + 1) * rank] if n == m else blank for n in range(3)], axis=0)
            for m in range(3)
        ],
        axis=1,
    )
    a_out = head_cols(chosen_a[3])
    out_map = (w_out.astype(F32) + tn(a_out, chosen_b[3])).astype(BF16)
    out_wide = jnp.concatenate([out_map, a_out.T, jnp.zeros((head_width, lanes - rank), BF16)], axis=1)
    router_rows = jnp.pad(w_router.T, ((0, lanes - expert_total), (0, 0)))
    router_up = jnp.pad(chosen_router, ((0, 0), (0, lanes - expert_total)))
    gains = jnp.stack([head_cols(query_gain, 0), head_cols(key_gain, 0)])
    tables = rope_tables(seq_len, HD)
    gain_first, gain_second = norm_first[None], norm_second[None]

    full_inputs = line_gather(inputs, chips, 1, 0)
    proj, mid, inv_first, squares = project(
        full_inputs, gain_first, (w_query, w_key, w_value), a_three, b_cols
    )
    inv = lax.rsqrt(col_sum(squares, 1) / full_width + norm_eps).T
    part_out, attended, rot_query, rot_key, value_rows, log_totals = attend(
        prefix, proj, inv, gains, tables, out_wide, reach, score_scale
    )
    wide = full_width + lanes
    row_shape = jax.ShapeDtypeStruct
    normed_two, hidden_rows, mid_out, mid_router, probs = line_turn(
        part_out,
        (held_rows(full_inputs), gain_second, chosen_a[4], router_rows, router_up),
        wide,
        (
            row_shape((own_rows, full_width), F32),
            row_shape((own_rows, lanes), BF16),
            row_shape((own_rows, rank), BF16),
            row_shape((own_rows, lanes), F32),
        ),
        functools.partial(turn_forward, full_width, expert_total),
        lambda kept, operands, results: None,
        chips,
        2,
    )
    full_cot = line_gather(cotangent, chips, 1, 4)

    early = tuple((e, e, 0) for e in range(local_experts - 1)) if local_experts > 1 else ()
    final = ((local_experts - 1, local_experts - 1, 0),)
    first = moe(
        normed_two,
        full_cot,
        routes,
        expert_total,
        early,
        sum([(full_gate, full_up, full_down[e]) for e, _, _ in early], ()),
    )
    moe_out, back_out = moe(
        normed_two,
        full_cot,
        routes,
        expert_total,
        final,
        (full_gate, full_up, full_down[-1]),
        first,
        hidden_rows,
    )
    grad_attn, late, router_late = line_turn(
        back_out,
        (
            held_rows(full_cot),
            hidden_rows,
            gain_second,
            chosen_a[4],
            router_rows,
            router_up,
            probs,
            mid_router,
            mid_out,
        ),
        full_width,
        (row_shape((2 * rank, full_width), F32), row_shape((rank, lanes), F32)),
        functools.partial(turn_backward, full_width, expert_total),
        turn_late,
        chips,
        7,
    )
    moe_out, grad_attn = lax.optimization_barrier((moe_out, grad_attn))
    layer_out = lax.psum_scatter(moe_out, "col", scatter_dimension=1, tiled=True)

    scaled, grad_value, norm_stats, grad_a_out = attend_back(
        prefix,
        grad_attn,
        out_map,
        chosen_b[3],
        (attended, rot_query, rot_key, value_rows, log_totals),
        proj,
        gains,
        tables,
        reach,
        score_scale,
    )
    stats = (col_sum(norm_stats, 10) / full_width).T
    extra = 128
    normed_part, grad_b_three = inputs_back(
        extra,
        scaled,
        grad_value,
        proj,
        inv,
        stats,
        w_query,
        w_key,
        w_value,
        b_three,
        a_three,
        full_inputs,
        inv_first,
        gain_first,
        mid,
        late,
        router_late,
    )
    summed_part = line_reduce(normed_part, chips, 1, 12)
    stat_rows = seq_len // width_part
    tail = summed_part[seq_len:]
    stat_start = 6 * rank
    first_stat = (
        tail[stat_start : stat_start + stat_rows] + tail[stat_start + 8 : stat_start + 8 + stat_rows]
    ).reshape(seq_len, 1)
    grad_inputs = (
        columns(grad_attn, 1).astype(F32)
        + inv_first * columns(norm_first, 0) * summed_part[:seq_len]
        - inputs.astype(F32) * (inv_first * inv_first * inv_first * first_stat / full_width)
    )

    held_adapters = adapter_a.shape[1] // row_count
    flat = jnp.concatenate(
        [
            tail[: 6 * rank],
            grad_a_out,
            grad_b_three,
            jnp.broadcast_to(adapter_slot.astype(F32), (8, width_part)),
        ]
    ).astype(BF16)
    every = lax.all_gather(flat, "row", axis=0).astype(F32)
    owners = every[:, -1, 0]
    held_ids = (row_index * held_adapters + jnp.arange(held_adapters)).astype(F32)
    pick = (owners[None, :] == held_ids[:, None])[:, :, None, None]
    summed = jnp.sum(jnp.where(pick, every[None], 0.0), axis=1)
    pieces = [summed[:, n * rank : (n + 1) * rank] for n in range(10)]
    query_a, key_a, value_a, router_a, out_b, router_up_grad, out_a, query_b, key_b, value_b = pieces
    grad_a = jnp.stack([query_a, key_a, value_a, out_a, router_a]).swapaxes(2, 3)
    grad_b = jnp.stack([query_b, key_b, value_b, out_b])
    grad_router = router_up_grad[:, :, :expert_total]
    return (layer_out, grad_inputs, grad_a, grad_b, grad_router)


def solution(mesh):
    placed = (
        P("row", "col"),
        P("row", "col"),
        P(),
        P(),
        P(),
        P(),
        P(None, "col"),
        P(None, "col"),
        P(None, "col"),
        P("col", None),
        P(),
        P("col", None, "row"),
        P("col", None, "row"),
        P("col", "row", None),
        P(),
        P(),
        P(),
        P("row", None),
        P("row"),
        P("row"),
    )
    return jax.shard_map(
        shards,
        mesh=mesh,
        in_specs=placed,
        out_specs=(
            P("row", "col"),
            P("row", "col"),
            P(None, "row", "col", None),
            P(None, "row", None, "col"),
            P("row", None, None),
        ),
        check_vma=False,
    )
```

```python
import functools

import jax
import jax.numpy as jnp
from jax import lax
from jax.experimental import pallas as pl
from jax.experimental.pallas import tpu as pltpu
from jax.sharding import PartitionSpec as P

HD = 128
F32, BF16 = jnp.float32, jnp.bfloat16
MESH_ID = pl.DeviceIdType.MESH
VM = pl.BlockSpec(memory_space=pltpu.VMEM)
ANY = pl.BlockSpec(memory_space=pl.ANY)
VMEM_LIMIT = 60 * 1024 * 1024

norm_eps = 1e-05
rope_base = 10000.0
masked_score = -1e30


def nn(left, right):
    return jnp.dot(left, right, preferred_element_type=F32)


def nt(left, right):
    return lax.dot_general(left, right, (((1,), (1,)), ((), ())), preferred_element_type=F32)


def tn(left, right):
    return lax.dot_general(left, right, (((0,), (0,)), ((), ())), preferred_element_type=F32)


def remote(src, dst, send_sem, recv_sem, device):
    return pltpu.make_async_remote_copy(
        src_ref=src,
        dst_ref=dst,
        send_sem=send_sem,
        recv_sem=recv_sem,
        device_id={"col": device},
        device_id_type=MESH_ID,
    )


def line_place():
    here = lax.axis_index("col")
    core = here % 2
    return here, here // 2, core, here + 1 - 2 * core


def line_barrier(chips, across=()):
    here, chip, core, mate = line_place()
    barrier = pltpu.get_barrier_semaphore()
    has_left, has_right = chip > 0, chip < chips - 1
    for other in across:
        pl.semaphore_signal(barrier, inc=1, device_id={"row": other}, device_id_type=MESH_ID)
    pl.semaphore_signal(barrier, inc=1, device_id={"col": mate}, device_id_type=MESH_ID)

    @pl.when(has_left)
    def _():
        pl.semaphore_signal(barrier, inc=1, device_id={"col": here - 2}, device_id_type=MESH_ID)

    @pl.when(has_right)
    def _():
        pl.semaphore_signal(barrier, inc=1, device_id={"col": here + 2}, device_id_type=MESH_ID)

    inner = jnp.logical_and(has_left, has_right)

    @pl.when(inner)
    def _():
        pl.semaphore_wait(barrier, 3 + len(across))

    @pl.when(jnp.logical_not(inner))
    def _():
        pl.semaphore_wait(barrier, 2 + len(across))


def spot(axis, size, parts, block, part):
    rows, cols = size
    step = rows // parts
    if axis == 0:
        return (pl.ds(pl.multiple_of(block * rows + part * step, 8), step), slice(None))
    return (pl.ds(part * step, step), pl.ds(pl.multiple_of(block * cols, 128), cols))


def run(*steps):
    steps = list(steps)
    while steps:
        for one in list(steps):
            if next(one, steps) is steps:
                steps.remove(one)


def gather_body(chips, parts, axis, x_ref, o_ref, *sems):
    line_barrier(chips)
    run(gather_steps(chips, parts, axis, x_ref, o_ref, *sems))


def gather_steps(chips, parts, axis, x_ref, o_ref, right_sem, left_sem, mate_sem, line_recv, mate_recv, own_sem):
    here, chip, core, mate = line_place()
    size = x_ref.shape
    step = size[0] // parts

    def at(block, part):
        return o_ref.at[spot(axis, size, parts, block, part)]

    def copy(j, part, sem, recv, device, first=False, block=None):
        block = 2 * j + core if block is None else block
        src = x_ref.at[pl.ds(part * step, step)] if first else at(block, part)
        return remote(src, at(block, part), sem.at[j, part], recv.at[j, part], device)

    def forward(j, part, rightward, leftward, first):
        if rightward:

            @pl.when(chip < chips - 1)
            def _():
                copy(j, part, right_sem, line_recv, here + 2, first).start()

        if leftward:

            @pl.when(chip > 0)
            def _():
                copy(j, part, left_sem, line_recv, here - 2, first).start()

        copy(j, part, mate_sem, mate_recv, mate, first).start()

    for part in range(parts):
        forward(chip, part, True, True, True)
    own = []
    for part in range(parts):
        own.append(
            pltpu.make_async_copy(x_ref.at[pl.ds(part * step, step)], at(here, part), own_sem.at[part])
        )
        own[-1].start()
    yield
    for far in range(1, chips):
        for part in range(parts):

            @pl.when(chip - far >= 0)
            def _():
                copy(chip - far, part, right_sem, line_recv, mate).wait_recv()
                forward(chip - far, part, True, False, False)

            @pl.when(chip + far < chips)
            def _():
                copy(chip + far, part, left_sem, line_recv, mate).wait_recv()
                forward(chip + far, part, False, True, False)

        yield

    for own_copy in own:
        own_copy.wait()
    for j in range(chips):
        for part in range(parts):
            copy(j, part, mate_sem, mate_recv, mate, block=2 * j + 1 - core).wait_recv()
            copy(j, part, mate_sem, mate_recv, mate).wait_send()

            @pl.when(jnp.logical_and(j <= chip, chip < chips - 1))
            def _():
                copy(j, part, right_sem, line_recv, here + 2).wait_send()

            @pl.when(jnp.logical_and(j >= chip, chip > 0))
            def _():
                copy(j, part, left_sem, line_recv, here - 2).wait_send()


def line_gather(x, chips, axis, ident, parts=2):
    rows, cols = x.shape
    sems = pltpu.SemaphoreType.DMA((chips, parts))
    shape = (2 * chips * rows, cols) if axis == 0 else (rows, 2 * chips * cols)
    return pl.pallas_call(
        functools.partial(gather_body, chips, parts, axis),
        out_shape=jax.ShapeDtypeStruct(shape, x.dtype),
        in_specs=[VM],
        out_specs=VM,
        scratch_shapes=[sems] * 5 + [pltpu.SemaphoreType.DMA((parts,))],
        compiler_params=pltpu.CompilerParams(
            collective_id=ident, has_side_effects=True, vmem_limit_bytes=VMEM_LIMIT
        ),
        name="line_gather",
    )(x)


def reduce_body(chips, parts, axis, *refs):
    line_barrier(chips)
    run(reduce_steps(chips, parts, axis, *refs))


def reduce_steps(
    chips, parts, axis, p_ref, o_ref, pair_buf, line_buf, sums, right_sem, left_sem, mate_sem, line_recv, mate_recv
):
    here, chip, core, mate = line_place()
    size = o_ref.shape
    step = size[0] // parts

    def rows(part):
        return pl.ds(part * step, step)

    def at(block, part):
        return spot(axis, size, parts, block, part)

    def mate_copy(j, part):
        return remote(
            p_ref.at[at(2 * j + 1 - core, part)],
            pair_buf.at[j, rows(part)],
            mate_sem.at[j, part],
            mate_recv.at[j, part],
            mate,
        )

    def line_copy(j, slot, part, sem, device):
        return remote(
            sums.at[j, rows(part)], line_buf.at[slot, rows(part)], sem.at[j, part], line_recv.at[slot, part], device
        )

    for far in range(chips - 1, -1, -1):
        for part in range(parts):

            @pl.when(chip + far < chips)
            def _():
                mate_copy(chip + far, part).start()

            if far > 0:

                @pl.when(chip - far >= 0)
                def _():
                    mate_copy(chip - far, part).start()

    yield

    def pair_sum(j, part):
        mate_copy(j, part).wait_recv()
        return p_ref[at(2 * j + core, part)].astype(F32) + pair_buf[j, rows(part)].astype(F32)

    def pass_on(j, slot, part, more, sem, device):
        @pl.when(more)
        def _():
            line_copy(j, j, part, sem, mate).wait_recv()
            total = pair_sum(j, part) + line_buf[j, rows(part)].astype(F32)
            sums[j, rows(part)] = total.astype(BF16)

        @pl.when(jnp.logical_not(more))
        def _():
            sums[j, rows(part)] = pair_sum(j, part).astype(BF16)

        line_copy(j, slot, part, sem, device).start()

    for far in range(chips - 1, 0, -1):
        for part in range(parts):

            @pl.when(chip + far < chips)
            def _():
                pass_on(chip + far, chip + far, part, chip > 0, right_sem, here + 2)

            @pl.when(chip - far >= 0)
            def _():
                pass_on(
                    chip - far, chips if far == 1 else chip - far, part, chip < chips - 1, left_sem, here - 2
                )

        yield

    for part in range(parts):
        o_ref[rows(part)] = pair_sum(chip, part)

        @pl.when(chip > 0)
        def _():
            line_copy(chip, chip, part, right_sem, mate).wait_recv()
            o_ref[rows(part)] += line_buf[chip, rows(part)].astype(F32)

        @pl.when(chip < chips - 1)
        def _():
            line_copy(chip, chips, part, left_sem, mate).wait_recv()
            o_ref[rows(part)] += line_buf[chips, rows(part)].astype(F32)

    for j in range(chips):
        for part in range(parts):
            mate_copy(j, part).wait_send()

            @pl.when(j > chip)
            def _():
                line_copy(j, j, part, right_sem, mate).wait_send()

            @pl.when(j < chip)
            def _():
                line_copy(j, j, part, left_sem, mate).wait_send()


def line_reduce(p, chips, axis, ident, parts=2):
    rows, cols = p.shape
    if axis == 0:
        rows //= 2 * chips
    else:
        cols //= 2 * chips
    sems = pltpu.SemaphoreType.DMA((chips, parts))
    return pl.pallas_call(
        functools.partial(reduce_body, chips, parts, axis),
        out_shape=jax.ShapeDtypeStruct((rows, cols), F32),
        in_specs=[VM],
        out_specs=VM,
        scratch_shapes=[
            pltpu.VMEM((chips, rows, cols), BF16),
            pltpu.VMEM((chips + 1, rows, cols), BF16),
            pltpu.VMEM((chips, rows, cols), BF16),
            sems,
            sems,
            sems,
            pltpu.SemaphoreType.DMA((chips + 1, parts)),
            sems,
        ],
        compiler_params=pltpu.CompilerParams(
            collective_id=ident, has_side_effects=True, vmem_limit_bytes=VMEM_LIMIT
        ),
        name="line_reduce",
    )(p)


def small_body(count, x_ref, o_ref, send_sem, recv_sem):
    here = lax.axis_index("col")
    barrier = pltpu.get_barrier_semaphore()
    for hop in range(1, count):
        other = lax.rem(here + hop, count)
        pl.semaphore_signal(barrier, inc=1, device_id={"col": other}, device_id_type=MESH_ID)
    o_ref[here] = x_ref[...]
    pl.semaphore_wait(barrier, count - 1)

    def copy(hop, block):
        other = lax.rem(here + hop, count)
        return remote(x_ref, o_ref.at[block], send_sem.at[hop], recv_sem.at[hop], other)

    for hop in range(1, count):
        copy(hop, here).start()
    for hop in range(1, count):
        copy(hop, lax.rem(here + count - hop, count)).wait_recv()
    for hop in range(1, count):
        copy(hop, here).wait_send()


def small_gather(x, count, ident):
    sems = pltpu.SemaphoreType.DMA((count,))
    return pl.pallas_call(
        functools.partial(small_body, count),
        out_shape=jax.ShapeDtypeStruct((count,) + x.shape, x.dtype),
        in_specs=[VM],
        out_specs=VM,
        scratch_shapes=[sems, sems],
        compiler_params=pltpu.CompilerParams(collective_id=ident, has_side_effects=True),
        name="small_gather",
    )(x)


def row_copy(src, dst, sems, which, device):
    return pltpu.make_async_remote_copy(
        src_ref=src,
        dst_ref=dst,
        send_sem=sems[0].at[which],
        recv_sem=sems[1].at[which],
        device_id={"row": device},
        device_id_type=MESH_ID,
    )


def row_partners():
    here = lax.axis_index("row")
    major, minor = here // 2, here % 2
    return 2 * major + 1 - minor, 2 * (1 - major) + minor


def row_gather_steps(x_ref, o_ref, *sems):
    near, next_one = row_partners()
    half = x_ref.shape[0] // 2

    def side(neighbour, first):
        slot, device = (0, near) if neighbour == 0 else (1, next_one)
        rows = pl.ds(first * half, half)
        return row_copy(x_ref.at[rows], o_ref.at[slot, rows], sems, 2 * slot + first, device)

    def onward(neighbour):
        slot, device = (0, next_one) if neighbour == 0 else (1, near)
        rows = pl.ds(slot * half, half)
        return row_copy(o_ref.at[slot, rows], o_ref.at[2, rows], sems, 4 + slot, device)

    side(0, 0).start()
    side(1, 1).start()
    side(0, 1).start()
    side(1, 0).start()
    yield
    yield
    yield
    yield
    side(0, 0).wait_recv()
    onward(0).start()
    side(1, 1).wait_recv()
    onward(1).start()
    yield
    for neighbour in range(2):
        side(neighbour, 1 - neighbour).wait_recv()
        onward(neighbour).wait_recv()
        onward(neighbour).wait_send()
        side(neighbour, 0).wait_send()
        side(neighbour, 1).wait_send()


def turn_body(chips, parts, first, last, held, late_count, riders, *refs):
    refs = list(refs)

    def take(count):
        taken = refs[:count]
        del refs[:count]
        return taken

    (p_ref,) = take(1)
    operands = take(held)
    rider_in = take(riders)
    (o_ref,) = take(1)
    results = take(late_count)
    rider_out = take(riders)
    sums_in, pair_buf, line_buf, sums = take(4)
    reduce_sems = take(5)
    gather_sems = take(5)
    line_barrier(chips, row_partners() if riders > 1 else ())
    steps = [reduce_steps(chips, parts, 0, p_ref, sums_in, pair_buf, line_buf, sums, *reduce_sems)]
    if riders > 0:
        steps.append(gather_steps(chips, 2, 1, rider_in[0], rider_out[0], *take(6)))
    if riders > 1:
        across = row_gather_steps(rider_in[1], rider_out[1], *take(2))
        next(across)
    run(*steps)
    here = lax.axis_index("col")
    own = o_ref.shape[0] // (2 * chips)
    kept = first(sums_in, operands, results, o_ref, pl.ds(pl.multiple_of(here * own, 8), own))

    def beside():
        if riders > 1:
            for _ in range(4):
                next(across)
        last(kept, operands, results)

    gather_rows(chips, parts, o_ref, *gather_sems, beside)
    if riders > 1:
        run(across)


def gather_rows(chips, parts, o_ref, right_sem, left_sem, mate_sem, line_recv, mate_recv, beside):
    here, chip, core, mate = line_place()
    size = (o_ref.shape[0] // (2 * chips), o_ref.shape[1])

    def copy(j, part, sem, recv, device, block=None):
        block = 2 * j + core if block is None else block
        ref = o_ref.at[spot(0, size, parts, block, part)]
        return remote(ref, ref, sem.at[j, part], recv.at[j, part], device)

    def forward(j, part, rightward, leftward):
        if rightward:

            @pl.when(chip < chips - 1)
            def _():
                copy(j, part, right_sem, line_recv, here + 2).start()

        if leftward:

            @pl.when(chip > 0)
            def _():
                copy(j, part, left_sem, line_recv, here - 2).start()

        copy(j, part, mate_sem, mate_recv, mate).start()

    for part in range(parts):
        forward(chip, part, True, True)
    beside()
    for far in range(1, chips):
        for part in range(parts):

            @pl.when(chip - far >= 0)
            def _():
                copy(chip - far, part, right_sem, line_recv, mate).wait_recv()
                forward(chip - far, part, True, False)

            @pl.when(chip + far < chips)
            def _():
                copy(chip + far, part, left_sem, line_recv, mate).wait_recv()
                forward(chip + far, part, False, True)

    for j in range(chips):
        for part in range(parts):
            copy(j, part, mate_sem, mate_recv, mate, block=2 * j + 1 - core).wait_recv()
            copy(j, part, mate_sem, mate_recv, mate).wait_send()

            @pl.when(jnp.logical_and(j <= chip, chip < chips - 1))
            def _():
                copy(j, part, right_sem, line_recv, here + 2).wait_send()

            @pl.when(jnp.logical_and(j >= chip, chip > 0))
            def _():
                copy(j, part, left_sem, line_recv, here - 2).wait_send()


def line_turn(p, operands, width, results, first, last, chips, ident, riders=(), parts=2):
    rows, cols = p.shape
    own = rows // (2 * chips)
    sems = pltpu.SemaphoreType.DMA((chips, parts))
    longer = pltpu.SemaphoreType.DMA((chips + 1, parts))
    more = []
    ridden = []
    if len(riders) > 0:
        height, part = riders[0].shape
        ridden.append(jax.ShapeDtypeStruct((height, 2 * chips * part), BF16))
        more += [pltpu.SemaphoreType.DMA((chips, 2))] * 5 + [pltpu.SemaphoreType.DMA((2,))]
    if len(riders) > 1:
        ridden.append(jax.ShapeDtypeStruct((3,) + riders[1].shape, BF16))
        more += [pltpu.SemaphoreType.DMA((6,))] * 2
    return pl.pallas_call(
        functools.partial(turn_body, chips, parts, first, last, len(operands), len(results), len(riders)),
        out_shape=(jax.ShapeDtypeStruct((rows, width), BF16),) + tuple(results) + tuple(ridden),
        in_specs=[VM] * (1 + len(operands)) + [VM, ANY][: len(riders)],
        out_specs=(VM,) * (1 + len(results)) + (VM, ANY)[: len(riders)],
        scratch_shapes=[
            pltpu.VMEM((own, cols), F32),
            pltpu.VMEM((chips, own, cols), BF16),
            pltpu.VMEM((chips + 1, own, cols), BF16),
            pltpu.VMEM((chips, own, cols), BF16),
            sems,
            sems,
            sems,
            longer,
            sems,
        ]
        + [sems] * 5
        + more,
        compiler_params=pltpu.CompilerParams(
            collective_id=ident, has_side_effects=True, vmem_limit_bytes=VMEM_LIMIT
        ),
        name="line_turn",
    )(p, *operands, *riders)


def inverse_rms(values):
    return lax.rsqrt(jnp.mean(values * values, axis=1, keepdims=True) + norm_eps)


def turn_forward(width, experts, sums, operands, results, o_ref, own):
    x_ref, gain_ref, a_ref, router_ref, up_ref = operands
    hidden_ref, mid_ref, mid_router_ref, probs_ref = results
    hidden = x_ref[...].astype(F32) + sums[:, :width]
    mid_ref[...] = sums[:, width:].astype(BF16)
    hidden_ref[...] = hidden
    normed = (hidden * inverse_rms(hidden) * gain_ref[...]).astype(BF16)
    o_ref[own, :width] = normed
    mid_router = nt(normed, a_ref[...]).astype(BF16)
    mid_router_ref[...] = mid_router
    logits = nt(normed, router_ref[...]) + nn(mid_router, up_ref[...])
    lane = lax.broadcasted_iota(jnp.int32, logits.shape, 1)
    logits = jnp.where(lane < experts, logits, masked_score)
    exponent = jnp.exp(logits - jnp.max(logits, axis=1, keepdims=True))
    probs = exponent / jnp.sum(exponent, axis=1, keepdims=True)
    probs_ref[...] = probs
    high = probs.astype(BF16)
    rest = probs - high.astype(F32)
    o_ref[own, width:] = (high.astype(F32) + pltpu.roll(rest, experts, 1)).astype(BF16)
    return None


def turn_backward(width, experts, sums, operands, results, o_ref, own):
    g_ref, hidden_ref, gain_ref, a_ref, router_ref, up_ref, probs_ref, mid_router_ref, mid_ref = operands
    pair = sums[:, width:]
    lanes = pair.shape[1]
    grad_probs = pair + pltpu.roll(pair, lanes - experts, 1)
    probs = probs_ref[...]
    grad_logits = (probs * (grad_probs - jnp.sum(probs * grad_probs, axis=1, keepdims=True))).astype(BF16)
    grad_mid = nt(grad_logits, up_ref[...]).astype(BF16)
    grad_normed = sums[:, :width] + nn(grad_logits, router_ref[...]) + nn(grad_mid, a_ref[...])
    hidden = hidden_ref[...]
    inv = inverse_rms(hidden)
    scaled = grad_normed * gain_ref[...]
    grad_hidden = (
        g_ref[...].astype(F32)
        + inv * scaled
        - hidden * (inv * inv * inv * jnp.mean(hidden * scaled, axis=1, keepdims=True))
    )
    grad_hidden = grad_hidden.astype(BF16)
    o_ref[own, :] = grad_hidden
    return grad_logits, grad_mid, grad_hidden


def turn_late(kept, operands, results):
    _, hidden_ref, gain_ref, _, _, _, _, mid_router_ref, mid_ref = operands
    grad_logits, grad_mid, grad_hidden = kept
    hidden = hidden_ref[...]
    normed = (hidden * inverse_rms(hidden) * gain_ref[...]).astype(BF16)
    rank = grad_mid.shape[1]
    late_ref, router_ref = results
    late_ref[pl.ds(0, rank)] = tn(grad_mid, normed)
    late_ref[pl.ds(rank, rank)] = tn(mid_ref[:, :rank], grad_hidden)
    router_ref[...] = tn(mid_router_ref[...], grad_logits)


def row_sums(values):
    lanes = 128
    values = sum(values[:, n : n + lanes] for n in range(0, values.shape[1], lanes))
    high = values.astype(BF16)
    rest = (values - high.astype(F32)).astype(BF16)
    ones = jnp.ones((8, values.shape[1]), BF16)
    return nt(ones, high) + nt(ones, rest)


def project_body(tile, x_ref, gain_ref, wq, wk, wv, a_ref, b_ref, proj_ref, mid_ref, inv_ref, sq_ref):
    part = wq.shape[1]
    for t in range(x_ref.shape[0] // tile):
        rows = pl.ds(t * tile, tile)
        x = x_ref[rows].astype(F32)
        inv = inverse_rms(x)
        inv_ref[rows] = inv
        normed = (x * inv * gain_ref[...]).astype(BF16)
        mid = nt(normed, a_ref[...]).astype(BF16)
        mid_ref[rows] = mid
        for m, w in enumerate((wq, wk, wv)):
            cols = pl.ds(m * part, part)
            proj = nn(normed, w[...]) + nn(mid, b_ref[:, cols])
            proj_ref[rows, cols] = proj
            if m < 2:
                sq_ref[pl.ds(m, 1), rows] = row_sums(proj * proj)[0:1]


def project(x, gain, weights, a_rows, b_cols):
    seq_len, width = x.shape
    part = weights[0].shape[1]
    rank = a_rows.shape[0]
    return pl.pallas_call(
        functools.partial(project_body, min(256, seq_len)),
        out_shape=(
            jax.ShapeDtypeStruct((seq_len, 3 * part), F32),
            jax.ShapeDtypeStruct((seq_len, rank), BF16),
            jax.ShapeDtypeStruct((seq_len, 1), F32),
            jax.ShapeDtypeStruct((2, seq_len), F32),
        ),
        in_specs=[VM] * 7,
        out_specs=(VM,) * 4,
        compiler_params=pltpu.CompilerParams(vmem_limit_bytes=VMEM_LIMIT),
        name="project",
    )(x, gain, *weights, a_rows, b_cols)


def key_limit(start, tile, seq_len, reach):
    return min(seq_len, max(start + tile, reach))


def allowed_keys(start, tile, limit, prefix_len):
    query = start + lax.broadcasted_iota(jnp.int32, (tile, limit), 0)
    key = lax.broadcasted_iota(jnp.int32, (tile, limit), 1)
    return jnp.logical_or(key <= query, key < prefix_len)


def attend_body(
    tile, reach, scale, prefix_ref, proj_ref, inv_ref, gains_ref, cos_ref, sin_ref, map_ref,
    p_ref, att_ref, q_ref, k_ref, v_ref, log_ref,
):
    seq_len, part = att_ref.shape
    prefix_len = prefix_ref[0]
    for h in range(part // HD):
        cols = pl.ds(h * HD, HD)
        for m, ref in ((0, q_ref), (1, k_ref)):
            plain = proj_ref[:, pl.ds(m * part + h * HD, HD)] * inv_ref[:, m : m + 1] * gains_ref[m : m + 1, cols]
            ref[:, cols] = (plain * cos_ref[...] + pltpu.roll(plain, HD // 2, 1) * sin_ref[...]).astype(BF16)
        v_ref[:, cols] = proj_ref[:, pl.ds(2 * part + h * HD, HD)].astype(BF16)
    for start in range(0, seq_len, tile):
        rows = pl.ds(start, tile)
        limit = key_limit(start, tile, seq_len, reach)
        allowed = allowed_keys(start, tile, limit, prefix_len)
        for h in range(part // HD):
            cols = pl.ds(h * HD, HD)
            scores = nt(q_ref[rows, cols], k_ref[pl.ds(0, limit), cols]) * scale
            scores = jnp.where(allowed, scores, masked_score)
            top = jnp.max(scores, axis=1, keepdims=True)
            exponent = jnp.exp(scores - top)
            total = jnp.sum(exponent, axis=1, keepdims=True)
            weights = (exponent / total).astype(BF16)
            att_ref[rows, cols] = nn(weights, v_ref[pl.ds(0, limit), cols]).astype(BF16)
            log_ref[rows, h : h + 1] = top + jnp.log(total)
        p_ref[rows] = nn(att_ref[rows], map_ref[...]).astype(BF16)


def attend(prefix, proj, inv, gains, tables, out_map, reach, scale):
    seq_len = proj.shape[0]
    part = proj.shape[1] // 3
    heads = jax.ShapeDtypeStruct((seq_len, part), BF16)
    return pl.pallas_call(
        functools.partial(attend_body, min(256, seq_len), reach, scale),
        out_shape=(
            jax.ShapeDtypeStruct((seq_len, out_map.shape[1]), BF16),
            heads,
            heads,
            heads,
            heads,
            jax.ShapeDtypeStruct((seq_len, part // HD), F32),
        ),
        in_specs=[pl.BlockSpec(memory_space=pltpu.SMEM)] + [VM] * 6,
        out_specs=(VM,) * 6,
        compiler_params=pltpu.CompilerParams(vmem_limit_bytes=VMEM_LIMIT),
        name="attend",
    )(prefix, proj, inv, gains, *tables, out_map)


def attend_back_body(
    tile, reach, scale, prefix_ref, g_ref, map_ref, b_ref, att_ref, q_ref, k_ref, v_ref, log_ref, proj_ref,
    gains_ref, cos_ref, sin_ref, scaled_ref, dv_ref, stat_ref, ga_ref, da_ref, dq_acc, dk_acc, dv_acc,
):
    seq_len, part = att_ref.shape
    prefix_len = prefix_ref[0]
    grad_a = jnp.zeros(ga_ref.shape, F32)
    for start in range(0, seq_len, tile):
        rows = pl.ds(start, tile)
        grads = g_ref[rows]
        da_ref[rows] = nt(grads, map_ref[...]).astype(BF16)
        grad_mid = nt(grads, b_ref[...]).astype(BF16)
        grad_a += tn(grad_mid, att_ref[rows])
    ga_ref[...] = grad_a
    dk_acc[...] = jnp.zeros_like(dk_acc)
    dv_acc[...] = jnp.zeros_like(dv_acc)
    for start in range(0, seq_len, tile):
        rows = pl.ds(start, tile)
        limit = key_limit(start, tile, seq_len, reach)
        keys = pl.ds(0, limit)
        allowed = allowed_keys(start, tile, limit, prefix_len)
        for h in range(part // HD):
            cols = pl.ds(h * HD, HD)
            query, key = q_ref[rows, cols], k_ref[keys, cols]
            grads = da_ref[rows, cols]
            scores = jnp.where(allowed, nt(query, key) * scale, masked_score)
            weights = jnp.exp(scores - log_ref[rows, h : h + 1])
            grad_weights = nt(grads, v_ref[keys, cols])
            dot = jnp.sum(weights * grad_weights, axis=1, keepdims=True)
            grad_scores = (weights * (grad_weights - dot)).astype(BF16)
            dq_acc[rows, cols] = nn(grad_scores, key) * scale
            dk_acc[keys, cols] += tn(grad_scores, query) * scale
            dv_acc[keys, cols] += tn(weights.astype(BF16), grads)
    dv_ref[...] = dv_acc[...].astype(BF16)
    for m, acc in ((0, dq_acc), (1, dk_acc)):
        for start in range(0, seq_len, tile):
            rows = pl.ds(start, tile)
            total = jnp.zeros((8, tile), F32)
            for h in range(part // HD):
                cols = pl.ds(h * HD, HD)
                here = pl.ds(m * part + h * HD, HD)
                plain = acc[rows, cols]
                turned = plain * cos_ref[rows] - pltpu.roll(plain, HD // 2, 1) * sin_ref[rows]
                scaled = turned * gains_ref[m : m + 1, cols]
                scaled_ref[rows, here] = scaled
                total += row_sums(proj_ref[rows, here] * scaled)
            stat_ref[pl.ds(m, 1), rows] = total[0:1]


def attend_back(prefix, grads, out_map, b_out, saved, proj, gains, tables, reach, scale):
    seq_len = proj.shape[0]
    part = proj.shape[1] // 3
    return pl.pallas_call(
        functools.partial(attend_back_body, min(256, seq_len), reach, scale),
        out_shape=(
            jax.ShapeDtypeStruct((seq_len, 2 * part), F32),
            jax.ShapeDtypeStruct((seq_len, part), BF16),
            jax.ShapeDtypeStruct((2, seq_len), F32),
            jax.ShapeDtypeStruct((b_out.shape[0], part), F32),
        ),
        in_specs=[pl.BlockSpec(memory_space=pltpu.SMEM)] + [VM] * 12,
        out_specs=(VM,) * 4,
        scratch_shapes=[pltpu.VMEM((seq_len, part), BF16)] + [pltpu.VMEM((seq_len, part), F32)] * 3,
        compiler_params=pltpu.CompilerParams(vmem_limit_bytes=VMEM_LIMIT),
        name="attend_back",
    )(prefix, grads, out_map, b_out, *saved, proj, gains, *tables)


def inputs_back_body(
    tile, extra, scaled_ref, dv_ref, proj_ref, inv_ref, stat_ref, wq, wk, wv, b_ref, a_ref, x_ref, inv1_ref,
    gain_ref, mid_ref, late_ref, router_ref, p_ref, gb_ref, w_ref, w_sems,
):
    seq_len, width = x_ref.shape
    part = dv_ref.shape[1]
    ranks = a_ref.shape[0]
    rank = ranks // 3
    fetches = [
        pltpu.make_async_copy(w, w_ref.at[:, pl.ds(m * part, part)], w_sems.at[m]) for m, w in enumerate((wq, wk, wv))
    ]
    for fetch in fetches:
        fetch.start()
    grad_b = jnp.zeros((ranks, 3 * part), F32)
    grad_a = jnp.zeros((ranks, width), F32)
    stats = jnp.zeros((8, width), F32)
    line = lax.broadcasted_iota(jnp.int32, (8, width), 0)
    for t in range(seq_len // tile):
        rows = pl.ds(t * tile, tile)
        grads = []
        for m in range(2):
            cols = pl.ds(m * part, part)
            inv = inv_ref[rows, m : m + 1]
            shift = inv * inv * inv * stat_ref[rows, m : m + 1]
            grads.append((inv * scaled_ref[rows, cols] - proj_ref[rows, cols] * shift).astype(BF16))
        grads = jnp.concatenate(grads + [dv_ref[rows]], axis=1)
        middle = nt(grads, b_ref[...]).astype(BF16)
        if t == 0:
            for fetch in fetches:
                fetch.wait()
        normed_part = nt(grads, w_ref[...]) + nn(middle, a_ref[...])
        grad_b += tn(mid_ref[rows], grads)
        p_ref[rows] = normed_part.astype(BF16)
        scaled_x = x_ref[rows].astype(F32) * gain_ref[...]
        normed = (scaled_x * inv1_ref[rows]).astype(BF16)
        grad_a += tn(middle, normed)
        first = row_sums(scaled_x * normed_part)
        for j in range(tile // part):
            wide = jnp.concatenate([first[:, j * part : (j + 1) * part]] * (width // part), axis=1)
            stats = jnp.where(line == (t * tile) // part + j, wide, stats)
    for m in range(3):
        gb_ref[pl.ds(m * rank, rank)] = grad_b[m * rank : (m + 1) * rank, m * part : (m + 1) * part]
    high = stats.astype(BF16).astype(F32)
    router = router_ref[...]
    if part > router.shape[1]:
        router = jnp.concatenate([router, jnp.zeros((rank, part - router.shape[1]), F32)], axis=1)
    pieces = [
        grad_a,
        late_ref[...],
        jnp.concatenate([router] * (width // part), axis=1),
        high,
        stats - high,
    ]
    used = sum(piece.shape[0] for piece in pieces)
    pieces.append(jnp.zeros((extra - used, width), F32))
    p_ref[pl.ds(seq_len, extra)] = jnp.concatenate(pieces, axis=0).astype(BF16)


def inputs_back(extra, *operands):
    x = operands[10]
    seq_len, width = x.shape
    part = operands[1].shape[1]
    ranks = operands[9].shape[0]
    return pl.pallas_call(
        functools.partial(inputs_back_body, min(256, seq_len), extra),
        out_shape=(
            jax.ShapeDtypeStruct((seq_len + extra, width), BF16),
            jax.ShapeDtypeStruct((ranks, part), F32),
        ),
        in_specs=[ANY if 5 <= n < 8 else VM for n in range(len(operands))],
        out_specs=(VM,) * 2,
        scratch_shapes=[pltpu.VMEM((width, 3 * part), BF16), pltpu.SemaphoreType.DMA((3,))],
        compiler_params=pltpu.CompilerParams(vmem_limit_bytes=VMEM_LIMIT),
        name="inputs_back",
    )(*operands)


def moe_body(experts, tile, count, x_ref, g_ref, routes_ref, hidden_ref, gate_w, up_w, *refs):
    downs = refs[:count]
    out_ref, dx_ref, out_acc, dx_acc, gate_acc, wgu, wd, sems = refs[count:]
    hidden = wd.shape[1]
    tokens, width = g_ref.shape
    lanes = gate_acc.shape[1]
    local = gate_w.shape[0]
    pieces = gate_w.shape[2] // hidden
    steps = local * pieces
    here = lax.axis_index("col")
    row = lax.axis_index("row")

    def start(step, slot):
        e, piece = step // pieces, step % pieces
        if count == 1:
            place = piece
        else:
            place = 2 * ((row // 2 + piece // 2) % 2) + (row + piece) % 2
        units = pl.ds(pl.multiple_of(place * hidden, 128), hidden)
        pltpu.make_async_copy(gate_w.at[e, :, units], wgu.at[slot, :, pl.ds(0, hidden)], sems.at[slot, 0]).start()
        pltpu.make_async_copy(up_w.at[e, :, units], wgu.at[slot, :, pl.ds(hidden, hidden)], sems.at[slot, 1]).start()
        if count == 1:
            pltpu.make_async_copy(downs[0].at[e, units], wd.at[slot], sems.at[slot, 2]).start()
        else:

            @pl.when(piece == 0)
            def _():
                pltpu.make_async_copy(downs[0].at[e], wd.at[slot], sems.at[slot, 2]).start()

            @pl.when(piece > 0)
            def _():
                other = lax.max(piece - 1, 0)
                pltpu.make_async_copy(downs[1].at[other, e], wd.at[slot], sems.at[slot, 2]).start()

    def finish(slot):
        units = pl.ds(0, hidden)
        pltpu.make_async_copy(gate_w.at[0, :, units], wgu.at[slot, :, units], sems.at[slot, 0]).wait()
        pltpu.make_async_copy(up_w.at[0, :, units], wgu.at[slot, :, units], sems.at[slot, 1]).wait()
        pltpu.make_async_copy(downs[0].at[0, units], wd.at[slot], sems.at[slot, 2]).wait()

    start(0, 0)
    out_acc[...] = jnp.zeros_like(out_acc)
    dx_acc[...] = jnp.zeros_like(dx_acc)
    gate_acc[...] = jnp.zeros_like(gate_acc)
    own = hidden_ref.shape[0]
    out_acc[pl.ds(pl.multiple_of(here * own, 8), own)] = hidden_ref[...]

    def one_step(step, carry):
        slot = step % 2
        finish(slot)

        @pl.when(step + 1 < steps)
        def _():
            start(step + 1, 1 - slot)

        e = here * local + step // pieces

        def one_tile(t, carry):
            rows = pl.ds(pl.multiple_of(t * tile, tile), tile)
            lane = lax.broadcasted_iota(jnp.int32, (tile, lanes), 1)
            mine = lane == e
            halves = jnp.logical_or(mine, lane == e + experts)
            named = jnp.sum(jnp.where(routes_ref[rows] == e, 1.0, 0.0), axis=1, keepdims=True)
            gate = jnp.sum(jnp.where(halves, x_ref[rows, width:].astype(F32), 0.0), axis=1, keepdims=True)
            gate = gate * named
            both = nn(x_ref[rows, :width], wgu[slot])
            gate_in, up_in = both[:, :hidden], both[:, hidden:]
            sigmoid = jax.nn.sigmoid(gate_in)
            silu = gate_in * sigmoid
            active = silu * up_in
            back = nt(g_ref[rows], wd[slot])
            d_gate = jnp.sum(active * back, axis=1, keepdims=True) * named
            gate_acc[rows] += jnp.where(mine, d_gate, 0.0)
            out_acc[rows] += nn((active * gate).astype(BF16), wd[slot])
            d_active = back * gate
            d_gate_in = d_active * up_in * (sigmoid + silu * (1.0 - sigmoid))
            d_up_in = d_active * silu
            d_both = jnp.concatenate([d_gate_in.astype(BF16), d_up_in.astype(BF16)], axis=1)
            dx_acc[rows] += nt(d_both, wgu[slot])
            return carry

        return lax.fori_loop(0, tokens // tile, one_tile, carry)

    lax.fori_loop(0, steps, one_step, 0)
    out_ref[...] = out_acc[...].astype(BF16)
    dx_ref[:, :width] = dx_acc[...].astype(BF16)
    high = gate_acc[...].astype(BF16).astype(F32)
    rest = gate_acc[...] - high
    dx_ref[:, width:] = (high + pltpu.roll(rest, experts, 1)).astype(BF16)


def moe(x, g, routes, hidden_rows, experts, gate_w, up_w, downs, tile=512):
    tokens, width = g.shape
    lanes = x.shape[1] - width
    hidden = downs[0].shape[1] if len(downs) > 1 else min(256, gate_w.shape[2])
    return pl.pallas_call(
        functools.partial(moe_body, experts, min(tile, tokens), len(downs)),
        out_shape=(
            jax.ShapeDtypeStruct((tokens, width), BF16),
            jax.ShapeDtypeStruct((tokens, width + lanes), BF16),
        ),
        in_specs=[VM] * 4 + [ANY] * (2 + len(downs)),
        out_specs=(VM, VM),
        scratch_shapes=[
            pltpu.VMEM((tokens, width), F32),
            pltpu.VMEM((tokens, width), F32),
            pltpu.VMEM((tokens, lanes), F32),
            pltpu.VMEM((2, width, 2 * hidden), BF16),
            pltpu.VMEM((2, hidden, width), BF16),
            pltpu.SemaphoreType.DMA((2, 3)),
        ],
        compiler_params=pltpu.CompilerParams(vmem_limit_bytes=VMEM_LIMIT),
        name="moe",
    )(x, g, routes, hidden_rows, gate_w, up_w, *downs)


def rope_tables(length, head_dim):
    half_dim = head_dim // 2
    frequency = rope_base ** (-(2.0 * jnp.arange(half_dim, dtype=F32)) / head_dim)
    angles = jnp.arange(length, dtype=F32)[:, None] * frequency[None, :]
    cosine, sine = jnp.cos(angles), jnp.sin(angles)
    return jnp.concatenate([cosine, cosine], axis=1), jnp.concatenate([-sine, sine], axis=1)


def shards(
    inputs,
    cotangent,
    norm_first,
    norm_second,
    query_gain,
    key_gain,
    w_query,
    w_key,
    w_value,
    w_out,
    w_router,
    w_gate,
    w_up,
    w_down,
    adapter_a,
    adapter_b,
    adapter_router,
    routes,
    prefix,
    adapter_index,
):
    seq_len, width_part = inputs.shape
    col_count = lax.axis_size("col")
    row_count = lax.axis_size("row")
    col_index = lax.axis_index("col")
    row_index = lax.axis_index("row")
    chips = col_count // 2
    full_width = width_part * col_count
    head_width = w_query.shape[1]
    local_experts = w_gate.shape[0]
    expert_total = w_router.shape[1]
    feature_start = col_index * width_part
    head_start = col_index * head_width
    own_rows = seq_len // col_count
    row_start = col_index * own_rows
    score_scale = HD ** (-0.5)
    reach = seq_len // 2
    lanes = 128

    def columns(array, axis_num):
        return lax.dynamic_slice_in_dim(array, feature_start, width_part, axis_num)

    def head_cols(array, axis_num=1):
        return lax.dynamic_slice_in_dim(array, head_start, head_width, axis_num)

    def held_rows(array):
        return lax.dynamic_slice_in_dim(array, row_start, own_rows, 0)

    def col_sum(pair, ident):
        return jnp.sum(small_gather(pair, col_count, ident), axis=0)

    full_gate = lax.all_gather(w_gate, "row", axis=2, tiled=True)
    full_up = lax.all_gather(w_up, "row", axis=2, tiled=True)
    across = row_count == 4
    riders = (cotangent, w_down) if across else (cotangent,)
    adapter_slot = adapter_index[0]
    chosen_a = lax.dynamic_index_in_dim(adapter_a, adapter_slot, 1, keepdims=False).swapaxes(1, 2)
    chosen_b = lax.dynamic_index_in_dim(adapter_b, adapter_slot, 1, keepdims=False)
    chosen_router = lax.dynamic_index_in_dim(adapter_router, adapter_slot, 0, keepdims=False)
    rank = chosen_a.shape[1]
    a_three = chosen_a[:3].reshape(3 * rank, full_width)
    b_three = head_cols(chosen_b[:3].reshape(3 * rank, full_width))
    blank = jnp.zeros((rank, head_width), BF16)
    b_cols = jnp.concatenate(
        [
            jnp.concatenate([b_three[m * rank : (m + 1) * rank] if n == m else blank for n in range(3)], axis=0)
            for m in range(3)
        ],
        axis=1,
    )
    a_out = head_cols(chosen_a[3])
    out_map = (w_out.astype(F32) + tn(a_out, chosen_b[3])).astype(BF16)
    out_wide = jnp.concatenate([out_map, a_out.T, jnp.zeros((head_width, lanes - rank), BF16)], axis=1)
    router_rows = jnp.pad(w_router.T, ((0, lanes - expert_total), (0, 0)))
    router_up = jnp.pad(chosen_router, ((0, 0), (0, lanes - expert_total)))
    gains = jnp.stack([head_cols(query_gain, 0), head_cols(key_gain, 0)])
    tables = rope_tables(seq_len, HD)
    gain_first, gain_second = norm_first[None], norm_second[None]

    full_inputs = line_gather(inputs, chips, 1, 0)
    proj, mid, inv_first, squares = project(
        full_inputs, gain_first, (w_query, w_key, w_value), a_three, b_cols
    )
    inv = lax.rsqrt(col_sum(squares, 1) / full_width + norm_eps).T
    part_out, attended, rot_query, rot_key, value_rows, log_totals = attend(
        prefix, proj, inv, gains, tables, out_wide, reach, score_scale
    )
    wide = full_width + lanes
    row_shape = jax.ShapeDtypeStruct
    normed_two, hidden_rows, mid_out, mid_router, probs, full_cot, *down_others = line_turn(
        part_out,
        (held_rows(full_inputs), gain_second, chosen_a[4], router_rows, router_up),
        wide,
        (
            row_shape((own_rows, full_width), F32),
            row_shape((own_rows, lanes), BF16),
            row_shape((own_rows, rank), BF16),
            row_shape((own_rows, lanes), F32),
        ),
        functools.partial(turn_forward, full_width, expert_total),
        lambda kept, operands, results: None,
        chips,
        2,
        riders,
    )
    if across:
        downs = (w_down,) + tuple(down_others)
    else:
        downs = (lax.all_gather(w_down, "row", axis=1, tiled=True),)

    moe_out, back_out = moe(normed_two, full_cot, routes, hidden_rows, expert_total, full_gate, full_up, downs)
    grad_attn, late, router_late = line_turn(
        back_out,
        (
            held_rows(full_cot),
            hidden_rows,
            gain_second,
            chosen_a[4],
            router_rows,
            router_up,
            probs,
            mid_router,
            mid_out,
        ),
        full_width,
        (row_shape((2 * rank, full_width), F32), row_shape((rank, lanes), F32)),
        functools.partial(turn_backward, full_width, expert_total),
        turn_late,
        chips,
        7,
    )
    moe_out, grad_attn = lax.optimization_barrier((moe_out, grad_attn))
    layer_out = lax.psum_scatter(moe_out, "col", scatter_dimension=1, tiled=True)

    scaled, grad_value, norm_stats, grad_a_out = attend_back(
        prefix,
        grad_attn,
        out_map,
        chosen_b[3],
        (attended, rot_query, rot_key, value_rows, log_totals),
        proj,
        gains,
        tables,
        reach,
        score_scale,
    )
    stats = (col_sum(norm_stats, 10) / full_width).T
    extra = 128
    normed_part, grad_b_three = inputs_back(
        extra,
        scaled,
        grad_value,
        proj,
        inv,
        stats,
        w_query,
        w_key,
        w_value,
        b_cols,
        a_three,
        full_inputs,
        inv_first,
        gain_first,
        mid,
        late,
        router_late,
    )
    summed_part = line_reduce(normed_part, chips, 1, 12)
    stat_rows = seq_len // width_part
    tail = summed_part[seq_len:]
    stat_start = 6 * rank
    first_stat = (
        tail[stat_start : stat_start + stat_rows] + tail[stat_start + 8 : stat_start + 8 + stat_rows]
    ).reshape(seq_len, 1)
    grad_inputs = (
        columns(grad_attn, 1).astype(F32)
        + inv_first * columns(norm_first, 0) * summed_part[:seq_len]
        - inputs.astype(F32) * (inv_first * inv_first * inv_first * first_stat / full_width)
    )

    held_adapters = adapter_a.shape[1] // row_count
    flat = jnp.concatenate(
        [
            tail[: 6 * rank],
            grad_a_out,
            grad_b_three,
            jnp.broadcast_to(adapter_slot.astype(F32), (8, width_part)),
        ]
    ).astype(BF16)
    every = lax.all_gather(flat, "row", axis=0).astype(F32)
    owners = every[:, -1, 0]
    held_ids = (row_index * held_adapters + jnp.arange(held_adapters)).astype(F32)
    pick = (owners[None, :] == held_ids[:, None])[:, :, None, None]
    summed = jnp.sum(jnp.where(pick, every[None], 0.0), axis=1)
    pieces = [summed[:, n * rank : (n + 1) * rank] for n in range(10)]
    query_a, key_a, value_a, router_a, out_b, router_up_grad, out_a, query_b, key_b, value_b = pieces
    grad_a = jnp.stack([query_a, key_a, value_a, out_a, router_a]).swapaxes(2, 3)
    grad_b = jnp.stack([query_b, key_b, value_b, out_b])
    grad_router = router_up_grad[:, :, :expert_total]
    return (layer_out, grad_inputs, grad_a, grad_b, grad_router)


def solution(mesh):
    placed = (
        P("row", "col"),
        P("row", "col"),
        P(),
        P(),
        P(),
        P(),
        P(None, "col"),
        P(None, "col"),
        P(None, "col"),
        P("col", None),
        P(),
        P("col", None, "row"),
        P("col", None, "row"),
        P("col", "row", None),
        P(),
        P(),
        P(),
        P("row", None),
        P("row"),
        P("row"),
    )
    return jax.shard_map(
        shards,
        mesh=mesh,
        in_specs=placed,
        out_specs=(
            P("row", "col"),
            P("row", "col"),
            P(None, "row", "col", None),
            P(None, "row", None, "col"),
            P("row", None, None),
        ),
        check_vma=False,
    )
```

```python
import functools

import jax
import jax.numpy as jnp
from jax import lax
from jax.experimental import pallas as pl
from jax.experimental.pallas import tpu as pltpu
from jax.sharding import PartitionSpec as P

HD = 128
F32, BF16 = jnp.float32, jnp.bfloat16
MESH_ID = pl.DeviceIdType.MESH
VM = pl.BlockSpec(memory_space=pltpu.VMEM)
ANY = pl.BlockSpec(memory_space=pl.ANY)
VMEM_LIMIT = 60 * 1024 * 1024
VMEM_MOST = 63 * 1024 * 1024

norm_eps = 1e-05
rope_base = 10000.0
masked_score = -1e30


def nn(left, right):
    return jnp.dot(left, right, preferred_element_type=F32)


def nt(left, right):
    return lax.dot_general(left, right, (((1,), (1,)), ((), ())), preferred_element_type=F32)


def tn(left, right):
    return lax.dot_general(left, right, (((0,), (0,)), ((), ())), preferred_element_type=F32)


def remote(src, dst, send_sem, recv_sem, device):
    return pltpu.make_async_remote_copy(
        src_ref=src,
        dst_ref=dst,
        send_sem=send_sem,
        recv_sem=recv_sem,
        device_id={"col": device},
        device_id_type=MESH_ID,
    )


def line_place():
    here = lax.axis_index("col")
    core = here % 2
    return here, here // 2, core, here + 1 - 2 * core


def line_barrier(chips, across=()):
    here, chip, core, mate = line_place()
    barrier = pltpu.get_barrier_semaphore()
    has_left, has_right = chip > 0, chip < chips - 1
    for other in across:
        pl.semaphore_signal(barrier, inc=1, device_id={"row": other}, device_id_type=MESH_ID)
    pl.semaphore_signal(barrier, inc=1, device_id={"col": mate}, device_id_type=MESH_ID)

    @pl.when(has_left)
    def _():
        pl.semaphore_signal(barrier, inc=1, device_id={"col": here - 2}, device_id_type=MESH_ID)

    @pl.when(has_right)
    def _():
        pl.semaphore_signal(barrier, inc=1, device_id={"col": here + 2}, device_id_type=MESH_ID)

    inner = jnp.logical_and(has_left, has_right)

    @pl.when(inner)
    def _():
        pl.semaphore_wait(barrier, 3 + len(across))

    @pl.when(jnp.logical_not(inner))
    def _():
        pl.semaphore_wait(barrier, 2 + len(across))


def spot(axis, size, parts, block, part):
    rows, cols = size
    step = rows // parts
    if axis == 0:
        return (pl.ds(pl.multiple_of(block * rows + part * step, 8), step), slice(None))
    return (pl.ds(part * step, step), pl.ds(pl.multiple_of(block * cols, 128), cols))


def run(*steps):
    steps = list(steps)
    while steps:
        for one in list(steps):
            if next(one, steps) is steps:
                steps.remove(one)


def gather_body(chips, parts, axis, x_ref, o_ref, *sems):
    line_barrier(chips)
    run(gather_steps(chips, parts, axis, x_ref, o_ref, *sems))


def gather_steps(chips, parts, axis, x_ref, o_ref, right_sem, left_sem, mate_sem, line_recv, mate_recv, own_sem):
    here, chip, core, mate = line_place()
    size = x_ref.shape
    step = size[0] // parts

    def at(block, part):
        return o_ref.at[spot(axis, size, parts, block, part)]

    def copy(j, part, sem, recv, device, first=False, block=None):
        block = 2 * j + core if block is None else block
        src = x_ref.at[pl.ds(part * step, step)] if first else at(block, part)
        return remote(src, at(block, part), sem.at[j, part], recv.at[j, part], device)

    def forward(j, part, rightward, leftward, first):
        if rightward:

            @pl.when(chip < chips - 1)
            def _():
                copy(j, part, right_sem, line_recv, here + 2, first).start()

        if leftward:

            @pl.when(chip > 0)
            def _():
                copy(j, part, left_sem, line_recv, here - 2, first).start()

        copy(j, part, mate_sem, mate_recv, mate, first).start()

    for part in range(parts):
        forward(chip, part, True, True, True)
    own = []
    for part in range(parts):
        own.append(
            pltpu.make_async_copy(x_ref.at[pl.ds(part * step, step)], at(here, part), own_sem.at[part])
        )
        own[-1].start()
    yield
    for far in range(1, chips):
        for part in range(parts):

            @pl.when(chip - far >= 0)
            def _():
                copy(chip - far, part, right_sem, line_recv, mate).wait_recv()
                forward(chip - far, part, True, False, False)

            @pl.when(chip + far < chips)
            def _():
                copy(chip + far, part, left_sem, line_recv, mate).wait_recv()
                forward(chip + far, part, False, True, False)

        yield

    for own_copy in own:
        own_copy.wait()
    for j in range(chips):
        for part in range(parts):
            copy(j, part, mate_sem, mate_recv, mate, block=2 * j + 1 - core).wait_recv()
            copy(j, part, mate_sem, mate_recv, mate).wait_send()

            @pl.when(jnp.logical_and(j <= chip, chip < chips - 1))
            def _():
                copy(j, part, right_sem, line_recv, here + 2).wait_send()

            @pl.when(jnp.logical_and(j >= chip, chip > 0))
            def _():
                copy(j, part, left_sem, line_recv, here - 2).wait_send()


def line_gather(x, chips, axis, ident, parts=2):
    rows, cols = x.shape
    sems = pltpu.SemaphoreType.DMA((chips, parts))
    shape = (2 * chips * rows, cols) if axis == 0 else (rows, 2 * chips * cols)
    return pl.pallas_call(
        functools.partial(gather_body, chips, parts, axis),
        out_shape=jax.ShapeDtypeStruct(shape, x.dtype),
        in_specs=[VM],
        out_specs=VM,
        scratch_shapes=[sems] * 5 + [pltpu.SemaphoreType.DMA((parts,))],
        compiler_params=pltpu.CompilerParams(
            collective_id=ident, has_side_effects=True, vmem_limit_bytes=VMEM_LIMIT
        ),
        name="line_gather",
    )(x)


def reduce_body(chips, parts, axis, *refs):
    line_barrier(chips)
    run(reduce_steps(chips, parts, axis, *refs))


def reduce_steps(
    chips, parts, axis, p_ref, o_ref, pair_buf, line_buf, sums, right_sem, left_sem, mate_sem, line_recv, mate_recv
):
    here, chip, core, mate = line_place()
    size = o_ref.shape
    step = size[0] // parts

    def rows(part):
        return pl.ds(part * step, step)

    def at(block, part):
        return spot(axis, size, parts, block, part)

    def mate_copy(j, part):
        return remote(
            p_ref.at[at(2 * j + 1 - core, part)],
            pair_buf.at[j, rows(part)],
            mate_sem.at[j, part],
            mate_recv.at[j, part],
            mate,
        )

    def line_copy(j, slot, part, sem, device):
        return remote(
            sums.at[j, rows(part)], line_buf.at[slot, rows(part)], sem.at[j, part], line_recv.at[slot, part], device
        )

    for far in range(chips - 1, -1, -1):
        for part in range(parts):

            @pl.when(chip + far < chips)
            def _():
                mate_copy(chip + far, part).start()

            if far > 0:

                @pl.when(chip - far >= 0)
                def _():
                    mate_copy(chip - far, part).start()

    yield

    def pair_sum(j, part):
        mate_copy(j, part).wait_recv()
        return p_ref[at(2 * j + core, part)].astype(F32) + pair_buf[j, rows(part)].astype(F32)

    def pass_on(j, slot, part, more, sem, device):
        @pl.when(more)
        def _():
            line_copy(j, j, part, sem, mate).wait_recv()
            total = pair_sum(j, part) + line_buf[j, rows(part)].astype(F32)
            sums[j, rows(part)] = total.astype(BF16)

        @pl.when(jnp.logical_not(more))
        def _():
            sums[j, rows(part)] = pair_sum(j, part).astype(BF16)

        line_copy(j, slot, part, sem, device).start()

    for far in range(chips - 1, 0, -1):
        for part in range(parts):

            @pl.when(chip + far < chips)
            def _():
                pass_on(chip + far, chip + far, part, chip > 0, right_sem, here + 2)

            @pl.when(chip - far >= 0)
            def _():
                pass_on(
                    chip - far, chips if far == 1 else chip - far, part, chip < chips - 1, left_sem, here - 2
                )

        yield

    for part in range(parts):
        o_ref[rows(part)] = pair_sum(chip, part)

        @pl.when(chip > 0)
        def _():
            line_copy(chip, chip, part, right_sem, mate).wait_recv()
            o_ref[rows(part)] += line_buf[chip, rows(part)].astype(F32)

        @pl.when(chip < chips - 1)
        def _():
            line_copy(chip, chips, part, left_sem, mate).wait_recv()
            o_ref[rows(part)] += line_buf[chips, rows(part)].astype(F32)

    for j in range(chips):
        for part in range(parts):
            mate_copy(j, part).wait_send()

            @pl.when(j > chip)
            def _():
                line_copy(j, j, part, right_sem, mate).wait_send()

            @pl.when(j < chip)
            def _():
                line_copy(j, j, part, left_sem, mate).wait_send()


def line_reduce(p, chips, axis, ident, parts=2):
    rows, cols = p.shape
    if axis == 0:
        rows //= 2 * chips
    else:
        cols //= 2 * chips
    sems = pltpu.SemaphoreType.DMA((chips, parts))
    return pl.pallas_call(
        functools.partial(reduce_body, chips, parts, axis),
        out_shape=jax.ShapeDtypeStruct((rows, cols), F32),
        in_specs=[VM],
        out_specs=VM,
        scratch_shapes=[
            pltpu.VMEM((chips, rows, cols), BF16),
            pltpu.VMEM((chips + 1, rows, cols), BF16),
            pltpu.VMEM((chips, rows, cols), BF16),
            sems,
            sems,
            sems,
            pltpu.SemaphoreType.DMA((chips + 1, parts)),
            sems,
        ],
        compiler_params=pltpu.CompilerParams(
            collective_id=ident, has_side_effects=True, vmem_limit_bytes=VMEM_LIMIT
        ),
        name="line_reduce",
    )(p)


def small_body(count, x_ref, o_ref, send_sem, recv_sem):
    here = lax.axis_index("col")
    barrier = pltpu.get_barrier_semaphore()
    for hop in range(1, count):
        other = lax.rem(here + hop, count)
        pl.semaphore_signal(barrier, inc=1, device_id={"col": other}, device_id_type=MESH_ID)
    o_ref[here] = x_ref[...]
    pl.semaphore_wait(barrier, count - 1)

    def copy(hop, block):
        other = lax.rem(here + hop, count)
        return remote(x_ref, o_ref.at[block], send_sem.at[hop], recv_sem.at[hop], other)

    for hop in range(1, count):
        copy(hop, here).start()
    for hop in range(1, count):
        copy(hop, lax.rem(here + count - hop, count)).wait_recv()
    for hop in range(1, count):
        copy(hop, here).wait_send()


def small_gather(x, count, ident):
    sems = pltpu.SemaphoreType.DMA((count,))
    return pl.pallas_call(
        functools.partial(small_body, count),
        out_shape=jax.ShapeDtypeStruct((count,) + x.shape, x.dtype),
        in_specs=[VM],
        out_specs=VM,
        scratch_shapes=[sems, sems],
        compiler_params=pltpu.CompilerParams(collective_id=ident, has_side_effects=True),
        name="small_gather",
    )(x)


def row_copy(src, dst, sems, which, device):
    return pltpu.make_async_remote_copy(
        src_ref=src,
        dst_ref=dst,
        send_sem=sems[0].at[which],
        recv_sem=sems[1].at[which],
        device_id={"row": device},
        device_id_type=MESH_ID,
    )


def row_partners():
    here = lax.axis_index("row")
    major, minor = here // 2, here % 2
    return 2 * major + 1 - minor, 2 * (1 - major) + minor


def row_gather_steps(x_ref, o_ref, *sems):
    near, next_one = row_partners()
    half = x_ref.shape[0] // 2

    def side(neighbour, first):
        slot, device = (0, near) if neighbour == 0 else (1, next_one)
        rows = pl.ds(first * half, half)
        return row_copy(x_ref.at[rows], o_ref.at[slot, rows], sems, 2 * slot + first, device)

    def onward(neighbour):
        slot, device = (0, next_one) if neighbour == 0 else (1, near)
        rows = pl.ds(slot * half, half)
        return row_copy(o_ref.at[slot, rows], o_ref.at[2, rows], sems, 4 + slot, device)

    side(0, 0).start()
    side(1, 1).start()
    side(0, 1).start()
    side(1, 0).start()
    yield
    yield
    yield
    yield
    side(0, 0).wait_recv()
    onward(0).start()
    side(1, 1).wait_recv()
    onward(1).start()
    yield
    for neighbour in range(2):
        side(neighbour, 1 - neighbour).wait_recv()
        onward(neighbour).wait_recv()
        onward(neighbour).wait_send()
        side(neighbour, 0).wait_send()
        side(neighbour, 1).wait_send()


def turn_body(chips, parts, first, last, held, late_count, riders, *refs):
    refs = list(refs)

    def take(count):
        taken = refs[:count]
        del refs[:count]
        return taken

    (p_ref,) = take(1)
    operands = take(held)
    rider_in = take(riders)
    (o_ref,) = take(1)
    results = take(late_count)
    rider_out = take(riders)
    sums_in, pair_buf, line_buf, sums = take(4)
    reduce_sems = take(5)
    gather_sems = take(5)
    line_barrier(chips, row_partners() if riders > 1 else ())
    steps = [reduce_steps(chips, parts, 0, p_ref, sums_in, pair_buf, line_buf, sums, *reduce_sems)]
    if riders > 0:
        steps.append(gather_steps(chips, 2, 1, rider_in[0], rider_out[0], *take(6)))
    if riders > 1:
        across = row_gather_steps(rider_in[1], rider_out[1], *take(2))
        next(across)
    run(*steps)
    here = lax.axis_index("col")
    own = o_ref.shape[0] // (2 * chips)
    kept = first(sums_in, operands, results, o_ref, pl.ds(pl.multiple_of(here * own, 8), own))

    def beside():
        if riders > 1:
            for _ in range(4):
                next(across)
        last(kept, operands, results)

    gather_rows(chips, parts, o_ref, *gather_sems, beside)
    if riders > 1:
        run(across)


def gather_rows(chips, parts, o_ref, right_sem, left_sem, mate_sem, line_recv, mate_recv, beside):
    here, chip, core, mate = line_place()
    size = (o_ref.shape[0] // (2 * chips), o_ref.shape[1])

    def copy(j, part, sem, recv, device, block=None):
        block = 2 * j + core if block is None else block
        ref = o_ref.at[spot(0, size, parts, block, part)]
        return remote(ref, ref, sem.at[j, part], recv.at[j, part], device)

    def forward(j, part, rightward, leftward):
        if rightward:

            @pl.when(chip < chips - 1)
            def _():
                copy(j, part, right_sem, line_recv, here + 2).start()

        if leftward:

            @pl.when(chip > 0)
            def _():
                copy(j, part, left_sem, line_recv, here - 2).start()

        copy(j, part, mate_sem, mate_recv, mate).start()

    for part in range(parts):
        forward(chip, part, True, True)
    beside()
    for far in range(1, chips):
        for part in range(parts):

            @pl.when(chip - far >= 0)
            def _():
                copy(chip - far, part, right_sem, line_recv, mate).wait_recv()
                forward(chip - far, part, True, False)

            @pl.when(chip + far < chips)
            def _():
                copy(chip + far, part, left_sem, line_recv, mate).wait_recv()
                forward(chip + far, part, False, True)

    for j in range(chips):
        for part in range(parts):
            copy(j, part, mate_sem, mate_recv, mate, block=2 * j + 1 - core).wait_recv()
            copy(j, part, mate_sem, mate_recv, mate).wait_send()

            @pl.when(jnp.logical_and(j <= chip, chip < chips - 1))
            def _():
                copy(j, part, right_sem, line_recv, here + 2).wait_send()

            @pl.when(jnp.logical_and(j >= chip, chip > 0))
            def _():
                copy(j, part, left_sem, line_recv, here - 2).wait_send()


def line_turn(p, operands, width, results, first, last, chips, ident, riders=(), parts=2):
    rows, cols = p.shape
    own = rows // (2 * chips)
    sems = pltpu.SemaphoreType.DMA((chips, parts))
    longer = pltpu.SemaphoreType.DMA((chips + 1, parts))
    more = []
    ridden = []
    if len(riders) > 0:
        height, part = riders[0].shape
        ridden.append(jax.ShapeDtypeStruct((height, 2 * chips * part), BF16))
        more += [pltpu.SemaphoreType.DMA((chips, 2))] * 5 + [pltpu.SemaphoreType.DMA((2,))]
    if len(riders) > 1:
        ridden.append(jax.ShapeDtypeStruct((3,) + riders[1].shape, BF16))
        more += [pltpu.SemaphoreType.DMA((6,))] * 2
    return pl.pallas_call(
        functools.partial(turn_body, chips, parts, first, last, len(operands), len(results), len(riders)),
        out_shape=(jax.ShapeDtypeStruct((rows, width), BF16),) + tuple(results) + tuple(ridden),
        in_specs=[VM] * (1 + len(operands)) + [VM, ANY][: len(riders)],
        out_specs=(VM,) * (1 + len(results)) + (VM, ANY)[: len(riders)],
        scratch_shapes=[
            pltpu.VMEM((own, cols), F32),
            pltpu.VMEM((chips, own, cols), BF16),
            pltpu.VMEM((chips + 1, own, cols), BF16),
            pltpu.VMEM((chips, own, cols), BF16),
            sems,
            sems,
            sems,
            longer,
            sems,
        ]
        + [sems] * 5
        + more,
        compiler_params=pltpu.CompilerParams(
            collective_id=ident, has_side_effects=True, vmem_limit_bytes=VMEM_LIMIT
        ),
        name="line_turn",
    )(p, *operands, *riders)


def inverse_rms(values):
    return lax.rsqrt(jnp.mean(values * values, axis=1, keepdims=True) + norm_eps)


def turn_forward(width, experts, sums, operands, results, o_ref, own):
    x_ref, gain_ref, a_ref, router_ref, up_ref = operands
    hidden_ref, mid_ref, mid_router_ref, probs_ref = results
    hidden = x_ref[...].astype(F32) + sums[:, :width]
    mid_ref[...] = sums[:, width:].astype(BF16)
    hidden_ref[...] = hidden
    normed = (hidden * inverse_rms(hidden) * gain_ref[...]).astype(BF16)
    o_ref[own, :width] = normed
    mid_router = nt(normed, a_ref[...]).astype(BF16)
    mid_router_ref[...] = mid_router
    logits = nt(normed, router_ref[...]) + nn(mid_router, up_ref[...])
    lane = lax.broadcasted_iota(jnp.int32, logits.shape, 1)
    logits = jnp.where(lane < experts, logits, masked_score)
    exponent = jnp.exp(logits - jnp.max(logits, axis=1, keepdims=True))
    probs = exponent / jnp.sum(exponent, axis=1, keepdims=True)
    probs_ref[...] = probs
    high = probs.astype(BF16)
    rest = probs - high.astype(F32)
    o_ref[own, width:] = (high.astype(F32) + pltpu.roll(rest, experts, 1)).astype(BF16)
    return None


def turn_backward(width, experts, sums, operands, results, o_ref, own):
    g_ref, hidden_ref, gain_ref, a_ref, router_ref, up_ref, probs_ref, mid_router_ref, mid_ref = operands
    pair = sums[:, width:]
    lanes = pair.shape[1]
    grad_probs = pair + pltpu.roll(pair, lanes - experts, 1)
    probs = probs_ref[...]
    grad_logits = (probs * (grad_probs - jnp.sum(probs * grad_probs, axis=1, keepdims=True))).astype(BF16)
    grad_mid = nt(grad_logits, up_ref[...]).astype(BF16)
    grad_normed = sums[:, :width] + nn(grad_logits, router_ref[...]) + nn(grad_mid, a_ref[...])
    hidden = hidden_ref[...]
    inv = inverse_rms(hidden)
    scaled = grad_normed * gain_ref[...]
    grad_hidden = (
        g_ref[...].astype(F32)
        + inv * scaled
        - hidden * (inv * inv * inv * jnp.mean(hidden * scaled, axis=1, keepdims=True))
    )
    grad_hidden = grad_hidden.astype(BF16)
    o_ref[own, :] = grad_hidden
    return grad_logits, grad_mid, grad_hidden


def turn_late(kept, operands, results):
    _, hidden_ref, gain_ref, _, _, _, _, mid_router_ref, mid_ref = operands
    grad_logits, grad_mid, grad_hidden = kept
    hidden = hidden_ref[...]
    normed = (hidden * inverse_rms(hidden) * gain_ref[...]).astype(BF16)
    rank = grad_mid.shape[1]
    late_ref, router_ref = results
    late_ref[pl.ds(0, rank)] = tn(grad_mid, normed)
    late_ref[pl.ds(rank, rank)] = tn(mid_ref[:, :rank], grad_hidden)
    router_ref[...] = tn(mid_router_ref[...], grad_logits)


def row_sums(values):
    lanes = 128
    values = sum(values[:, n : n + lanes] for n in range(0, values.shape[1], lanes))
    high = values.astype(BF16)
    rest = (values - high.astype(F32)).astype(BF16)
    ones = jnp.ones((8, values.shape[1]), BF16)
    return nt(ones, high) + nt(ones, rest)


def project_body(tile, x_ref, gain_ref, wq, wk, wv, a_ref, b_ref, proj_ref, mid_ref, inv_ref, sq_ref):
    part = wq.shape[1]
    for t in range(x_ref.shape[0] // tile):
        rows = pl.ds(t * tile, tile)
        x = x_ref[rows].astype(F32)
        inv = inverse_rms(x)
        inv_ref[rows] = inv
        normed = (x * inv * gain_ref[...]).astype(BF16)
        mid = nt(normed, a_ref[...]).astype(BF16)
        mid_ref[rows] = mid
        for m, w in enumerate((wq, wk, wv)):
            cols = pl.ds(m * part, part)
            proj = nn(normed, w[...]) + nn(mid, b_ref[:, cols])
            proj_ref[rows, cols] = proj
            if m < 2:
                sq_ref[pl.ds(m, 1), rows] = row_sums(proj * proj)[0:1]


def project(x, gain, weights, a_rows, b_cols):
    seq_len, width = x.shape
    part = weights[0].shape[1]
    rank = a_rows.shape[0]
    return pl.pallas_call(
        functools.partial(project_body, min(256, seq_len)),
        out_shape=(
            jax.ShapeDtypeStruct((seq_len, 3 * part), F32),
            jax.ShapeDtypeStruct((seq_len, rank), BF16),
            jax.ShapeDtypeStruct((seq_len, 1), F32),
            jax.ShapeDtypeStruct((2, seq_len), F32),
        ),
        in_specs=[VM] * 7,
        out_specs=(VM,) * 4,
        compiler_params=pltpu.CompilerParams(vmem_limit_bytes=VMEM_LIMIT),
        name="project",
    )(x, gain, *weights, a_rows, b_cols)


def key_limit(start, tile, seq_len, reach):
    return min(seq_len, max(start + tile, reach))


def allowed_keys(start, tile, limit, prefix_len):
    query = start + lax.broadcasted_iota(jnp.int32, (tile, limit), 0)
    key = lax.broadcasted_iota(jnp.int32, (tile, limit), 1)
    return jnp.logical_or(key <= query, key < prefix_len)


def attend_body(
    tile, reach, scale, prefix_ref, proj_ref, inv_ref, gains_ref, cos_ref, sin_ref, map_ref,
    p_ref, att_ref, q_ref, k_ref, v_ref, log_ref,
):
    seq_len, part = att_ref.shape
    prefix_len = prefix_ref[0]
    for h in range(part // HD):
        cols = pl.ds(h * HD, HD)
        for m, ref in ((0, q_ref), (1, k_ref)):
            plain = proj_ref[:, pl.ds(m * part + h * HD, HD)] * inv_ref[:, m : m + 1] * gains_ref[m : m + 1, cols]
            ref[:, cols] = (plain * cos_ref[...] + pltpu.roll(plain, HD // 2, 1) * sin_ref[...]).astype(BF16)
        v_ref[:, cols] = proj_ref[:, pl.ds(2 * part + h * HD, HD)].astype(BF16)
    for start in range(0, seq_len, tile):
        rows = pl.ds(start, tile)
        limit = key_limit(start, tile, seq_len, reach)
        allowed = allowed_keys(start, tile, limit, prefix_len)
        for h in range(part // HD):
            cols = pl.ds(h * HD, HD)
            scores = nt(q_ref[rows, cols], k_ref[pl.ds(0, limit), cols]) * scale
            scores = jnp.where(allowed, scores, masked_score)
            top = jnp.max(scores, axis=1, keepdims=True)
            exponent = jnp.exp(scores - top)
            total = jnp.sum(exponent, axis=1, keepdims=True)
            weights = (exponent / total).astype(BF16)
            att_ref[rows, cols] = nn(weights, v_ref[pl.ds(0, limit), cols]).astype(BF16)
            log_ref[rows, h : h + 1] = top + jnp.log(total)
        p_ref[rows] = nn(att_ref[rows], map_ref[...]).astype(BF16)


def attend(prefix, proj, inv, gains, tables, out_map, reach, scale):
    seq_len = proj.shape[0]
    part = proj.shape[1] // 3
    heads = jax.ShapeDtypeStruct((seq_len, part), BF16)
    return pl.pallas_call(
        functools.partial(attend_body, min(256, seq_len), reach, scale),
        out_shape=(
            jax.ShapeDtypeStruct((seq_len, out_map.shape[1]), BF16),
            heads,
            heads,
            heads,
            heads,
            jax.ShapeDtypeStruct((seq_len, part // HD), F32),
        ),
        in_specs=[pl.BlockSpec(memory_space=pltpu.SMEM)] + [VM] * 6,
        out_specs=(VM,) * 6,
        compiler_params=pltpu.CompilerParams(vmem_limit_bytes=VMEM_LIMIT),
        name="attend",
    )(prefix, proj, inv, gains, *tables, out_map)


def attend_back_body(
    tile, reach, scale, prefix_ref, g_ref, map_ref, b_ref, att_ref, q_ref, k_ref, v_ref, log_ref, proj_ref,
    gains_ref, cos_ref, sin_ref, scaled_ref, dv_ref, stat_ref, ga_ref, da_ref, dq_acc, dk_acc, dv_acc,
):
    seq_len, part = att_ref.shape
    prefix_len = prefix_ref[0]
    grad_a = jnp.zeros(ga_ref.shape, F32)
    for start in range(0, seq_len, tile):
        rows = pl.ds(start, tile)
        grads = g_ref[rows]
        da_ref[rows] = nt(grads, map_ref[...]).astype(BF16)
        grad_mid = nt(grads, b_ref[...]).astype(BF16)
        grad_a += tn(grad_mid, att_ref[rows])
    ga_ref[...] = grad_a
    dk_acc[...] = jnp.zeros_like(dk_acc)
    dv_acc[...] = jnp.zeros_like(dv_acc)
    for start in range(0, seq_len, tile):
        rows = pl.ds(start, tile)
        limit = key_limit(start, tile, seq_len, reach)
        keys = pl.ds(0, limit)
        allowed = allowed_keys(start, tile, limit, prefix_len)
        for h in range(part // HD):
            cols = pl.ds(h * HD, HD)
            query, key = q_ref[rows, cols], k_ref[keys, cols]
            grads = da_ref[rows, cols]
            scores = jnp.where(allowed, nt(query, key) * scale, masked_score)
            weights = jnp.exp(scores - log_ref[rows, h : h + 1])
            grad_weights = nt(grads, v_ref[keys, cols])
            dot = jnp.sum(weights * grad_weights, axis=1, keepdims=True)
            grad_scores = (weights * (grad_weights - dot)).astype(BF16)
            dq_acc[rows, cols] = nn(grad_scores, key) * scale
            dk_acc[keys, cols] += tn(grad_scores, query) * scale
            dv_acc[keys, cols] += tn(weights.astype(BF16), grads)
    dv_ref[...] = dv_acc[...].astype(BF16)
    for m, acc in ((0, dq_acc), (1, dk_acc)):
        for start in range(0, seq_len, tile):
            rows = pl.ds(start, tile)
            total = jnp.zeros((8, tile), F32)
            for h in range(part // HD):
                cols = pl.ds(h * HD, HD)
                here = pl.ds(m * part + h * HD, HD)
                plain = acc[rows, cols]
                turned = plain * cos_ref[rows] - pltpu.roll(plain, HD // 2, 1) * sin_ref[rows]
                scaled = turned * gains_ref[m : m + 1, cols]
                scaled_ref[rows, here] = scaled
                total += row_sums(proj_ref[rows, here] * scaled)
            stat_ref[pl.ds(m, 1), rows] = total[0:1]


def attend_back(prefix, grads, out_map, b_out, saved, proj, gains, tables, reach, scale):
    seq_len = proj.shape[0]
    part = proj.shape[1] // 3
    return pl.pallas_call(
        functools.partial(attend_back_body, min(256, seq_len), reach, scale),
        out_shape=(
            jax.ShapeDtypeStruct((seq_len, 2 * part), F32),
            jax.ShapeDtypeStruct((seq_len, part), BF16),
            jax.ShapeDtypeStruct((2, seq_len), F32),
            jax.ShapeDtypeStruct((b_out.shape[0], part), F32),
        ),
        in_specs=[pl.BlockSpec(memory_space=pltpu.SMEM)] + [VM] * 12,
        out_specs=(VM,) * 4,
        scratch_shapes=[pltpu.VMEM((seq_len, part), BF16)] + [pltpu.VMEM((seq_len, part), F32)] * 3,
        compiler_params=pltpu.CompilerParams(vmem_limit_bytes=VMEM_LIMIT),
        name="attend_back",
    )(prefix, grads, out_map, b_out, *saved, proj, gains, *tables)


def inputs_back_body(
    tile, extra, scaled_ref, dv_ref, proj_ref, inv_ref, stat_ref, wq, wk, wv, b_ref, a_ref, x_ref, inv1_ref,
    gain_ref, mid_ref, late_ref, router_ref, p_ref, gb_ref, w_ref, w_sems,
):
    seq_len, width = x_ref.shape
    part = dv_ref.shape[1]
    ranks = a_ref.shape[0]
    rank = ranks // 3
    fetches = [
        pltpu.make_async_copy(w, w_ref.at[:, pl.ds(m * part, part)], w_sems.at[m]) for m, w in enumerate((wq, wk, wv))
    ]
    for fetch in fetches:
        fetch.start()
    grad_b = jnp.zeros((ranks, 3 * part), F32)
    grad_a = jnp.zeros((ranks, width), F32)
    stats = jnp.zeros((8, width), F32)
    line = lax.broadcasted_iota(jnp.int32, (8, width), 0)
    for t in range(seq_len // tile):
        rows = pl.ds(t * tile, tile)
        grads = []
        for m in range(2):
            cols = pl.ds(m * part, part)
            inv = inv_ref[rows, m : m + 1]
            shift = inv * inv * inv * stat_ref[rows, m : m + 1]
            grads.append((inv * scaled_ref[rows, cols] - proj_ref[rows, cols] * shift).astype(BF16))
        grads = jnp.concatenate(grads + [dv_ref[rows]], axis=1)
        middle = nt(grads, b_ref[...]).astype(BF16)
        if t == 0:
            for fetch in fetches:
                fetch.wait()
        normed_part = nt(grads, w_ref[...]) + nn(middle, a_ref[...])
        grad_b += tn(mid_ref[rows], grads)
        p_ref[rows] = normed_part.astype(BF16)
        scaled_x = x_ref[rows].astype(F32) * gain_ref[...]
        normed = (scaled_x * inv1_ref[rows]).astype(BF16)
        grad_a += tn(middle, normed)
        first = row_sums(scaled_x * normed_part)
        for j in range(tile // part):
            wide = jnp.concatenate([first[:, j * part : (j + 1) * part]] * (width // part), axis=1)
            stats = jnp.where(line == (t * tile) // part + j, wide, stats)
    for m in range(3):
        gb_ref[pl.ds(m * rank, rank)] = grad_b[m * rank : (m + 1) * rank, m * part : (m + 1) * part]
    high = stats.astype(BF16).astype(F32)
    router = router_ref[...]
    if part > router.shape[1]:
        router = jnp.concatenate([router, jnp.zeros((rank, part - router.shape[1]), F32)], axis=1)
    pieces = [
        grad_a,
        late_ref[...],
        jnp.concatenate([router] * (width // part), axis=1),
        high,
        stats - high,
    ]
    used = sum(piece.shape[0] for piece in pieces)
    pieces.append(jnp.zeros((extra - used, width), F32))
    p_ref[pl.ds(seq_len, extra)] = jnp.concatenate(pieces, axis=0).astype(BF16)


def inputs_back(extra, *operands):
    x = operands[10]
    seq_len, width = x.shape
    part = operands[1].shape[1]
    ranks = operands[9].shape[0]
    return pl.pallas_call(
        functools.partial(inputs_back_body, min(256, seq_len), extra),
        out_shape=(
            jax.ShapeDtypeStruct((seq_len + extra, width), BF16),
            jax.ShapeDtypeStruct((ranks, part), F32),
        ),
        in_specs=[ANY if 5 <= n < 8 else VM for n in range(len(operands))],
        out_specs=(VM,) * 2,
        scratch_shapes=[pltpu.VMEM((width, 3 * part), BF16), pltpu.SemaphoreType.DMA((3,))],
        compiler_params=pltpu.CompilerParams(vmem_limit_bytes=VMEM_LIMIT),
        name="inputs_back",
    )(*operands)


def moments(chips, subs):
    when = {}
    for j in range(chips):
        for chip in range(j):
            own = subs * (chips - j) + 1
            when[chip, j] = max(own, when[chip - 1, j] + 3) if chip > 0 else own
        for chip in range(chips - 1, j, -1):
            own = subs * (chips - chip + j) + 1
            when[chip, j] = max(own, when[chip + 1, j] + 3) if chip < chips - 1 else own
    last = chips * subs
    return {place: min(time, last) for place, time in when.items()}


def moe_turn_body(experts, chips, subs, count, x_ref, g_ref, routes_ref, *refs):
    refs = list(refs)

    def take(number):
        taken = refs[:number]
        del refs[:number]
        return taken

    operands = take(9)
    gate_w, up_w = take(2)
    downs = take(count)
    out_ref, o_ref = take(2)
    results = take(2)
    p_ref, out_acc, dx_acc, gate_acc, wgu, wd, x_buf, g_buf = take(8)
    sums_in, pair_buf, line_buf, sums = take(4)
    w_sems, tile_sems, right_sem, left_sem, mate_sem, line_recv, mate_recv = take(7)
    gather_sems = refs
    here, chip, core, mate = line_place()
    row = lax.axis_index("row")
    hidden = wd.shape[1]
    tokens, width = out_ref.shape
    own = tokens // (2 * chips)
    tile = 2 * own
    lanes = gate_acc.shape[1]
    local = gate_w.shape[0]
    pieces = gate_w.shape[2] // hidden
    steps = local * pieces
    each = steps // subs

    def fetches(step, e, piece):
        if count == 1:
            place = piece
            down = downs[0].at[e, pl.ds(piece * hidden, hidden)]
        else:
            place = 2 * ((row // 2 + piece // 2) % 2) + (row + piece) % 2
            down = downs[1].at[piece - 1, e] if piece > 0 else downs[0].at[e]
        units = pl.ds(pl.multiple_of(place * hidden, 128), hidden)
        return (
            pltpu.make_async_copy(gate_w.at[e, :, units], wgu.at[step, :, pl.ds(0, hidden)], w_sems.at[step, 0]),
            pltpu.make_async_copy(up_w.at[e, :, units], wgu.at[step, :, pl.ds(hidden, hidden)], w_sems.at[step, 1]),
            pltpu.make_async_copy(down, wd.at[step], w_sems.at[step, 2]),
        )

    def order(s):
        right = chips - 1 - chip
        return jnp.where(s < right, chips - 1 - s, jnp.where(s < chips - 1, s - right, chip))

    def tile_rows(s):
        return pl.ds(pl.multiple_of(order(s) * tile, 8), tile)

    def tiles(s):
        slot = s % 2
        return (
            pltpu.make_async_copy(x_ref.at[tile_rows(s)], x_buf.at[slot], tile_sems.at[slot, 0]),
            pltpu.make_async_copy(g_ref.at[tile_rows(s)], g_buf.at[slot], tile_sems.at[slot, 1]),
        )

    for copy in tiles(0):
        copy.start()
    for step in range(steps):
        for copy in fetches(step, step // pieces, step % pieces):
            copy.start()
    line_barrier(chips)

    def block(number):
        return pl.ds(pl.multiple_of(number * own, 8), own)

    def mate_copy(j):
        return remote(p_ref.at[block(2 * j + 1 - core)], pair_buf.at[j], mate_sem.at[j], mate_recv.at[j], mate)

    def line_copy(j, slot, sem, device):
        return remote(sums.at[j], line_buf.at[slot], sem.at[j], line_recv.at[slot], device)

    def pair_sum(j):
        mate_copy(j).wait_recv()
        return p_ref[block(2 * j + core)].astype(F32) + pair_buf[j].astype(F32)

    def pass_on(at, j):
        rightward = j > at
        total = pair_sum(j)
        if 0 < at < chips - 1:
            line_copy(j, j, right_sem if rightward else left_sem, mate).wait_recv()
            total = total + line_buf[j].astype(F32)
        sums[j] = total.astype(BF16)
        if rightward:
            line_copy(j, j, right_sem, here + 2).start()
        else:
            line_copy(j, chips if at - j == 1 else j, left_sem, here - 2).start()

    when = moments(chips, subs)

    def one_sub(k, carry):
        s, sub = k // subs, k % subs
        slot = s % 2
        rows = tile_rows(s)

        @pl.when(sub == 0)
        def _():
            for copy in tiles(s):
                copy.wait()

            @pl.when(s + 1 < chips)
            def _():
                for copy in tiles(s + 1):
                    copy.start()

            out_acc[...] = jnp.zeros_like(out_acc)
            dx_acc[...] = jnp.zeros_like(dx_acc)
            gate_acc[...] = jnp.zeros_like(gate_acc)

        def one_step(step, carry):
            @pl.when(s == 0)
            def _():
                units = pl.ds(0, hidden)
                for number, (source, place) in enumerate(((gate_w, 0), (up_w, hidden))):
                    pltpu.make_async_copy(
                        source.at[0, :, units], wgu.at[step, :, pl.ds(place, hidden)], w_sems.at[step, number]
                    ).wait()
                pltpu.make_async_copy(downs[0].at[0, units], wd.at[step], w_sems.at[step, 2]).wait()

            e = here * local + step // pieces
            lane = lax.broadcasted_iota(jnp.int32, (tile, lanes), 1)
            mine = lane == e
            halves = jnp.logical_or(mine, lane == e + experts)
            named = jnp.sum(jnp.where(routes_ref[rows] == e, 1.0, 0.0), axis=1, keepdims=True)
            gate = jnp.sum(jnp.where(halves, x_buf[slot, :, width:].astype(F32), 0.0), axis=1, keepdims=True)
            gate = gate * named
            both = nn(x_buf[slot, :, :width], wgu[step])
            gate_in, up_in = both[:, :hidden], both[:, hidden:]
            sigmoid = jax.nn.sigmoid(gate_in)
            silu = gate_in * sigmoid
            active = silu * up_in
            back = nt(g_buf[slot], wd[step])
            d_gate = jnp.sum(active * back, axis=1, keepdims=True) * named
            gate_acc[...] += jnp.where(mine, d_gate, 0.0)
            out_acc[...] += nn((active * gate).astype(BF16), wd[step])
            d_active = back * gate
            d_gate_in = d_active * up_in * (sigmoid + silu * (1.0 - sigmoid))
            d_up_in = d_active * silu
            d_both = jnp.concatenate([d_gate_in.astype(BF16), d_up_in.astype(BF16)], axis=1)
            dx_acc[...] += nt(d_both, wgu[step])
            return carry

        lax.fori_loop(sub * each, (sub + 1) * each, one_step, 0)

        @pl.when(sub == subs - 1)
        def _():
            out_ref[rows] = out_acc[...].astype(BF16)
            p_ref[rows, :width] = dx_acc[...].astype(BF16)
            high = gate_acc[...].astype(BF16).astype(F32)
            rest = gate_acc[...] - high
            p_ref[rows, width:] = (high + pltpu.roll(rest, experts, 1)).astype(BF16)
            mate_copy(order(s)).start()

            @pl.when(s == chips - 1)
            def _():
                out_ref[block(here)] = (out_acc[pl.ds(pl.multiple_of(core * own, 8), own)] + operands[1][...]).astype(BF16)

        for (at, j), time in sorted(when.items(), key=lambda item: (item[1], abs(item[0][0] - item[0][1]))):

            @pl.when(jnp.logical_and(chip == at, k == time - 1))
            def _():
                pass_on(at, j)

        return carry

    lax.fori_loop(0, chips * subs, one_sub, 0)
    sums_in[...] = pair_sum(chip)

    @pl.when(chip > 0)
    def _():
        line_copy(chip, chip, right_sem, mate).wait_recv()
        sums_in[...] += line_buf[chip].astype(F32)

    @pl.when(chip < chips - 1)
    def _():
        line_copy(chip, chips, left_sem, mate).wait_recv()
        sums_in[...] += line_buf[chips].astype(F32)

    for j in range(chips):
        mate_copy(j).wait_send()

        @pl.when(j > chip)
        def _():
            line_copy(j, j, right_sem, mate).wait_send()

        @pl.when(j < chip)
        def _():
            line_copy(j, j, left_sem, mate).wait_send()

    kept = turn_backward(width, experts, sums_in, operands, results, o_ref, block(here))
    gather_rows(chips, 2, o_ref, *gather_sems, lambda: turn_late(kept, operands, results))


def moe_turn(x, g, routes, operands, experts, gate_w, up_w, downs, results, chips, ident):
    tokens, width = g.shape
    wide = x.shape[1]
    lanes = wide - width
    own = tokens // (2 * chips)
    hidden = downs[0].shape[1] if len(downs) > 1 else min(256, gate_w.shape[2] // 4)
    steps = gate_w.shape[0] * gate_w.shape[2] // hidden
    subs = min(4, steps)
    whole = jax.ShapeDtypeStruct((tokens, width), BF16)
    per_chip = pltpu.SemaphoreType.DMA((chips,))
    halves = pltpu.SemaphoreType.DMA((chips, 2))
    return pl.pallas_call(
        functools.partial(moe_turn_body, experts, chips, subs, len(downs)),
        out_shape=(whole, whole) + tuple(results),
        in_specs=[ANY, ANY] + [VM] * (1 + len(operands)) + [ANY] * (2 + len(downs)),
        out_specs=(VM,) * (2 + len(results)),
        scratch_shapes=[
            pltpu.VMEM((tokens, wide), BF16),
            pltpu.VMEM((2 * own, width), F32),
            pltpu.VMEM((2 * own, width), F32),
            pltpu.VMEM((2 * own, lanes), F32),
            pltpu.VMEM((steps, width, 2 * hidden), BF16),
            pltpu.VMEM((steps, hidden, width), BF16),
            pltpu.VMEM((2, 2 * own, wide), BF16),
            pltpu.VMEM((2, 2 * own, width), BF16),
            pltpu.VMEM((own, wide), F32),
            pltpu.VMEM((chips, own, wide), BF16),
            pltpu.VMEM((chips + 1, own, wide), BF16),
            pltpu.VMEM((chips, own, wide), BF16),
            pltpu.SemaphoreType.DMA((steps, 3)),
            pltpu.SemaphoreType.DMA((2, 2)),
            per_chip,
            per_chip,
            per_chip,
            pltpu.SemaphoreType.DMA((chips + 1,)),
            per_chip,
        ]
        + [halves] * 5,
        compiler_params=pltpu.CompilerParams(
            collective_id=ident, has_side_effects=True, vmem_limit_bytes=VMEM_MOST
        ),
        name="moe_turn",
    )(x, g, routes, *operands, gate_w, up_w, *downs)


def rope_tables(length, head_dim):
    half_dim = head_dim // 2
    frequency = rope_base ** (-(2.0 * jnp.arange(half_dim, dtype=F32)) / head_dim)
    angles = jnp.arange(length, dtype=F32)[:, None] * frequency[None, :]
    cosine, sine = jnp.cos(angles), jnp.sin(angles)
    return jnp.concatenate([cosine, cosine], axis=1), jnp.concatenate([-sine, sine], axis=1)


def shards(
    inputs,
    cotangent,
    norm_first,
    norm_second,
    query_gain,
    key_gain,
    w_query,
    w_key,
    w_value,
    w_out,
    w_router,
    w_gate,
    w_up,
    w_down,
    adapter_a,
    adapter_b,
    adapter_router,
    routes,
    prefix,
    adapter_index,
):
    seq_len, width_part = inputs.shape
    col_count = lax.axis_size("col")
    row_count = lax.axis_size("row")
    col_index = lax.axis_index("col")
    row_index = lax.axis_index("row")
    chips = col_count // 2
    full_width = width_part * col_count
    head_width = w_query.shape[1]
    local_experts = w_gate.shape[0]
    expert_total = w_router.shape[1]
    feature_start = col_index * width_part
    head_start = col_index * head_width
    own_rows = seq_len // col_count
    row_start = col_index * own_rows
    score_scale = HD ** (-0.5)
    reach = seq_len // 2
    lanes = 128

    def columns(array, axis_num):
        return lax.dynamic_slice_in_dim(array, feature_start, width_part, axis_num)

    def head_cols(array, axis_num=1):
        return lax.dynamic_slice_in_dim(array, head_start, head_width, axis_num)

    def held_rows(array):
        return lax.dynamic_slice_in_dim(array, row_start, own_rows, 0)

    def col_sum(pair, ident):
        return jnp.sum(small_gather(pair, col_count, ident), axis=0)

    full_gate = lax.all_gather(w_gate, "row", axis=2, tiled=True)
    full_up = lax.all_gather(w_up, "row", axis=2, tiled=True)
    across = row_count == 4
    riders = (cotangent, w_down) if across else (cotangent,)
    adapter_slot = adapter_index[0]
    chosen_a = lax.dynamic_index_in_dim(adapter_a, adapter_slot, 1, keepdims=False).swapaxes(1, 2)
    chosen_b = lax.dynamic_index_in_dim(adapter_b, adapter_slot, 1, keepdims=False)
    chosen_router = lax.dynamic_index_in_dim(adapter_router, adapter_slot, 0, keepdims=False)
    rank = chosen_a.shape[1]
    a_three = chosen_a[:3].reshape(3 * rank, full_width)
    b_three = head_cols(chosen_b[:3].reshape(3 * rank, full_width))
    blank = jnp.zeros((rank, head_width), BF16)
    b_cols = jnp.concatenate(
        [
            jnp.concatenate([b_three[m * rank : (m + 1) * rank] if n == m else blank for n in range(3)], axis=0)
            for m in range(3)
        ],
        axis=1,
    )
    a_out = head_cols(chosen_a[3])
    out_map = (w_out.astype(F32) + tn(a_out, chosen_b[3])).astype(BF16)
    out_wide = jnp.concatenate([out_map, a_out.T, jnp.zeros((head_width, lanes - rank), BF16)], axis=1)
    router_rows = jnp.pad(w_router.T, ((0, lanes - expert_total), (0, 0)))
    router_up = jnp.pad(chosen_router, ((0, 0), (0, lanes - expert_total)))
    gains = jnp.stack([head_cols(query_gain, 0), head_cols(key_gain, 0)])
    tables = rope_tables(seq_len, HD)
    gain_first, gain_second = norm_first[None], norm_second[None]

    full_inputs = line_gather(inputs, chips, 1, 0)
    proj, mid, inv_first, squares = project(
        full_inputs, gain_first, (w_query, w_key, w_value), a_three, b_cols
    )
    inv = lax.rsqrt(col_sum(squares, 1) / full_width + norm_eps).T
    part_out, attended, rot_query, rot_key, value_rows, log_totals = attend(
        prefix, proj, inv, gains, tables, out_wide, reach, score_scale
    )
    wide = full_width + lanes
    row_shape = jax.ShapeDtypeStruct
    normed_two, hidden_rows, mid_out, mid_router, probs, full_cot, *down_others = line_turn(
        part_out,
        (held_rows(full_inputs), gain_second, chosen_a[4], router_rows, router_up),
        wide,
        (
            row_shape((own_rows, full_width), F32),
            row_shape((own_rows, lanes), BF16),
            row_shape((own_rows, rank), BF16),
            row_shape((own_rows, lanes), F32),
        ),
        functools.partial(turn_forward, full_width, expert_total),
        lambda kept, operands, results: None,
        chips,
        2,
        riders,
    )
    if across:
        downs = (w_down,) + tuple(down_others)
    else:
        downs = (lax.all_gather(w_down, "row", axis=1, tiled=True),)

    moe_out, grad_attn, late, router_late = moe_turn(
        normed_two,
        full_cot,
        routes,
        (
            held_rows(full_cot),
            hidden_rows,
            gain_second,
            chosen_a[4],
            router_rows,
            router_up,
            probs,
            mid_router,
            mid_out,
        ),
        expert_total,
        full_gate,
        full_up,
        downs,
        (row_shape((2 * rank, full_width), F32), row_shape((rank, lanes), F32)),
        chips,
        7,
    )
    moe_out, grad_attn = lax.optimization_barrier((moe_out, grad_attn))
    layer_out = lax.psum_scatter(moe_out, "col", scatter_dimension=1, tiled=True)

    scaled, grad_value, norm_stats, grad_a_out = attend_back(
        prefix,
        grad_attn,
        out_map,
        chosen_b[3],
        (attended, rot_query, rot_key, value_rows, log_totals),
        proj,
        gains,
        tables,
        reach,
        score_scale,
    )
    stats = (col_sum(norm_stats, 10) / full_width).T
    extra = 128
    normed_part, grad_b_three = inputs_back(
        extra,
        scaled,
        grad_value,
        proj,
        inv,
        stats,
        w_query,
        w_key,
        w_value,
        b_cols,
        a_three,
        full_inputs,
        inv_first,
        gain_first,
        mid,
        late,
        router_late,
    )
    summed_part = line_reduce(normed_part, chips, 1, 12)
    stat_rows = seq_len // width_part
    tail = summed_part[seq_len:]
    stat_start = 6 * rank
    first_stat = (
        tail[stat_start : stat_start + stat_rows] + tail[stat_start + 8 : stat_start + 8 + stat_rows]
    ).reshape(seq_len, 1)
    grad_inputs = (
        columns(grad_attn, 1).astype(F32)
        + inv_first * columns(norm_first, 0) * summed_part[:seq_len]
        - inputs.astype(F32) * (inv_first * inv_first * inv_first * first_stat / full_width)
    )

    held_adapters = adapter_a.shape[1] // row_count
    flat = jnp.concatenate(
        [
            tail[: 6 * rank],
            grad_a_out,
            grad_b_three,
            jnp.broadcast_to(adapter_slot.astype(F32), (8, width_part)),
        ]
    ).astype(BF16)
    every = lax.all_gather(flat, "row", axis=0).astype(F32)
    owners = every[:, -1, 0]
    held_ids = (row_index * held_adapters + jnp.arange(held_adapters)).astype(F32)
    pick = (owners[None, :] == held_ids[:, None])[:, :, None, None]
    summed = jnp.sum(jnp.where(pick, every[None], 0.0), axis=1)
    pieces = [summed[:, n * rank : (n + 1) * rank] for n in range(10)]
    query_a, key_a, value_a, router_a, out_b, router_up_grad, out_a, query_b, key_b, value_b = pieces
    grad_a = jnp.stack([query_a, key_a, value_a, out_a, router_a]).swapaxes(2, 3)
    grad_b = jnp.stack([query_b, key_b, value_b, out_b])
    grad_router = router_up_grad[:, :, :expert_total]
    return (layer_out, grad_inputs, grad_a, grad_b, grad_router)


def solution(mesh):
    placed = (
        P("row", "col"),
        P("row", "col"),
        P(),
        P(),
        P(),
        P(),
        P(None, "col"),
        P(None, "col"),
        P(None, "col"),
        P("col", None),
        P(),
        P("col", None, "row"),
        P("col", None, "row"),
        P("col", "row", None),
        P(),
        P(),
        P(),
        P("row", None),
        P("row"),
        P("row"),
    )
    return jax.shard_map(
        shards,
        mesh=mesh,
        in_specs=placed,
        out_specs=(
            P("row", "col"),
            P("row", "col"),
            P(None, "row", "col", None),
            P(None, "row", None, "col"),
            P("row", None, None),
        ),
        check_vma=False,
    )
```

```python
import functools

import jax
import jax.numpy as jnp
from jax import lax
from jax.experimental import pallas as pl
from jax.experimental.pallas import tpu as pltpu
from jax.sharding import PartitionSpec as P

HD = 128
F32, BF16 = jnp.float32, jnp.bfloat16
MESH_ID = pl.DeviceIdType.MESH
VM = pl.BlockSpec(memory_space=pltpu.VMEM)
ANY = pl.BlockSpec(memory_space=pl.ANY)
VMEM_LIMIT = 60 * 1024 * 1024
VMEM_MOST = 63 * 1024 * 1024

norm_eps = 1e-05
rope_base = 10000.0
masked_score = -1e30


def nn(left, right):
    return jnp.dot(left, right, preferred_element_type=F32)


def nt(left, right):
    return lax.dot_general(left, right, (((1,), (1,)), ((), ())), preferred_element_type=F32)


def tn(left, right):
    return lax.dot_general(left, right, (((0,), (0,)), ((), ())), preferred_element_type=F32)


def remote(src, dst, send_sem, recv_sem, device):
    return pltpu.make_async_remote_copy(
        src_ref=src,
        dst_ref=dst,
        send_sem=send_sem,
        recv_sem=recv_sem,
        device_id={"col": device},
        device_id_type=MESH_ID,
    )


def line_place():
    here = lax.axis_index("col")
    core = here % 2
    return here, here // 2, core, here + 1 - 2 * core


def line_barrier(chips, across=()):
    here, chip, core, mate = line_place()
    barrier = pltpu.get_barrier_semaphore()
    has_left, has_right = chip > 0, chip < chips - 1
    for other in across:
        pl.semaphore_signal(barrier, inc=1, device_id={"row": other}, device_id_type=MESH_ID)
    pl.semaphore_signal(barrier, inc=1, device_id={"col": mate}, device_id_type=MESH_ID)

    @pl.when(has_left)
    def _():
        pl.semaphore_signal(barrier, inc=1, device_id={"col": here - 2}, device_id_type=MESH_ID)

    @pl.when(has_right)
    def _():
        pl.semaphore_signal(barrier, inc=1, device_id={"col": here + 2}, device_id_type=MESH_ID)

    inner = jnp.logical_and(has_left, has_right)

    @pl.when(inner)
    def _():
        pl.semaphore_wait(barrier, 3 + len(across))

    @pl.when(jnp.logical_not(inner))
    def _():
        pl.semaphore_wait(barrier, 2 + len(across))


def spot(axis, size, parts, block, part):
    rows, cols = size
    step = rows // parts
    if axis == 0:
        return (pl.ds(pl.multiple_of(block * rows + part * step, 8), step), slice(None))
    return (pl.ds(part * step, step), pl.ds(pl.multiple_of(block * cols, 128), cols))


def run(*steps):
    steps = list(steps)
    while steps:
        for one in list(steps):
            if next(one, steps) is steps:
                steps.remove(one)


def gather_body(chips, parts, axis, riders, x_ref, *refs):
    line_barrier(chips, row_partners() if riders else ())
    o_ref = refs[riders]
    sems = refs[2 * riders + 1 :]
    steps = [gather_steps(chips, parts, axis, x_ref, o_ref, *sems[:6])]
    if riders:
        steps.append(row_gather_steps(2, refs[0], refs[2], *sems[6:]))
    run(*steps)


def gather_steps(chips, parts, axis, x_ref, o_ref, right_sem, left_sem, mate_sem, line_recv, mate_recv, own_sem):
    here, chip, core, mate = line_place()
    size = x_ref.shape
    step = size[0] // parts

    def at(block, part):
        return o_ref.at[spot(axis, size, parts, block, part)]

    def copy(j, part, sem, recv, device, first=False, block=None):
        block = 2 * j + core if block is None else block
        src = x_ref.at[pl.ds(part * step, step)] if first else at(block, part)
        return remote(src, at(block, part), sem.at[j, part], recv.at[j, part], device)

    def forward(j, part, rightward, leftward, first):
        if rightward:

            @pl.when(chip < chips - 1)
            def _():
                copy(j, part, right_sem, line_recv, here + 2, first).start()

        if leftward:

            @pl.when(chip > 0)
            def _():
                copy(j, part, left_sem, line_recv, here - 2, first).start()

        copy(j, part, mate_sem, mate_recv, mate, first).start()

    for part in range(parts):
        forward(chip, part, True, True, True)
    own = []
    for part in range(parts):
        own.append(
            pltpu.make_async_copy(x_ref.at[pl.ds(part * step, step)], at(here, part), own_sem.at[part])
        )
        own[-1].start()
    yield
    for far in range(1, chips):
        for part in range(parts):

            @pl.when(chip - far >= 0)
            def _():
                copy(chip - far, part, right_sem, line_recv, mate).wait_recv()
                forward(chip - far, part, True, False, False)

            @pl.when(chip + far < chips)
            def _():
                copy(chip + far, part, left_sem, line_recv, mate).wait_recv()
                forward(chip + far, part, False, True, False)

        yield

    for own_copy in own:
        own_copy.wait()
    for j in range(chips):
        for part in range(parts):
            copy(j, part, mate_sem, mate_recv, mate, block=2 * j + 1 - core).wait_recv()
            copy(j, part, mate_sem, mate_recv, mate).wait_send()

            @pl.when(jnp.logical_and(j <= chip, chip < chips - 1))
            def _():
                copy(j, part, right_sem, line_recv, here + 2).wait_send()

            @pl.when(jnp.logical_and(j >= chip, chip > 0))
            def _():
                copy(j, part, left_sem, line_recv, here - 2).wait_send()


def line_gather(x, chips, axis, ident, parts=2, rider=None):
    rows, cols = x.shape
    sems = pltpu.SemaphoreType.DMA((chips, parts))
    shape = (2 * chips * rows, cols) if axis == 0 else (rows, 2 * chips * cols)
    whole = jax.ShapeDtypeStruct(shape, x.dtype)
    more = () if rider is None else (rider,)
    ridden = tuple(jax.ShapeDtypeStruct((3,) + one.shape, one.dtype) for one in more)
    return pl.pallas_call(
        functools.partial(gather_body, chips, parts, axis, len(more)),
        out_shape=(whole,) + ridden,
        in_specs=[VM] + [ANY] * len(more),
        out_specs=(VM,) + (ANY,) * len(more),
        scratch_shapes=[sems] * 5
        + [pltpu.SemaphoreType.DMA((parts,))]
        + [pltpu.SemaphoreType.DMA((6,))] * (2 * len(more)),
        compiler_params=pltpu.CompilerParams(
            collective_id=ident, has_side_effects=True, vmem_limit_bytes=VMEM_LIMIT
        ),
        name="line_gather",
    )(x, *more)


def reduce_steps(
    chips, parts, axis, p_ref, o_ref, pair_buf, line_buf, sums, right_sem, left_sem, mate_sem, line_recv, mate_recv
):
    here, chip, core, mate = line_place()
    size = o_ref.shape
    step = size[0] // parts

    def rows(part):
        return pl.ds(part * step, step)

    def at(block, part):
        return spot(axis, size, parts, block, part)

    def mate_copy(j, part):
        return remote(
            p_ref.at[at(2 * j + 1 - core, part)],
            pair_buf.at[j, rows(part)],
            mate_sem.at[j, part],
            mate_recv.at[j, part],
            mate,
        )

    def line_copy(j, slot, part, sem, device):
        return remote(
            sums.at[j, rows(part)], line_buf.at[slot, rows(part)], sem.at[j, part], line_recv.at[slot, part], device
        )

    for far in range(chips - 1, -1, -1):
        for part in range(parts):

            @pl.when(chip + far < chips)
            def _():
                mate_copy(chip + far, part).start()

            if far > 0:

                @pl.when(chip - far >= 0)
                def _():
                    mate_copy(chip - far, part).start()

    yield

    def pair_sum(j, part):
        mate_copy(j, part).wait_recv()
        return p_ref[at(2 * j + core, part)].astype(F32) + pair_buf[j, rows(part)].astype(F32)

    def pass_on(j, slot, part, more, sem, device):
        @pl.when(more)
        def _():
            line_copy(j, j, part, sem, mate).wait_recv()
            total = pair_sum(j, part) + line_buf[j, rows(part)].astype(F32)
            sums[j, rows(part)] = total.astype(BF16)

        @pl.when(jnp.logical_not(more))
        def _():
            sums[j, rows(part)] = pair_sum(j, part).astype(BF16)

        line_copy(j, slot, part, sem, device).start()

    for far in range(chips - 1, 0, -1):
        for part in range(parts):

            @pl.when(chip + far < chips)
            def _():
                pass_on(chip + far, chip + far, part, chip > 0, right_sem, here + 2)

            @pl.when(chip - far >= 0)
            def _():
                pass_on(
                    chip - far, chips if far == 1 else chip - far, part, chip < chips - 1, left_sem, here - 2
                )

        yield

    for part in range(parts):
        o_ref[rows(part)] = pair_sum(chip, part)

        @pl.when(chip > 0)
        def _():
            line_copy(chip, chip, part, right_sem, mate).wait_recv()
            o_ref[rows(part)] += line_buf[chip, rows(part)].astype(F32)

        @pl.when(chip < chips - 1)
        def _():
            line_copy(chip, chips, part, left_sem, mate).wait_recv()
            o_ref[rows(part)] += line_buf[chips, rows(part)].astype(F32)

    for j in range(chips):
        for part in range(parts):
            mate_copy(j, part).wait_send()

            @pl.when(j > chip)
            def _():
                line_copy(j, j, part, right_sem, mate).wait_send()

            @pl.when(j < chip)
            def _():
                line_copy(j, j, part, left_sem, mate).wait_send()


def small_body(count, x_ref, o_ref, send_sem, recv_sem):
    here = lax.axis_index("col")
    barrier = pltpu.get_barrier_semaphore()
    for hop in range(1, count):
        other = lax.rem(here + hop, count)
        pl.semaphore_signal(barrier, inc=1, device_id={"col": other}, device_id_type=MESH_ID)
    o_ref[here] = x_ref[...]
    pl.semaphore_wait(barrier, count - 1)

    def copy(hop, block):
        other = lax.rem(here + hop, count)
        return remote(x_ref, o_ref.at[block], send_sem.at[hop], recv_sem.at[hop], other)

    for hop in range(1, count):
        copy(hop, here).start()
    for hop in range(1, count):
        copy(hop, lax.rem(here + count - hop, count)).wait_recv()
    for hop in range(1, count):
        copy(hop, here).wait_send()


def small_gather(x, count, ident):
    sems = pltpu.SemaphoreType.DMA((count,))
    return pl.pallas_call(
        functools.partial(small_body, count),
        out_shape=jax.ShapeDtypeStruct((count,) + x.shape, x.dtype),
        in_specs=[VM],
        out_specs=VM,
        scratch_shapes=[sems, sems],
        compiler_params=pltpu.CompilerParams(collective_id=ident, has_side_effects=True),
        name="small_gather",
    )(x)


def row_copy(src, dst, sems, which, device):
    return pltpu.make_async_remote_copy(
        src_ref=src,
        dst_ref=dst,
        send_sem=sems[0].at[which],
        recv_sem=sems[1].at[which],
        device_id={"row": device},
        device_id_type=MESH_ID,
    )


def row_partners():
    here = lax.axis_index("row")
    major, minor = here // 2, here % 2
    return 2 * major + 1 - minor, 2 * (1 - major) + minor


def row_gather_steps(pauses, x_ref, o_ref, *sems):
    near, next_one = row_partners()
    half = x_ref.shape[0] // 2

    def side(neighbour, first):
        slot, device = (0, near) if neighbour == 0 else (1, next_one)
        rows = pl.ds(first * half, half)
        return row_copy(x_ref.at[rows], o_ref.at[slot, rows], sems, 2 * slot + first, device)

    def onward(neighbour):
        slot, device = (0, next_one) if neighbour == 0 else (1, near)
        rows = pl.ds(slot * half, half)
        return row_copy(o_ref.at[slot, rows], o_ref.at[2, rows], sems, 4 + slot, device)

    side(0, 0).start()
    side(1, 1).start()
    side(0, 1).start()
    side(1, 0).start()
    for _ in range(pauses):
        yield
    side(0, 0).wait_recv()
    onward(0).start()
    side(1, 1).wait_recv()
    onward(1).start()
    yield
    for neighbour in range(2):
        side(neighbour, 1 - neighbour).wait_recv()
        onward(neighbour).wait_recv()
        onward(neighbour).wait_send()
        side(neighbour, 0).wait_send()
        side(neighbour, 1).wait_send()


def turn_body(chips, parts, first, last, held, late_count, riders, *refs):
    refs = list(refs)

    def take(count):
        taken = refs[:count]
        del refs[:count]
        return taken

    (p_ref,) = take(1)
    operands = take(held)
    rider_in = take(riders)
    (o_ref,) = take(1)
    results = take(late_count)
    rider_out = take(riders)
    sums_in, pair_buf, line_buf, sums = take(4)
    reduce_sems = take(5)
    gather_sems = take(5)
    line_barrier(chips, row_partners() if riders > 1 else ())
    steps = [reduce_steps(chips, parts, 0, p_ref, sums_in, pair_buf, line_buf, sums, *reduce_sems)]
    if riders > 0:
        steps.append(gather_steps(chips, 2, 1, rider_in[0], rider_out[0], *take(6)))
    if riders > 1:
        across = row_gather_steps(1, rider_in[1], rider_out[1], *take(2))
        next(across)
    run(*steps)
    here = lax.axis_index("col")
    own = o_ref.shape[0] // (2 * chips)
    kept = first(sums_in, operands, results, o_ref, pl.ds(pl.multiple_of(here * own, 8), own))

    def beside():
        if riders > 1:
            next(across)
        last(kept, operands, results)

    gather_rows(chips, parts, o_ref, *gather_sems, beside)
    if riders > 1:
        run(across)


def gather_rows(chips, parts, o_ref, right_sem, left_sem, mate_sem, line_recv, mate_recv, beside):
    here, chip, core, mate = line_place()
    size = (o_ref.shape[0] // (2 * chips), o_ref.shape[1])

    def copy(j, part, sem, recv, device, block=None):
        block = 2 * j + core if block is None else block
        ref = o_ref.at[spot(0, size, parts, block, part)]
        return remote(ref, ref, sem.at[j, part], recv.at[j, part], device)

    def forward(j, part, rightward, leftward):
        if rightward:

            @pl.when(chip < chips - 1)
            def _():
                copy(j, part, right_sem, line_recv, here + 2).start()

        if leftward:

            @pl.when(chip > 0)
            def _():
                copy(j, part, left_sem, line_recv, here - 2).start()

        copy(j, part, mate_sem, mate_recv, mate).start()

    for part in range(parts):
        forward(chip, part, True, True)
    beside()
    for far in range(1, chips):
        for part in range(parts):

            @pl.when(chip - far >= 0)
            def _():
                copy(chip - far, part, right_sem, line_recv, mate).wait_recv()
                forward(chip - far, part, True, False)

            @pl.when(chip + far < chips)
            def _():
                copy(chip + far, part, left_sem, line_recv, mate).wait_recv()
                forward(chip + far, part, False, True)

    for j in range(chips):
        for part in range(parts):
            copy(j, part, mate_sem, mate_recv, mate, block=2 * j + 1 - core).wait_recv()
            copy(j, part, mate_sem, mate_recv, mate).wait_send()

            @pl.when(jnp.logical_and(j <= chip, chip < chips - 1))
            def _():
                copy(j, part, right_sem, line_recv, here + 2).wait_send()

            @pl.when(jnp.logical_and(j >= chip, chip > 0))
            def _():
                copy(j, part, left_sem, line_recv, here - 2).wait_send()


def line_turn(p, operands, width, results, first, last, chips, ident, riders=(), parts=2):
    rows, cols = p.shape
    own = rows // (2 * chips)
    sems = pltpu.SemaphoreType.DMA((chips, parts))
    longer = pltpu.SemaphoreType.DMA((chips + 1, parts))
    more = []
    ridden = []
    if len(riders) > 0:
        height, part = riders[0].shape
        ridden.append(jax.ShapeDtypeStruct((height, 2 * chips * part), BF16))
        more += [pltpu.SemaphoreType.DMA((chips, 2))] * 5 + [pltpu.SemaphoreType.DMA((2,))]
    if len(riders) > 1:
        ridden.append(jax.ShapeDtypeStruct((3,) + riders[1].shape, BF16))
        more += [pltpu.SemaphoreType.DMA((6,))] * 2
    return pl.pallas_call(
        functools.partial(turn_body, chips, parts, first, last, len(operands), len(results), len(riders)),
        out_shape=(jax.ShapeDtypeStruct((rows, width), BF16),) + tuple(results) + tuple(ridden),
        in_specs=[VM] * (1 + len(operands)) + [VM, ANY][: len(riders)],
        out_specs=(VM,) * (1 + len(results)) + (VM, ANY)[: len(riders)],
        scratch_shapes=[
            pltpu.VMEM((own, cols), F32),
            pltpu.VMEM((chips, own, cols), BF16),
            pltpu.VMEM((chips + 1, own, cols), BF16),
            pltpu.VMEM((chips, own, cols), BF16),
            sems,
            sems,
            sems,
            longer,
            sems,
        ]
        + [sems] * 5
        + more,
        compiler_params=pltpu.CompilerParams(
            collective_id=ident, has_side_effects=True, vmem_limit_bytes=VMEM_LIMIT
        ),
        name="line_turn",
    )(p, *operands, *riders)


def inverse_rms(values):
    return lax.rsqrt(jnp.mean(values * values, axis=1, keepdims=True) + norm_eps)


def turn_forward(width, experts, sums, operands, results, o_ref, own):
    x_ref, gain_ref, a_ref, router_ref, up_ref = operands
    hidden_ref, mid_ref, mid_router_ref, probs_ref = results
    hidden = x_ref[...].astype(F32) + sums[:, :width]
    mid_ref[...] = sums[:, width:].astype(BF16)
    hidden_ref[...] = hidden
    normed = (hidden * inverse_rms(hidden) * gain_ref[...]).astype(BF16)
    o_ref[own, :width] = normed
    mid_router = nt(normed, a_ref[...]).astype(BF16)
    mid_router_ref[...] = mid_router
    logits = nt(normed, router_ref[...]) + nn(mid_router, up_ref[...])
    lane = lax.broadcasted_iota(jnp.int32, logits.shape, 1)
    logits = jnp.where(lane < experts, logits, masked_score)
    exponent = jnp.exp(logits - jnp.max(logits, axis=1, keepdims=True))
    probs = exponent / jnp.sum(exponent, axis=1, keepdims=True)
    probs_ref[...] = probs
    high = probs.astype(BF16)
    rest = probs - high.astype(F32)
    o_ref[own, width:] = (high.astype(F32) + pltpu.roll(rest, experts, 1)).astype(BF16)
    return None


def turn_backward(width, experts, sums, operands, results, o_ref, own):
    g_ref, hidden_ref, gain_ref, a_ref, router_ref, up_ref, probs_ref, mid_router_ref, mid_ref = operands
    pair = sums[:, width:]
    lanes = pair.shape[1]
    grad_probs = pair + pltpu.roll(pair, lanes - experts, 1)
    probs = probs_ref[...]
    grad_logits = (probs * (grad_probs - jnp.sum(probs * grad_probs, axis=1, keepdims=True))).astype(BF16)
    grad_mid = nt(grad_logits, up_ref[...]).astype(BF16)
    grad_normed = sums[:, :width] + nn(grad_logits, router_ref[...]) + nn(grad_mid, a_ref[...])
    hidden = hidden_ref[...]
    inv = inverse_rms(hidden)
    scaled = grad_normed * gain_ref[...]
    grad_hidden = (
        g_ref[...].astype(F32)
        + inv * scaled
        - hidden * (inv * inv * inv * jnp.mean(hidden * scaled, axis=1, keepdims=True))
    )
    grad_hidden = grad_hidden.astype(BF16)
    o_ref[own, :] = grad_hidden
    return grad_logits, grad_mid, grad_hidden


def turn_late(kept, operands, results):
    _, hidden_ref, gain_ref, _, _, _, _, mid_router_ref, mid_ref = operands
    grad_logits, grad_mid, grad_hidden = kept
    hidden = hidden_ref[...]
    normed = (hidden * inverse_rms(hidden) * gain_ref[...]).astype(BF16)
    rank = grad_mid.shape[1]
    late_ref, router_ref = results
    late_ref[pl.ds(0, rank)] = tn(grad_mid, normed)
    late_ref[pl.ds(rank, rank)] = tn(mid_ref[:, :rank], grad_hidden)
    router_ref[...] = tn(mid_router_ref[...], grad_logits)


def row_sums(values):
    lanes = 128
    values = sum(values[:, n : n + lanes] for n in range(0, values.shape[1], lanes))
    high = values.astype(BF16)
    rest = (values - high.astype(F32)).astype(BF16)
    ones = jnp.ones((8, values.shape[1]), BF16)
    return nt(ones, high) + nt(ones, rest)


def project_body(tile, x_ref, gain_ref, wq, wk, wv, a_ref, b_ref, proj_ref, mid_ref, inv_ref, sq_ref):
    part = wq.shape[1]
    for t in range(x_ref.shape[0] // tile):
        rows = pl.ds(t * tile, tile)
        x = x_ref[rows].astype(F32)
        inv = inverse_rms(x)
        inv_ref[rows] = inv
        normed = (x * inv * gain_ref[...]).astype(BF16)
        mid = nt(normed, a_ref[...]).astype(BF16)
        mid_ref[rows] = mid
        for m, w in enumerate((wq, wk, wv)):
            cols = pl.ds(m * part, part)
            proj = nn(normed, w[...]) + nn(mid, b_ref[:, cols])
            proj_ref[rows, cols] = proj
            if m < 2:
                sq_ref[pl.ds(m, 1), rows] = row_sums(proj * proj)[0:1]


def project(x, gain, weights, a_rows, b_cols):
    seq_len, width = x.shape
    part = weights[0].shape[1]
    rank = a_rows.shape[0]
    return pl.pallas_call(
        functools.partial(project_body, min(256, seq_len)),
        out_shape=(
            jax.ShapeDtypeStruct((seq_len, 3 * part), F32),
            jax.ShapeDtypeStruct((seq_len, rank), BF16),
            jax.ShapeDtypeStruct((seq_len, 1), F32),
            jax.ShapeDtypeStruct((2, seq_len), F32),
        ),
        in_specs=[VM] * 7,
        out_specs=(VM,) * 4,
        compiler_params=pltpu.CompilerParams(vmem_limit_bytes=VMEM_LIMIT),
        name="project",
    )(x, gain, *weights, a_rows, b_cols)


def key_limit(start, tile, seq_len, reach):
    return min(seq_len, max(start + tile, reach))


def allowed_keys(start, tile, limit, prefix_len):
    query = start + lax.broadcasted_iota(jnp.int32, (tile, limit), 0)
    key = lax.broadcasted_iota(jnp.int32, (tile, limit), 1)
    return jnp.logical_or(key <= query, key < prefix_len)


def attend_body(
    tile, reach, scale, prefix_ref, proj_ref, inv_ref, gains_ref, cos_ref, sin_ref, map_ref,
    p_ref, att_ref, q_ref, k_ref, v_ref, log_ref,
):
    seq_len, part = att_ref.shape
    prefix_len = prefix_ref[0]
    for h in range(part // HD):
        cols = pl.ds(h * HD, HD)
        for m, ref in ((0, q_ref), (1, k_ref)):
            plain = proj_ref[:, pl.ds(m * part + h * HD, HD)] * inv_ref[:, m : m + 1] * gains_ref[m : m + 1, cols]
            ref[:, cols] = (plain * cos_ref[...] + pltpu.roll(plain, HD // 2, 1) * sin_ref[...]).astype(BF16)
        v_ref[:, cols] = proj_ref[:, pl.ds(2 * part + h * HD, HD)].astype(BF16)
    for start in range(0, seq_len, tile):
        rows = pl.ds(start, tile)
        limit = key_limit(start, tile, seq_len, reach)
        allowed = allowed_keys(start, tile, limit, prefix_len)
        for h in range(part // HD):
            cols = pl.ds(h * HD, HD)
            scores = nt(q_ref[rows, cols], k_ref[pl.ds(0, limit), cols]) * scale
            scores = jnp.where(allowed, scores, masked_score)
            top = jnp.max(scores, axis=1, keepdims=True)
            exponent = jnp.exp(scores - top)
            total = jnp.sum(exponent, axis=1, keepdims=True)
            weights = (exponent / total).astype(BF16)
            att_ref[rows, cols] = nn(weights, v_ref[pl.ds(0, limit), cols]).astype(BF16)
            log_ref[rows, h : h + 1] = top + jnp.log(total)
        p_ref[rows] = nn(att_ref[rows], map_ref[...]).astype(BF16)


def attend(prefix, proj, inv, gains, tables, out_map, reach, scale):
    seq_len = proj.shape[0]
    part = proj.shape[1] // 3
    heads = jax.ShapeDtypeStruct((seq_len, part), BF16)
    return pl.pallas_call(
        functools.partial(attend_body, min(256, seq_len), reach, scale),
        out_shape=(
            jax.ShapeDtypeStruct((seq_len, out_map.shape[1]), BF16),
            heads,
            heads,
            heads,
            heads,
            jax.ShapeDtypeStruct((seq_len, part // HD), F32),
        ),
        in_specs=[pl.BlockSpec(memory_space=pltpu.SMEM)] + [VM] * 6,
        out_specs=(VM,) * 6,
        compiler_params=pltpu.CompilerParams(vmem_limit_bytes=VMEM_LIMIT),
        name="attend",
    )(prefix, proj, inv, gains, *tables, out_map)


def attend_back(
    tile, reach, scale, prefix_ref, g_ref, map_ref, b_ref, att_ref, q_ref, k_ref, v_ref, log_ref, proj_ref,
    gains_ref, cos_ref, sin_ref, scaled_ref, dv_ref, stat_ref, ga_ref, da_ref, dq_acc, dk_acc, dv_acc,
):
    seq_len, part = att_ref.shape
    prefix_len = prefix_ref[0]
    grad_a = jnp.zeros(ga_ref.shape, F32)
    for start in range(0, seq_len, tile):
        rows = pl.ds(start, tile)
        grads = g_ref[rows]
        da_ref[rows] = nt(grads, map_ref[...]).astype(BF16)
        grad_mid = nt(grads, b_ref[...]).astype(BF16)
        grad_a += tn(grad_mid, att_ref[rows])
    ga_ref[...] = grad_a
    dk_acc[...] = jnp.zeros_like(dk_acc)
    dv_acc[...] = jnp.zeros_like(dv_acc)
    for start in range(0, seq_len, tile):
        rows = pl.ds(start, tile)
        limit = key_limit(start, tile, seq_len, reach)
        keys = pl.ds(0, limit)
        allowed = allowed_keys(start, tile, limit, prefix_len)
        for h in range(part // HD):
            cols = pl.ds(h * HD, HD)
            query, key = q_ref[rows, cols], k_ref[keys, cols]
            grads = da_ref[rows, cols]
            scores = jnp.where(allowed, nt(query, key) * scale, masked_score)
            weights = jnp.exp(scores - log_ref[rows, h : h + 1])
            grad_weights = nt(grads, v_ref[keys, cols])
            dot = jnp.sum(weights * grad_weights, axis=1, keepdims=True)
            grad_scores = (weights * (grad_weights - dot)).astype(BF16)
            dq_acc[rows, cols] = nn(grad_scores, key) * scale
            dk_acc[keys, cols] += tn(grad_scores, query) * scale
            dv_acc[keys, cols] += tn(weights.astype(BF16), grads)
    dv_ref[...] = dv_acc[...].astype(BF16)
    for m, acc in ((0, dq_acc), (1, dk_acc)):
        for start in range(0, seq_len, tile):
            rows = pl.ds(start, tile)
            total = jnp.zeros((8, tile), F32)
            for h in range(part // HD):
                cols = pl.ds(h * HD, HD)
                here = pl.ds(m * part + h * HD, HD)
                plain = acc[rows, cols]
                turned = plain * cos_ref[rows] - pltpu.roll(plain, HD // 2, 1) * sin_ref[rows]
                scaled = turned * gains_ref[m : m + 1, cols]
                scaled_ref[rows, here] = scaled
                total += row_sums(proj_ref[rows, here] * scaled)
            stat_ref[pl.ds(m, 1), rows] = total[0:1]


def back_body(tile, reach, scale, chips, row_count, extra, prefix_ref, slot_ref, *refs):
    refs = list(refs)

    def take(number):
        taken = refs[:number]
        del refs[:number]
        return taken

    g_ref, map_ref, bo_ref, att_ref, q_ref, k_ref, v_ref, log_ref, proj_ref, gains_ref, cos_ref, sin_ref = take(12)
    inv_ref, b_ref, a_ref, x_ref, inv1_ref, gain_ref, mid_ref, late_ref, router_ref = take(9)
    weights = take(3)
    gi_ref, held_ref = take(2)
    scaled_ref, dv_ref, stat_ref, stats_ref, ga_ref, da_ref, dq_acc, dk_acc, dv_acc = take(9)
    w_ref, d_ref, middle_ref, p_ref, o_ref, pair_buf, line_buf, sums, flat_ref, every_ref = take(10)
    w_sems, stat_send, stat_recv, row_send, row_recv = take(5)
    right_sem, left_sem, mate_sem, line_recv, mate_recv = take(5)
    here, chip, core, mate = line_place()
    row = lax.axis_index("row")
    count = 2 * chips
    seq_len, width = x_ref.shape
    part = dv_ref.shape[1]
    ranks = a_ref.shape[0]
    rank = ranks // 3
    parts = 2

    fetches = [
        pltpu.make_async_copy(w, w_ref.at[:, pl.ds(m * part, part)], w_sems.at[m]) for m, w in enumerate(weights)
    ]
    for fetch in fetches:
        fetch.start()
    barrier = pltpu.get_barrier_semaphore()
    for hop in range(1, count):
        other = lax.rem(here + hop, count)
        pl.semaphore_signal(barrier, inc=1, device_id={"col": other}, device_id_type=MESH_ID)
    for hop in range(1, row_count):
        other = lax.rem(row + hop, row_count)
        pl.semaphore_signal(barrier, inc=1, device_id={"row": other}, device_id_type=MESH_ID)
    attend_back(
        tile, reach, scale, prefix_ref, g_ref, map_ref, bo_ref, att_ref, q_ref, k_ref, v_ref, log_ref, proj_ref,
        gains_ref, cos_ref, sin_ref, scaled_ref, dv_ref, stat_ref, ga_ref, da_ref, dq_acc, dk_acc, dv_acc,
    )
    pl.semaphore_wait(barrier, count + row_count - 2)

    def stat_copy(hop, block):
        other = lax.rem(here + hop, count)
        return remote(stat_ref, stats_ref.at[block], stat_send.at[hop], stat_recv.at[hop], other)

    for hop in range(1, count):
        stat_copy(hop, here).start()
    stats_ref[here] = stat_ref[...]
    for hop in range(1, count):
        stat_copy(hop, lax.rem(here + count - hop, count)).wait_recv()
    total = stats_ref[0]
    for n in range(1, count):
        total = total + stats_ref[n]
    total = jnp.concatenate([total, jnp.zeros((6, seq_len), F32)], axis=0) * (1.0 / width)

    grad_b = jnp.zeros((ranks, 3 * part), F32)
    first_stats = jnp.zeros((8, part), F32)
    line = lax.broadcasted_iota(jnp.int32, (8, part), 0)
    for t in range(seq_len // tile):
        rows = pl.ds(t * tile, tile)
        upright = jnp.transpose(total[:, t * tile : (t + 1) * tile])
        products = jnp.zeros((tile, part), F32)
        for m in range(3):
            cols = pl.ds(m * part, part)
            if m < 2:
                inv = inv_ref[rows, m : m + 1]
                shift = inv * inv * inv * upright[:, m : m + 1]
                grad = (inv * scaled_ref[rows, cols] - proj_ref[rows, cols] * shift).astype(BF16)
            else:
                grad = dv_ref[rows]
            d_ref[rows, cols] = grad
            products += grad.astype(F32) * proj_ref[rows, cols]
        grads = d_ref[rows]
        middle_ref[rows] = nt(grads, b_ref[...]).astype(BF16)
        grad_b += tn(mid_ref[rows], grads)
        first = row_sums(products / inv1_ref[rows])
        for j in range(tile // part):
            first_stats = jnp.where(
                line == (t * tile) // part + j, first[:, j * part : (j + 1) * part], first_stats
            )
    high = first_stats.astype(BF16).astype(F32)
    router = router_ref[...]
    if part > router.shape[1]:
        router = jnp.concatenate([router, jnp.zeros((rank, part - router.shape[1]), F32)], axis=1)
    common = jnp.concatenate([router, high, first_stats - high], axis=0).astype(BF16)
    common = jnp.concatenate([common] * count, axis=1)
    p_ref[pl.ds(ranks, 2 * rank)] = late_ref[...].astype(BF16)
    p_ref[pl.ds(ranks + 2 * rank, rank + 16)] = common
    used = ranks + 3 * rank + 16
    p_ref[pl.ds(used, extra - used)] = jnp.zeros((extra - used, width), BF16)
    for fetch in fetches:
        fetch.wait()

    size = o_ref.shape
    step = size[0] // parts

    def rows_of(piece):
        return pl.ds(piece * step, step)

    def at(block, piece):
        return spot(1, size, parts, block, piece)

    def mate_copy(j, piece):
        return remote(
            p_ref.at[at(2 * j + 1 - core, piece)],
            pair_buf.at[j, rows_of(piece)],
            mate_sem.at[j, piece],
            mate_recv.at[j, piece],
            mate,
        )

    def line_copy(j, slot, piece, sem, device):
        return remote(
            sums.at[j, rows_of(piece)],
            line_buf.at[slot, rows_of(piece)],
            sem.at[j, piece],
            line_recv.at[slot, piece],
            device,
        )

    def order(s):
        right = chips - 1 - chip
        return jnp.where(s < right, chips - 1 - s, jnp.where(s < chips - 1, s - right, chip))

    def work_out(s):
        cols = pl.ds(pl.multiple_of(order(s) * (2 * part), 128), 2 * part)
        gain = gain_ref[:, cols]
        spread = a_ref[:, cols]
        chunk = w_ref[cols]

        def one_tile(t, grad_a):
            rows = pl.ds(pl.multiple_of(t * tile, tile), tile)
            middle = middle_ref[rows]
            normed_part = nt(d_ref[rows], chunk) + nn(middle, spread)
            p_ref[pl.ds(pl.multiple_of(extra + t * tile, 16), tile), cols] = normed_part.astype(BF16)
            normed = (x_ref[rows, cols].astype(F32) * inv1_ref[rows] * gain).astype(BF16)
            return grad_a + tn(middle, normed)

        grad_a = lax.fori_loop(0, seq_len // tile, one_tile, jnp.zeros((ranks, 2 * part), F32))
        p_ref[pl.ds(0, ranks), cols] = grad_a.astype(BF16)
        for piece in range(parts):
            mate_copy(order(s), piece).start()

    def pair_sum(j, piece):
        mate_copy(j, piece).wait_recv()
        return p_ref[at(2 * j + core, piece)].astype(F32) + pair_buf[j, rows_of(piece)].astype(F32)

    def one_block(s, carry):
        work_out(s)

        @pl.when(jnp.logical_and(chip == 0, s > 0))
        def _():
            for piece in range(parts):
                j = order(s - 1)
                sums[j, rows_of(piece)] = pair_sum(j, piece).astype(BF16)
                line_copy(j, j, piece, right_sem, here + 2).start()

        @pl.when(jnp.logical_and(chip == chips - 1, s > 0))
        def _():
            for piece in range(parts):
                j = order(s - 1)
                sums[j, rows_of(piece)] = pair_sum(j, piece).astype(BF16)

                @pl.when(j == chips - 2)
                def _():
                    line_copy(j, chips, piece, left_sem, here - 2).start()

                @pl.when(j < chips - 2)
                def _():
                    line_copy(j, j, piece, left_sem, here - 2).start()

        return carry

    lax.fori_loop(0, chips, one_block, 0)
    inner = jnp.logical_and(chip > 0, chip < chips - 1)

    def pass_on(j, slot, piece, sem, device):
        line_copy(j, j, piece, sem, mate).wait_recv()
        sums[j, rows_of(piece)] = (pair_sum(j, piece) + line_buf[j, rows_of(piece)].astype(F32)).astype(BF16)
        line_copy(j, slot, piece, sem, device).start()

    for far in range(chips - 2, 0, -1):
        for piece in range(parts):

            @pl.when(jnp.logical_and(inner, chip + far < chips))
            def _():
                pass_on(chip + far, chip + far, piece, right_sem, here + 2)

            @pl.when(jnp.logical_and(inner, chip - far >= 0))
            def _():
                pass_on(chip - far, chips if far == 1 else chip - far, piece, left_sem, here - 2)

    def row_copy(hop, block):
        other = lax.rem(row + hop, row_count)
        return pltpu.make_async_remote_copy(
            src_ref=flat_ref,
            dst_ref=every_ref.at[block],
            send_sem=row_send.at[hop],
            recv_sem=row_recv.at[hop],
            device_id={"row": other},
            device_id_type=MESH_ID,
        )

    for piece in range(parts):
        o_ref[rows_of(piece)] = pair_sum(chip, piece)

        @pl.when(chip > 0)
        def _():
            line_copy(chip, chip, piece, right_sem, mate).wait_recv()
            o_ref[rows_of(piece)] += line_buf[chip, rows_of(piece)].astype(F32)

        @pl.when(chip < chips - 1)
        def _():
            line_copy(chip, chips, piece, left_sem, mate).wait_recv()
            o_ref[rows_of(piece)] += line_buf[chips, rows_of(piece)].astype(F32)

        if piece == 0:
            flat_ref[pl.ds(0, 6 * rank)] = o_ref[pl.ds(0, 6 * rank)].astype(BF16)
            flat_ref[pl.ds(6 * rank, rank)] = ga_ref[...].astype(BF16)
            for m in range(3):
                flat_ref[pl.ds((7 + m) * rank, rank)] = grad_b[
                    m * rank : (m + 1) * rank, m * part : (m + 1) * part
                ].astype(BF16)
            owner = jnp.full((16, part), slot_ref[0].astype(F32), F32)
            flat_ref[pl.ds(10 * rank, 16)] = owner.astype(BF16)
            for hop in range(1, row_count):
                row_copy(hop, row).start()
            every_ref[row] = flat_ref[...]

    stat_rows = o_ref[pl.ds(ranks + 3 * rank, 8)] + o_ref[pl.ds(ranks + 3 * rank + 8, 8)]
    upright = jnp.transpose(stat_rows)
    own = pl.ds(pl.multiple_of(here * part, 128), part)
    gain = gain_ref[:, own]
    for t in range(seq_len // part):
        rows = pl.ds(t * part, part)
        inv = inv1_ref[rows]
        pull = inv * inv * inv * upright[:, t : t + 1] * (1.0 / width)
        gi_ref[rows] = (
            g_ref[rows, own].astype(F32)
            + inv * gain * o_ref[pl.ds(extra + t * part, part)]
            - x_ref[rows, own].astype(F32) * pull
        )
    for hop in range(1, row_count):
        row_copy(hop, lax.rem(row + row_count - hop, row_count)).wait_recv()
    held = held_ref.shape[0]
    for h in range(held):
        chosen = (row * held + h).astype(F32)
        picked = jnp.zeros((10 * rank, part), F32)
        for r in range(row_count):
            owner = every_ref[r, pl.ds(10 * rank, 16)].astype(F32)[0:1]
            picked += jnp.where(owner == chosen, every_ref[r, pl.ds(0, 10 * rank)].astype(F32), 0.0)
        held_ref[h] = picked

    for hop in range(1, row_count):
        row_copy(hop, row).wait_send()
    for hop in range(1, count):
        stat_copy(hop, here).wait_send()
    for j in range(chips):
        for piece in range(parts):
            mate_copy(j, piece).wait_send()

            @pl.when(j > chip)
            def _():
                line_copy(j, j, piece, right_sem, mate).wait_send()

            @pl.when(j < chip)
            def _():
                line_copy(j, j, piece, left_sem, mate).wait_send()


def back(prefix, slot, operands, weights, reach, scale, chips, row_count, held, ident):
    x = operands[15]
    seq_len, width = x.shape
    part = weights[0].shape[1]
    count = 2 * chips
    ranks = operands[14].shape[0]
    rank = ranks // 3
    extra = 128
    tall = seq_len + extra
    sems = pltpu.SemaphoreType.DMA((chips, 2))
    hops = pltpu.SemaphoreType.DMA((count,))
    row_hops = pltpu.SemaphoreType.DMA((row_count,))
    smem = pl.BlockSpec(memory_space=pltpu.SMEM)
    return pl.pallas_call(
        functools.partial(back_body, min(256, seq_len), reach, scale, chips, row_count, extra),
        out_shape=(
            jax.ShapeDtypeStruct((seq_len, part), F32),
            jax.ShapeDtypeStruct((held, 10 * rank, part), F32),
        ),
        in_specs=[smem, smem] + [VM] * len(operands) + [ANY] * 3,
        out_specs=(VM, VM),
        scratch_shapes=[
            pltpu.VMEM((seq_len, 2 * part), F32),
            pltpu.VMEM((seq_len, part), BF16),
            pltpu.VMEM((2, seq_len), F32),
            pltpu.VMEM((count, 2, seq_len), F32),
            pltpu.VMEM((rank, part), F32),
            pltpu.VMEM((seq_len, part), BF16),
            pltpu.VMEM((seq_len, part), F32),
            pltpu.VMEM((seq_len, part), F32),
            pltpu.VMEM((seq_len, part), F32),
            pltpu.VMEM((width, 3 * part), BF16),
            pltpu.VMEM((seq_len, 3 * part), BF16),
            pltpu.VMEM((seq_len, ranks), BF16),
            pltpu.VMEM((tall, width), BF16),
            pltpu.VMEM((tall, part), F32),
            pltpu.VMEM((chips, tall, part), BF16),
            pltpu.VMEM((chips + 1, tall, part), BF16),
            pltpu.VMEM((chips, tall, part), BF16),
            pltpu.VMEM((10 * rank + 16, part), BF16),
            pltpu.VMEM((row_count, 10 * rank + 16, part), BF16),
            pltpu.SemaphoreType.DMA((3,)),
            hops,
            hops,
            row_hops,
            row_hops,
            sems,
            sems,
            sems,
            pltpu.SemaphoreType.DMA((chips + 1, 2)),
            sems,
        ],
        compiler_params=pltpu.CompilerParams(
            collective_id=ident, has_side_effects=True, vmem_limit_bytes=VMEM_LIMIT
        ),
        name="back",
    )(prefix, slot, *operands, *weights)


def moments(chips, subs):
    when = {}
    for j in range(chips):
        for chip in range(j):
            own = subs * (chips - j) + 1
            when[chip, j] = max(own, when[chip - 1, j] + 3) if chip > 0 else own
        for chip in range(chips - 1, j, -1):
            own = subs * (chips - chip + j) + 1
            when[chip, j] = max(own, when[chip + 1, j] + 3) if chip < chips - 1 else own
    last = chips * subs
    return {place: min(time, last) for place, time in when.items()}


def moe_turn_body(experts, chips, subs, count, x_ref, g_ref, routes_ref, *refs):
    refs = list(refs)

    def take(number):
        taken = refs[:number]
        del refs[:number]
        return taken

    operands = take(9)
    gate_w, up_w = take(2)
    downs = take(count)
    out_ref, o_ref = take(2)
    results = take(2)
    p_ref, out_acc, dx_acc, gate_acc, wgu, wd, x_buf, g_buf = take(8)
    sums_in, pair_buf, line_buf, sums = take(4)
    w_sems, tile_sems, right_sem, left_sem, mate_sem, line_recv, mate_recv = take(7)
    gather_sems = refs
    here, chip, core, mate = line_place()
    row = lax.axis_index("row")
    hidden = wd.shape[1]
    tokens, width = out_ref.shape
    own = tokens // (2 * chips)
    tile = 2 * own
    lanes = gate_acc.shape[1]
    local = gate_w.shape[0]
    pieces = gate_w.shape[2] // hidden
    steps = local * pieces
    each = steps // subs

    def fetches(step, e, piece):
        if count == 1:
            place = piece
            down = downs[0].at[e, pl.ds(piece * hidden, hidden)]
        else:
            place = 2 * ((row // 2 + piece // 2) % 2) + (row + piece) % 2
            down = downs[1 + e].at[piece - 1] if piece > 0 else downs[0].at[e]
        units = pl.ds(pl.multiple_of(place * hidden, 128), hidden)
        return (
            pltpu.make_async_copy(gate_w.at[e, :, units], wgu.at[step, :, pl.ds(0, hidden)], w_sems.at[step, 0]),
            pltpu.make_async_copy(up_w.at[e, :, units], wgu.at[step, :, pl.ds(hidden, hidden)], w_sems.at[step, 1]),
            pltpu.make_async_copy(down, wd.at[step], w_sems.at[step, 2]),
        )

    def order(s):
        right = chips - 1 - chip
        return jnp.where(s < right, chips - 1 - s, jnp.where(s < chips - 1, s - right, chip))

    def tile_rows(s):
        return pl.ds(pl.multiple_of(order(s) * tile, 8), tile)

    def tiles(s):
        slot = s % 2
        return (
            pltpu.make_async_copy(x_ref.at[tile_rows(s)], x_buf.at[slot], tile_sems.at[slot, 0]),
            pltpu.make_async_copy(g_ref.at[tile_rows(s)], g_buf.at[slot], tile_sems.at[slot, 1]),
        )

    for copy in tiles(0):
        copy.start()
    for step in range(steps):
        for copy in fetches(step, step // pieces, step % pieces):
            copy.start()
    line_barrier(chips)

    def block(number):
        return pl.ds(pl.multiple_of(number * own, 8), own)

    def mate_copy(j):
        return remote(p_ref.at[block(2 * j + 1 - core)], pair_buf.at[j], mate_sem.at[j], mate_recv.at[j], mate)

    def line_copy(j, slot, sem, device):
        return remote(sums.at[j], line_buf.at[slot], sem.at[j], line_recv.at[slot], device)

    def pair_sum(j):
        mate_copy(j).wait_recv()
        return p_ref[block(2 * j + core)].astype(F32) + pair_buf[j].astype(F32)

    def pass_on(at, j):
        rightward = j > at
        total = pair_sum(j)
        if 0 < at < chips - 1:
            line_copy(j, j, right_sem if rightward else left_sem, mate).wait_recv()
            total = total + line_buf[j].astype(F32)
        sums[j] = total.astype(BF16)
        if rightward:
            line_copy(j, j, right_sem, here + 2).start()
        else:
            line_copy(j, chips if at - j == 1 else j, left_sem, here - 2).start()

    when = moments(chips, subs)

    def one_sub(k, carry):
        s, sub = k // subs, k % subs
        slot = s % 2
        rows = tile_rows(s)

        @pl.when(sub == 0)
        def _():
            for copy in tiles(s):
                copy.wait()

            @pl.when(s + 1 < chips)
            def _():
                for copy in tiles(s + 1):
                    copy.start()

            out_acc[...] = jnp.zeros_like(out_acc)
            dx_acc[...] = jnp.zeros_like(dx_acc)
            gate_acc[...] = jnp.zeros_like(gate_acc)

        def one_step(step, carry):
            @pl.when(s == 0)
            def _():
                units = pl.ds(0, hidden)
                for number, (source, place) in enumerate(((gate_w, 0), (up_w, hidden))):
                    pltpu.make_async_copy(
                        source.at[0, :, units], wgu.at[step, :, pl.ds(place, hidden)], w_sems.at[step, number]
                    ).wait()
                pltpu.make_async_copy(downs[0].at[0, units], wd.at[step], w_sems.at[step, 2]).wait()

            e = here * local + step // pieces
            lane = lax.broadcasted_iota(jnp.int32, (tile, lanes), 1)
            mine = lane == e
            halves = jnp.logical_or(mine, lane == e + experts)
            named = jnp.sum(jnp.where(routes_ref[rows] == e, 1.0, 0.0), axis=1, keepdims=True)
            gate = jnp.sum(jnp.where(halves, x_buf[slot, :, width:].astype(F32), 0.0), axis=1, keepdims=True)
            gate = gate * named
            both = nn(x_buf[slot, :, :width], wgu[step])
            gate_in, up_in = both[:, :hidden], both[:, hidden:]
            sigmoid = jax.nn.sigmoid(gate_in)
            silu = gate_in * sigmoid
            active = silu * up_in
            back = nt(g_buf[slot], wd[step])
            d_gate = jnp.sum(active * back, axis=1, keepdims=True) * named
            gate_acc[...] += jnp.where(mine, d_gate, 0.0)
            out_acc[...] += nn((active * gate).astype(BF16), wd[step])
            d_active = back * gate
            d_gate_in = d_active * up_in * (sigmoid + silu * (1.0 - sigmoid))
            d_up_in = d_active * silu
            d_both = jnp.concatenate([d_gate_in.astype(BF16), d_up_in.astype(BF16)], axis=1)
            dx_acc[...] += nt(d_both, wgu[step])
            return carry

        lax.fori_loop(sub * each, (sub + 1) * each, one_step, 0)

        @pl.when(sub == subs - 1)
        def _():
            out_ref[rows] = out_acc[...].astype(BF16)
            p_ref[rows, :width] = dx_acc[...].astype(BF16)
            high = gate_acc[...].astype(BF16).astype(F32)
            rest = gate_acc[...] - high
            p_ref[rows, width:] = (high + pltpu.roll(rest, experts, 1)).astype(BF16)
            mate_copy(order(s)).start()

            @pl.when(s == chips - 1)
            def _():
                out_ref[block(here)] = (out_acc[pl.ds(pl.multiple_of(core * own, 8), own)] + operands[1][...]).astype(BF16)

        for (at, j), time in sorted(when.items(), key=lambda item: (item[1], abs(item[0][0] - item[0][1]))):

            @pl.when(jnp.logical_and(chip == at, k == time - 1))
            def _():
                pass_on(at, j)

        return carry

    lax.fori_loop(0, chips * subs, one_sub, 0)
    sums_in[...] = pair_sum(chip)

    @pl.when(chip > 0)
    def _():
        line_copy(chip, chip, right_sem, mate).wait_recv()
        sums_in[...] += line_buf[chip].astype(F32)

    @pl.when(chip < chips - 1)
    def _():
        line_copy(chip, chips, left_sem, mate).wait_recv()
        sums_in[...] += line_buf[chips].astype(F32)

    for j in range(chips):
        mate_copy(j).wait_send()

        @pl.when(j > chip)
        def _():
            line_copy(j, j, right_sem, mate).wait_send()

        @pl.when(j < chip)
        def _():
            line_copy(j, j, left_sem, mate).wait_send()

    kept = turn_backward(width, experts, sums_in, operands, results, o_ref, block(here))
    gather_rows(chips, 2, o_ref, *gather_sems, lambda: turn_late(kept, operands, results))


def moe_turn(x, g, routes, operands, experts, gate_w, up_w, downs, results, chips, ident):
    tokens, width = g.shape
    wide = x.shape[1]
    lanes = wide - width
    own = tokens // (2 * chips)
    hidden = downs[0].shape[1] if len(downs) > 1 else min(256, gate_w.shape[2] // 4)
    steps = gate_w.shape[0] * gate_w.shape[2] // hidden
    subs = min(4, steps)
    whole = jax.ShapeDtypeStruct((tokens, width), BF16)
    per_chip = pltpu.SemaphoreType.DMA((chips,))
    halves = pltpu.SemaphoreType.DMA((chips, 2))
    return pl.pallas_call(
        functools.partial(moe_turn_body, experts, chips, subs, len(downs)),
        out_shape=(whole, whole) + tuple(results),
        in_specs=[ANY, ANY] + [VM] * (1 + len(operands)) + [ANY] * (2 + len(downs)),
        out_specs=(VM,) * (2 + len(results)),
        scratch_shapes=[
            pltpu.VMEM((tokens, wide), BF16),
            pltpu.VMEM((2 * own, width), F32),
            pltpu.VMEM((2 * own, width), F32),
            pltpu.VMEM((2 * own, lanes), F32),
            pltpu.VMEM((steps, width, 2 * hidden), BF16),
            pltpu.VMEM((steps, hidden, width), BF16),
            pltpu.VMEM((2, 2 * own, wide), BF16),
            pltpu.VMEM((2, 2 * own, width), BF16),
            pltpu.VMEM((own, wide), F32),
            pltpu.VMEM((chips, own, wide), BF16),
            pltpu.VMEM((chips + 1, own, wide), BF16),
            pltpu.VMEM((chips, own, wide), BF16),
            pltpu.SemaphoreType.DMA((steps, 3)),
            pltpu.SemaphoreType.DMA((2, 2)),
            per_chip,
            per_chip,
            per_chip,
            pltpu.SemaphoreType.DMA((chips + 1,)),
            per_chip,
        ]
        + [halves] * 5,
        compiler_params=pltpu.CompilerParams(
            collective_id=ident, has_side_effects=True, vmem_limit_bytes=VMEM_MOST
        ),
        name="moe_turn",
    )(x, g, routes, *operands, gate_w, up_w, *downs)


def rope_tables(length, head_dim):
    half_dim = head_dim // 2
    frequency = rope_base ** (-(2.0 * jnp.arange(half_dim, dtype=F32)) / head_dim)
    angles = jnp.arange(length, dtype=F32)[:, None] * frequency[None, :]
    cosine, sine = jnp.cos(angles), jnp.sin(angles)
    return jnp.concatenate([cosine, cosine], axis=1), jnp.concatenate([-sine, sine], axis=1)


def shards(
    inputs,
    cotangent,
    norm_first,
    norm_second,
    query_gain,
    key_gain,
    w_query,
    w_key,
    w_value,
    w_out,
    w_router,
    w_gate,
    w_up,
    w_down,
    adapter_a,
    adapter_b,
    adapter_router,
    routes,
    prefix,
    adapter_index,
):
    seq_len, width_part = inputs.shape
    col_count = lax.axis_size("col")
    row_count = lax.axis_size("row")
    col_index = lax.axis_index("col")
    row_index = lax.axis_index("row")
    chips = col_count // 2
    full_width = width_part * col_count
    head_width = w_query.shape[1]
    local_experts = w_gate.shape[0]
    expert_total = w_router.shape[1]
    feature_start = col_index * width_part
    head_start = col_index * head_width
    own_rows = seq_len // col_count
    row_start = col_index * own_rows
    score_scale = HD ** (-0.5)
    reach = seq_len // 2
    lanes = 128

    def columns(array, axis_num):
        return lax.dynamic_slice_in_dim(array, feature_start, width_part, axis_num)

    def head_cols(array, axis_num=1):
        return lax.dynamic_slice_in_dim(array, head_start, head_width, axis_num)

    def held_rows(array):
        return lax.dynamic_slice_in_dim(array, row_start, own_rows, 0)

    def col_sum(pair, ident):
        return jnp.sum(small_gather(pair, col_count, ident), axis=0)

    full_gate = lax.all_gather(w_gate, "row", axis=2, tiled=True)
    full_up = lax.all_gather(w_up, "row", axis=2, tiled=True)
    across = row_count == 4 and local_experts == 2
    down_halves = w_down.reshape((local_experts, 2, w_down.shape[1] // 2, full_width))
    riders = (cotangent, down_halves[1]) if across else (cotangent,)
    adapter_slot = adapter_index[0]
    chosen_a = lax.dynamic_index_in_dim(adapter_a, adapter_slot, 1, keepdims=False).swapaxes(1, 2)
    chosen_b = lax.dynamic_index_in_dim(adapter_b, adapter_slot, 1, keepdims=False)
    chosen_router = lax.dynamic_index_in_dim(adapter_router, adapter_slot, 0, keepdims=False)
    rank = chosen_a.shape[1]
    a_three = chosen_a[:3].reshape(3 * rank, full_width)
    b_three = head_cols(chosen_b[:3].reshape(3 * rank, full_width))
    blank = jnp.zeros((rank, head_width), BF16)
    b_cols = jnp.concatenate(
        [
            jnp.concatenate([b_three[m * rank : (m + 1) * rank] if n == m else blank for n in range(3)], axis=0)
            for m in range(3)
        ],
        axis=1,
    )
    a_out = head_cols(chosen_a[3])
    out_map = (w_out.astype(F32) + tn(a_out, chosen_b[3])).astype(BF16)
    out_wide = jnp.concatenate([out_map, a_out.T, jnp.zeros((head_width, lanes - rank), BF16)], axis=1)
    router_rows = jnp.pad(w_router.T, ((0, lanes - expert_total), (0, 0)))
    router_up = jnp.pad(chosen_router, ((0, 0), (0, lanes - expert_total)))
    gains = jnp.stack([head_cols(query_gain, 0), head_cols(key_gain, 0)])
    tables = rope_tables(seq_len, HD)
    gain_first, gain_second = norm_first[None], norm_second[None]

    full_inputs, *down_first = line_gather(inputs, chips, 1, 0, rider=down_halves[0] if across else None)
    proj, mid, inv_first, squares = project(
        full_inputs, gain_first, (w_query, w_key, w_value), a_three, b_cols
    )
    inv = lax.rsqrt(col_sum(squares, 1) / full_width + norm_eps).T
    part_out, attended, rot_query, rot_key, value_rows, log_totals = attend(
        prefix, proj, inv, gains, tables, out_wide, reach, score_scale
    )
    wide = full_width + lanes
    row_shape = jax.ShapeDtypeStruct
    normed_two, hidden_rows, mid_out, mid_router, probs, full_cot, *down_second = line_turn(
        part_out,
        (held_rows(full_inputs), gain_second, chosen_a[4], router_rows, router_up),
        wide,
        (
            row_shape((own_rows, full_width), F32),
            row_shape((own_rows, lanes), BF16),
            row_shape((own_rows, rank), BF16),
            row_shape((own_rows, lanes), F32),
        ),
        functools.partial(turn_forward, full_width, expert_total),
        lambda kept, operands, results: None,
        chips,
        2,
        riders,
    )
    if across:
        downs = (w_down,) + tuple(
            others.reshape((3,) + w_down.shape[1:]) for others in down_first + down_second
        )
    else:
        downs = (lax.all_gather(w_down, "row", axis=1, tiled=True),)

    moe_out, grad_attn, late, router_late = moe_turn(
        normed_two,
        full_cot,
        routes,
        (
            held_rows(full_cot),
            hidden_rows,
            gain_second,
            chosen_a[4],
            router_rows,
            router_up,
            probs,
            mid_router,
            mid_out,
        ),
        expert_total,
        full_gate,
        full_up,
        downs,
        (row_shape((2 * rank, full_width), F32), row_shape((rank, lanes), F32)),
        chips,
        7,
    )
    moe_out, grad_attn = lax.optimization_barrier((moe_out, grad_attn))
    layer_out = lax.psum_scatter(moe_out, "col", scatter_dimension=1, tiled=True)

    held_adapters = adapter_a.shape[1] // row_count
    grad_inputs, held = back(
        prefix,
        adapter_index,
        (
            grad_attn,
            out_map,
            chosen_b[3],
            attended,
            rot_query,
            rot_key,
            value_rows,
            log_totals,
            proj,
            gains,
            *tables,
            inv,
            b_cols,
            a_three,
            full_inputs,
            inv_first,
            gain_first,
            mid,
            late,
            router_late,
        ),
        (w_query, w_key, w_value),
        reach,
        score_scale,
        chips,
        row_count,
        held_adapters,
        12,
    )
    pieces = [held[:, n * rank : (n + 1) * rank] for n in range(10)]
    query_a, key_a, value_a, router_a, out_b, router_up_grad, out_a, query_b, key_b, value_b = pieces
    grad_a = jnp.stack([query_a, key_a, value_a, out_a, router_a]).swapaxes(2, 3)
    grad_b = jnp.stack([query_b, key_b, value_b, out_b])
    grad_router = router_up_grad[:, :, :expert_total]
    return (layer_out, grad_inputs, grad_a, grad_b, grad_router)


def solution(mesh):
    placed = (
        P("row", "col"),
        P("row", "col"),
        P(),
        P(),
        P(),
        P(),
        P(None, "col"),
        P(None, "col"),
        P(None, "col"),
        P("col", None),
        P(),
        P("col", None, "row"),
        P("col", None, "row"),
        P("col", "row", None),
        P(),
        P(),
        P(),
        P("row", None),
        P("row"),
        P("row"),
    )
    return jax.shard_map(
        shards,
        mesh=mesh,
        in_specs=placed,
        out_specs=(
            P("row", "col"),
            P("row", "col"),
            P(None, "row", "col", None),
            P(None, "row", None, "col"),
            P("row", None, None),
        ),
        check_vma=False,
    )
```

```python
import functools

import jax
import jax.numpy as jnp
from jax import lax
from jax.experimental import pallas as pl
from jax.experimental.pallas import tpu as pltpu
from jax.sharding import PartitionSpec as P

HD = 128
F32, BF16 = jnp.float32, jnp.bfloat16
MESH_ID = pl.DeviceIdType.MESH
VM = pl.BlockSpec(memory_space=pltpu.VMEM)
ANY = pl.BlockSpec(memory_space=pl.ANY)
VMEM_LIMIT = 60 * 1024 * 1024
VMEM_MOST = 67_000_000
SHARES, FIRST_SHARE = 8, 2

norm_eps = 1e-05
rope_base = 10000.0
masked_score = -1e30


def nn(left, right):
    return jnp.dot(left, right, preferred_element_type=F32)


def nt(left, right):
    return lax.dot_general(left, right, (((1,), (1,)), ((), ())), preferred_element_type=F32)


def tn(left, right):
    return lax.dot_general(left, right, (((0,), (0,)), ((), ())), preferred_element_type=F32)


def remote(src, dst, send_sem, recv_sem, device):
    return pltpu.make_async_remote_copy(
        src_ref=src,
        dst_ref=dst,
        send_sem=send_sem,
        recv_sem=recv_sem,
        device_id={"col": device},
        device_id_type=MESH_ID,
    )


def line_place():
    here = lax.axis_index("col")
    core = here % 2
    return here, here // 2, core, here + 1 - 2 * core


def line_barrier(chips, across=()):
    here, chip, core, mate = line_place()
    barrier = pltpu.get_barrier_semaphore()
    has_left, has_right = chip > 0, chip < chips - 1
    for other in across:
        pl.semaphore_signal(barrier, inc=1, device_id={"row": other}, device_id_type=MESH_ID)
    pl.semaphore_signal(barrier, inc=1, device_id={"col": mate}, device_id_type=MESH_ID)

    @pl.when(has_left)
    def _():
        pl.semaphore_signal(barrier, inc=1, device_id={"col": here - 2}, device_id_type=MESH_ID)

    @pl.when(has_right)
    def _():
        pl.semaphore_signal(barrier, inc=1, device_id={"col": here + 2}, device_id_type=MESH_ID)

    inner = jnp.logical_and(has_left, has_right)

    @pl.when(inner)
    def _():
        pl.semaphore_wait(barrier, 3 + len(across))

    @pl.when(jnp.logical_not(inner))
    def _():
        pl.semaphore_wait(barrier, 2 + len(across))


def spot(axis, size, parts, block, part):
    rows, cols = size
    step = rows // parts
    if axis == 0:
        return (pl.ds(pl.multiple_of(block * rows + part * step, 8), step), slice(None))
    return (pl.ds(part * step, step), pl.ds(pl.multiple_of(block * cols, 128), cols))


def run(*steps):
    steps = list(steps)
    while steps:
        for one in list(steps):
            if next(one, steps) is steps:
                steps.remove(one)


def gather_body(chips, parts, axis, riders, x_ref, *refs):
    line_barrier(chips, row_partners() if riders else ())
    o_ref = refs[riders]
    sems = refs[2 * riders + 1 :]
    steps = [gather_steps(chips, parts, axis, x_ref, o_ref, *sems[:6])]
    if riders:
        steps.append(row_gather_steps(2, 0, refs[0], refs[2], *sems[6:]))
    run(*steps)


def gather_steps(chips, parts, axis, x_ref, o_ref, right_sem, left_sem, mate_sem, line_recv, mate_recv, own_sem):
    here, chip, core, mate = line_place()
    size = x_ref.shape
    step = size[0] // parts

    def at(block, part):
        return o_ref.at[spot(axis, size, parts, block, part)]

    def copy(j, part, sem, recv, device, first=False, block=None):
        block = 2 * j + core if block is None else block
        src = x_ref.at[pl.ds(part * step, step)] if first else at(block, part)
        return remote(src, at(block, part), sem.at[j, part], recv.at[j, part], device)

    def forward(j, part, rightward, leftward, first):
        if rightward:

            @pl.when(chip < chips - 1)
            def _():
                copy(j, part, right_sem, line_recv, here + 2, first).start()

        if leftward:

            @pl.when(chip > 0)
            def _():
                copy(j, part, left_sem, line_recv, here - 2, first).start()

        copy(j, part, mate_sem, mate_recv, mate, first).start()

    for part in range(parts):
        forward(chip, part, True, True, True)
    own = []
    for part in range(parts):
        own.append(
            pltpu.make_async_copy(x_ref.at[pl.ds(part * step, step)], at(here, part), own_sem.at[part])
        )
        own[-1].start()
    yield
    for far in range(1, chips):
        for part in range(parts):

            @pl.when(chip - far >= 0)
            def _():
                copy(chip - far, part, right_sem, line_recv, mate).wait_recv()
                forward(chip - far, part, True, False, False)

            @pl.when(chip + far < chips)
            def _():
                copy(chip + far, part, left_sem, line_recv, mate).wait_recv()
                forward(chip + far, part, False, True, False)

        yield

    for own_copy in own:
        own_copy.wait()
    for j in range(chips):
        for part in range(parts):
            copy(j, part, mate_sem, mate_recv, mate, block=2 * j + 1 - core).wait_recv()
            copy(j, part, mate_sem, mate_recv, mate).wait_send()

            @pl.when(jnp.logical_and(j <= chip, chip < chips - 1))
            def _():
                copy(j, part, right_sem, line_recv, here + 2).wait_send()

            @pl.when(jnp.logical_and(j >= chip, chip > 0))
            def _():
                copy(j, part, left_sem, line_recv, here - 2).wait_send()


def line_gather(x, chips, axis, ident, parts=2, rider=None):
    rows, cols = x.shape
    sems = pltpu.SemaphoreType.DMA((chips, parts))
    shape = (2 * chips * rows, cols) if axis == 0 else (rows, 2 * chips * cols)
    whole = jax.ShapeDtypeStruct(shape, x.dtype)
    more = () if rider is None else (rider,)
    ridden = tuple(jax.ShapeDtypeStruct((3, FIRST_SHARE) + one.shape[1:], one.dtype) for one in more)
    return pl.pallas_call(
        functools.partial(gather_body, chips, parts, axis, len(more)),
        out_shape=(whole,) + ridden,
        in_specs=[VM] + [ANY] * len(more),
        out_specs=(VM,) + (ANY,) * len(more),
        scratch_shapes=[sems] * 5
        + [pltpu.SemaphoreType.DMA((parts,))]
        + [pltpu.SemaphoreType.DMA((6,))] * (2 * len(more)),
        compiler_params=pltpu.CompilerParams(
            collective_id=ident, has_side_effects=True, vmem_limit_bytes=VMEM_LIMIT
        ),
        name="line_gather",
    )(x, *more)


def reduce_steps(
    chips, parts, axis, p_ref, o_ref, pair_buf, line_buf, sums, right_sem, left_sem, mate_sem, line_recv, mate_recv
):
    here, chip, core, mate = line_place()
    size = o_ref.shape
    step = size[0] // parts

    def rows(part):
        return pl.ds(part * step, step)

    def at(block, part):
        return spot(axis, size, parts, block, part)

    def mate_copy(j, part):
        return remote(
            p_ref.at[at(2 * j + 1 - core, part)],
            pair_buf.at[j, rows(part)],
            mate_sem.at[j, part],
            mate_recv.at[j, part],
            mate,
        )

    def line_copy(j, slot, part, sem, device):
        return remote(
            sums.at[j, rows(part)], line_buf.at[slot, rows(part)], sem.at[j, part], line_recv.at[slot, part], device
        )

    for far in range(chips - 1, -1, -1):
        for part in range(parts):

            @pl.when(chip + far < chips)
            def _():
                mate_copy(chip + far, part).start()

            if far > 0:

                @pl.when(chip - far >= 0)
                def _():
                    mate_copy(chip - far, part).start()

    yield

    def pair_sum(j, part):
        mate_copy(j, part).wait_recv()
        return p_ref[at(2 * j + core, part)].astype(F32) + pair_buf[j, rows(part)].astype(F32)

    def pass_on(j, slot, part, more, sem, device):
        @pl.when(more)
        def _():
            line_copy(j, j, part, sem, mate).wait_recv()
            total = pair_sum(j, part) + line_buf[j, rows(part)].astype(F32)
            sums[j, rows(part)] = total.astype(BF16)

        @pl.when(jnp.logical_not(more))
        def _():
            sums[j, rows(part)] = pair_sum(j, part).astype(BF16)

        line_copy(j, slot, part, sem, device).start()

    for far in range(chips - 1, 0, -1):
        for part in range(parts):

            @pl.when(chip + far < chips)
            def _():
                pass_on(chip + far, chip + far, part, chip > 0, right_sem, here + 2)

            @pl.when(chip - far >= 0)
            def _():
                pass_on(
                    chip - far, chips if far == 1 else chip - far, part, chip < chips - 1, left_sem, here - 2
                )

        yield

    for part in range(parts):
        o_ref[rows(part)] = pair_sum(chip, part)

        @pl.when(chip > 0)
        def _():
            line_copy(chip, chip, part, right_sem, mate).wait_recv()
            o_ref[rows(part)] += line_buf[chip, rows(part)].astype(F32)

        @pl.when(chip < chips - 1)
        def _():
            line_copy(chip, chips, part, left_sem, mate).wait_recv()
            o_ref[rows(part)] += line_buf[chips, rows(part)].astype(F32)

    for j in range(chips):
        for part in range(parts):
            mate_copy(j, part).wait_send()

            @pl.when(j > chip)
            def _():
                line_copy(j, j, part, right_sem, mate).wait_send()

            @pl.when(j < chip)
            def _():
                line_copy(j, j, part, left_sem, mate).wait_send()


def small_body(count, x_ref, o_ref, send_sem, recv_sem):
    here = lax.axis_index("col")
    barrier = pltpu.get_barrier_semaphore()
    for hop in range(1, count):
        other = lax.rem(here + hop, count)
        pl.semaphore_signal(barrier, inc=1, device_id={"col": other}, device_id_type=MESH_ID)
    o_ref[here] = x_ref[...]
    pl.semaphore_wait(barrier, count - 1)

    def copy(hop, block):
        other = lax.rem(here + hop, count)
        return remote(x_ref, o_ref.at[block], send_sem.at[hop], recv_sem.at[hop], other)

    for hop in range(1, count):
        copy(hop, here).start()
    for hop in range(1, count):
        copy(hop, lax.rem(here + count - hop, count)).wait_recv()
    for hop in range(1, count):
        copy(hop, here).wait_send()


def small_gather(x, count, ident):
    sems = pltpu.SemaphoreType.DMA((count,))
    return pl.pallas_call(
        functools.partial(small_body, count),
        out_shape=jax.ShapeDtypeStruct((count,) + x.shape, x.dtype),
        in_specs=[VM],
        out_specs=VM,
        scratch_shapes=[sems, sems],
        compiler_params=pltpu.CompilerParams(collective_id=ident, has_side_effects=True),
        name="small_gather",
    )(x)


def row_copy(src, dst, sems, which, device):
    return pltpu.make_async_remote_copy(
        src_ref=src,
        dst_ref=dst,
        send_sem=sems[0].at[which],
        recv_sem=sems[1].at[which],
        device_id={"row": device},
        device_id_type=MESH_ID,
    )


def row_partners():
    here = lax.axis_index("row")
    major, minor = here // 2, here % 2
    return 2 * major + 1 - minor, 2 * (1 - major) + minor


def row_gather_steps(pauses, begin, x_ref, o_ref, *sems):
    near, next_one = row_partners()
    half = o_ref.shape[1] // 2

    def side(neighbour, first):
        slot, device = (0, near) if neighbour == 0 else (1, next_one)
        rows = pl.ds(first * half, half)
        source = x_ref.at[pl.ds(begin + first * half, half)]
        return row_copy(source, o_ref.at[slot, rows], sems, 2 * slot + first, device)

    def onward(neighbour):
        slot, device = (0, next_one) if neighbour == 0 else (1, near)
        rows = pl.ds(slot * half, half)
        return row_copy(o_ref.at[slot, rows], o_ref.at[2, rows], sems, 4 + slot, device)

    side(0, 0).start()
    side(1, 1).start()
    side(0, 1).start()
    side(1, 0).start()
    for _ in range(pauses):
        yield
    side(0, 0).wait_recv()
    onward(0).start()
    side(1, 1).wait_recv()
    onward(1).start()
    yield
    for neighbour in range(2):
        side(neighbour, 1 - neighbour).wait_recv()
        onward(neighbour).wait_recv()
        onward(neighbour).wait_send()
        side(neighbour, 0).wait_send()
        side(neighbour, 1).wait_send()


def turn_body(chips, parts, first, last, held, late_count, riders, *refs):
    refs = list(refs)

    def take(count):
        taken = refs[:count]
        del refs[:count]
        return taken

    (p_ref,) = take(1)
    operands = take(held)
    rider_in = take(riders)
    (o_ref,) = take(1)
    results = take(late_count)
    rider_out = take(riders)
    sums_in, pair_buf, line_buf, sums = take(4)
    reduce_sems = take(5)
    gather_sems = take(5)
    line_barrier(chips, row_partners() if riders > 1 else ())
    steps = [reduce_steps(chips, parts, 0, p_ref, sums_in, pair_buf, line_buf, sums, *reduce_sems)]
    if riders > 0:
        steps.append(gather_steps(chips, 2, 1, rider_in[0], rider_out[0], *take(6)))
    if riders > 1:
        across = row_gather_steps(1, FIRST_SHARE, rider_in[1], rider_out[1], *take(2))
        next(across)
    run(*steps)
    here = lax.axis_index("col")
    own = o_ref.shape[0] // (2 * chips)
    kept = first(sums_in, operands, results, o_ref, pl.ds(pl.multiple_of(here * own, 8), own))

    def beside():
        if riders > 1:
            next(across)
        last(kept, operands, results)

    run(gather_rows_steps(chips, parts, o_ref, *gather_sems, beside))
    if riders > 1:
        run(across)


def gather_rows_steps(chips, parts, o_ref, right_sem, left_sem, mate_sem, line_recv, mate_recv, beside):
    here, chip, core, mate = line_place()
    size = (o_ref.shape[0] // (2 * chips), o_ref.shape[1])

    def copy(j, part, sem, recv, device, block=None):
        block = 2 * j + core if block is None else block
        ref = o_ref.at[spot(0, size, parts, block, part)]
        return remote(ref, ref, sem.at[j, part], recv.at[j, part], device)

    def forward(j, part, rightward, leftward):
        if rightward:

            @pl.when(chip < chips - 1)
            def _():
                copy(j, part, right_sem, line_recv, here + 2).start()

        if leftward:

            @pl.when(chip > 0)
            def _():
                copy(j, part, left_sem, line_recv, here - 2).start()

        copy(j, part, mate_sem, mate_recv, mate).start()

    for part in range(parts):
        forward(chip, part, True, True)
    beside()
    yield
    for far in range(1, chips):
        for part in range(parts):

            @pl.when(chip - far >= 0)
            def _():
                copy(chip - far, part, right_sem, line_recv, mate).wait_recv()
                forward(chip - far, part, True, False)

            @pl.when(chip + far < chips)
            def _():
                copy(chip + far, part, left_sem, line_recv, mate).wait_recv()
                forward(chip + far, part, False, True)

        yield

    for j in range(chips):
        for part in range(parts):
            copy(j, part, mate_sem, mate_recv, mate, block=2 * j + 1 - core).wait_recv()
            copy(j, part, mate_sem, mate_recv, mate).wait_send()

            @pl.when(jnp.logical_and(j <= chip, chip < chips - 1))
            def _():
                copy(j, part, right_sem, line_recv, here + 2).wait_send()

            @pl.when(jnp.logical_and(j >= chip, chip > 0))
            def _():
                copy(j, part, left_sem, line_recv, here - 2).wait_send()


def line_turn(p, operands, width, results, first, last, chips, ident, riders=(), parts=2):
    rows, cols = p.shape
    own = rows // (2 * chips)
    sems = pltpu.SemaphoreType.DMA((chips, parts))
    longer = pltpu.SemaphoreType.DMA((chips + 1, parts))
    more = []
    ridden = []
    if len(riders) > 0:
        height, part = riders[0].shape
        ridden.append(jax.ShapeDtypeStruct((height, 2 * chips * part), BF16))
        more += [pltpu.SemaphoreType.DMA((chips, 2))] * 5 + [pltpu.SemaphoreType.DMA((2,))]
    if len(riders) > 1:
        ridden.append(jax.ShapeDtypeStruct((3, SHARES - FIRST_SHARE) + riders[1].shape[1:], BF16))
        more += [pltpu.SemaphoreType.DMA((6,))] * 2
    return pl.pallas_call(
        functools.partial(turn_body, chips, parts, first, last, len(operands), len(results), len(riders)),
        out_shape=(jax.ShapeDtypeStruct((rows, width), BF16),) + tuple(results) + tuple(ridden),
        in_specs=[VM] * (1 + len(operands)) + [VM, ANY][: len(riders)],
        out_specs=(VM,) * (1 + len(results)) + (VM, ANY)[: len(riders)],
        scratch_shapes=[
            pltpu.VMEM((own, cols), F32),
            pltpu.VMEM((chips, own, cols), BF16),
            pltpu.VMEM((chips + 1, own, cols), BF16),
            pltpu.VMEM((chips, own, cols), BF16),
            sems,
            sems,
            sems,
            longer,
            sems,
        ]
        + [sems] * 5
        + more,
        compiler_params=pltpu.CompilerParams(
            collective_id=ident, has_side_effects=True, vmem_limit_bytes=VMEM_LIMIT
        ),
        name="line_turn",
    )(p, *operands, *riders)


def inverse_rms(values):
    return lax.rsqrt(jnp.mean(values * values, axis=1, keepdims=True) + norm_eps)


def turn_forward(width, experts, sums, operands, results, o_ref, own):
    x_ref, gain_ref, a_ref, router_ref, up_ref = operands
    hidden_ref, mid_ref, mid_router_ref, probs_ref = results
    hidden = x_ref[...].astype(F32) + sums[:, :width]
    mid_ref[...] = sums[:, width:].astype(BF16)
    hidden_ref[...] = hidden
    normed = (hidden * inverse_rms(hidden) * gain_ref[...]).astype(BF16)
    o_ref[own, :width] = normed
    mid_router = nt(normed, a_ref[...]).astype(BF16)
    mid_router_ref[...] = mid_router
    logits = nt(normed, router_ref[...]) + nn(mid_router, up_ref[...])
    lane = lax.broadcasted_iota(jnp.int32, logits.shape, 1)
    logits = jnp.where(lane < experts, logits, masked_score)
    exponent = jnp.exp(logits - jnp.max(logits, axis=1, keepdims=True))
    probs = exponent / jnp.sum(exponent, axis=1, keepdims=True)
    probs_ref[...] = probs
    high = probs.astype(BF16)
    rest = probs - high.astype(F32)
    o_ref[own, width:] = (high.astype(F32) + pltpu.roll(rest, experts, 1)).astype(BF16)
    return None


def turn_backward(experts, grads, pair, operands, results, o_ref, own):
    g_ref, hidden_ref, gain_ref, a_ref, router_ref, up_ref, probs_ref, mid_router_ref, mid_ref = operands
    lanes = pair.shape[1]
    grad_probs = pair + pltpu.roll(pair, lanes - experts, 1)
    probs = probs_ref[...]
    grad_logits = (probs * (grad_probs - jnp.sum(probs * grad_probs, axis=1, keepdims=True))).astype(BF16)
    grad_mid = nt(grad_logits, up_ref[...]).astype(BF16)
    grad_normed = grads + nn(grad_logits, router_ref[...]) + nn(grad_mid, a_ref[...])
    hidden = hidden_ref[...]
    inv = inverse_rms(hidden)
    scaled = grad_normed * gain_ref[...]
    grad_hidden = (
        g_ref[...].astype(F32)
        + inv * scaled
        - hidden * (inv * inv * inv * jnp.mean(hidden * scaled, axis=1, keepdims=True))
    )
    grad_hidden = grad_hidden.astype(BF16)
    o_ref[own, :] = grad_hidden
    return grad_logits, grad_mid, grad_hidden


def turn_late(kept, operands, results):
    _, hidden_ref, gain_ref, _, _, _, _, mid_router_ref, mid_ref = operands
    grad_logits, grad_mid, grad_hidden = kept
    hidden = hidden_ref[...]
    normed = (hidden * inverse_rms(hidden) * gain_ref[...]).astype(BF16)
    rank = grad_mid.shape[1]
    late_ref, router_ref = results
    late_ref[pl.ds(0, rank)] = tn(grad_mid, normed)
    late_ref[pl.ds(rank, rank)] = tn(mid_ref[:, :rank], grad_hidden)
    router_ref[...] = tn(mid_router_ref[...], grad_logits)


def row_sums(values):
    lanes = 128
    values = sum(values[:, n : n + lanes] for n in range(0, values.shape[1], lanes))
    high = values.astype(BF16)
    rest = (values - high.astype(F32)).astype(BF16)
    ones = jnp.ones((8, values.shape[1]), BF16)
    return nt(ones, high) + nt(ones, rest)


def project_body(tile, x_ref, gain_ref, wq, wk, wv, a_ref, b_ref, proj_ref, mid_ref, inv_ref, sq_ref):
    part = wq.shape[1]
    for t in range(x_ref.shape[0] // tile):
        rows = pl.ds(t * tile, tile)
        x = x_ref[rows].astype(F32)
        inv = inverse_rms(x)
        inv_ref[rows] = inv
        normed = (x * inv * gain_ref[...]).astype(BF16)
        mid = nt(normed, a_ref[...]).astype(BF16)
        mid_ref[rows] = mid
        for m, w in enumerate((wq, wk, wv)):
            cols = pl.ds(m * part, part)
            proj = nn(normed, w[...]) + nn(mid, b_ref[:, cols])
            proj_ref[rows, cols] = proj
            if m < 2:
                sq_ref[pl.ds(m, 1), rows] = row_sums(proj * proj)[0:1]


def project(x, gain, weights, a_rows, b_cols):
    seq_len, width = x.shape
    part = weights[0].shape[1]
    rank = a_rows.shape[0]
    return pl.pallas_call(
        functools.partial(project_body, min(256, seq_len)),
        out_shape=(
            jax.ShapeDtypeStruct((seq_len, 3 * part), F32),
            jax.ShapeDtypeStruct((seq_len, rank), BF16),
            jax.ShapeDtypeStruct((seq_len, 1), F32),
            jax.ShapeDtypeStruct((2, seq_len), F32),
        ),
        in_specs=[VM] * 7,
        out_specs=(VM,) * 4,
        compiler_params=pltpu.CompilerParams(vmem_limit_bytes=VMEM_LIMIT),
        name="project",
    )(x, gain, *weights, a_rows, b_cols)


def key_limit(start, tile, seq_len, reach):
    return min(seq_len, max(start + tile, reach))


def allowed_keys(start, tile, limit, prefix_len):
    query = start + lax.broadcasted_iota(jnp.int32, (tile, limit), 0)
    key = lax.broadcasted_iota(jnp.int32, (tile, limit), 1)
    return jnp.logical_or(key <= query, key < prefix_len)


def attend_body(
    tile, reach, scale, prefix_ref, proj_ref, inv_ref, gains_ref, cos_ref, sin_ref, map_ref,
    p_ref, att_ref, q_ref, k_ref, v_ref, log_ref,
):
    seq_len, part = att_ref.shape
    prefix_len = prefix_ref[0]
    for h in range(part // HD):
        cols = pl.ds(h * HD, HD)
        for m, ref in ((0, q_ref), (1, k_ref)):
            plain = proj_ref[:, pl.ds(m * part + h * HD, HD)] * inv_ref[:, m : m + 1] * gains_ref[m : m + 1, cols]
            ref[:, cols] = (plain * cos_ref[...] + pltpu.roll(plain, HD // 2, 1) * sin_ref[...]).astype(BF16)
        v_ref[:, cols] = proj_ref[:, pl.ds(2 * part + h * HD, HD)].astype(BF16)
    for start in range(0, seq_len, tile):
        rows = pl.ds(start, tile)
        limit = key_limit(start, tile, seq_len, reach)
        allowed = allowed_keys(start, tile, limit, prefix_len)
        for h in range(part // HD):
            cols = pl.ds(h * HD, HD)
            scores = nt(q_ref[rows, cols], k_ref[pl.ds(0, limit), cols]) * scale
            scores = jnp.where(allowed, scores, masked_score)
            top = jnp.max(scores, axis=1, keepdims=True)
            exponent = jnp.exp(scores - top)
            total = jnp.sum(exponent, axis=1, keepdims=True)
            weights = (exponent / total).astype(BF16)
            att_ref[rows, cols] = nn(weights, v_ref[pl.ds(0, limit), cols]).astype(BF16)
            log_ref[rows, h : h + 1] = top + jnp.log(total)
        p_ref[rows] = nn(att_ref[rows], map_ref[...]).astype(BF16)


def attend(prefix, proj, inv, gains, tables, out_map, reach, scale):
    seq_len = proj.shape[0]
    part = proj.shape[1] // 3
    heads = jax.ShapeDtypeStruct((seq_len, part), BF16)
    return pl.pallas_call(
        functools.partial(attend_body, min(256, seq_len), reach, scale),
        out_shape=(
            jax.ShapeDtypeStruct((seq_len, out_map.shape[1]), BF16),
            heads,
            heads,
            heads,
            heads,
            jax.ShapeDtypeStruct((seq_len, part // HD), F32),
        ),
        in_specs=[pl.BlockSpec(memory_space=pltpu.SMEM)] + [VM] * 6,
        out_specs=(VM,) * 6,
        compiler_params=pltpu.CompilerParams(vmem_limit_bytes=VMEM_LIMIT),
        name="attend",
    )(prefix, proj, inv, gains, *tables, out_map)


def attend_back(
    tile, reach, scale, prefix_ref, g_ref, map_ref, b_ref, att_ref, q_ref, k_ref, v_ref, log_ref, proj_ref,
    gains_ref, cos_ref, sin_ref, scaled_ref, dv_ref, stat_ref, ga_ref, da_ref, dq_acc, dk_acc, dv_acc,
):
    seq_len, part = att_ref.shape
    prefix_len = prefix_ref[0]
    grad_a = jnp.zeros(ga_ref.shape, F32)
    for start in range(0, seq_len, tile):
        rows = pl.ds(start, tile)
        grads = g_ref[rows]
        da_ref[rows] = nt(grads, map_ref[...]).astype(BF16)
        grad_mid = nt(grads, b_ref[...]).astype(BF16)
        grad_a += tn(grad_mid, att_ref[rows])
    ga_ref[...] = grad_a
    dk_acc[...] = jnp.zeros_like(dk_acc)
    dv_acc[...] = jnp.zeros_like(dv_acc)
    for start in range(0, seq_len, tile):
        rows = pl.ds(start, tile)
        limit = key_limit(start, tile, seq_len, reach)
        keys = pl.ds(0, limit)
        allowed = allowed_keys(start, tile, limit, prefix_len)
        for h in range(part // HD):
            cols = pl.ds(h * HD, HD)
            query, key = q_ref[rows, cols], k_ref[keys, cols]
            grads = da_ref[rows, cols]
            scores = jnp.where(allowed, nt(query, key) * scale, masked_score)
            weights = jnp.exp(scores - log_ref[rows, h : h + 1])
            grad_weights = nt(grads, v_ref[keys, cols])
            dot = jnp.sum(weights * grad_weights, axis=1, keepdims=True)
            grad_scores = (weights * (grad_weights - dot)).astype(BF16)
            dq_acc[rows, cols] = nn(grad_scores, key) * scale
            dk_acc[keys, cols] += tn(grad_scores, query) * scale
            dv_acc[keys, cols] += tn(weights.astype(BF16), grads)
    dv_ref[...] = dv_acc[...].astype(BF16)
    for m, acc in ((0, dq_acc), (1, dk_acc)):
        for start in range(0, seq_len, tile):
            rows = pl.ds(start, tile)
            total = jnp.zeros((8, tile), F32)
            for h in range(part // HD):
                cols = pl.ds(h * HD, HD)
                here = pl.ds(m * part + h * HD, HD)
                plain = acc[rows, cols]
                turned = plain * cos_ref[rows] - pltpu.roll(plain, HD // 2, 1) * sin_ref[rows]
                scaled = turned * gains_ref[m : m + 1, cols]
                scaled_ref[rows, here] = scaled
                total += row_sums(proj_ref[rows, here] * scaled)
            stat_ref[pl.ds(m, 1), rows] = total[0:1]


def back_body(tile, reach, scale, chips, row_count, extra, prefix_ref, slot_ref, *refs):
    refs = list(refs)

    def take(number):
        taken = refs[:number]
        del refs[:number]
        return taken

    g_ref, map_ref, bo_ref, att_ref, q_ref, k_ref, v_ref, log_ref, proj_ref, gains_ref, cos_ref, sin_ref = take(12)
    inv_ref, b_ref, a_ref, x_ref, inv1_ref, gain_ref, mid_ref, late_ref, router_ref = take(9)
    weights = take(3)
    gi_ref, held_a, held_b, held_router = take(4)
    scaled_ref, dv_ref, stat_ref, stats_ref, ga_ref, da_ref, dq_acc, dk_acc, dv_acc = take(9)
    w_ref, d_ref, middle_ref, p_ref, o_ref, pair_buf, line_buf, sums, flat_ref, every_ref = take(10)
    w_sems, stat_send, stat_recv, row_send, row_recv = take(5)
    right_sem, left_sem, mate_sem, line_recv, mate_recv = take(5)
    here, chip, core, mate = line_place()
    row = lax.axis_index("row")
    count = 2 * chips
    seq_len, width = x_ref.shape
    part = dv_ref.shape[1]
    ranks = a_ref.shape[0]
    rank = ranks // 3
    parts = 2

    fetches = [
        pltpu.make_async_copy(w, w_ref.at[:, pl.ds(m * part, part)], w_sems.at[m]) for m, w in enumerate(weights)
    ]
    for fetch in fetches:
        fetch.start()
    barrier = pltpu.get_barrier_semaphore()
    for hop in range(1, count):
        other = lax.rem(here + hop, count)
        pl.semaphore_signal(barrier, inc=1, device_id={"col": other}, device_id_type=MESH_ID)
    for hop in range(1, row_count):
        other = lax.rem(row + hop, row_count)
        pl.semaphore_signal(barrier, inc=1, device_id={"row": other}, device_id_type=MESH_ID)
    attend_back(
        tile, reach, scale, prefix_ref, g_ref, map_ref, bo_ref, att_ref, q_ref, k_ref, v_ref, log_ref, proj_ref,
        gains_ref, cos_ref, sin_ref, scaled_ref, dv_ref, stat_ref, ga_ref, da_ref, dq_acc, dk_acc, dv_acc,
    )
    pl.semaphore_wait(barrier, count + row_count - 2)

    def stat_copy(hop, block):
        other = lax.rem(here + hop, count)
        return remote(stat_ref, stats_ref.at[block], stat_send.at[hop], stat_recv.at[hop], other)

    for hop in range(1, count):
        stat_copy(hop, here).start()
    stats_ref[here] = stat_ref[...]
    for hop in range(1, count):
        stat_copy(hop, lax.rem(here + count - hop, count)).wait_recv()
    total = stats_ref[0]
    for n in range(1, count):
        total = total + stats_ref[n]
    total = jnp.concatenate([total, jnp.zeros((6, seq_len), F32)], axis=0) * (1.0 / width)

    grad_b = jnp.zeros((ranks, 3 * part), F32)
    first_stats = jnp.zeros((8, part), F32)
    line = lax.broadcasted_iota(jnp.int32, (8, part), 0)
    for t in range(seq_len // tile):
        rows = pl.ds(t * tile, tile)
        upright = jnp.transpose(total[:, t * tile : (t + 1) * tile])
        products = jnp.zeros((tile, part), F32)
        for m in range(3):
            cols = pl.ds(m * part, part)
            if m < 2:
                inv = inv_ref[rows, m : m + 1]
                shift = inv * inv * inv * upright[:, m : m + 1]
                grad = (inv * scaled_ref[rows, cols] - proj_ref[rows, cols] * shift).astype(BF16)
            else:
                grad = dv_ref[rows]
            d_ref[rows, cols] = grad
            products += grad.astype(F32) * proj_ref[rows, cols]
        grads = d_ref[rows]
        middle_ref[rows] = nt(grads, b_ref[...]).astype(BF16)
        grad_b += tn(mid_ref[rows], grads)
        first = row_sums(products / inv1_ref[rows])
        for j in range(tile // part):
            first_stats = jnp.where(
                line == (t * tile) // part + j, first[:, j * part : (j + 1) * part], first_stats
            )
    high = first_stats.astype(BF16).astype(F32)
    router = router_ref[...]
    if part > router.shape[1]:
        router = jnp.concatenate([router, jnp.zeros((rank, part - router.shape[1]), F32)], axis=1)
    common = jnp.concatenate([router, high, first_stats - high], axis=0).astype(BF16)
    common = jnp.concatenate([common] * count, axis=1)
    p_ref[pl.ds(ranks, 2 * rank)] = late_ref[...].astype(BF16)
    p_ref[pl.ds(ranks + 2 * rank, rank + 16)] = common
    used = ranks + 3 * rank + 16
    p_ref[pl.ds(used, extra - used)] = jnp.zeros((extra - used, width), BF16)
    for fetch in fetches:
        fetch.wait()

    size = o_ref.shape
    step = size[0] // parts

    def rows_of(piece):
        return pl.ds(piece * step, step)

    def at(block, piece):
        return spot(1, size, parts, block, piece)

    def mate_copy(j, piece):
        return remote(
            p_ref.at[at(2 * j + 1 - core, piece)],
            pair_buf.at[j, rows_of(piece)],
            mate_sem.at[j, piece],
            mate_recv.at[j, piece],
            mate,
        )

    def line_copy(j, slot, piece, sem, device):
        return remote(
            sums.at[j, rows_of(piece)],
            line_buf.at[slot, rows_of(piece)],
            sem.at[j, piece],
            line_recv.at[slot, piece],
            device,
        )

    def order(s):
        right = chips - 1 - chip
        return jnp.where(s < right, chips - 1 - s, jnp.where(s < chips - 1, s - right, chip))

    def work_out(s):
        cols = pl.ds(pl.multiple_of(order(s) * (2 * part), 128), 2 * part)
        gain = gain_ref[:, cols]
        spread = a_ref[:, cols]
        chunk = w_ref[cols]

        def one_tile(t, grad_a):
            rows = pl.ds(pl.multiple_of(t * tile, tile), tile)
            middle = middle_ref[rows]
            normed_part = nt(d_ref[rows], chunk) + nn(middle, spread)
            p_ref[pl.ds(pl.multiple_of(extra + t * tile, 16), tile), cols] = normed_part.astype(BF16)
            normed = (x_ref[rows, cols].astype(F32) * inv1_ref[rows] * gain).astype(BF16)
            return grad_a + tn(middle, normed)

        grad_a = lax.fori_loop(0, seq_len // tile, one_tile, jnp.zeros((ranks, 2 * part), F32))
        p_ref[pl.ds(0, ranks), cols] = grad_a.astype(BF16)
        for piece in range(parts):
            mate_copy(order(s), piece).start()

    def pair_sum(j, piece):
        mate_copy(j, piece).wait_recv()
        return p_ref[at(2 * j + core, piece)].astype(F32) + pair_buf[j, rows_of(piece)].astype(F32)

    def one_block(s, carry):
        work_out(s)

        @pl.when(jnp.logical_and(chip == 0, s > 0))
        def _():
            for piece in range(parts):
                j = order(s - 1)
                sums[j, rows_of(piece)] = pair_sum(j, piece).astype(BF16)
                line_copy(j, j, piece, right_sem, here + 2).start()

        @pl.when(jnp.logical_and(chip == chips - 1, s > 0))
        def _():
            for piece in range(parts):
                j = order(s - 1)
                sums[j, rows_of(piece)] = pair_sum(j, piece).astype(BF16)

                @pl.when(j == chips - 2)
                def _():
                    line_copy(j, chips, piece, left_sem, here - 2).start()

                @pl.when(j < chips - 2)
                def _():
                    line_copy(j, j, piece, left_sem, here - 2).start()

        return carry

    lax.fori_loop(0, chips, one_block, 0)
    inner = jnp.logical_and(chip > 0, chip < chips - 1)

    def pass_on(j, slot, piece, sem, device):
        line_copy(j, j, piece, sem, mate).wait_recv()
        sums[j, rows_of(piece)] = (pair_sum(j, piece) + line_buf[j, rows_of(piece)].astype(F32)).astype(BF16)
        line_copy(j, slot, piece, sem, device).start()

    for far in range(chips - 2, 0, -1):
        for piece in range(parts):

            @pl.when(jnp.logical_and(inner, chip + far < chips))
            def _():
                pass_on(chip + far, chip + far, piece, right_sem, here + 2)

            @pl.when(jnp.logical_and(inner, chip - far >= 0))
            def _():
                pass_on(chip - far, chips if far == 1 else chip - far, piece, left_sem, here - 2)

    def row_copy(hop, block):
        other = lax.rem(row + hop, row_count)
        return pltpu.make_async_remote_copy(
            src_ref=flat_ref,
            dst_ref=every_ref.at[block],
            send_sem=row_send.at[hop],
            recv_sem=row_recv.at[hop],
            device_id={"row": other},
            device_id_type=MESH_ID,
        )

    for piece in range(parts):
        o_ref[rows_of(piece)] = pair_sum(chip, piece)

        @pl.when(chip > 0)
        def _():
            line_copy(chip, chip, piece, right_sem, mate).wait_recv()
            o_ref[rows_of(piece)] += line_buf[chip, rows_of(piece)].astype(F32)

        @pl.when(chip < chips - 1)
        def _():
            line_copy(chip, chips, piece, left_sem, mate).wait_recv()
            o_ref[rows_of(piece)] += line_buf[chips, rows_of(piece)].astype(F32)

        if piece == 0:
            flat_ref[pl.ds(0, 6 * rank)] = o_ref[pl.ds(0, 6 * rank)].astype(BF16)
            flat_ref[pl.ds(6 * rank, rank)] = ga_ref[...].astype(BF16)
            for m in range(3):
                flat_ref[pl.ds((7 + m) * rank, rank)] = grad_b[
                    m * rank : (m + 1) * rank, m * part : (m + 1) * part
                ].astype(BF16)
            owner = jnp.full((16, part), slot_ref[0].astype(F32), F32)
            flat_ref[pl.ds(10 * rank, 16)] = owner.astype(BF16)
            for hop in range(1, row_count):
                row_copy(hop, row).start()
            every_ref[row] = flat_ref[...]

    stat_rows = o_ref[pl.ds(ranks + 3 * rank, 8)] + o_ref[pl.ds(ranks + 3 * rank + 8, 8)]
    upright = jnp.transpose(stat_rows)
    own = pl.ds(pl.multiple_of(here * part, 128), part)
    gain = gain_ref[:, own]
    for t in range(seq_len // part):
        rows = pl.ds(t * part, part)
        inv = inv1_ref[rows]
        pull = inv * inv * inv * upright[:, t : t + 1] * (1.0 / width)
        gi_ref[rows] = (
            g_ref[rows, own].astype(F32)
            + inv * gain * o_ref[pl.ds(extra + t * part, part)]
            - x_ref[rows, own].astype(F32) * pull
        )
    for hop in range(1, row_count):
        row_copy(hop, lax.rem(row + row_count - hop, row_count)).wait_recv()
    held = held_router.shape[0]
    for h in range(held):
        chosen = (row * held + h).astype(F32)
        picked = jnp.zeros((10 * rank, part), F32)
        for r in range(row_count):
            owner = every_ref[r, pl.ds(10 * rank, 16)].astype(F32)[0:1]
            picked += jnp.where(owner == chosen, every_ref[r, pl.ds(0, 10 * rank)].astype(F32), 0.0)
        for n, piece in enumerate((0, 1, 2, 6, 3)):
            held_a[n, h] = picked[piece * rank : (piece + 1) * rank]
        for n, piece in enumerate((7, 8, 9, 4)):
            held_b[n, h] = picked[piece * rank : (piece + 1) * rank]
        held_router[h] = picked[5 * rank : 6 * rank]

    for hop in range(1, row_count):
        row_copy(hop, row).wait_send()
    for hop in range(1, count):
        stat_copy(hop, here).wait_send()
    for j in range(chips):
        for piece in range(parts):
            mate_copy(j, piece).wait_send()

            @pl.when(j > chip)
            def _():
                line_copy(j, j, piece, right_sem, mate).wait_send()

            @pl.when(j < chip)
            def _():
                line_copy(j, j, piece, left_sem, mate).wait_send()


def back(prefix, slot, operands, weights, reach, scale, chips, row_count, held, ident):
    x = operands[15]
    seq_len, width = x.shape
    part = weights[0].shape[1]
    count = 2 * chips
    ranks = operands[14].shape[0]
    rank = ranks // 3
    extra = 128
    tall = seq_len + extra
    sems = pltpu.SemaphoreType.DMA((chips, 2))
    hops = pltpu.SemaphoreType.DMA((count,))
    row_hops = pltpu.SemaphoreType.DMA((row_count,))
    smem = pl.BlockSpec(memory_space=pltpu.SMEM)
    return pl.pallas_call(
        functools.partial(back_body, min(256, seq_len), reach, scale, chips, row_count, extra),
        out_shape=(
            jax.ShapeDtypeStruct((seq_len, part), F32),
            jax.ShapeDtypeStruct((5, held, rank, part), F32),
            jax.ShapeDtypeStruct((4, held, rank, part), F32),
            jax.ShapeDtypeStruct((held, rank, part), F32),
        ),
        in_specs=[smem, smem] + [VM] * len(operands) + [ANY] * 3,
        out_specs=(VM,) * 4,
        scratch_shapes=[
            pltpu.VMEM((seq_len, 2 * part), F32),
            pltpu.VMEM((seq_len, part), BF16),
            pltpu.VMEM((2, seq_len), F32),
            pltpu.VMEM((count, 2, seq_len), F32),
            pltpu.VMEM((rank, part), F32),
            pltpu.VMEM((seq_len, part), BF16),
            pltpu.VMEM((seq_len, part), F32),
            pltpu.VMEM((seq_len, part), F32),
            pltpu.VMEM((seq_len, part), F32),
            pltpu.VMEM((width, 3 * part), BF16),
            pltpu.VMEM((seq_len, 3 * part), BF16),
            pltpu.VMEM((seq_len, ranks), BF16),
            pltpu.VMEM((tall, width), BF16),
            pltpu.VMEM((tall, part), F32),
            pltpu.VMEM((chips, tall, part), BF16),
            pltpu.VMEM((chips + 1, tall, part), BF16),
            pltpu.VMEM((chips, tall, part), BF16),
            pltpu.VMEM((10 * rank + 16, part), BF16),
            pltpu.VMEM((row_count, 10 * rank + 16, part), BF16),
            pltpu.SemaphoreType.DMA((3,)),
            hops,
            hops,
            row_hops,
            row_hops,
            sems,
            sems,
            sems,
            pltpu.SemaphoreType.DMA((chips + 1, 2)),
            sems,
        ],
        compiler_params=pltpu.CompilerParams(
            collective_id=ident, has_side_effects=True, vmem_limit_bytes=VMEM_LIMIT
        ),
        name="back",
    )(prefix, slot, *operands, *weights)


def moments(chips, subs):
    when = {}
    for j in range(chips):
        for chip in range(j):
            own = subs * (chips - j) + 1
            when[chip, j] = max(own, when[chip - 1, j] + 3) if chip > 0 else own
        for chip in range(chips - 1, j, -1):
            own = subs * (chips - chip + j) + 1
            when[chip, j] = max(own, when[chip + 1, j] + 3) if chip < chips - 1 else own
    last = chips * subs
    return {place: min(time, last) for place, time in when.items()}


def moe_turn_body(experts, chips, subs, count, x_ref, g_ref, routes_ref, *refs):
    refs = list(refs)

    def take(number):
        taken = refs[:number]
        del refs[:number]
        return taken

    operands = [None] + take(8)
    gate_w, up_w = take(2)
    downs = take(count)
    layer_ref, o_ref = take(2)
    results = take(2)
    out_ref, out_pair, out_line = take(3)
    p_ref, out_acc, dx_acc, gate_acc, wgu, wd, x_buf, g_buf = take(8)
    pair_buf, line_buf, sums = take(3)
    w_sems, tile_sems, right_sem, left_sem, mate_sem, line_recv, mate_recv = take(7)
    gather_sems = take(5)
    out_sems = refs
    here, chip, core, mate = line_place()
    row = lax.axis_index("row")
    hidden = wd.shape[1]
    tokens, width = out_ref.shape
    own = tokens // (2 * chips)
    tile = 2 * own
    lanes = gate_acc.shape[1]
    local = gate_w.shape[0]
    pieces = gate_w.shape[2] // hidden
    steps = local * pieces
    each = steps // subs

    def fetches(step, e, piece):
        if count == 1:
            place = piece
            pairs = [(downs[0].at[e, pl.ds(piece * hidden, hidden)], wd.at[step])]
        else:
            place = 2 * ((row // 2 + piece // 2) % 2) + (row + piece) % 2
            if piece == 0:
                pairs = [(downs[0].at[e], wd.at[step])]
            else:
                early = downs[1].shape[1]
                pairs = [
                    (
                        ref.at[piece - 1, pl.ds(low - start, high - low)],
                        wd.at[step, pl.ds(low - e * hidden, high - low)],
                    )
                    for ref, start, low, high in (
                        (downs[1], 0, e * hidden, min(early, (e + 1) * hidden)),
                        (downs[2], early, max(early, e * hidden), (e + 1) * hidden),
                    )
                    if high > low
                ]
        units = pl.ds(pl.multiple_of(place * hidden, 128), hidden)
        return (
            pltpu.make_async_copy(gate_w.at[e, :, units], wgu.at[step, :, pl.ds(0, hidden)], w_sems.at[step, 0]),
            pltpu.make_async_copy(up_w.at[e, :, units], wgu.at[step, :, pl.ds(hidden, hidden)], w_sems.at[step, 1]),
        ) + tuple(pltpu.make_async_copy(source, place, w_sems.at[step, 2]) for source, place in pairs)

    def order(s):
        right = chips - 1 - chip
        return jnp.where(s < right, chips - 1 - s, jnp.where(s < chips - 1, s - right, chip))

    def tile_rows(s):
        return pl.ds(pl.multiple_of(order(s) * tile, 8), tile)

    def tiles(s):
        return (
            pltpu.make_async_copy(x_ref.at[tile_rows(s)], x_buf, tile_sems.at[0]),
            pltpu.make_async_copy(g_ref.at[tile_rows(s)], g_buf, tile_sems.at[1]),
        )

    for copy in tiles(0):
        copy.start()
    for step in range(steps):
        for copy in fetches(step, step // pieces, step % pieces):
            copy.start()
    line_barrier(chips)

    def block(number):
        return pl.ds(pl.multiple_of(number * own, 8), own)

    def mate_copy(j):
        return remote(p_ref.at[block(2 * j + 1 - core)], pair_buf.at[j], mate_sem.at[j], mate_recv.at[j], mate)

    def line_copy(j, slot, sem, device):
        return remote(sums.at[j], line_buf.at[slot], sem.at[j], line_recv.at[slot], device)

    def pair_sum(j):
        mate_copy(j).wait_recv()
        return p_ref[block(2 * j + core)].astype(F32) + pair_buf[j].astype(F32)

    def pass_on(at, j):
        rightward = j > at
        total = pair_sum(j)
        if 0 < at < chips - 1:
            line_copy(j, j, right_sem if rightward else left_sem, mate).wait_recv()
            total = total + line_buf[j].astype(F32)
        sums[j] = total.astype(BF16)
        if rightward:
            line_copy(j, j, right_sem, here + 2).start()
        else:
            line_copy(j, chips if at - j == 1 else j, left_sem, here - 2).start()

    when = moments(chips, subs)

    def one_sub(k, carry):
        s, sub = k // subs, k % subs
        rows = tile_rows(s)

        @pl.when(sub == 0)
        def _():
            for copy in tiles(s):
                copy.wait()

            out_acc[...] = jnp.zeros_like(out_acc)
            dx_acc[...] = jnp.zeros_like(dx_acc)
            gate_acc[...] = jnp.zeros_like(gate_acc)

        def one_step(step, carry):
            @pl.when(s == 0)
            def _():
                units = pl.ds(0, hidden)
                for number, (source, place) in enumerate(((gate_w, 0), (up_w, hidden))):
                    pltpu.make_async_copy(
                        source.at[0, :, units], wgu.at[step, :, pl.ds(place, hidden)], w_sems.at[step, number]
                    ).wait()
                pltpu.make_async_copy(downs[0].at[0, units], wd.at[step], w_sems.at[step, 2]).wait()

            e = here * local + step // pieces
            lane = lax.broadcasted_iota(jnp.int32, (tile, lanes), 1)
            mine = lane == e
            halves = jnp.logical_or(mine, lane == e + experts)
            named = jnp.sum(jnp.where(routes_ref[rows] == e, 1.0, 0.0), axis=1, keepdims=True)
            gate = jnp.sum(jnp.where(halves, x_buf[:, width:].astype(F32), 0.0), axis=1, keepdims=True)
            gate = gate * named
            both = nn(x_buf[:, :width], wgu[step])
            gate_in, up_in = both[:, :hidden], both[:, hidden:]
            sigmoid = jax.nn.sigmoid(gate_in)
            silu = gate_in * sigmoid
            active = silu * up_in
            back = nt(g_buf[...], wd[step])
            d_gate = jnp.sum(active * back, axis=1, keepdims=True) * named
            gate_acc[...] += jnp.where(mine, d_gate, 0.0)
            out_acc[...] += nn((active * gate).astype(BF16), wd[step])
            d_active = back * gate
            d_gate_in = d_active * up_in * (sigmoid + silu * (1.0 - sigmoid))
            d_up_in = d_active * silu
            d_both = jnp.concatenate([d_gate_in.astype(BF16), d_up_in.astype(BF16)], axis=1)
            dx_acc[...] += nt(d_both, wgu[step])
            return carry

        lax.fori_loop(sub * each, (sub + 1) * each, one_step, 0)

        @pl.when(sub == subs - 1)
        def _():
            out_ref[rows] = out_acc[...].astype(BF16)
            p_ref[rows, :width] = dx_acc[...].astype(BF16)
            high = gate_acc[...].astype(BF16).astype(F32)
            rest = gate_acc[...] - high
            p_ref[rows, width:] = (high + pltpu.roll(rest, experts, 1)).astype(BF16)
            mate_copy(order(s)).start()

            @pl.when(s + 1 < chips)
            def _():
                for copy in tiles(s + 1):
                    copy.start()

            @pl.when(s == chips - 1)
            def _():
                fetch = pltpu.make_async_copy(operands[1], dx_acc.at[pl.ds(own, own)], tile_sems.at[0])
                fetch.start()
                fetch.wait()
                mine = out_acc[pl.ds(pl.multiple_of(core * own, 8), own)]
                out_ref[block(here)] = (mine + dx_acc[pl.ds(own, own)]).astype(BF16)

        for (at, j), time in sorted(when.items(), key=lambda item: (item[1], abs(item[0][0] - item[0][1]))):

            @pl.when(jnp.logical_and(chip == at, k == time - 1))
            def _():
                pass_on(at, j)

        return carry

    lax.fori_loop(0, chips * subs, one_sub, 0)
    out_sums = wgu.at[:, pl.ds(0, tokens), pl.ds(0, layer_ref.shape[1])]
    operands[0] = g_buf.at[pl.ds(pl.multiple_of(core * own, 8), own)]
    operands[1] = dx_acc.at[pl.ds(own, own)]
    layer = reduce_steps(chips, 2, 1, out_ref, layer_ref, out_pair, out_line, out_sums, *out_sems)
    next(layer)
    next(layer)
    first = pl.ds(0, own)

    def add(total):
        dx_acc[first] += total[:, :width]
        gate_acc[first] += total[:, width:]

    total = pair_sum(chip)
    dx_acc[first] = total[:, :width]
    gate_acc[first] = total[:, width:]

    @pl.when(chip > 0)
    def _():
        line_copy(chip, chip, right_sem, mate).wait_recv()
        add(line_buf[chip].astype(F32))

    @pl.when(chip < chips - 1)
    def _():
        line_copy(chip, chips, left_sem, mate).wait_recv()
        add(line_buf[chips].astype(F32))

    for j in range(chips):
        mate_copy(j).wait_send()

        @pl.when(j > chip)
        def _():
            line_copy(j, j, right_sem, mate).wait_send()

        @pl.when(j < chip)
        def _():
            line_copy(j, j, left_sem, mate).wait_send()

    kept = turn_backward(experts, dx_acc[first], gate_acc[first], operands, results, o_ref, block(here))
    run(gather_rows_steps(chips, 2, o_ref, *gather_sems, lambda: turn_late(kept, operands, results)), layer)


def moe_turn(x, g, routes, operands, experts, gate_w, up_w, downs, results, chips, ident):
    tokens, width = g.shape
    wide = x.shape[1]
    lanes = wide - width
    own = tokens // (2 * chips)
    hidden = downs[0].shape[1] if len(downs) > 1 else min(256, gate_w.shape[2] // 4)
    steps = gate_w.shape[0] * gate_w.shape[2] // hidden
    subs = min(4, steps)
    whole = jax.ShapeDtypeStruct((tokens, width), BF16)
    part = width // (2 * chips)
    per_chip = pltpu.SemaphoreType.DMA((chips,))
    halves = pltpu.SemaphoreType.DMA((chips, 2))
    return pl.pallas_call(
        functools.partial(moe_turn_body, experts, chips, subs, len(downs)),
        out_shape=(jax.ShapeDtypeStruct((tokens, part), F32), whole) + tuple(results),
        in_specs=[ANY, ANY, VM, ANY] + [VM] * (len(operands) - 1) + [ANY] * (2 + len(downs)),
        out_specs=(VM,) * (2 + len(results)),
        scratch_shapes=[
            pltpu.VMEM((tokens, width), BF16),
            pltpu.VMEM((chips, tokens, part), BF16),
            pltpu.VMEM((chips + 1, tokens, part), BF16),
            pltpu.VMEM((tokens, wide), BF16),
            pltpu.VMEM((2 * own, width), F32),
            pltpu.VMEM((2 * own, width), F32),
            pltpu.VMEM((2 * own, lanes), F32),
            pltpu.VMEM((steps, width, 2 * hidden), BF16),
            pltpu.VMEM((steps, hidden, width), BF16),
            pltpu.VMEM((2 * own, wide), BF16),
            pltpu.VMEM((2 * own, width), BF16),
            pltpu.VMEM((chips, own, wide), BF16),
            pltpu.VMEM((chips + 1, own, wide), BF16),
            pltpu.VMEM((chips, own, wide), BF16),
            pltpu.SemaphoreType.DMA((steps, 3)),
            pltpu.SemaphoreType.DMA((2,)),
            per_chip,
            per_chip,
            per_chip,
            pltpu.SemaphoreType.DMA((chips + 1,)),
            per_chip,
        ]
        + [halves] * 8
        + [pltpu.SemaphoreType.DMA((chips + 1, 2)), halves],
        compiler_params=pltpu.CompilerParams(
            collective_id=ident, has_side_effects=True, vmem_limit_bytes=VMEM_MOST
        ),
        name="moe_turn",
    )(x, g, routes, *operands, gate_w, up_w, *downs)


def rope_tables(length, head_dim):
    half_dim = head_dim // 2
    frequency = rope_base ** (-(2.0 * jnp.arange(half_dim, dtype=F32)) / head_dim)
    angles = jnp.arange(length, dtype=F32)[:, None] * frequency[None, :]
    cosine, sine = jnp.cos(angles), jnp.sin(angles)
    return jnp.concatenate([cosine, cosine], axis=1), jnp.concatenate([-sine, sine], axis=1)


def shards(
    inputs,
    cotangent,
    norm_first,
    norm_second,
    query_gain,
    key_gain,
    w_query,
    w_key,
    w_value,
    w_out,
    w_router,
    w_gate,
    w_up,
    w_down,
    adapter_a,
    adapter_b,
    adapter_router,
    routes,
    prefix,
    adapter_index,
):
    seq_len, width_part = inputs.shape
    col_count = lax.axis_size("col")
    row_count = lax.axis_size("row")
    col_index = lax.axis_index("col")
    row_index = lax.axis_index("row")
    chips = col_count // 2
    full_width = width_part * col_count
    head_width = w_query.shape[1]
    local_experts = w_gate.shape[0]
    expert_total = w_router.shape[1]
    feature_start = col_index * width_part
    head_start = col_index * head_width
    own_rows = seq_len // col_count
    row_start = col_index * own_rows
    score_scale = HD ** (-0.5)
    reach = seq_len // 2
    lanes = 128

    def columns(array, axis_num):
        return lax.dynamic_slice_in_dim(array, feature_start, width_part, axis_num)

    def head_cols(array, axis_num=1):
        return lax.dynamic_slice_in_dim(array, head_start, head_width, axis_num)

    def held_rows(array):
        return lax.dynamic_slice_in_dim(array, row_start, own_rows, 0)

    def col_sum(pair, ident):
        return jnp.sum(small_gather(pair, col_count, ident), axis=0)

    full_gate = lax.all_gather(w_gate, "row", axis=2, tiled=True)
    full_up = lax.all_gather(w_up, "row", axis=2, tiled=True)
    across = row_count == 4 and local_experts == 2
    down_shares = w_down.reshape(SHARES, -1, full_width)
    riders = (cotangent, down_shares) if across else (cotangent,)
    adapter_slot = adapter_index[0]
    chosen_a = lax.dynamic_index_in_dim(adapter_a, adapter_slot, 1, keepdims=False).swapaxes(1, 2)
    chosen_b = lax.dynamic_index_in_dim(adapter_b, adapter_slot, 1, keepdims=False)
    chosen_router = lax.dynamic_index_in_dim(adapter_router, adapter_slot, 0, keepdims=False)
    rank = chosen_a.shape[1]
    a_three = chosen_a[:3].reshape(3 * rank, full_width)
    b_three = head_cols(chosen_b[:3].reshape(3 * rank, full_width))
    blank = jnp.zeros((rank, head_width), BF16)
    b_cols = jnp.concatenate(
        [
            jnp.concatenate([b_three[m * rank : (m + 1) * rank] if n == m else blank for n in range(3)], axis=0)
            for m in range(3)
        ],
        axis=1,
    )
    a_out = head_cols(chosen_a[3])
    out_map = (w_out.astype(F32) + tn(a_out, chosen_b[3])).astype(BF16)
    out_wide = jnp.concatenate([out_map, a_out.T, jnp.zeros((head_width, lanes - rank), BF16)], axis=1)
    router_rows = jnp.pad(w_router.T, ((0, lanes - expert_total), (0, 0)))
    router_up = jnp.pad(chosen_router, ((0, 0), (0, lanes - expert_total)))
    gains = jnp.stack([head_cols(query_gain, 0), head_cols(key_gain, 0)])
    tables = rope_tables(seq_len, HD)
    gain_first, gain_second = norm_first[None], norm_second[None]

    full_inputs, *down_first = line_gather(inputs, chips, 1, 0, rider=down_shares if across else None)
    proj, mid, inv_first, squares = project(
        full_inputs, gain_first, (w_query, w_key, w_value), a_three, b_cols
    )
    inv = lax.rsqrt(col_sum(squares, 1) / full_width + norm_eps).T
    part_out, attended, rot_query, rot_key, value_rows, log_totals = attend(
        prefix, proj, inv, gains, tables, out_wide, reach, score_scale
    )
    wide = full_width + lanes
    row_shape = jax.ShapeDtypeStruct
    normed_two, hidden_rows, mid_out, mid_router, probs, full_cot, *down_second = line_turn(
        part_out,
        (held_rows(full_inputs), gain_second, chosen_a[4], router_rows, router_up),
        wide,
        (
            row_shape((own_rows, full_width), F32),
            row_shape((own_rows, lanes), BF16),
            row_shape((own_rows, rank), BF16),
            row_shape((own_rows, lanes), F32),
        ),
        functools.partial(turn_forward, full_width, expert_total),
        lambda kept, operands, results: None,
        chips,
        2,
        riders,
    )
    if across:
        downs = (w_down,) + tuple(
            others.reshape(3, -1, full_width) for others in down_first + down_second
        )
    else:
        downs = (lax.all_gather(w_down, "row", axis=1, tiled=True),)

    layer_out, grad_attn, late, router_late = moe_turn(
        normed_two,
        full_cot,
        routes,
        (
            hidden_rows,
            gain_second,
            chosen_a[4],
            router_rows,
            router_up,
            probs,
            mid_router,
            mid_out,
        ),
        expert_total,
        full_gate,
        full_up,
        downs,
        (row_shape((2 * rank, full_width), F32), row_shape((rank, lanes), F32)),
        chips,
        7,
    )
    layer_out = layer_out.astype(BF16)

    held_adapters = adapter_a.shape[1] // row_count
    grad_inputs, grad_a, grad_b, grad_router = back(
        prefix,
        adapter_index,
        (
            grad_attn,
            out_map,
            chosen_b[3],
            attended,
            rot_query,
            rot_key,
            value_rows,
            log_totals,
            proj,
            gains,
            *tables,
            inv,
            b_cols,
            a_three,
            full_inputs,
            inv_first,
            gain_first,
            mid,
            late,
            router_late,
        ),
        (w_query, w_key, w_value),
        reach,
        score_scale,
        chips,
        row_count,
        held_adapters,
        12,
    )
    grad_a = grad_a.swapaxes(2, 3)
    grad_router = grad_router[:, :, :expert_total]
    return (layer_out, grad_inputs, grad_a, grad_b, grad_router)


def solution(mesh):
    placed = (
        P("row", "col"),
        P("row", "col"),
        P(),
        P(),
        P(),
        P(),
        P(None, "col"),
        P(None, "col"),
        P(None, "col"),
        P("col", None),
        P(),
        P("col", None, "row"),
        P("col", None, "row"),
        P("col", "row", None),
        P(),
        P(),
        P(),
        P("row", None),
        P("row"),
        P("row"),
    )
    return jax.shard_map(
        shards,
        mesh=mesh,
        in_specs=placed,
        out_specs=(
            P("row", "col"),
            P("row", "col"),
            P(None, "row", "col", None),
            P(None, "row", None, "col"),
            P("row", None, None),
        ),
        check_vma=False,
    )
```

```python
import functools

import jax
import jax.numpy as jnp
from jax import lax
from jax.experimental import pallas as pl
from jax.experimental.pallas import tpu as pltpu
from jax.sharding import PartitionSpec as P

HD = 128
F32, BF16 = jnp.float32, jnp.bfloat16
MESH_ID = pl.DeviceIdType.MESH
VM = pl.BlockSpec(memory_space=pltpu.VMEM)
ANY = pl.BlockSpec(memory_space=pl.ANY)
VMEM_LIMIT = 60 * 1024 * 1024
VMEM_MOST = 67_000_000
SHARES, FIRST_SHARE = 8, 2

norm_eps = 1e-05
rope_base = 10000.0
masked_score = -1e30


def nn(left, right):
    return jnp.dot(left, right, preferred_element_type=F32)


def nt(left, right):
    return lax.dot_general(left, right, (((1,), (1,)), ((), ())), preferred_element_type=F32)


def tn(left, right):
    return lax.dot_general(left, right, (((0,), (0,)), ((), ())), preferred_element_type=F32)


def remote(src, dst, send_sem, recv_sem, device):
    return pltpu.make_async_remote_copy(
        src_ref=src,
        dst_ref=dst,
        send_sem=send_sem,
        recv_sem=recv_sem,
        device_id={"col": device},
        device_id_type=MESH_ID,
    )


def line_place():
    here = lax.axis_index("col")
    core = here % 2
    return here, here // 2, core, here + 1 - 2 * core


def line_barrier(chips, across=()):
    here, chip, core, mate = line_place()
    barrier = pltpu.get_barrier_semaphore()
    has_left, has_right = chip > 0, chip < chips - 1
    for other in across:
        pl.semaphore_signal(barrier, inc=1, device_id={"row": other}, device_id_type=MESH_ID)
    pl.semaphore_signal(barrier, inc=1, device_id={"col": mate}, device_id_type=MESH_ID)

    @pl.when(has_left)
    def _():
        pl.semaphore_signal(barrier, inc=1, device_id={"col": here - 2}, device_id_type=MESH_ID)

    @pl.when(has_right)
    def _():
        pl.semaphore_signal(barrier, inc=1, device_id={"col": here + 2}, device_id_type=MESH_ID)

    inner = jnp.logical_and(has_left, has_right)

    @pl.when(inner)
    def _():
        pl.semaphore_wait(barrier, 3 + len(across))

    @pl.when(jnp.logical_not(inner))
    def _():
        pl.semaphore_wait(barrier, 2 + len(across))


def in_chunks(rows, size, body):
    def one(c, carry):
        body(pl.multiple_of(c * size, size))
        return carry

    lax.fori_loop(0, rows // size, one, 0)


def spot(axis, size, parts, block, part):
    rows, cols = size
    step = rows // parts
    if axis == 0:
        return (pl.ds(pl.multiple_of(block * rows + part * step, 8), step), slice(None))
    return (pl.ds(part * step, step), pl.ds(pl.multiple_of(block * cols, 128), cols))


def run(*steps):
    steps = list(steps)
    while steps:
        for one in list(steps):
            if next(one, steps) is steps:
                steps.remove(one)


def gather_body(chips, parts, axis, riders, x_ref, *refs):
    line_barrier(chips, row_partners() if riders else ())
    o_ref = refs[riders]
    sems = refs[2 * riders + 1 :]
    steps = [gather_steps(chips, parts, axis, x_ref, o_ref, *sems[:6])]
    if riders:
        steps.append(row_gather_steps(2, 0, refs[0], refs[2], *sems[6:]))
    run(*steps)


def gather_steps(chips, parts, axis, x_ref, o_ref, right_sem, left_sem, mate_sem, line_recv, mate_recv, own_sem):
    here, chip, core, mate = line_place()
    size = x_ref.shape
    step = size[0] // parts

    def at(block, part):
        return o_ref.at[spot(axis, size, parts, block, part)]

    def copy(j, part, sem, recv, device, first=False, block=None):
        block = 2 * j + core if block is None else block
        src = x_ref.at[pl.ds(part * step, step)] if first else at(block, part)
        return remote(src, at(block, part), sem.at[j, part], recv.at[j, part], device)

    def forward(j, part, rightward, leftward, first):
        if rightward:

            @pl.when(chip < chips - 1)
            def _():
                copy(j, part, right_sem, line_recv, here + 2, first).start()

        if leftward:

            @pl.when(chip > 0)
            def _():
                copy(j, part, left_sem, line_recv, here - 2, first).start()

        copy(j, part, mate_sem, mate_recv, mate, first).start()

    for part in range(parts):
        forward(chip, part, True, True, True)
    own = []
    for part in range(parts):
        own.append(
            pltpu.make_async_copy(x_ref.at[pl.ds(part * step, step)], at(here, part), own_sem.at[part])
        )
        own[-1].start()
    yield
    for far in range(1, chips):
        for part in range(parts):

            @pl.when(chip - far >= 0)
            def _():
                copy(chip - far, part, right_sem, line_recv, mate).wait_recv()
                forward(chip - far, part, True, False, False)

            @pl.when(chip + far < chips)
            def _():
                copy(chip + far, part, left_sem, line_recv, mate).wait_recv()
                forward(chip + far, part, False, True, False)

        yield

    for own_copy in own:
        own_copy.wait()
    for j in range(chips):
        for part in range(parts):
            copy(j, part, mate_sem, mate_recv, mate, block=2 * j + 1 - core).wait_recv()
            copy(j, part, mate_sem, mate_recv, mate).wait_send()

            @pl.when(jnp.logical_and(j <= chip, chip < chips - 1))
            def _():
                copy(j, part, right_sem, line_recv, here + 2).wait_send()

            @pl.when(jnp.logical_and(j >= chip, chip > 0))
            def _():
                copy(j, part, left_sem, line_recv, here - 2).wait_send()


def line_gather(x, chips, axis, ident, parts=2, rider=None):
    rows, cols = x.shape
    sems = pltpu.SemaphoreType.DMA((chips, parts))
    shape = (2 * chips * rows, cols) if axis == 0 else (rows, 2 * chips * cols)
    whole = jax.ShapeDtypeStruct(shape, x.dtype)
    more = () if rider is None else (rider,)
    ridden = tuple(jax.ShapeDtypeStruct((3, FIRST_SHARE) + one.shape[1:], one.dtype) for one in more)
    return pl.pallas_call(
        functools.partial(gather_body, chips, parts, axis, len(more)),
        out_shape=(whole,) + ridden,
        in_specs=[VM] + [ANY] * len(more),
        out_specs=(VM,) + (ANY,) * len(more),
        scratch_shapes=[sems] * 5
        + [pltpu.SemaphoreType.DMA((parts,))]
        + [pltpu.SemaphoreType.DMA((6,))] * (2 * len(more)),
        compiler_params=pltpu.CompilerParams(
            collective_id=ident, has_side_effects=True, vmem_limit_bytes=VMEM_LIMIT
        ),
        name="line_gather",
    )(x, *more)


def reduce_steps(
    chips, parts, axis, p_ref, o_ref, pair_buf, line_buf, sums, right_sem, left_sem, mate_sem, line_recv, mate_recv
):
    here, chip, core, mate = line_place()
    size = o_ref.shape
    step = size[0] // parts

    def rows(part):
        return pl.ds(part * step, step)

    def at(block, part):
        return spot(axis, size, parts, block, part)

    def mate_copy(j, part):
        return remote(
            p_ref.at[at(2 * j + 1 - core, part)],
            pair_buf.at[j, rows(part)],
            mate_sem.at[j, part],
            mate_recv.at[j, part],
            mate,
        )

    def line_copy(j, slot, part, sem, device):
        return remote(
            sums.at[j, rows(part)], line_buf.at[slot, rows(part)], sem.at[j, part], line_recv.at[slot, part], device
        )

    for far in range(chips - 1, -1, -1):
        for part in range(parts):

            @pl.when(chip + far < chips)
            def _():
                mate_copy(chip + far, part).start()

            if far > 0:

                @pl.when(chip - far >= 0)
                def _():
                    mate_copy(chip - far, part).start()

    yield

    chunk = 16 if axis == 0 else 64

    def pair_sum(j, part, low):
        block = 2 * j + core
        if axis == 0:
            where = (pl.ds(pl.multiple_of(block * size[0] + part * step + low, 16), chunk), slice(None))
        else:
            cols = pl.ds(pl.multiple_of(block * size[1], 128), size[1])
            where = (pl.ds(pl.multiple_of(part * step + low, 16), chunk), cols)
        return p_ref[where].astype(F32) + pair_buf[j, chunk_rows(part, low)].astype(F32)

    def chunk_rows(part, low):
        return pl.ds(pl.multiple_of(part * step + low, 16), chunk)

    def pass_on(j, slot, part, more, sem, device):
        mate_copy(j, part).wait_recv()

        @pl.when(more)
        def _():
            line_copy(j, j, part, sem, mate).wait_recv()

            def add_up(low):
                total = pair_sum(j, part, low) + line_buf[j, chunk_rows(part, low)].astype(F32)
                sums[j, chunk_rows(part, low)] = total.astype(BF16)

            in_chunks(step, chunk, add_up)

        @pl.when(jnp.logical_not(more))
        def _():
            def add_up(low):
                sums[j, chunk_rows(part, low)] = pair_sum(j, part, low).astype(BF16)

            in_chunks(step, chunk, add_up)

        line_copy(j, slot, part, sem, device).start()

    for far in range(chips - 1, 0, -1):
        for part in range(parts):

            @pl.when(chip + far < chips)
            def _():
                pass_on(chip + far, chip + far, part, chip > 0, right_sem, here + 2)

            @pl.when(chip - far >= 0)
            def _():
                pass_on(
                    chip - far, chips if far == 1 else chip - far, part, chip < chips - 1, left_sem, here - 2
                )

        yield

    for part in range(parts):
        mate_copy(chip, part).wait_recv()

        def begin(low):
            o_ref[chunk_rows(part, low)] = pair_sum(chip, part, low)

        in_chunks(step, chunk, begin)

        def add_line(slot):
            def add_up(low):
                o_ref[chunk_rows(part, low)] += line_buf[slot, chunk_rows(part, low)].astype(F32)

            in_chunks(step, chunk, add_up)

        @pl.when(chip > 0)
        def _():
            line_copy(chip, chip, part, right_sem, mate).wait_recv()
            add_line(chip)

        @pl.when(chip < chips - 1)
        def _():
            line_copy(chip, chips, part, left_sem, mate).wait_recv()
            add_line(chips)

    for j in range(chips):
        for part in range(parts):
            mate_copy(j, part).wait_send()

            @pl.when(j > chip)
            def _():
                line_copy(j, j, part, right_sem, mate).wait_send()

            @pl.when(j < chip)
            def _():
                line_copy(j, j, part, left_sem, mate).wait_send()


def small_body(count, x_ref, o_ref, send_sem, recv_sem):
    here = lax.axis_index("col")
    barrier = pltpu.get_barrier_semaphore()
    for hop in range(1, count):
        other = lax.rem(here + hop, count)
        pl.semaphore_signal(barrier, inc=1, device_id={"col": other}, device_id_type=MESH_ID)
    o_ref[here] = x_ref[...]
    pl.semaphore_wait(barrier, count - 1)

    def copy(hop, block):
        other = lax.rem(here + hop, count)
        return remote(x_ref, o_ref.at[block], send_sem.at[hop], recv_sem.at[hop], other)

    for hop in range(1, count):
        copy(hop, here).start()
    for hop in range(1, count):
        copy(hop, lax.rem(here + count - hop, count)).wait_recv()
    for hop in range(1, count):
        copy(hop, here).wait_send()


def small_gather(x, count, ident):
    sems = pltpu.SemaphoreType.DMA((count,))
    return pl.pallas_call(
        functools.partial(small_body, count),
        out_shape=jax.ShapeDtypeStruct((count,) + x.shape, x.dtype),
        in_specs=[VM],
        out_specs=VM,
        scratch_shapes=[sems, sems],
        compiler_params=pltpu.CompilerParams(collective_id=ident, has_side_effects=True),
        name="small_gather",
    )(x)


def row_copy(src, dst, sems, which, device):
    return pltpu.make_async_remote_copy(
        src_ref=src,
        dst_ref=dst,
        send_sem=sems[0].at[which],
        recv_sem=sems[1].at[which],
        device_id={"row": device},
        device_id_type=MESH_ID,
    )


def row_partners():
    here = lax.axis_index("row")
    major, minor = here // 2, here % 2
    return 2 * major + 1 - minor, 2 * (1 - major) + minor


def row_gather_steps(pauses, begin, x_ref, o_ref, *sems):
    near, next_one = row_partners()
    half = o_ref.shape[1] // 2

    def side(neighbour, first):
        slot, device = (0, near) if neighbour == 0 else (1, next_one)
        rows = pl.ds(first * half, half)
        source = x_ref.at[pl.ds(begin + first * half, half)]
        return row_copy(source, o_ref.at[slot, rows], sems, 2 * slot + first, device)

    def onward(neighbour):
        slot, device = (0, next_one) if neighbour == 0 else (1, near)
        rows = pl.ds(slot * half, half)
        return row_copy(o_ref.at[slot, rows], o_ref.at[2, rows], sems, 4 + slot, device)

    side(0, 0).start()
    side(1, 1).start()
    side(0, 1).start()
    side(1, 0).start()
    for _ in range(pauses):
        yield
    side(0, 0).wait_recv()
    onward(0).start()
    side(1, 1).wait_recv()
    onward(1).start()
    yield
    for neighbour in range(2):
        side(neighbour, 1 - neighbour).wait_recv()
        onward(neighbour).wait_recv()
        onward(neighbour).wait_send()
        side(neighbour, 0).wait_send()
        side(neighbour, 1).wait_send()


def turn_body(chips, parts, first, last, held, late_count, riders, *refs):
    refs = list(refs)

    def take(count):
        taken = refs[:count]
        del refs[:count]
        return taken

    (p_ref,) = take(1)
    operands = take(held)
    rider_in = take(riders)
    (o_ref,) = take(1)
    results = take(late_count)
    rider_out = take(riders)
    sums_in, pair_buf, line_buf, sums = take(4)
    reduce_sems = take(5)
    gather_sems = take(5)
    line_barrier(chips, row_partners() if riders > 1 else ())
    steps = [reduce_steps(chips, parts, 0, p_ref, sums_in, pair_buf, line_buf, sums, *reduce_sems)]
    if riders > 0:
        steps.append(gather_steps(chips, 2, 1, rider_in[0], rider_out[0], *take(6)))
    if riders > 1:
        across = row_gather_steps(1, FIRST_SHARE, rider_in[1], rider_out[1], *take(2))
        next(across)
    run(*steps)
    here = lax.axis_index("col")
    own = o_ref.shape[0] // (2 * chips)
    kept = first(sums_in, operands, results, o_ref, pl.ds(pl.multiple_of(here * own, 8), own))

    def beside():
        if riders > 1:
            next(across)
        last(kept, operands, results)

    run(gather_rows_steps(chips, parts, o_ref, *gather_sems, beside))
    if riders > 1:
        run(across)


def gather_rows_steps(chips, parts, o_ref, right_sem, left_sem, mate_sem, line_recv, mate_recv, beside):
    here, chip, core, mate = line_place()
    size = (o_ref.shape[0] // (2 * chips), o_ref.shape[1])

    def copy(j, part, sem, recv, device, block=None):
        block = 2 * j + core if block is None else block
        ref = o_ref.at[spot(0, size, parts, block, part)]
        return remote(ref, ref, sem.at[j, part], recv.at[j, part], device)

    def forward(j, part, rightward, leftward):
        if rightward:

            @pl.when(chip < chips - 1)
            def _():
                copy(j, part, right_sem, line_recv, here + 2).start()

        if leftward:

            @pl.when(chip > 0)
            def _():
                copy(j, part, left_sem, line_recv, here - 2).start()

        copy(j, part, mate_sem, mate_recv, mate).start()

    for part in range(parts):
        forward(chip, part, True, True)
    beside()
    yield
    for far in range(1, chips):
        for part in range(parts):

            @pl.when(chip - far >= 0)
            def _():
                copy(chip - far, part, right_sem, line_recv, mate).wait_recv()
                forward(chip - far, part, True, False)

            @pl.when(chip + far < chips)
            def _():
                copy(chip + far, part, left_sem, line_recv, mate).wait_recv()
                forward(chip + far, part, False, True)

        yield

    for j in range(chips):
        for part in range(parts):
            copy(j, part, mate_sem, mate_recv, mate, block=2 * j + 1 - core).wait_recv()
            copy(j, part, mate_sem, mate_recv, mate).wait_send()

            @pl.when(jnp.logical_and(j <= chip, chip < chips - 1))
            def _():
                copy(j, part, right_sem, line_recv, here + 2).wait_send()

            @pl.when(jnp.logical_and(j >= chip, chip > 0))
            def _():
                copy(j, part, left_sem, line_recv, here - 2).wait_send()


def line_turn(p, operands, width, results, first, last, chips, ident, riders=(), parts=2):
    rows, cols = p.shape
    own = rows // (2 * chips)
    sems = pltpu.SemaphoreType.DMA((chips, parts))
    longer = pltpu.SemaphoreType.DMA((chips + 1, parts))
    more = []
    ridden = []
    if len(riders) > 0:
        height, part = riders[0].shape
        ridden.append(jax.ShapeDtypeStruct((height, 2 * chips * part), BF16))
        more += [pltpu.SemaphoreType.DMA((chips, 2))] * 5 + [pltpu.SemaphoreType.DMA((2,))]
    if len(riders) > 1:
        ridden.append(jax.ShapeDtypeStruct((3, SHARES - FIRST_SHARE) + riders[1].shape[1:], BF16))
        more += [pltpu.SemaphoreType.DMA((6,))] * 2
    return pl.pallas_call(
        functools.partial(turn_body, chips, parts, first, last, len(operands), len(results), len(riders)),
        out_shape=(jax.ShapeDtypeStruct((rows, width), BF16),) + tuple(results) + tuple(ridden),
        in_specs=[VM] * (1 + len(operands)) + [VM, ANY][: len(riders)],
        out_specs=(VM,) * (1 + len(results)) + (VM, ANY)[: len(riders)],
        scratch_shapes=[
            pltpu.VMEM((own, cols), F32),
            pltpu.VMEM((chips, own, cols), BF16),
            pltpu.VMEM((chips + 1, own, cols), BF16),
            pltpu.VMEM((chips, own, cols), BF16),
            sems,
            sems,
            sems,
            longer,
            sems,
        ]
        + [sems] * 5
        + more,
        compiler_params=pltpu.CompilerParams(
            collective_id=ident, has_side_effects=True, vmem_limit_bytes=VMEM_LIMIT
        ),
        name="line_turn",
    )(p, *operands, *riders)


def inverse_rms(values):
    return lax.rsqrt(jnp.mean(values * values, axis=1, keepdims=True) + norm_eps)


def turn_forward(width, experts, sums, operands, results, o_ref, own):
    x_ref, gain_ref, a_ref, router_ref, up_ref = operands
    hidden_ref, mid_ref, mid_router_ref, probs_ref = results
    hidden = x_ref[...].astype(F32) + sums[:, :width]
    mid_ref[...] = sums[:, width:].astype(BF16)
    hidden_ref[...] = hidden
    normed = (hidden * inverse_rms(hidden) * gain_ref[...]).astype(BF16)
    o_ref[own, :width] = normed
    mid_router = nt(normed, a_ref[...]).astype(BF16)
    mid_router_ref[...] = mid_router
    logits = nt(normed, router_ref[...]) + nn(mid_router, up_ref[...])
    lane = lax.broadcasted_iota(jnp.int32, logits.shape, 1)
    logits = jnp.where(lane < experts, logits, masked_score)
    exponent = jnp.exp(logits - jnp.max(logits, axis=1, keepdims=True))
    probs = exponent / jnp.sum(exponent, axis=1, keepdims=True)
    probs_ref[...] = probs
    high = probs.astype(BF16)
    rest = probs - high.astype(F32)
    o_ref[own, width:] = (high.astype(F32) + pltpu.roll(rest, experts, 1)).astype(BF16)
    return None


def turn_backward(experts, grads, pair, operands, results, o_ref, own):
    g_ref, hidden_ref, gain_ref, a_ref, router_ref, up_ref, probs_ref, mid_router_ref, mid_ref = operands
    lanes = pair.shape[1]
    grad_probs = pair + pltpu.roll(pair, lanes - experts, 1)
    probs = probs_ref[...]
    grad_logits = (probs * (grad_probs - jnp.sum(probs * grad_probs, axis=1, keepdims=True))).astype(BF16)
    grad_mid = nt(grad_logits, up_ref[...]).astype(BF16)
    grad_normed = grads + nn(grad_logits, router_ref[...]) + nn(grad_mid, a_ref[...])
    hidden = hidden_ref[...]
    inv = inverse_rms(hidden)
    scaled = grad_normed * gain_ref[...]
    grad_hidden = (
        g_ref[...].astype(F32)
        + inv * scaled
        - hidden * (inv * inv * inv * jnp.mean(hidden * scaled, axis=1, keepdims=True))
    )
    grad_hidden = grad_hidden.astype(BF16)
    o_ref[own, :] = grad_hidden
    return grad_logits, grad_mid, grad_hidden


def turn_late(kept, operands, results):
    _, hidden_ref, gain_ref, _, _, _, _, mid_router_ref, mid_ref = operands
    grad_logits, grad_mid, grad_hidden = kept
    hidden = hidden_ref[...]
    normed = (hidden * inverse_rms(hidden) * gain_ref[...]).astype(BF16)
    rank = grad_mid.shape[1]
    late_ref, router_ref = results
    late_ref[pl.ds(0, rank)] = tn(grad_mid, normed)
    late_ref[pl.ds(rank, rank)] = tn(mid_ref[:, :rank], grad_hidden)
    router_ref[...] = tn(mid_router_ref[...], grad_logits)


def row_sums(values):
    lanes = 128
    values = sum(values[:, n : n + lanes] for n in range(0, values.shape[1], lanes))
    high = values.astype(BF16)
    rest = (values - high.astype(F32)).astype(BF16)
    ones = jnp.ones((8, values.shape[1]), BF16)
    return nt(ones, high) + nt(ones, rest)


def project_body(tile, x_ref, gain_ref, wq, wk, wv, a_ref, b_ref, proj_ref, mid_ref, inv_ref, sq_ref):
    part = wq.shape[1]
    def one_tile(t, carry):
        rows = pl.ds(pl.multiple_of(t * tile, tile), tile)
        x = x_ref[rows].astype(F32)
        inv = inverse_rms(x)
        inv_ref[rows] = inv
        normed = (x * inv * gain_ref[...]).astype(BF16)
        mid = nt(normed, a_ref[...]).astype(BF16)
        mid_ref[rows] = mid
        for m, w in enumerate((wq, wk, wv)):
            cols = pl.ds(m * part, part)
            proj = nn(normed, w[...]) + nn(mid, b_ref[:, cols])
            proj_ref[rows, cols] = proj
            if m < 2:
                sq_ref[pl.ds(m, 1), rows] = row_sums(proj * proj)[0:1]
        return carry

    lax.fori_loop(0, x_ref.shape[0] // tile, one_tile, 0)


def project(x, gain, weights, a_rows, b_cols):
    seq_len, width = x.shape
    part = weights[0].shape[1]
    rank = a_rows.shape[0]
    return pl.pallas_call(
        functools.partial(project_body, min(256, seq_len)),
        out_shape=(
            jax.ShapeDtypeStruct((seq_len, 3 * part), F32),
            jax.ShapeDtypeStruct((seq_len, rank), BF16),
            jax.ShapeDtypeStruct((seq_len, 1), F32),
            jax.ShapeDtypeStruct((2, seq_len), F32),
        ),
        in_specs=[VM] * 7,
        out_specs=(VM,) * 4,
        compiler_params=pltpu.CompilerParams(vmem_limit_bytes=VMEM_LIMIT),
        name="project",
    )(x, gain, *weights, a_rows, b_cols)


def key_limit(start, tile, seq_len, reach):
    return min(seq_len, max(start + tile, reach))


def allowed_keys(start, tile, limit, prefix_len):
    query = start + lax.broadcasted_iota(jnp.int32, (tile, limit), 0)
    key = lax.broadcasted_iota(jnp.int32, (tile, limit), 1)
    return jnp.logical_or(key <= query, key < prefix_len)


def attend_body(
    tile, reach, scale, prefix_ref, proj_ref, inv_ref, gains_ref, cos_ref, sin_ref, map_ref,
    p_ref, att_ref, q_ref, k_ref, v_ref, log_ref,
):
    seq_len, part = att_ref.shape
    prefix_len = prefix_ref[0]

    def one_tile(t, carry):
        rows = pl.ds(pl.multiple_of(t * tile, tile), tile)
        for h in range(part // HD):
            cols = pl.ds(h * HD, HD)
            for m, ref in ((0, q_ref), (1, k_ref)):
                plain = proj_ref[rows, pl.ds(m * part + h * HD, HD)] * inv_ref[rows, m : m + 1]
                plain = plain * gains_ref[m : m + 1, cols]
                ref[rows, cols] = (plain * cos_ref[rows] + pltpu.roll(plain, HD // 2, 1) * sin_ref[rows]).astype(BF16)
            v_ref[rows, cols] = proj_ref[rows, pl.ds(2 * part + h * HD, HD)].astype(BF16)
        return carry

    lax.fori_loop(0, seq_len // tile, one_tile, 0)
    for start in range(0, seq_len, tile):
        rows = pl.ds(start, tile)
        limit = key_limit(start, tile, seq_len, reach)
        allowed = allowed_keys(start, tile, limit, prefix_len)
        for h in range(part // HD):
            cols = pl.ds(h * HD, HD)
            scores = nt(q_ref[rows, cols], k_ref[pl.ds(0, limit), cols]) * scale
            scores = jnp.where(allowed, scores, masked_score)
            top = jnp.max(scores, axis=1, keepdims=True)
            exponent = jnp.exp(scores - top)
            total = jnp.sum(exponent, axis=1, keepdims=True)
            weights = (exponent / total).astype(BF16)
            att_ref[rows, cols] = nn(weights, v_ref[pl.ds(0, limit), cols]).astype(BF16)
            log_ref[rows, h : h + 1] = top + jnp.log(total)
        p_ref[rows] = nn(att_ref[rows], map_ref[...]).astype(BF16)


def attend(prefix, proj, inv, gains, tables, out_map, reach, scale):
    seq_len = proj.shape[0]
    part = proj.shape[1] // 3
    heads = jax.ShapeDtypeStruct((seq_len, part), BF16)
    return pl.pallas_call(
        functools.partial(attend_body, min(256, seq_len), reach, scale),
        out_shape=(
            jax.ShapeDtypeStruct((seq_len, out_map.shape[1]), BF16),
            heads,
            heads,
            heads,
            heads,
            jax.ShapeDtypeStruct((seq_len, part // HD), F32),
        ),
        in_specs=[pl.BlockSpec(memory_space=pltpu.SMEM)] + [VM] * 6,
        out_specs=(VM,) * 6,
        compiler_params=pltpu.CompilerParams(vmem_limit_bytes=VMEM_LIMIT),
        name="attend",
    )(prefix, proj, inv, gains, *tables, out_map)


def attend_back(
    tile, reach, scale, prefix_ref, g_ref, map_ref, b_ref, att_ref, q_ref, k_ref, v_ref, log_ref, proj_ref,
    gains_ref, cos_ref, sin_ref, scaled_ref, dv_ref, stat_ref, ga_ref, da_ref, dq_acc, dk_acc, dv_acc,
):
    seq_len, part = att_ref.shape
    prefix_len = prefix_ref[0]
    grad_a = jnp.zeros(ga_ref.shape, F32)

    def first_tile(t, grad_a):
        rows = pl.ds(pl.multiple_of(t * tile, tile), tile)
        grads = g_ref[rows]
        da_ref[rows] = nt(grads, map_ref[...]).astype(BF16)
        grad_mid = nt(grads, b_ref[...]).astype(BF16)
        return grad_a + tn(grad_mid, att_ref[rows])

    ga_ref[...] = lax.fori_loop(0, seq_len // tile, first_tile, grad_a)
    dk_acc[...] = jnp.zeros_like(dk_acc)
    dv_acc[...] = jnp.zeros_like(dv_acc)
    for start in range(0, seq_len, tile):
        rows = pl.ds(start, tile)
        limit = key_limit(start, tile, seq_len, reach)
        keys = pl.ds(0, limit)
        allowed = allowed_keys(start, tile, limit, prefix_len)
        for h in range(part // HD):
            cols = pl.ds(h * HD, HD)
            query, key = q_ref[rows, cols], k_ref[keys, cols]
            grads = da_ref[rows, cols]
            scores = jnp.where(allowed, nt(query, key) * scale, masked_score)
            weights = jnp.exp(scores - log_ref[rows, h : h + 1])
            grad_weights = nt(grads, v_ref[keys, cols])
            dot = jnp.sum(weights * grad_weights, axis=1, keepdims=True)
            grad_scores = (weights * (grad_weights - dot)).astype(BF16)
            dq_acc[rows, cols] = nn(grad_scores, key) * scale
            dk_acc[keys, cols] += tn(grad_scores, query) * scale
            dv_acc[keys, cols] += tn(weights.astype(BF16), grads)
    dv_ref[...] = dv_acc[...].astype(BF16)
    for m, acc in ((0, dq_acc), (1, dk_acc)):

        def turn_back(t, carry):
            rows = pl.ds(pl.multiple_of(t * tile, tile), tile)
            total = jnp.zeros((8, tile), F32)
            for h in range(part // HD):
                cols = pl.ds(h * HD, HD)
                here = pl.ds(m * part + h * HD, HD)
                plain = acc[rows, cols]
                turned = plain * cos_ref[rows] - pltpu.roll(plain, HD // 2, 1) * sin_ref[rows]
                scaled = turned * gains_ref[m : m + 1, cols]
                scaled_ref[rows, here] = scaled
                total += row_sums(proj_ref[rows, here] * scaled)
            stat_ref[pl.ds(m, 1), rows] = total[0:1]
            return carry

        lax.fori_loop(0, seq_len // tile, turn_back, 0)


def back_body(tile, reach, scale, chips, row_count, extra, prefix_ref, slot_ref, *refs):
    refs = list(refs)

    def take(number):
        taken = refs[:number]
        del refs[:number]
        return taken

    g_ref, map_ref, bo_ref, att_ref, q_ref, k_ref, v_ref, log_ref, proj_ref, gains_ref, cos_ref, sin_ref = take(12)
    inv_ref, b_ref, a_ref, x_ref, inv1_ref, gain_ref, mid_ref, late_ref, router_ref = take(9)
    weights = take(3)
    gi_ref, held_a, held_b, held_router = take(4)
    scaled_ref, dv_ref, stat_ref, stats_ref, ga_ref, da_ref, dq_acc, dk_acc, dv_acc = take(9)
    w_ref, d_ref, middle_ref, p_ref, o_ref, pair_buf, line_buf, sums, flat_ref, every_ref = take(10)
    w_sems, stat_send, stat_recv, row_send, row_recv = take(5)
    right_sem, left_sem, mate_sem, line_recv, mate_recv = take(5)
    here, chip, core, mate = line_place()
    row = lax.axis_index("row")
    count = 2 * chips
    seq_len, width = x_ref.shape
    part = dv_ref.shape[1]
    ranks = a_ref.shape[0]
    rank = ranks // 3
    parts = 2

    fetches = [
        pltpu.make_async_copy(w, w_ref.at[:, pl.ds(m * part, part)], w_sems.at[m]) for m, w in enumerate(weights)
    ]
    for fetch in fetches:
        fetch.start()
    barrier = pltpu.get_barrier_semaphore()
    for hop in range(1, count):
        other = lax.rem(here + hop, count)
        pl.semaphore_signal(barrier, inc=1, device_id={"col": other}, device_id_type=MESH_ID)
    for hop in range(1, row_count):
        other = lax.rem(row + hop, row_count)
        pl.semaphore_signal(barrier, inc=1, device_id={"row": other}, device_id_type=MESH_ID)
    attend_back(
        tile, reach, scale, prefix_ref, g_ref, map_ref, bo_ref, att_ref, q_ref, k_ref, v_ref, log_ref, proj_ref,
        gains_ref, cos_ref, sin_ref, scaled_ref, dv_ref, stat_ref, ga_ref, da_ref, dq_acc, dk_acc, dv_acc,
    )
    pl.semaphore_wait(barrier, count + row_count - 2)

    def stat_copy(hop, block):
        other = lax.rem(here + hop, count)
        return remote(stat_ref, stats_ref.at[block], stat_send.at[hop], stat_recv.at[hop], other)

    for hop in range(1, count):
        stat_copy(hop, here).start()
    stats_ref[here] = stat_ref[...]
    for hop in range(1, count):
        stat_copy(hop, lax.rem(here + count - hop, count)).wait_recv()
    total = stats_ref[0]
    for n in range(1, count):
        total = total + stats_ref[n]
    stats_ref[0] = total * (1.0 / width)

    grad_b = jnp.zeros((ranks, 3 * part), F32)
    first_stats = jnp.zeros((8, part), F32)
    line = lax.broadcasted_iota(jnp.int32, (8, part), 0)

    def grads_tile(t, carry):
        grad_b, first_stats = carry
        rows = pl.ds(pl.multiple_of(t * tile, tile), tile)
        upright = jnp.transpose(jnp.concatenate([stats_ref[0, :, rows], jnp.zeros((6, tile), F32)], axis=0))
        products = jnp.zeros((tile, part), F32)
        for m in range(3):
            cols = pl.ds(m * part, part)
            if m < 2:
                inv = inv_ref[rows, m : m + 1]
                shift = inv * inv * inv * upright[:, m : m + 1]
                grad = (inv * scaled_ref[rows, cols] - proj_ref[rows, cols] * shift).astype(BF16)
            else:
                grad = dv_ref[rows]
            d_ref[rows, cols] = grad
            products += grad.astype(F32) * proj_ref[rows, cols]
        grads = d_ref[rows]
        middle_ref[rows] = nt(grads, b_ref[...]).astype(BF16)
        grad_b += tn(mid_ref[rows], grads)
        first = row_sums(products / inv1_ref[rows])
        for j in range(tile // part):
            first_stats = jnp.where(
                line == (t * tile) // part + j, first[:, j * part : (j + 1) * part], first_stats
            )
        return grad_b, first_stats

    grad_b, first_stats = lax.fori_loop(0, seq_len // tile, grads_tile, (grad_b, first_stats))
    high = first_stats.astype(BF16).astype(F32)
    router = router_ref[...]
    if part > router.shape[1]:
        router = jnp.concatenate([router, jnp.zeros((rank, part - router.shape[1]), F32)], axis=1)
    common = jnp.concatenate([router, high, first_stats - high], axis=0).astype(BF16)
    common = jnp.concatenate([common] * count, axis=1)
    p_ref[pl.ds(ranks, 2 * rank)] = late_ref[...].astype(BF16)
    p_ref[pl.ds(ranks + 2 * rank, rank + 16)] = common
    used = ranks + 3 * rank + 16
    p_ref[pl.ds(used, extra - used)] = jnp.zeros((extra - used, width), BF16)
    for fetch in fetches:
        fetch.wait()

    size = o_ref.shape
    step = size[0] // parts

    def rows_of(piece):
        return pl.ds(piece * step, step)

    def at(block, piece):
        return spot(1, size, parts, block, piece)

    def mate_copy(j, piece):
        return remote(
            p_ref.at[at(2 * j + 1 - core, piece)],
            pair_buf.at[j, rows_of(piece)],
            mate_sem.at[j, piece],
            mate_recv.at[j, piece],
            mate,
        )

    def line_copy(j, slot, piece, sem, device):
        return remote(
            sums.at[j, rows_of(piece)],
            line_buf.at[slot, rows_of(piece)],
            sem.at[j, piece],
            line_recv.at[slot, piece],
            device,
        )

    def order(s):
        right = chips - 1 - chip
        return jnp.where(s < right, chips - 1 - s, jnp.where(s < chips - 1, s - right, chip))

    def work_out(s):
        cols = pl.ds(pl.multiple_of(order(s) * (2 * part), 128), 2 * part)
        gain = gain_ref[:, cols]
        spread = a_ref[:, cols]
        chunk = w_ref[cols]

        def one_tile(t, grad_a):
            rows = pl.ds(pl.multiple_of(t * tile, tile), tile)
            middle = middle_ref[rows]
            normed_part = nt(d_ref[rows], chunk) + nn(middle, spread)
            p_ref[pl.ds(pl.multiple_of(extra + t * tile, 16), tile), cols] = normed_part.astype(BF16)
            normed = (x_ref[rows, cols].astype(F32) * inv1_ref[rows] * gain).astype(BF16)
            return grad_a + tn(middle, normed)

        grad_a = lax.fori_loop(0, seq_len // tile, one_tile, jnp.zeros((ranks, 2 * part), F32))
        p_ref[pl.ds(0, ranks), cols] = grad_a.astype(BF16)
        for piece in range(parts):
            mate_copy(order(s), piece).start()

    chunk = 64

    def chunk_rows(piece, low):
        return pl.ds(pl.multiple_of(piece * step + low, 16), chunk)

    def pair_sum(j, piece, low):
        cols = pl.ds(pl.multiple_of((2 * j + core) * part, 128), part)
        rows = chunk_rows(piece, low)
        return p_ref[rows, cols].astype(F32) + pair_buf[j, rows].astype(F32)

    def pair_up(j, piece):
        mate_copy(j, piece).wait_recv()

        def add_up(low):
            sums[j, chunk_rows(piece, low)] = pair_sum(j, piece, low).astype(BF16)

        in_chunks(step, chunk, add_up)

    def one_block(s, carry):
        work_out(s)

        @pl.when(jnp.logical_and(chip == 0, s > 0))
        def _():
            for piece in range(parts):
                j = order(s - 1)
                pair_up(j, piece)
                line_copy(j, j, piece, right_sem, here + 2).start()

        @pl.when(jnp.logical_and(chip == chips - 1, s > 0))
        def _():
            for piece in range(parts):
                j = order(s - 1)
                pair_up(j, piece)

                @pl.when(j == chips - 2)
                def _():
                    line_copy(j, chips, piece, left_sem, here - 2).start()

                @pl.when(j < chips - 2)
                def _():
                    line_copy(j, j, piece, left_sem, here - 2).start()

        return carry

    lax.fori_loop(0, chips, one_block, 0)
    inner = jnp.logical_and(chip > 0, chip < chips - 1)

    def pass_on(j, slot, piece, sem, device):
        line_copy(j, j, piece, sem, mate).wait_recv()
        mate_copy(j, piece).wait_recv()

        def add_up(low):
            rows = chunk_rows(piece, low)
            sums[j, rows] = (pair_sum(j, piece, low) + line_buf[j, rows].astype(F32)).astype(BF16)

        in_chunks(step, chunk, add_up)
        line_copy(j, slot, piece, sem, device).start()

    for far in range(chips - 2, 0, -1):
        for piece in range(parts):

            @pl.when(jnp.logical_and(inner, chip + far < chips))
            def _():
                pass_on(chip + far, chip + far, piece, right_sem, here + 2)

            @pl.when(jnp.logical_and(inner, chip - far >= 0))
            def _():
                pass_on(chip - far, chips if far == 1 else chip - far, piece, left_sem, here - 2)

    def row_copy(hop, block):
        other = lax.rem(row + hop, row_count)
        return pltpu.make_async_remote_copy(
            src_ref=flat_ref,
            dst_ref=every_ref.at[block],
            send_sem=row_send.at[hop],
            recv_sem=row_recv.at[hop],
            device_id={"row": other},
            device_id_type=MESH_ID,
        )

    for piece in range(parts):
        mate_copy(chip, piece).wait_recv()

        def begin(low):
            o_ref[chunk_rows(piece, low)] = pair_sum(chip, piece, low)

        in_chunks(step, chunk, begin)

        def add_line(slot):
            def add_up(low):
                o_ref[chunk_rows(piece, low)] += line_buf[slot, chunk_rows(piece, low)].astype(F32)

            in_chunks(step, chunk, add_up)

        @pl.when(chip > 0)
        def _():
            line_copy(chip, chip, piece, right_sem, mate).wait_recv()
            add_line(chip)

        @pl.when(chip < chips - 1)
        def _():
            line_copy(chip, chips, piece, left_sem, mate).wait_recv()
            add_line(chips)

        if piece == 0:
            flat_ref[pl.ds(0, 6 * rank)] = o_ref[pl.ds(0, 6 * rank)].astype(BF16)
            flat_ref[pl.ds(6 * rank, rank)] = ga_ref[...].astype(BF16)
            for m in range(3):
                flat_ref[pl.ds((7 + m) * rank, rank)] = grad_b[
                    m * rank : (m + 1) * rank, m * part : (m + 1) * part
                ].astype(BF16)
            owner = jnp.full((16, part), slot_ref[0].astype(F32), F32)
            flat_ref[pl.ds(10 * rank, 16)] = owner.astype(BF16)
            for hop in range(1, row_count):
                row_copy(hop, row).start()
            every_ref[row] = flat_ref[...]

    stat_rows = o_ref[pl.ds(ranks + 3 * rank, 8)] + o_ref[pl.ds(ranks + 3 * rank + 8, 8)]
    upright = jnp.transpose(stat_rows)
    own = pl.ds(pl.multiple_of(here * part, 128), part)
    gain = gain_ref[:, own]
    for t in range(seq_len // part):
        rows = pl.ds(t * part, part)
        inv = inv1_ref[rows]
        pull = inv * inv * inv * upright[:, t : t + 1] * (1.0 / width)
        gi_ref[rows] = (
            g_ref[rows, own].astype(F32)
            + inv * gain * o_ref[pl.ds(extra + t * part, part)]
            - x_ref[rows, own].astype(F32) * pull
        )
    for hop in range(1, row_count):
        row_copy(hop, lax.rem(row + row_count - hop, row_count)).wait_recv()
    held = held_router.shape[0]
    for h in range(held):
        chosen = (row * held + h).astype(F32)
        picked = jnp.zeros((10 * rank, part), F32)
        for r in range(row_count):
            owner = every_ref[r, pl.ds(10 * rank, 16)].astype(F32)[0:1]
            picked += jnp.where(owner == chosen, every_ref[r, pl.ds(0, 10 * rank)].astype(F32), 0.0)
        for n, piece in enumerate((0, 1, 2, 6, 3)):
            held_a[n, h] = picked[piece * rank : (piece + 1) * rank]
        for n, piece in enumerate((7, 8, 9, 4)):
            held_b[n, h] = picked[piece * rank : (piece + 1) * rank]
        held_router[h] = picked[5 * rank : 6 * rank]

    for hop in range(1, row_count):
        row_copy(hop, row).wait_send()
    for hop in range(1, count):
        stat_copy(hop, here).wait_send()
    for j in range(chips):
        for piece in range(parts):
            mate_copy(j, piece).wait_send()

            @pl.when(j > chip)
            def _():
                line_copy(j, j, piece, right_sem, mate).wait_send()

            @pl.when(j < chip)
            def _():
                line_copy(j, j, piece, left_sem, mate).wait_send()


def back(prefix, slot, operands, weights, reach, scale, chips, row_count, held, ident):
    x = operands[15]
    seq_len, width = x.shape
    part = weights[0].shape[1]
    count = 2 * chips
    ranks = operands[14].shape[0]
    rank = ranks // 3
    extra = 128
    tall = seq_len + extra
    sems = pltpu.SemaphoreType.DMA((chips, 2))
    hops = pltpu.SemaphoreType.DMA((count,))
    row_hops = pltpu.SemaphoreType.DMA((row_count,))
    smem = pl.BlockSpec(memory_space=pltpu.SMEM)
    return pl.pallas_call(
        functools.partial(back_body, min(256, seq_len), reach, scale, chips, row_count, extra),
        out_shape=(
            jax.ShapeDtypeStruct((seq_len, part), F32),
            jax.ShapeDtypeStruct((5, held, rank, part), F32),
            jax.ShapeDtypeStruct((4, held, rank, part), F32),
            jax.ShapeDtypeStruct((held, rank, part), F32),
        ),
        in_specs=[smem, smem] + [VM] * len(operands) + [ANY] * 3,
        out_specs=(VM,) * 4,
        scratch_shapes=[
            pltpu.VMEM((seq_len, 2 * part), F32),
            pltpu.VMEM((seq_len, part), BF16),
            pltpu.VMEM((2, seq_len), F32),
            pltpu.VMEM((count, 2, seq_len), F32),
            pltpu.VMEM((rank, part), F32),
            pltpu.VMEM((seq_len, part), BF16),
            pltpu.VMEM((seq_len, part), F32),
            pltpu.VMEM((seq_len, part), F32),
            pltpu.VMEM((seq_len, part), F32),
            pltpu.VMEM((width, 3 * part), BF16),
            pltpu.VMEM((seq_len, 3 * part), BF16),
            pltpu.VMEM((seq_len, ranks), BF16),
            pltpu.VMEM((tall, width), BF16),
            pltpu.VMEM((tall, part), F32),
            pltpu.VMEM((chips, tall, part), BF16),
            pltpu.VMEM((chips + 1, tall, part), BF16),
            pltpu.VMEM((chips, tall, part), BF16),
            pltpu.VMEM((10 * rank + 16, part), BF16),
            pltpu.VMEM((row_count, 10 * rank + 16, part), BF16),
            pltpu.SemaphoreType.DMA((3,)),
            hops,
            hops,
            row_hops,
            row_hops,
            sems,
            sems,
            sems,
            pltpu.SemaphoreType.DMA((chips + 1, 2)),
            sems,
        ],
        compiler_params=pltpu.CompilerParams(
            collective_id=ident, has_side_effects=True, vmem_limit_bytes=VMEM_LIMIT
        ),
        name="back",
    )(prefix, slot, *operands, *weights)


def moments(chips, subs):
    when = {}
    for j in range(chips):
        for chip in range(j):
            own = subs * (chips - j) + 1
            when[chip, j] = max(own, when[chip - 1, j] + 3) if chip > 0 else own
        for chip in range(chips - 1, j, -1):
            own = subs * (chips - chip + j) + 1
            when[chip, j] = max(own, when[chip + 1, j] + 3) if chip < chips - 1 else own
    last = chips * subs
    return {place: min(time, last) for place, time in when.items()}


def moe_turn_body(experts, chips, subs, count, x_ref, g_ref, routes_ref, *refs):
    refs = list(refs)

    def take(number):
        taken = refs[:number]
        del refs[:number]
        return taken

    operands = [None] + take(8)
    gate_w, up_w = take(2)
    downs = take(count)
    layer_ref, o_ref = take(2)
    results = take(2)
    out_ref, out_pair, out_line = take(3)
    p_ref, out_acc, dx_acc, gate_acc, wgu, wd, x_buf, g_buf = take(8)
    pair_buf, line_buf, sums = take(3)
    w_sems, tile_sems, right_sem, left_sem, mate_sem, line_recv, mate_recv = take(7)
    gather_sems = take(5)
    out_sems = take(5)
    out_more = refs
    here, chip, core, mate = line_place()
    row = lax.axis_index("row")
    hidden = wd.shape[1] // 2
    both_hidden = 2 * hidden
    tokens, width = out_ref.shape
    own = tokens // (2 * chips)
    tile = 2 * own
    lanes = gate_acc.shape[1]
    local = gate_w.shape[0]
    pieces = gate_w.shape[2] // hidden
    steps = local * pieces
    each = steps // subs // 2

    def fetches(step, e, piece):
        slot, shift = step // 2, (step % 2) * hidden
        if count == 1:
            place = piece
            pairs = [(downs[0].at[e, pl.ds(piece * hidden, hidden)], wd.at[slot, pl.ds(shift, hidden)])]
        else:
            place = 2 * ((row // 2 + piece // 2) % 2) + (row + piece) % 2
            if piece == 0:
                pairs = [(downs[0].at[e], wd.at[slot, pl.ds(shift, hidden)])]
            else:
                early = downs[1].shape[1]
                pairs = [
                    (
                        ref.at[piece - 1, pl.ds(low - start, high - low)],
                        wd.at[slot, pl.ds(shift + low - e * hidden, high - low)],
                    )
                    for ref, start, low, high in (
                        (downs[1], 0, e * hidden, min(early, (e + 1) * hidden)),
                        (downs[2], early, max(early, e * hidden), (e + 1) * hidden),
                    )
                    if high > low
                ]
        units = pl.ds(pl.multiple_of(place * hidden, 128), hidden)
        return (
            pltpu.make_async_copy(gate_w.at[e, :, units], wgu.at[slot, :, pl.ds(shift, hidden)], w_sems.at[slot, 0]),
            pltpu.make_async_copy(
                up_w.at[e, :, units], wgu.at[slot, :, pl.ds(both_hidden + shift, hidden)], w_sems.at[slot, 1]
            ),
        ) + tuple(pltpu.make_async_copy(source, target, w_sems.at[slot, 2]) for source, target in pairs)

    def order(s):
        right = chips - 1 - chip
        return jnp.where(s < right, chips - 1 - s, jnp.where(s < chips - 1, s - right, chip))

    def tile_rows(s):
        return pl.ds(pl.multiple_of(order(s) * tile, 8), tile)

    def tiles(s):
        return (
            pltpu.make_async_copy(x_ref.at[tile_rows(s)], x_buf, tile_sems.at[0]),
            pltpu.make_async_copy(g_ref.at[tile_rows(s)], g_buf, tile_sems.at[1]),
        )

    for copy in tiles(0):
        copy.start()
    for step in range(steps):
        for copy in fetches(step, step // pieces, step % pieces):
            copy.start()
    line_barrier(chips)

    def block(number):
        return pl.ds(pl.multiple_of(number * own, 8), own)

    def mate_copy(j):
        return remote(p_ref.at[block(2 * j + 1 - core)], pair_buf.at[j], mate_sem.at[j], mate_recv.at[j], mate)

    def line_copy(j, slot, sem, device):
        return remote(sums.at[j], line_buf.at[slot], sem.at[j], line_recv.at[slot], device)

    def pair_sum(j):
        mate_copy(j).wait_recv()
        return p_ref[block(2 * j + core)].astype(F32) + pair_buf[j].astype(F32)

    def pass_on(at, j):
        rightward = j > at
        mate_copy(j).wait_recv()
        inner = 0 < at < chips - 1
        if inner:
            line_copy(j, j, right_sem if rightward else left_sem, mate).wait_recv()

        def add_up(low):
            rows = pl.ds(low, 16)
            mine = p_ref[pl.ds(pl.multiple_of((2 * j + core) * own + low, 16), 16)]
            total = mine.astype(F32) + pair_buf[j, rows].astype(F32)
            if inner:
                total = total + line_buf[j, rows].astype(F32)
            sums[j, rows] = total.astype(BF16)

        in_chunks(own, 16, add_up)
        if rightward:
            line_copy(j, j, right_sem, here + 2).start()
        else:
            line_copy(j, chips if at - j == 1 else j, left_sem, here - 2).start()

    when = moments(chips, subs)

    def one_sub(k, carry):
        s, sub = k // subs, k % subs
        rows = tile_rows(s)

        @pl.when(sub == 0)
        def _():
            for copy in tiles(s):
                copy.wait()

            out_acc[...] = jnp.zeros_like(out_acc)
            dx_acc[...] = jnp.zeros_like(dx_acc)
            gate_acc[...] = jnp.zeros_like(gate_acc)

        def one_step(step, carry):
            @pl.when(s == 0)
            def _():
                units = pl.ds(0, both_hidden)
                for number in range(2):
                    target = wgu.at[step, :, pl.ds(number * both_hidden, both_hidden)]
                    pltpu.make_async_copy(gate_w.at[0, :, units], target, w_sems.at[step, number]).wait()
                pltpu.make_async_copy(wd.at[step], wd.at[step], w_sems.at[step, 2]).wait()

            e = here * local + (2 * step) // pieces
            lane = lax.broadcasted_iota(jnp.int32, (tile, lanes), 1)
            mine = lane == e
            halves = jnp.logical_or(mine, lane == e + experts)
            named = jnp.sum(jnp.where(routes_ref[rows] == e, 1.0, 0.0), axis=1, keepdims=True)
            gate = jnp.sum(jnp.where(halves, x_buf[:, width:].astype(F32), 0.0), axis=1, keepdims=True)
            gate = gate * named
            both = nn(x_buf[:, :width], wgu[step])
            gate_in, up_in = both[:, :both_hidden], both[:, both_hidden:]
            sigmoid = jax.nn.sigmoid(gate_in)
            silu = gate_in * sigmoid
            active = silu * up_in
            back = nt(g_buf[...], wd[step])
            d_gate = jnp.sum(active * back, axis=1, keepdims=True) * named
            gate_acc[...] += jnp.where(mine, d_gate, 0.0)
            out_acc[...] += nn((active * gate).astype(BF16), wd[step])
            d_active = back * gate
            d_gate_in = d_active * up_in * (sigmoid + silu * (1.0 - sigmoid))
            d_up_in = d_active * silu
            d_both = jnp.concatenate([d_gate_in.astype(BF16), d_up_in.astype(BF16)], axis=1)
            dx_acc[...] += nt(d_both, wgu[step])
            return carry

        lax.fori_loop(sub * each, (sub + 1) * each, one_step, 0)

        @pl.when(sub == subs - 1)
        def _():
            out_ref[rows] = out_acc[...].astype(BF16)
            p_ref[rows, :width] = dx_acc[...].astype(BF16)
            high = gate_acc[...].astype(BF16).astype(F32)
            rest = gate_acc[...] - high
            p_ref[rows, width:] = (high + pltpu.roll(rest, experts, 1)).astype(BF16)
            mate_copy(order(s)).start()

            @pl.when(s + 1 < chips)
            def _():
                for copy in tiles(s + 1):
                    copy.start()

            @pl.when(s == chips - 1)
            def _():
                fetch = pltpu.make_async_copy(operands[1], dx_acc.at[pl.ds(own, own)], tile_sems.at[0])
                fetch.start()
                fetch.wait()
                mine = out_acc[pl.ds(pl.multiple_of(core * own, 8), own)]
                out_ref[block(here)] = (mine + dx_acc[pl.ds(own, own)]).astype(BF16)

        for (at, j), time in sorted(when.items(), key=lambda item: (item[1], abs(item[0][0] - item[0][1]))):

            @pl.when(jnp.logical_and(chip == at, k == time - 1))
            def _():
                pass_on(at, j)

        return carry

    lax.fori_loop(0, chips * subs, one_sub, 0)
    if wgu.shape[0] >= chips:
        out_sums = wgu.at[:, pl.ds(0, tokens), pl.ds(0, layer_ref.shape[1])]
    else:
        (out_sums,) = out_more
    operands[0] = g_buf.at[pl.ds(pl.multiple_of(core * own, 8), own)]
    operands[1] = dx_acc.at[pl.ds(own, own)]
    layer = reduce_steps(chips, 2, 1, out_ref, layer_ref, out_pair, out_line, out_sums, *out_sems)
    next(layer)
    next(layer)
    first = pl.ds(0, own)

    def add(total):
        dx_acc[first] += total[:, :width]
        gate_acc[first] += total[:, width:]

    total = pair_sum(chip)
    dx_acc[first] = total[:, :width]
    gate_acc[first] = total[:, width:]

    @pl.when(chip > 0)
    def _():
        line_copy(chip, chip, right_sem, mate).wait_recv()
        add(line_buf[chip].astype(F32))

    @pl.when(chip < chips - 1)
    def _():
        line_copy(chip, chips, left_sem, mate).wait_recv()
        add(line_buf[chips].astype(F32))

    for j in range(chips):
        mate_copy(j).wait_send()

        @pl.when(j > chip)
        def _():
            line_copy(j, j, right_sem, mate).wait_send()

        @pl.when(j < chip)
        def _():
            line_copy(j, j, left_sem, mate).wait_send()

    kept = turn_backward(experts, dx_acc[first], gate_acc[first], operands, results, o_ref, block(here))
    run(gather_rows_steps(chips, 2, o_ref, *gather_sems, lambda: turn_late(kept, operands, results)), layer)


def moe_turn(x, g, routes, operands, experts, gate_w, up_w, downs, results, chips, ident):
    tokens, width = g.shape
    wide = x.shape[1]
    lanes = wide - width
    own = tokens // (2 * chips)
    hidden = downs[0].shape[1] if len(downs) > 1 else min(256, gate_w.shape[2] // 4)
    steps = gate_w.shape[0] * gate_w.shape[2] // hidden
    subs = min(4, steps // 2)
    whole = jax.ShapeDtypeStruct((tokens, width), BF16)
    part = width // (2 * chips)
    per_chip = pltpu.SemaphoreType.DMA((chips,))
    halves = pltpu.SemaphoreType.DMA((chips, 2))
    return pl.pallas_call(
        functools.partial(moe_turn_body, experts, chips, subs, len(downs)),
        out_shape=(jax.ShapeDtypeStruct((tokens, part), F32), whole) + tuple(results),
        in_specs=[ANY, ANY, VM, ANY] + [VM] * (len(operands) - 1) + [ANY] * (2 + len(downs)),
        out_specs=(VM,) * (2 + len(results)),
        scratch_shapes=[
            pltpu.VMEM((tokens, width), BF16),
            pltpu.VMEM((chips, tokens, part), BF16),
            pltpu.VMEM((chips + 1, tokens, part), BF16),
            pltpu.VMEM((tokens, wide), BF16),
            pltpu.VMEM((2 * own, width), F32),
            pltpu.VMEM((2 * own, width), F32),
            pltpu.VMEM((2 * own, lanes), F32),
            pltpu.VMEM((steps // 2, width, 4 * hidden), BF16),
            pltpu.VMEM((steps // 2, 2 * hidden, width), BF16),
            pltpu.VMEM((2 * own, wide), BF16),
            pltpu.VMEM((2 * own, width), BF16),
            pltpu.VMEM((chips, own, wide), BF16),
            pltpu.VMEM((chips + 1, own, wide), BF16),
            pltpu.VMEM((chips, own, wide), BF16),
            pltpu.SemaphoreType.DMA((steps // 2, 3)),
            pltpu.SemaphoreType.DMA((2,)),
            per_chip,
            per_chip,
            per_chip,
            pltpu.SemaphoreType.DMA((chips + 1,)),
            per_chip,
        ]
        + [halves] * 8
        + [pltpu.SemaphoreType.DMA((chips + 1, 2)), halves]
        + ([] if steps // 2 >= chips else [pltpu.VMEM((chips, tokens, part), BF16)]),
        compiler_params=pltpu.CompilerParams(
            collective_id=ident, has_side_effects=True, vmem_limit_bytes=VMEM_MOST
        ),
        name="moe_turn",
    )(x, g, routes, *operands, gate_w, up_w, *downs)


def rope_tables(length, head_dim):
    half_dim = head_dim // 2
    frequency = rope_base ** (-(2.0 * jnp.arange(half_dim, dtype=F32)) / head_dim)
    angles = jnp.arange(length, dtype=F32)[:, None] * frequency[None, :]
    cosine, sine = jnp.cos(angles), jnp.sin(angles)
    return jnp.concatenate([cosine, cosine], axis=1), jnp.concatenate([-sine, sine], axis=1)


def shards(
    inputs,
    cotangent,
    norm_first,
    norm_second,
    query_gain,
    key_gain,
    w_query,
    w_key,
    w_value,
    w_out,
    w_router,
    w_gate,
    w_up,
    w_down,
    adapter_a,
    adapter_b,
    adapter_router,
    routes,
    prefix,
    adapter_index,
):
    seq_len, width_part = inputs.shape
    col_count = lax.axis_size("col")
    row_count = lax.axis_size("row")
    col_index = lax.axis_index("col")
    row_index = lax.axis_index("row")
    chips = col_count // 2
    full_width = width_part * col_count
    head_width = w_query.shape[1]
    local_experts = w_gate.shape[0]
    expert_total = w_router.shape[1]
    feature_start = col_index * width_part
    head_start = col_index * head_width
    own_rows = seq_len // col_count
    row_start = col_index * own_rows
    score_scale = HD ** (-0.5)
    reach = seq_len // 2
    lanes = 128

    def columns(array, axis_num):
        return lax.dynamic_slice_in_dim(array, feature_start, width_part, axis_num)

    def head_cols(array, axis_num=1):
        return lax.dynamic_slice_in_dim(array, head_start, head_width, axis_num)

    def held_rows(array):
        return lax.dynamic_slice_in_dim(array, row_start, own_rows, 0)

    def col_sum(pair, ident):
        return jnp.sum(small_gather(pair, col_count, ident), axis=0)

    full_gate = lax.all_gather(w_gate, "row", axis=2, tiled=True)
    full_up = lax.all_gather(w_up, "row", axis=2, tiled=True)
    across = row_count == 4 and local_experts == 2
    down_shares = w_down.reshape(SHARES, -1, full_width)
    riders = (cotangent, down_shares) if across else (cotangent,)
    adapter_slot = adapter_index[0]
    chosen_a = lax.dynamic_index_in_dim(adapter_a, adapter_slot, 1, keepdims=False).swapaxes(1, 2)
    chosen_b = lax.dynamic_index_in_dim(adapter_b, adapter_slot, 1, keepdims=False)
    chosen_router = lax.dynamic_index_in_dim(adapter_router, adapter_slot, 0, keepdims=False)
    rank = chosen_a.shape[1]
    a_three = chosen_a[:3].reshape(3 * rank, full_width)
    b_three = head_cols(chosen_b[:3].reshape(3 * rank, full_width))
    blank = jnp.zeros((rank, head_width), BF16)
    b_cols = jnp.concatenate(
        [
            jnp.concatenate([b_three[m * rank : (m + 1) * rank] if n == m else blank for n in range(3)], axis=0)
            for m in range(3)
        ],
        axis=1,
    )
    a_out = head_cols(chosen_a[3])
    out_map = (w_out.astype(F32) + tn(a_out, chosen_b[3])).astype(BF16)
    out_wide = jnp.concatenate([out_map, a_out.T, jnp.zeros((head_width, lanes - rank), BF16)], axis=1)
    router_rows = jnp.pad(w_router.T, ((0, lanes - expert_total), (0, 0)))
    router_up = jnp.pad(chosen_router, ((0, 0), (0, lanes - expert_total)))
    gains = jnp.stack([head_cols(query_gain, 0), head_cols(key_gain, 0)])
    tables = rope_tables(seq_len, HD)
    gain_first, gain_second = norm_first[None], norm_second[None]

    full_inputs, *down_first = line_gather(inputs, chips, 1, 0, rider=down_shares if across else None)
    proj, mid, inv_first, squares = project(
        full_inputs, gain_first, (w_query, w_key, w_value), a_three, b_cols
    )
    inv = lax.rsqrt(col_sum(squares, 1) / full_width + norm_eps).T
    part_out, attended, rot_query, rot_key, value_rows, log_totals = attend(
        prefix, proj, inv, gains, tables, out_wide, reach, score_scale
    )
    wide = full_width + lanes
    row_shape = jax.ShapeDtypeStruct
    normed_two, hidden_rows, mid_out, mid_router, probs, full_cot, *down_second = line_turn(
        part_out,
        (held_rows(full_inputs), gain_second, chosen_a[4], router_rows, router_up),
        wide,
        (
            row_shape((own_rows, full_width), F32),
            row_shape((own_rows, lanes), BF16),
            row_shape((own_rows, rank), BF16),
            row_shape((own_rows, lanes), F32),
        ),
        functools.partial(turn_forward, full_width, expert_total),
        lambda kept, operands, results: None,
        chips,
        2,
        riders,
    )
    if across:
        downs = (w_down,) + tuple(
            others.reshape(3, -1, full_width) for others in down_first + down_second
        )
    else:
        downs = (lax.all_gather(w_down, "row", axis=1, tiled=True),)

    layer_out, grad_attn, late, router_late = moe_turn(
        normed_two,
        full_cot,
        routes,
        (
            hidden_rows,
            gain_second,
            chosen_a[4],
            router_rows,
            router_up,
            probs,
            mid_router,
            mid_out,
        ),
        expert_total,
        full_gate,
        full_up,
        downs,
        (row_shape((2 * rank, full_width), F32), row_shape((rank, lanes), F32)),
        chips,
        7,
    )
    layer_out = layer_out.astype(BF16)

    held_adapters = adapter_a.shape[1] // row_count
    grad_inputs, grad_a, grad_b, grad_router = back(
        prefix,
        adapter_index,
        (
            grad_attn,
            out_map,
            chosen_b[3],
            attended,
            rot_query,
            rot_key,
            value_rows,
            log_totals,
            proj,
            gains,
            *tables,
            inv,
            b_cols,
            a_three,
            full_inputs,
            inv_first,
            gain_first,
            mid,
            late,
            router_late,
        ),
        (w_query, w_key, w_value),
        reach,
        score_scale,
        chips,
        row_count,
        held_adapters,
        12,
    )
    grad_a = grad_a.swapaxes(2, 3)
    grad_router = grad_router[:, :, :expert_total]
    return (layer_out, grad_inputs, grad_a, grad_b, grad_router)


def solution(mesh):
    placed = (
        P("row", "col"),
        P("row", "col"),
        P(),
        P(),
        P(),
        P(),
        P(None, "col"),
        P(None, "col"),
        P(None, "col"),
        P("col", None),
        P(),
        P("col", None, "row"),
        P("col", None, "row"),
        P("col", "row", None),
        P(),
        P(),
        P(),
        P("row", None),
        P("row"),
        P("row"),
    )
    return jax.shard_map(
        shards,
        mesh=mesh,
        in_specs=placed,
        out_specs=(
            P("row", "col"),
            P("row", "col"),
            P(None, "row", "col", None),
            P(None, "row", None, "col"),
            P("row", None, None),
        ),
        check_vma=False,
    )
```

```python
import functools

import jax
import jax.numpy as jnp
from jax import lax
from jax.experimental import pallas as pl
from jax.experimental.pallas import tpu as pltpu
from jax.sharding import PartitionSpec as P

HD = 128
F32, BF16 = jnp.float32, jnp.bfloat16
MESH_ID = pl.DeviceIdType.MESH
VM = pl.BlockSpec(memory_space=pltpu.VMEM)
ANY = pl.BlockSpec(memory_space=pl.ANY)
VMEM_LIMIT = 60 * 1024 * 1024
VMEM_MOST = 67_000_000
SHARES, FIRST_SHARE = 16, 6

norm_eps = 1e-05
rope_base = 10000.0
masked_score = -1e30


def nn(left, right):
    return jnp.dot(left, right, preferred_element_type=F32)


def nt(left, right):
    return lax.dot_general(left, right, (((1,), (1,)), ((), ())), preferred_element_type=F32)


def tn(left, right):
    return lax.dot_general(left, right, (((0,), (0,)), ((), ())), preferred_element_type=F32)


def remote(src, dst, send_sem, recv_sem, device):
    return pltpu.make_async_remote_copy(
        src_ref=src,
        dst_ref=dst,
        send_sem=send_sem,
        recv_sem=recv_sem,
        device_id={"col": device},
        device_id_type=MESH_ID,
    )


def line_place():
    here = lax.axis_index("col")
    core = here % 2
    return here, here // 2, core, here + 1 - 2 * core


def line_barrier(chips, across=()):
    here, chip, core, mate = line_place()
    barrier = pltpu.get_barrier_semaphore()
    has_left, has_right = chip > 0, chip < chips - 1
    for other in across:
        pl.semaphore_signal(barrier, inc=1, device_id={"row": other}, device_id_type=MESH_ID)
    pl.semaphore_signal(barrier, inc=1, device_id={"col": mate}, device_id_type=MESH_ID)

    @pl.when(has_left)
    def _():
        pl.semaphore_signal(barrier, inc=1, device_id={"col": here - 2}, device_id_type=MESH_ID)

    @pl.when(has_right)
    def _():
        pl.semaphore_signal(barrier, inc=1, device_id={"col": here + 2}, device_id_type=MESH_ID)

    inner = jnp.logical_and(has_left, has_right)

    @pl.when(inner)
    def _():
        pl.semaphore_wait(barrier, 3 + len(across))

    @pl.when(jnp.logical_not(inner))
    def _():
        pl.semaphore_wait(barrier, 2 + len(across))


def in_chunks(rows, size, body):
    def one(c, carry):
        body(pl.multiple_of(c * size, size))
        return carry

    lax.fori_loop(0, rows // size, one, 0)


def spot(axis, size, parts, block, part):
    rows, cols = size
    step = rows // parts
    if axis == 0:
        return (pl.ds(pl.multiple_of(block * rows + part * step, 8), step), slice(None))
    return (pl.ds(part * step, step), pl.ds(pl.multiple_of(block * cols, 128), cols))


def run(*steps):
    steps = list(steps)
    while steps:
        for one in list(steps):
            if next(one, steps) is steps:
                steps.remove(one)


def gather_body(chips, parts, axis, riders, x_ref, *refs):
    line_barrier(chips, row_partners() if riders else ())
    o_ref = refs[riders]
    sems = refs[2 * riders + 1 :]
    steps = [gather_steps(chips, parts, axis, x_ref, o_ref, *sems[:6])]
    if riders:
        steps.append(row_gather_steps(2, 0, refs[0], refs[2], *sems[6:]))
    run(*steps)


def gather_steps(chips, parts, axis, x_ref, o_ref, right_sem, left_sem, mate_sem, line_recv, mate_recv, own_sem):
    here, chip, core, mate = line_place()
    size = x_ref.shape
    step = size[0] // parts

    def at(block, part):
        return o_ref.at[spot(axis, size, parts, block, part)]

    def copy(j, part, sem, recv, device, first=False, block=None):
        block = 2 * j + core if block is None else block
        src = x_ref.at[pl.ds(part * step, step)] if first else at(block, part)
        return remote(src, at(block, part), sem.at[j, part], recv.at[j, part], device)

    def forward(j, part, rightward, leftward, first):
        if rightward:

            @pl.when(chip < chips - 1)
            def _():
                copy(j, part, right_sem, line_recv, here + 2, first).start()

        if leftward:

            @pl.when(chip > 0)
            def _():
                copy(j, part, left_sem, line_recv, here - 2, first).start()

        copy(j, part, mate_sem, mate_recv, mate, first).start()

    for part in range(parts):
        forward(chip, part, True, True, True)
    own = []
    for part in range(parts):
        own.append(
            pltpu.make_async_copy(x_ref.at[pl.ds(part * step, step)], at(here, part), own_sem.at[part])
        )
        own[-1].start()
    yield
    for far in range(1, chips):
        for part in range(parts):

            @pl.when(chip - far >= 0)
            def _():
                copy(chip - far, part, right_sem, line_recv, mate).wait_recv()
                forward(chip - far, part, True, False, False)

            @pl.when(chip + far < chips)
            def _():
                copy(chip + far, part, left_sem, line_recv, mate).wait_recv()
                forward(chip + far, part, False, True, False)

        yield

    for own_copy in own:
        own_copy.wait()
    for j in range(chips):
        for part in range(parts):
            copy(j, part, mate_sem, mate_recv, mate, block=2 * j + 1 - core).wait_recv()
            copy(j, part, mate_sem, mate_recv, mate).wait_send()

            @pl.when(jnp.logical_and(j <= chip, chip < chips - 1))
            def _():
                copy(j, part, right_sem, line_recv, here + 2).wait_send()

            @pl.when(jnp.logical_and(j >= chip, chip > 0))
            def _():
                copy(j, part, left_sem, line_recv, here - 2).wait_send()


def line_gather(x, chips, axis, ident, parts=2, rider=None):
    rows, cols = x.shape
    sems = pltpu.SemaphoreType.DMA((chips, parts))
    shape = (2 * chips * rows, cols) if axis == 0 else (rows, 2 * chips * cols)
    whole = jax.ShapeDtypeStruct(shape, x.dtype)
    more = () if rider is None else (rider,)
    ridden = tuple(jax.ShapeDtypeStruct((3, FIRST_SHARE) + one.shape[1:], one.dtype) for one in more)
    return pl.pallas_call(
        functools.partial(gather_body, chips, parts, axis, len(more)),
        out_shape=(whole,) + ridden,
        in_specs=[VM] + [ANY] * len(more),
        out_specs=(VM,) + (ANY,) * len(more),
        scratch_shapes=[sems] * 5
        + [pltpu.SemaphoreType.DMA((parts,))]
        + [pltpu.SemaphoreType.DMA((6,))] * (2 * len(more)),
        compiler_params=pltpu.CompilerParams(
            collective_id=ident, has_side_effects=True, vmem_limit_bytes=VMEM_LIMIT
        ),
        name="line_gather",
    )(x, *more)


def reduce_steps(
    chips, parts, axis, p_ref, o_ref, pair_buf, line_buf, sums, right_sem, left_sem, mate_sem, line_recv, mate_recv
):
    here, chip, core, mate = line_place()
    size = o_ref.shape
    step = size[0] // parts

    def rows(part):
        return pl.ds(part * step, step)

    def at(block, part):
        return spot(axis, size, parts, block, part)

    def mate_copy(j, part):
        return remote(
            p_ref.at[at(2 * j + 1 - core, part)],
            pair_buf.at[j, rows(part)],
            mate_sem.at[j, part],
            mate_recv.at[j, part],
            mate,
        )

    def line_copy(j, slot, part, sem, device):
        return remote(
            sums.at[j, rows(part)], line_buf.at[slot, rows(part)], sem.at[j, part], line_recv.at[slot, part], device
        )

    for far in range(chips - 1, -1, -1):
        for part in range(parts):

            @pl.when(chip + far < chips)
            def _():
                mate_copy(chip + far, part).start()

            if far > 0:

                @pl.when(chip - far >= 0)
                def _():
                    mate_copy(chip - far, part).start()

    yield

    chunk = 16 if axis == 0 else 64

    def pair_sum(j, part, low):
        block = 2 * j + core
        if axis == 0:
            where = (pl.ds(pl.multiple_of(block * size[0] + part * step + low, 16), chunk), slice(None))
        else:
            cols = pl.ds(pl.multiple_of(block * size[1], 128), size[1])
            where = (pl.ds(pl.multiple_of(part * step + low, 16), chunk), cols)
        return p_ref[where].astype(F32) + pair_buf[j, chunk_rows(part, low)].astype(F32)

    def chunk_rows(part, low):
        return pl.ds(pl.multiple_of(part * step + low, 16), chunk)

    def pass_on(j, slot, part, more, sem, device):
        mate_copy(j, part).wait_recv()

        @pl.when(more)
        def _():
            line_copy(j, j, part, sem, mate).wait_recv()

            def add_up(low):
                total = pair_sum(j, part, low) + line_buf[j, chunk_rows(part, low)].astype(F32)
                sums[j, chunk_rows(part, low)] = total.astype(BF16)

            in_chunks(step, chunk, add_up)

        @pl.when(jnp.logical_not(more))
        def _():
            def add_up(low):
                sums[j, chunk_rows(part, low)] = pair_sum(j, part, low).astype(BF16)

            in_chunks(step, chunk, add_up)

        line_copy(j, slot, part, sem, device).start()

    for far in range(chips - 1, 0, -1):
        for part in range(parts):

            @pl.when(chip + far < chips)
            def _():
                pass_on(chip + far, chip + far, part, chip > 0, right_sem, here + 2)

            @pl.when(chip - far >= 0)
            def _():
                pass_on(
                    chip - far, chips if far == 1 else chip - far, part, chip < chips - 1, left_sem, here - 2
                )

        yield

    for part in range(parts):
        mate_copy(chip, part).wait_recv()

        def begin(low):
            o_ref[chunk_rows(part, low)] = pair_sum(chip, part, low)

        in_chunks(step, chunk, begin)

        def add_line(slot):
            def add_up(low):
                o_ref[chunk_rows(part, low)] += line_buf[slot, chunk_rows(part, low)].astype(F32)

            in_chunks(step, chunk, add_up)

        @pl.when(chip > 0)
        def _():
            line_copy(chip, chip, part, right_sem, mate).wait_recv()
            add_line(chip)

        @pl.when(chip < chips - 1)
        def _():
            line_copy(chip, chips, part, left_sem, mate).wait_recv()
            add_line(chips)

    for j in range(chips):
        for part in range(parts):
            mate_copy(j, part).wait_send()

            @pl.when(j > chip)
            def _():
                line_copy(j, j, part, right_sem, mate).wait_send()

            @pl.when(j < chip)
            def _():
                line_copy(j, j, part, left_sem, mate).wait_send()


def small_body(count, x_ref, o_ref, send_sem, recv_sem):
    here = lax.axis_index("col")
    barrier = pltpu.get_barrier_semaphore()
    for hop in range(1, count):
        other = lax.rem(here + hop, count)
        pl.semaphore_signal(barrier, inc=1, device_id={"col": other}, device_id_type=MESH_ID)
    o_ref[here] = x_ref[...]
    pl.semaphore_wait(barrier, count - 1)

    def copy(hop, block):
        other = lax.rem(here + hop, count)
        return remote(x_ref, o_ref.at[block], send_sem.at[hop], recv_sem.at[hop], other)

    for hop in range(1, count):
        copy(hop, here).start()
    for hop in range(1, count):
        copy(hop, lax.rem(here + count - hop, count)).wait_recv()
    for hop in range(1, count):
        copy(hop, here).wait_send()


def small_gather(x, count, ident):
    sems = pltpu.SemaphoreType.DMA((count,))
    return pl.pallas_call(
        functools.partial(small_body, count),
        out_shape=jax.ShapeDtypeStruct((count,) + x.shape, x.dtype),
        in_specs=[VM],
        out_specs=VM,
        scratch_shapes=[sems, sems],
        compiler_params=pltpu.CompilerParams(collective_id=ident, has_side_effects=True),
        name="small_gather",
    )(x)


def row_copy(src, dst, sems, which, device):
    return pltpu.make_async_remote_copy(
        src_ref=src,
        dst_ref=dst,
        send_sem=sems[0].at[which],
        recv_sem=sems[1].at[which],
        device_id={"row": device},
        device_id_type=MESH_ID,
    )


def row_partners():
    here = lax.axis_index("row")
    major, minor = here // 2, here % 2
    return 2 * major + 1 - minor, 2 * (1 - major) + minor


def row_gather_steps(pauses, begin, x_ref, o_ref, *sems):
    near, next_one = row_partners()
    half = o_ref.shape[1] // 2

    def side(neighbour, first):
        slot, device = (0, near) if neighbour == 0 else (1, next_one)
        rows = pl.ds(first * half, half)
        source = x_ref.at[pl.ds(begin + first * half, half)]
        return row_copy(source, o_ref.at[slot, rows], sems, 2 * slot + first, device)

    def onward(neighbour):
        slot, device = (0, next_one) if neighbour == 0 else (1, near)
        rows = pl.ds(slot * half, half)
        return row_copy(o_ref.at[slot, rows], o_ref.at[2, rows], sems, 4 + slot, device)

    side(0, 0).start()
    side(1, 1).start()
    side(0, 1).start()
    side(1, 0).start()
    for _ in range(pauses):
        yield
    side(0, 0).wait_recv()
    onward(0).start()
    side(1, 1).wait_recv()
    onward(1).start()
    yield
    for neighbour in range(2):
        side(neighbour, 1 - neighbour).wait_recv()
        onward(neighbour).wait_recv()
        onward(neighbour).wait_send()
        side(neighbour, 0).wait_send()
        side(neighbour, 1).wait_send()


def turn_body(chips, parts, first, last, held, late_count, riders, *refs):
    refs = list(refs)

    def take(count):
        taken = refs[:count]
        del refs[:count]
        return taken

    (p_ref,) = take(1)
    operands = take(held)
    rider_in = take(riders)
    (o_ref,) = take(1)
    results = take(late_count)
    rider_out = take(riders)
    sums_in, pair_buf, line_buf, sums = take(4)
    reduce_sems = take(5)
    gather_sems = take(5)
    line_barrier(chips, row_partners() if riders > 1 else ())
    steps = [reduce_steps(chips, parts, 0, p_ref, sums_in, pair_buf, line_buf, sums, *reduce_sems)]
    if riders > 0:
        steps.append(gather_steps(chips, 2, 1, rider_in[0], rider_out[0], *take(6)))
    if riders > 1:
        across = row_gather_steps(1, FIRST_SHARE, rider_in[1], rider_out[1], *take(2))
        next(across)
    run(*steps)
    here = lax.axis_index("col")
    own = o_ref.shape[0] // (2 * chips)
    kept = first(sums_in, operands, results, o_ref, pl.ds(pl.multiple_of(here * own, 8), own))

    def beside():
        if riders > 1:
            next(across)
        last(kept, operands, results)

    run(gather_rows_steps(chips, parts, o_ref, *gather_sems, beside))
    if riders > 1:
        run(across)


def gather_rows_steps(chips, parts, o_ref, right_sem, left_sem, mate_sem, line_recv, mate_recv, beside):
    here, chip, core, mate = line_place()
    size = (o_ref.shape[0] // (2 * chips), o_ref.shape[1])

    def copy(j, part, sem, recv, device, block=None):
        block = 2 * j + core if block is None else block
        ref = o_ref.at[spot(0, size, parts, block, part)]
        return remote(ref, ref, sem.at[j, part], recv.at[j, part], device)

    def forward(j, part, rightward, leftward):
        if rightward:

            @pl.when(chip < chips - 1)
            def _():
                copy(j, part, right_sem, line_recv, here + 2).start()

        if leftward:

            @pl.when(chip > 0)
            def _():
                copy(j, part, left_sem, line_recv, here - 2).start()

        copy(j, part, mate_sem, mate_recv, mate).start()

    for part in range(parts):
        forward(chip, part, True, True)
    beside()
    yield
    for far in range(1, chips):
        for part in range(parts):

            @pl.when(chip - far >= 0)
            def _():
                copy(chip - far, part, right_sem, line_recv, mate).wait_recv()
                forward(chip - far, part, True, False)

            @pl.when(chip + far < chips)
            def _():
                copy(chip + far, part, left_sem, line_recv, mate).wait_recv()
                forward(chip + far, part, False, True)

        yield

    for j in range(chips):
        for part in range(parts):
            copy(j, part, mate_sem, mate_recv, mate, block=2 * j + 1 - core).wait_recv()
            copy(j, part, mate_sem, mate_recv, mate).wait_send()

            @pl.when(jnp.logical_and(j <= chip, chip < chips - 1))
            def _():
                copy(j, part, right_sem, line_recv, here + 2).wait_send()

            @pl.when(jnp.logical_and(j >= chip, chip > 0))
            def _():
                copy(j, part, left_sem, line_recv, here - 2).wait_send()


def line_turn(p, operands, width, results, first, last, chips, ident, riders=(), parts=2):
    rows, cols = p.shape
    own = rows // (2 * chips)
    sems = pltpu.SemaphoreType.DMA((chips, parts))
    longer = pltpu.SemaphoreType.DMA((chips + 1, parts))
    more = []
    ridden = []
    if len(riders) > 0:
        height, part = riders[0].shape
        ridden.append(jax.ShapeDtypeStruct((height, 2 * chips * part), BF16))
        more += [pltpu.SemaphoreType.DMA((chips, 2))] * 5 + [pltpu.SemaphoreType.DMA((2,))]
    if len(riders) > 1:
        ridden.append(jax.ShapeDtypeStruct((3, SHARES - FIRST_SHARE) + riders[1].shape[1:], BF16))
        more += [pltpu.SemaphoreType.DMA((6,))] * 2
    return pl.pallas_call(
        functools.partial(turn_body, chips, parts, first, last, len(operands), len(results), len(riders)),
        out_shape=(jax.ShapeDtypeStruct((rows, width), BF16),) + tuple(results) + tuple(ridden),
        in_specs=[VM] * (1 + len(operands)) + [VM, ANY][: len(riders)],
        out_specs=(VM,) * (1 + len(results)) + (VM, ANY)[: len(riders)],
        scratch_shapes=[
            pltpu.VMEM((own, cols), F32),
            pltpu.VMEM((chips, own, cols), BF16),
            pltpu.VMEM((chips + 1, own, cols), BF16),
            pltpu.VMEM((chips, own, cols), BF16),
            sems,
            sems,
            sems,
            longer,
            sems,
        ]
        + [sems] * 5
        + more,
        compiler_params=pltpu.CompilerParams(
            collective_id=ident, has_side_effects=True, vmem_limit_bytes=VMEM_LIMIT
        ),
        name="line_turn",
    )(p, *operands, *riders)


def inverse_rms(values):
    return lax.rsqrt(jnp.mean(values * values, axis=1, keepdims=True) + norm_eps)


def turn_forward(width, experts, sums, operands, results, o_ref, own):
    x_ref, gain_ref, a_ref, router_ref, up_ref = operands
    hidden_ref, mid_ref, mid_router_ref, probs_ref = results
    hidden = x_ref[...].astype(F32) + sums[:, :width]
    mid_ref[...] = sums[:, width:].astype(BF16)
    hidden_ref[...] = hidden
    normed = (hidden * inverse_rms(hidden) * gain_ref[...]).astype(BF16)
    o_ref[own, :width] = normed
    mid_router = nt(normed, a_ref[...]).astype(BF16)
    mid_router_ref[...] = mid_router
    logits = nt(normed, router_ref[...]) + nn(mid_router, up_ref[...])
    lane = lax.broadcasted_iota(jnp.int32, logits.shape, 1)
    logits = jnp.where(lane < experts, logits, masked_score)
    exponent = jnp.exp(logits - jnp.max(logits, axis=1, keepdims=True))
    probs = exponent / jnp.sum(exponent, axis=1, keepdims=True)
    probs_ref[...] = probs
    high = probs.astype(BF16)
    rest = probs - high.astype(F32)
    o_ref[own, width:] = (high.astype(F32) + pltpu.roll(rest, experts, 1)).astype(BF16)
    return None


def turn_backward(experts, grads, pair, operands, results, o_ref, own):
    g_ref, hidden_ref, gain_ref, a_ref, router_ref, up_ref, probs_ref, mid_router_ref, mid_ref = operands
    lanes = pair.shape[1]
    grad_probs = pair + pltpu.roll(pair, lanes - experts, 1)
    probs = probs_ref[...]
    grad_logits = (probs * (grad_probs - jnp.sum(probs * grad_probs, axis=1, keepdims=True))).astype(BF16)
    grad_mid = nt(grad_logits, up_ref[...]).astype(BF16)
    grad_normed = grads + nn(grad_logits, router_ref[...]) + nn(grad_mid, a_ref[...])
    hidden = hidden_ref[...]
    inv = inverse_rms(hidden)
    scaled = grad_normed * gain_ref[...]
    grad_hidden = (
        g_ref[...].astype(F32)
        + inv * scaled
        - hidden * (inv * inv * inv * jnp.mean(hidden * scaled, axis=1, keepdims=True))
    )
    grad_hidden = grad_hidden.astype(BF16)
    o_ref[own, :] = grad_hidden
    return grad_logits, grad_mid, grad_hidden


def turn_late(kept, operands, results):
    _, hidden_ref, gain_ref, _, _, _, _, mid_router_ref, mid_ref = operands
    grad_logits, grad_mid, grad_hidden = kept
    hidden = hidden_ref[...]
    normed = (hidden * inverse_rms(hidden) * gain_ref[...]).astype(BF16)
    rank = grad_mid.shape[1]
    late_ref, router_ref = results
    late_ref[pl.ds(0, rank)] = tn(grad_mid, normed)
    late_ref[pl.ds(rank, rank)] = tn(mid_ref[:, :rank], grad_hidden)
    router_ref[...] = tn(mid_router_ref[...], grad_logits)


def row_sums(values):
    lanes = 128
    values = sum(values[:, n : n + lanes] for n in range(0, values.shape[1], lanes))
    high = values.astype(BF16)
    rest = (values - high.astype(F32)).astype(BF16)
    ones = jnp.ones((8, values.shape[1]), BF16)
    return nt(ones, high) + nt(ones, rest)


def project_body(tile, x_ref, gain_ref, wq, wk, wv, a_ref, b_ref, proj_ref, mid_ref, inv_ref, sq_ref):
    part = wq.shape[1]
    def one_tile(t, carry):
        rows = pl.ds(pl.multiple_of(t * tile, tile), tile)
        x = x_ref[rows].astype(F32)
        inv = inverse_rms(x)
        inv_ref[rows] = inv
        normed = (x * inv * gain_ref[...]).astype(BF16)
        mid = nt(normed, a_ref[...]).astype(BF16)
        mid_ref[rows] = mid
        for m, w in enumerate((wq, wk, wv)):
            cols = pl.ds(m * part, part)
            proj = nn(normed, w[...]) + nn(mid, b_ref[:, cols])
            proj_ref[rows, cols] = proj
            if m < 2:
                sq_ref[pl.ds(m, 1), rows] = row_sums(proj * proj)[0:1]
        return carry

    lax.fori_loop(0, x_ref.shape[0] // tile, one_tile, 0)


def project(x, gain, weights, a_rows, b_cols):
    seq_len, width = x.shape
    part = weights[0].shape[1]
    rank = a_rows.shape[0]
    return pl.pallas_call(
        functools.partial(project_body, min(256, seq_len)),
        out_shape=(
            jax.ShapeDtypeStruct((seq_len, 3 * part), F32),
            jax.ShapeDtypeStruct((seq_len, rank), BF16),
            jax.ShapeDtypeStruct((seq_len, 1), F32),
            jax.ShapeDtypeStruct((2, seq_len), F32),
        ),
        in_specs=[VM] * 7,
        out_specs=(VM,) * 4,
        compiler_params=pltpu.CompilerParams(vmem_limit_bytes=VMEM_LIMIT),
        name="project",
    )(x, gain, *weights, a_rows, b_cols)


def key_limit(start, tile, seq_len, reach):
    return min(seq_len, max(start + tile, reach))


def allowed_keys(start, tile, limit, prefix_len):
    query = start + lax.broadcasted_iota(jnp.int32, (tile, limit), 0)
    key = lax.broadcasted_iota(jnp.int32, (tile, limit), 1)
    return jnp.logical_or(key <= query, key < prefix_len)


def attend_body(
    tile, reach, scale, prefix_ref, proj_ref, inv_ref, gains_ref, cos_ref, sin_ref, map_ref,
    p_ref, att_ref, q_ref, k_ref, v_ref, log_ref,
):
    seq_len, part = att_ref.shape
    prefix_len = prefix_ref[0]

    def one_tile(t, carry):
        rows = pl.ds(pl.multiple_of(t * tile, tile), tile)
        for h in range(part // HD):
            cols = pl.ds(h * HD, HD)
            for m, ref in ((0, q_ref), (1, k_ref)):
                plain = proj_ref[rows, pl.ds(m * part + h * HD, HD)] * inv_ref[rows, m : m + 1]
                plain = plain * gains_ref[m : m + 1, cols]
                ref[rows, cols] = (plain * cos_ref[rows] + pltpu.roll(plain, HD // 2, 1) * sin_ref[rows]).astype(BF16)
            v_ref[rows, cols] = proj_ref[rows, pl.ds(2 * part + h * HD, HD)].astype(BF16)
        return carry

    lax.fori_loop(0, seq_len // tile, one_tile, 0)
    for start in range(0, seq_len, tile):
        rows = pl.ds(start, tile)
        limit = key_limit(start, tile, seq_len, reach)
        allowed = allowed_keys(start, tile, limit, prefix_len)
        for h in range(part // HD):
            cols = pl.ds(h * HD, HD)
            scores = nt(q_ref[rows, cols], k_ref[pl.ds(0, limit), cols]) * scale
            scores = jnp.where(allowed, scores, masked_score)
            top = jnp.max(scores, axis=1, keepdims=True)
            exponent = jnp.exp(scores - top)
            total = jnp.sum(exponent, axis=1, keepdims=True)
            weights = (exponent / total).astype(BF16)
            att_ref[rows, cols] = nn(weights, v_ref[pl.ds(0, limit), cols]).astype(BF16)
            log_ref[rows, h : h + 1] = top + jnp.log(total)
        p_ref[rows] = nn(att_ref[rows], map_ref[...]).astype(BF16)


def attend(prefix, proj, inv, gains, tables, out_map, reach, scale):
    seq_len = proj.shape[0]
    part = proj.shape[1] // 3
    heads = jax.ShapeDtypeStruct((seq_len, part), BF16)
    return pl.pallas_call(
        functools.partial(attend_body, min(256, seq_len), reach, scale),
        out_shape=(
            jax.ShapeDtypeStruct((seq_len, out_map.shape[1]), BF16),
            heads,
            heads,
            heads,
            heads,
            jax.ShapeDtypeStruct((seq_len, part // HD), F32),
        ),
        in_specs=[pl.BlockSpec(memory_space=pltpu.SMEM)] + [VM] * 6,
        out_specs=(VM,) * 6,
        compiler_params=pltpu.CompilerParams(vmem_limit_bytes=VMEM_LIMIT),
        name="attend",
    )(prefix, proj, inv, gains, *tables, out_map)


def attend_back(
    tile, reach, scale, prefix_ref, g_ref, map_ref, b_ref, att_ref, q_ref, k_ref, v_ref, log_ref, proj_ref,
    gains_ref, cos_ref, sin_ref, scaled_ref, dv_ref, stat_ref, ga_ref, da_ref, dq_acc, dk_acc, dv_acc,
):
    seq_len, part = att_ref.shape
    prefix_len = prefix_ref[0]
    grad_a = jnp.zeros(ga_ref.shape, F32)

    def first_tile(t, grad_a):
        rows = pl.ds(pl.multiple_of(t * tile, tile), tile)
        grads = g_ref[rows]
        da_ref[rows] = nt(grads, map_ref[...]).astype(BF16)
        grad_mid = nt(grads, b_ref[...]).astype(BF16)
        return grad_a + tn(grad_mid, att_ref[rows])

    ga_ref[...] = lax.fori_loop(0, seq_len // tile, first_tile, grad_a)
    dk_acc[...] = jnp.zeros_like(dk_acc)
    dv_acc[...] = jnp.zeros_like(dv_acc)
    for start in range(0, seq_len, tile):
        rows = pl.ds(start, tile)
        limit = key_limit(start, tile, seq_len, reach)
        keys = pl.ds(0, limit)
        allowed = allowed_keys(start, tile, limit, prefix_len)
        for h in range(part // HD):
            cols = pl.ds(h * HD, HD)
            query, key = q_ref[rows, cols], k_ref[keys, cols]
            grads = da_ref[rows, cols]
            scores = jnp.where(allowed, nt(query, key) * scale, masked_score)
            weights = jnp.exp(scores - log_ref[rows, h : h + 1])
            grad_weights = nt(grads, v_ref[keys, cols])
            dot = jnp.sum(weights * grad_weights, axis=1, keepdims=True)
            grad_scores = (weights * (grad_weights - dot)).astype(BF16)
            dq_acc[rows, cols] = nn(grad_scores, key) * scale
            dk_acc[keys, cols] += tn(grad_scores, query) * scale
            dv_acc[keys, cols] += tn(weights.astype(BF16), grads)
    dv_ref[...] = dv_acc[...].astype(BF16)
    for m, acc in ((0, dq_acc), (1, dk_acc)):

        def turn_back(t, carry):
            rows = pl.ds(pl.multiple_of(t * tile, tile), tile)
            total = jnp.zeros((8, tile), F32)
            for h in range(part // HD):
                cols = pl.ds(h * HD, HD)
                here = pl.ds(m * part + h * HD, HD)
                plain = acc[rows, cols]
                turned = plain * cos_ref[rows] - pltpu.roll(plain, HD // 2, 1) * sin_ref[rows]
                scaled = turned * gains_ref[m : m + 1, cols]
                scaled_ref[rows, here] = scaled
                total += row_sums(proj_ref[rows, here] * scaled)
            stat_ref[pl.ds(m, 1), rows] = total[0:1]
            return carry

        lax.fori_loop(0, seq_len // tile, turn_back, 0)


def back_body(tile, reach, scale, chips, row_count, extra, prefix_ref, slot_ref, *refs):
    refs = list(refs)

    def take(number):
        taken = refs[:number]
        del refs[:number]
        return taken

    g_ref, map_ref, bo_ref, att_ref, q_ref, k_ref, v_ref, log_ref, proj_ref, gains_ref, cos_ref, sin_ref = take(12)
    inv_ref, b_ref, a_ref, x_ref, inv1_ref, gain_ref, mid_ref, late_ref, router_ref = take(9)
    weights = take(3)
    gi_ref, held_a, held_b, held_router = take(4)
    scaled_ref, dv_ref, stat_ref, stats_ref, ga_ref, da_ref, dq_acc, dk_acc, dv_acc = take(9)
    w_ref, d_ref, middle_ref, p_ref, o_ref, pair_buf, line_buf, sums, flat_ref, every_ref = take(10)
    w_sems, stat_send, stat_recv, row_send, row_recv = take(5)
    right_sem, left_sem, mate_sem, line_recv, mate_recv = take(5)
    here, chip, core, mate = line_place()
    row = lax.axis_index("row")
    count = 2 * chips
    seq_len, width = x_ref.shape
    part = dv_ref.shape[1]
    ranks = a_ref.shape[0]
    rank = ranks // 3
    parts = 2

    fetches = [
        pltpu.make_async_copy(w, w_ref.at[:, pl.ds(m * part, part)], w_sems.at[m]) for m, w in enumerate(weights)
    ]
    for fetch in fetches:
        fetch.start()
    barrier = pltpu.get_barrier_semaphore()
    for hop in range(1, count):
        other = lax.rem(here + hop, count)
        pl.semaphore_signal(barrier, inc=1, device_id={"col": other}, device_id_type=MESH_ID)
    for hop in range(1, row_count):
        other = lax.rem(row + hop, row_count)
        pl.semaphore_signal(barrier, inc=1, device_id={"row": other}, device_id_type=MESH_ID)
    attend_back(
        tile, reach, scale, prefix_ref, g_ref, map_ref, bo_ref, att_ref, q_ref, k_ref, v_ref, log_ref, proj_ref,
        gains_ref, cos_ref, sin_ref, scaled_ref, dv_ref, stat_ref, ga_ref, da_ref, dq_acc, dk_acc, dv_acc,
    )
    pl.semaphore_wait(barrier, count + row_count - 2)

    def stat_copy(hop, block):
        other = lax.rem(here + hop, count)
        return remote(stat_ref, stats_ref.at[block], stat_send.at[hop], stat_recv.at[hop], other)

    for hop in range(1, count):
        stat_copy(hop, here).start()
    stats_ref[here] = stat_ref[...]
    for hop in range(1, count):
        stat_copy(hop, lax.rem(here + count - hop, count)).wait_recv()
    total = stats_ref[0]
    for n in range(1, count):
        total = total + stats_ref[n]
    stats_ref[0] = total * (1.0 / width)

    grad_b = jnp.zeros((ranks, 3 * part), F32)
    first_stats = jnp.zeros((8, part), F32)
    line = lax.broadcasted_iota(jnp.int32, (8, part), 0)

    def grads_tile(t, carry):
        grad_b, first_stats = carry
        rows = pl.ds(pl.multiple_of(t * tile, tile), tile)
        upright = jnp.transpose(jnp.concatenate([stats_ref[0, :, rows], jnp.zeros((6, tile), F32)], axis=0))
        products = jnp.zeros((tile, part), F32)
        for m in range(3):
            cols = pl.ds(m * part, part)
            if m < 2:
                inv = inv_ref[rows, m : m + 1]
                shift = inv * inv * inv * upright[:, m : m + 1]
                grad = (inv * scaled_ref[rows, cols] - proj_ref[rows, cols] * shift).astype(BF16)
            else:
                grad = dv_ref[rows]
            d_ref[rows, cols] = grad
            products += grad.astype(F32) * proj_ref[rows, cols]
        grads = d_ref[rows]
        middle_ref[rows] = nt(grads, b_ref[...]).astype(BF16)
        grad_b += tn(mid_ref[rows], grads)
        first = row_sums(products / inv1_ref[rows])
        for j in range(tile // part):
            first_stats = jnp.where(
                line == (t * tile) // part + j, first[:, j * part : (j + 1) * part], first_stats
            )
        return grad_b, first_stats

    grad_b, first_stats = lax.fori_loop(0, seq_len // tile, grads_tile, (grad_b, first_stats))
    high = first_stats.astype(BF16).astype(F32)
    router = router_ref[...]
    if part > router.shape[1]:
        router = jnp.concatenate([router, jnp.zeros((rank, part - router.shape[1]), F32)], axis=1)
    common = jnp.concatenate([router, high, first_stats - high], axis=0).astype(BF16)
    common = jnp.concatenate([common] * count, axis=1)
    p_ref[pl.ds(ranks, 2 * rank)] = late_ref[...].astype(BF16)
    p_ref[pl.ds(ranks + 2 * rank, rank + 16)] = common
    used = ranks + 3 * rank + 16
    p_ref[pl.ds(used, extra - used)] = jnp.zeros((extra - used, width), BF16)
    for fetch in fetches:
        fetch.wait()

    size = o_ref.shape
    step = size[0] // parts

    def rows_of(piece):
        return pl.ds(piece * step, step)

    def at(block, piece):
        return spot(1, size, parts, block, piece)

    def mate_copy(j, piece):
        return remote(
            p_ref.at[at(2 * j + 1 - core, piece)],
            pair_buf.at[j, rows_of(piece)],
            mate_sem.at[j, piece],
            mate_recv.at[j, piece],
            mate,
        )

    def line_copy(j, slot, piece, sem, device):
        return remote(
            sums.at[j, rows_of(piece)],
            line_buf.at[slot, rows_of(piece)],
            sem.at[j, piece],
            line_recv.at[slot, piece],
            device,
        )

    def order(s):
        right = chips - 1 - chip
        return jnp.where(s < right, chips - 1 - s, jnp.where(s < chips - 1, s - right, chip))

    def work_out(s):
        cols = pl.ds(pl.multiple_of(order(s) * (2 * part), 128), 2 * part)
        gain = gain_ref[:, cols]
        spread = a_ref[:, cols]
        chunk = w_ref[cols]

        def one_tile(t, grad_a):
            rows = pl.ds(pl.multiple_of(t * tile, tile), tile)
            middle = middle_ref[rows]
            normed_part = nt(d_ref[rows], chunk) + nn(middle, spread)
            p_ref[pl.ds(pl.multiple_of(extra + t * tile, 16), tile), cols] = normed_part.astype(BF16)
            normed = (x_ref[rows, cols].astype(F32) * inv1_ref[rows] * gain).astype(BF16)
            return grad_a + tn(middle, normed)

        grad_a = lax.fori_loop(0, seq_len // tile, one_tile, jnp.zeros((ranks, 2 * part), F32))
        p_ref[pl.ds(0, ranks), cols] = grad_a.astype(BF16)
        for piece in range(parts):
            mate_copy(order(s), piece).start()

    chunk = 64

    def chunk_rows(piece, low):
        return pl.ds(pl.multiple_of(piece * step + low, 16), chunk)

    def pair_sum(j, piece, low):
        cols = pl.ds(pl.multiple_of((2 * j + core) * part, 128), part)
        rows = chunk_rows(piece, low)
        return p_ref[rows, cols].astype(F32) + pair_buf[j, rows].astype(F32)

    def pair_up(j, piece):
        mate_copy(j, piece).wait_recv()

        def add_up(low):
            sums[j, chunk_rows(piece, low)] = pair_sum(j, piece, low).astype(BF16)

        in_chunks(step, chunk, add_up)

    def one_block(s, carry):
        work_out(s)

        @pl.when(jnp.logical_and(chip == 0, s > 0))
        def _():
            for piece in range(parts):
                j = order(s - 1)
                pair_up(j, piece)
                line_copy(j, j, piece, right_sem, here + 2).start()

        @pl.when(jnp.logical_and(chip == chips - 1, s > 0))
        def _():
            for piece in range(parts):
                j = order(s - 1)
                pair_up(j, piece)

                @pl.when(j == chips - 2)
                def _():
                    line_copy(j, chips, piece, left_sem, here - 2).start()

                @pl.when(j < chips - 2)
                def _():
                    line_copy(j, j, piece, left_sem, here - 2).start()

        return carry

    lax.fori_loop(0, chips, one_block, 0)
    inner = jnp.logical_and(chip > 0, chip < chips - 1)

    def pass_on(j, slot, piece, sem, device):
        line_copy(j, j, piece, sem, mate).wait_recv()
        mate_copy(j, piece).wait_recv()

        def add_up(low):
            rows = chunk_rows(piece, low)
            sums[j, rows] = (pair_sum(j, piece, low) + line_buf[j, rows].astype(F32)).astype(BF16)

        in_chunks(step, chunk, add_up)
        line_copy(j, slot, piece, sem, device).start()

    for far in range(chips - 2, 0, -1):
        for piece in range(parts):

            @pl.when(jnp.logical_and(inner, chip + far < chips))
            def _():
                pass_on(chip + far, chip + far, piece, right_sem, here + 2)

            @pl.when(jnp.logical_and(inner, chip - far >= 0))
            def _():
                pass_on(chip - far, chips if far == 1 else chip - far, piece, left_sem, here - 2)

    def row_copy(hop, block):
        other = lax.rem(row + hop, row_count)
        return pltpu.make_async_remote_copy(
            src_ref=flat_ref,
            dst_ref=every_ref.at[block],
            send_sem=row_send.at[hop],
            recv_sem=row_recv.at[hop],
            device_id={"row": other},
            device_id_type=MESH_ID,
        )

    for piece in range(parts):
        mate_copy(chip, piece).wait_recv()

        def begin(low):
            o_ref[chunk_rows(piece, low)] = pair_sum(chip, piece, low)

        in_chunks(step, chunk, begin)

        def add_line(slot):
            def add_up(low):
                o_ref[chunk_rows(piece, low)] += line_buf[slot, chunk_rows(piece, low)].astype(F32)

            in_chunks(step, chunk, add_up)

        @pl.when(chip > 0)
        def _():
            line_copy(chip, chip, piece, right_sem, mate).wait_recv()
            add_line(chip)

        @pl.when(chip < chips - 1)
        def _():
            line_copy(chip, chips, piece, left_sem, mate).wait_recv()
            add_line(chips)

        if piece == 0:
            flat_ref[pl.ds(0, 6 * rank)] = o_ref[pl.ds(0, 6 * rank)].astype(BF16)
            flat_ref[pl.ds(6 * rank, rank)] = ga_ref[...].astype(BF16)
            for m in range(3):
                flat_ref[pl.ds((7 + m) * rank, rank)] = grad_b[
                    m * rank : (m + 1) * rank, m * part : (m + 1) * part
                ].astype(BF16)
            owner = jnp.full((16, part), slot_ref[0].astype(F32), F32)
            flat_ref[pl.ds(10 * rank, 16)] = owner.astype(BF16)
            for hop in range(1, row_count):
                row_copy(hop, row).start()
            every_ref[row] = flat_ref[...]

    stat_rows = o_ref[pl.ds(ranks + 3 * rank, 8)] + o_ref[pl.ds(ranks + 3 * rank + 8, 8)]
    upright = jnp.transpose(stat_rows)
    own = pl.ds(pl.multiple_of(here * part, 128), part)
    gain = gain_ref[:, own]
    for t in range(seq_len // part):
        rows = pl.ds(t * part, part)
        inv = inv1_ref[rows]
        pull = inv * inv * inv * upright[:, t : t + 1] * (1.0 / width)
        gi_ref[rows] = (
            g_ref[rows, own].astype(F32)
            + inv * gain * o_ref[pl.ds(extra + t * part, part)]
            - x_ref[rows, own].astype(F32) * pull
        )
    for hop in range(1, row_count):
        row_copy(hop, lax.rem(row + row_count - hop, row_count)).wait_recv()
    held = held_router.shape[0]
    for h in range(held):
        chosen = (row * held + h).astype(F32)
        picked = jnp.zeros((10 * rank, part), F32)
        for r in range(row_count):
            owner = every_ref[r, pl.ds(10 * rank, 16)].astype(F32)[0:1]
            picked += jnp.where(owner == chosen, every_ref[r, pl.ds(0, 10 * rank)].astype(F32), 0.0)
        for n, piece in enumerate((0, 1, 2, 6, 3)):
            held_a[n, h] = picked[piece * rank : (piece + 1) * rank]
        for n, piece in enumerate((7, 8, 9, 4)):
            held_b[n, h] = picked[piece * rank : (piece + 1) * rank]
        held_router[h] = picked[5 * rank : 6 * rank]

    for hop in range(1, row_count):
        row_copy(hop, row).wait_send()
    for hop in range(1, count):
        stat_copy(hop, here).wait_send()
    for j in range(chips):
        for piece in range(parts):
            mate_copy(j, piece).wait_send()

            @pl.when(j > chip)
            def _():
                line_copy(j, j, piece, right_sem, mate).wait_send()

            @pl.when(j < chip)
            def _():
                line_copy(j, j, piece, left_sem, mate).wait_send()


def back(prefix, slot, operands, weights, reach, scale, chips, row_count, held, ident):
    x = operands[15]
    seq_len, width = x.shape
    part = weights[0].shape[1]
    count = 2 * chips
    ranks = operands[14].shape[0]
    rank = ranks // 3
    extra = 128
    tall = seq_len + extra
    sems = pltpu.SemaphoreType.DMA((chips, 2))
    hops = pltpu.SemaphoreType.DMA((count,))
    row_hops = pltpu.SemaphoreType.DMA((row_count,))
    smem = pl.BlockSpec(memory_space=pltpu.SMEM)
    return pl.pallas_call(
        functools.partial(back_body, min(256, seq_len), reach, scale, chips, row_count, extra),
        out_shape=(
            jax.ShapeDtypeStruct((seq_len, part), F32),
            jax.ShapeDtypeStruct((5, held, rank, part), F32),
            jax.ShapeDtypeStruct((4, held, rank, part), F32),
            jax.ShapeDtypeStruct((held, rank, part), F32),
        ),
        in_specs=[smem, smem] + [VM] * len(operands) + [ANY] * 3,
        out_specs=(VM,) * 4,
        scratch_shapes=[
            pltpu.VMEM((seq_len, 2 * part), F32),
            pltpu.VMEM((seq_len, part), BF16),
            pltpu.VMEM((2, seq_len), F32),
            pltpu.VMEM((count, 2, seq_len), F32),
            pltpu.VMEM((rank, part), F32),
            pltpu.VMEM((seq_len, part), BF16),
            pltpu.VMEM((seq_len, part), F32),
            pltpu.VMEM((seq_len, part), F32),
            pltpu.VMEM((seq_len, part), F32),
            pltpu.VMEM((width, 3 * part), BF16),
            pltpu.VMEM((seq_len, 3 * part), BF16),
            pltpu.VMEM((seq_len, ranks), BF16),
            pltpu.VMEM((tall, width), BF16),
            pltpu.VMEM((tall, part), F32),
            pltpu.VMEM((chips, tall, part), BF16),
            pltpu.VMEM((chips + 1, tall, part), BF16),
            pltpu.VMEM((chips, tall, part), BF16),
            pltpu.VMEM((10 * rank + 16, part), BF16),
            pltpu.VMEM((row_count, 10 * rank + 16, part), BF16),
            pltpu.SemaphoreType.DMA((3,)),
            hops,
            hops,
            row_hops,
            row_hops,
            sems,
            sems,
            sems,
            pltpu.SemaphoreType.DMA((chips + 1, 2)),
            sems,
        ],
        compiler_params=pltpu.CompilerParams(
            collective_id=ident, has_side_effects=True, vmem_limit_bytes=VMEM_LIMIT
        ),
        name="back",
    )(prefix, slot, *operands, *weights)


def moments(chips, subs):
    when = {}
    for j in range(chips):
        for chip in range(j):
            own = subs * (chips - j) + 1
            when[chip, j] = max(own, when[chip - 1, j] + 3) if chip > 0 else own
        for chip in range(chips - 1, j, -1):
            own = subs * (chips - chip + j) + 1
            when[chip, j] = max(own, when[chip + 1, j] + 3) if chip < chips - 1 else own
    last = chips * subs
    return {place: min(time, last) for place, time in when.items()}


def moe_turn_body(experts, chips, subs, count, x_ref, g_ref, routes_ref, *refs):
    refs = list(refs)

    def take(number):
        taken = refs[:number]
        del refs[:number]
        return taken

    operands = [None] + take(8)
    gate_w, up_w = take(2)
    downs = take(count)
    layer_ref, o_ref = take(2)
    results = take(2)
    out_ref, out_pair, out_line = take(3)
    p_ref, out_acc, dx_acc, gate_acc, wgu, wd, x_buf, g_buf = take(8)
    pair_buf, line_buf, sums = take(3)
    w_sems, tile_sems, right_sem, left_sem, mate_sem, line_recv, mate_recv = take(7)
    gather_sems = take(5)
    out_sems = take(5)
    out_more = refs
    here, chip, core, mate = line_place()
    row = lax.axis_index("row")
    hidden = wd.shape[1] // 2
    both_hidden = 2 * hidden
    tokens, width = out_ref.shape
    own = tokens // (2 * chips)
    tile = 2 * own
    lanes = gate_acc.shape[1]
    local = gate_w.shape[0]
    pieces = gate_w.shape[2] // hidden
    steps = local * pieces
    each = steps // subs // 2

    def fetches(step, e, piece):
        slot, shift = step // 2, (step % 2) * hidden
        if count == 1:
            place = piece
            pairs = [(downs[0].at[e, pl.ds(piece * hidden, hidden)], wd.at[slot, pl.ds(shift, hidden)])]
        else:
            place = 2 * ((row // 2 + piece // 2) % 2) + (row + piece) % 2
            if piece == 0:
                pairs = [(downs[0].at[e], wd.at[slot, pl.ds(shift, hidden)])]
            else:
                early = downs[1].shape[1]
                pairs = [
                    (
                        ref.at[piece - 1, pl.ds(low - start, high - low)],
                        wd.at[slot, pl.ds(shift + low - e * hidden, high - low)],
                    )
                    for ref, start, low, high in (
                        (downs[1], 0, e * hidden, min(early, (e + 1) * hidden)),
                        (downs[2], early, max(early, e * hidden), (e + 1) * hidden),
                    )
                    if high > low
                ]
        units = pl.ds(pl.multiple_of(place * hidden, 128), hidden)
        return (
            pltpu.make_async_copy(gate_w.at[e, :, units], wgu.at[slot, :, pl.ds(shift, hidden)], w_sems.at[slot, 0]),
            pltpu.make_async_copy(
                up_w.at[e, :, units], wgu.at[slot, :, pl.ds(both_hidden + shift, hidden)], w_sems.at[slot, 1]
            ),
        ) + tuple(pltpu.make_async_copy(source, target, w_sems.at[slot, 2]) for source, target in pairs)

    def order(s):
        right = chips - 1 - chip
        return jnp.where(s < right, chips - 1 - s, jnp.where(s < chips - 1, s - right, chip))

    def tile_rows(s):
        return pl.ds(pl.multiple_of(order(s) * tile, 8), tile)

    def tiles(s):
        return (
            pltpu.make_async_copy(x_ref.at[tile_rows(s)], x_buf, tile_sems.at[0]),
            pltpu.make_async_copy(g_ref.at[tile_rows(s)], g_buf, tile_sems.at[1]),
        )

    for copy in tiles(0):
        copy.start()
    for step in range(steps):
        for copy in fetches(step, step // pieces, step % pieces):
            copy.start()
    line_barrier(chips)

    def block(number):
        return pl.ds(pl.multiple_of(number * own, 8), own)

    def mate_copy(j):
        return remote(p_ref.at[block(2 * j + 1 - core)], pair_buf.at[j], mate_sem.at[j], mate_recv.at[j], mate)

    def line_copy(j, slot, sem, device):
        return remote(sums.at[j], line_buf.at[slot], sem.at[j], line_recv.at[slot], device)

    def pair_sum(j):
        mate_copy(j).wait_recv()
        return p_ref[block(2 * j + core)].astype(F32) + pair_buf[j].astype(F32)

    def pass_on(at, j):
        rightward = j > at
        mate_copy(j).wait_recv()
        inner = 0 < at < chips - 1
        if inner:
            line_copy(j, j, right_sem if rightward else left_sem, mate).wait_recv()

        def add_up(low):
            rows = pl.ds(low, 16)
            mine = p_ref[pl.ds(pl.multiple_of((2 * j + core) * own + low, 16), 16)]
            total = mine.astype(F32) + pair_buf[j, rows].astype(F32)
            if inner:
                total = total + line_buf[j, rows].astype(F32)
            sums[j, rows] = total.astype(BF16)

        in_chunks(own, 16, add_up)
        if rightward:
            line_copy(j, j, right_sem, here + 2).start()
        else:
            line_copy(j, chips if at - j == 1 else j, left_sem, here - 2).start()

    when = moments(chips, subs)

    def one_sub(k, carry):
        s, sub = k // subs, k % subs
        rows = tile_rows(s)

        @pl.when(sub == 0)
        def _():
            for copy in tiles(s):
                copy.wait()

            out_acc[...] = jnp.zeros_like(out_acc)
            dx_acc[...] = jnp.zeros_like(dx_acc)
            gate_acc[...] = jnp.zeros_like(gate_acc)

        def one_step(step, carry):
            @pl.when(s == 0)
            def _():
                units = pl.ds(0, both_hidden)
                for number in range(2):
                    target = wgu.at[step, :, pl.ds(number * both_hidden, both_hidden)]
                    pltpu.make_async_copy(gate_w.at[0, :, units], target, w_sems.at[step, number]).wait()
                pltpu.make_async_copy(wd.at[step], wd.at[step], w_sems.at[step, 2]).wait()

            e = here * local + (2 * step) // pieces
            lane = lax.broadcasted_iota(jnp.int32, (tile, lanes), 1)
            mine = lane == e
            halves = jnp.logical_or(mine, lane == e + experts)
            named = jnp.sum(jnp.where(routes_ref[rows] == e, 1.0, 0.0), axis=1, keepdims=True)
            gate = jnp.sum(jnp.where(halves, x_buf[:, width:].astype(F32), 0.0), axis=1, keepdims=True)
            gate = gate * named
            both = nn(x_buf[:, :width], wgu[step])
            gate_in, up_in = both[:, :both_hidden], both[:, both_hidden:]
            sigmoid = jax.nn.sigmoid(gate_in)
            silu = gate_in * sigmoid
            active = silu * up_in
            back = nt(g_buf[...], wd[step])
            d_gate = jnp.sum(active * back, axis=1, keepdims=True) * named
            gate_acc[...] += jnp.where(mine, d_gate, 0.0)
            out_acc[...] += nn((active * gate).astype(BF16), wd[step])
            d_active = back * gate
            d_gate_in = d_active * up_in * (sigmoid + silu * (1.0 - sigmoid))
            d_up_in = d_active * silu
            d_both = jnp.concatenate([d_gate_in.astype(BF16), d_up_in.astype(BF16)], axis=1)
            dx_acc[...] += nt(d_both, wgu[step])
            return carry

        lax.fori_loop(sub * each, (sub + 1) * each, one_step, 0)

        @pl.when(sub == subs - 1)
        def _():
            out_ref[rows] = out_acc[...].astype(BF16)
            p_ref[rows, :width] = dx_acc[...].astype(BF16)
            high = gate_acc[...].astype(BF16).astype(F32)
            rest = gate_acc[...] - high
            p_ref[rows, width:] = (high + pltpu.roll(rest, experts, 1)).astype(BF16)
            mate_copy(order(s)).start()

            @pl.when(s + 1 < chips)
            def _():
                for copy in tiles(s + 1):
                    copy.start()

            @pl.when(s == chips - 1)
            def _():
                fetch = pltpu.make_async_copy(operands[1], dx_acc.at[pl.ds(own, own)], tile_sems.at[0])
                fetch.start()
                fetch.wait()
                mine = out_acc[pl.ds(pl.multiple_of(core * own, 8), own)]
                out_ref[block(here)] = (mine + dx_acc[pl.ds(own, own)]).astype(BF16)

        for (at, j), time in sorted(when.items(), key=lambda item: (item[1], abs(item[0][0] - item[0][1]))):

            @pl.when(jnp.logical_and(chip == at, k == time - 1))
            def _():
                pass_on(at, j)

        return carry

    lax.fori_loop(0, chips * subs, one_sub, 0)
    if wgu.shape[0] >= chips:
        out_sums = wgu.at[:, pl.ds(0, tokens), pl.ds(0, layer_ref.shape[1])]
    else:
        (out_sums,) = out_more
    operands[0] = g_buf.at[pl.ds(pl.multiple_of(core * own, 8), own)]
    operands[1] = dx_acc.at[pl.ds(own, own)]
    layer = reduce_steps(chips, 2, 1, out_ref, layer_ref, out_pair, out_line, out_sums, *out_sems)
    next(layer)
    next(layer)
    first = pl.ds(0, own)

    def add(total):
        dx_acc[first] += total[:, :width]
        gate_acc[first] += total[:, width:]

    total = pair_sum(chip)
    dx_acc[first] = total[:, :width]
    gate_acc[first] = total[:, width:]

    @pl.when(chip > 0)
    def _():
        line_copy(chip, chip, right_sem, mate).wait_recv()
        add(line_buf[chip].astype(F32))

    @pl.when(chip < chips - 1)
    def _():
        line_copy(chip, chips, left_sem, mate).wait_recv()
        add(line_buf[chips].astype(F32))

    for j in range(chips):
        mate_copy(j).wait_send()

        @pl.when(j > chip)
        def _():
            line_copy(j, j, right_sem, mate).wait_send()

        @pl.when(j < chip)
        def _():
            line_copy(j, j, left_sem, mate).wait_send()

    kept = turn_backward(experts, dx_acc[first], gate_acc[first], operands, results, o_ref, block(here))
    run(gather_rows_steps(chips, 2, o_ref, *gather_sems, lambda: turn_late(kept, operands, results)), layer)


def moe_turn(x, g, routes, operands, experts, gate_w, up_w, downs, results, chips, ident):
    tokens, width = g.shape
    wide = x.shape[1]
    lanes = wide - width
    own = tokens // (2 * chips)
    hidden = downs[0].shape[1] if len(downs) > 1 else min(256, gate_w.shape[2] // 4)
    steps = gate_w.shape[0] * gate_w.shape[2] // hidden
    subs = min(4, steps // 2)
    whole = jax.ShapeDtypeStruct((tokens, width), BF16)
    part = width // (2 * chips)
    per_chip = pltpu.SemaphoreType.DMA((chips,))
    halves = pltpu.SemaphoreType.DMA((chips, 2))
    return pl.pallas_call(
        functools.partial(moe_turn_body, experts, chips, subs, len(downs)),
        out_shape=(jax.ShapeDtypeStruct((tokens, part), F32), whole) + tuple(results),
        in_specs=[ANY, ANY, VM, ANY] + [VM] * (len(operands) - 1) + [ANY] * (2 + len(downs)),
        out_specs=(VM,) * (2 + len(results)),
        scratch_shapes=[
            pltpu.VMEM((tokens, width), BF16),
            pltpu.VMEM((chips, tokens, part), BF16),
            pltpu.VMEM((chips + 1, tokens, part), BF16),
            pltpu.VMEM((tokens, wide), BF16),
            pltpu.VMEM((2 * own, width), F32),
            pltpu.VMEM((2 * own, width), F32),
            pltpu.VMEM((2 * own, lanes), F32),
            pltpu.VMEM((steps // 2, width, 4 * hidden), BF16),
            pltpu.VMEM((steps // 2, 2 * hidden, width), BF16),
            pltpu.VMEM((2 * own, wide), BF16),
            pltpu.VMEM((2 * own, width), BF16),
            pltpu.VMEM((chips, own, wide), BF16),
            pltpu.VMEM((chips + 1, own, wide), BF16),
            pltpu.VMEM((chips, own, wide), BF16),
            pltpu.SemaphoreType.DMA((steps // 2, 3)),
            pltpu.SemaphoreType.DMA((2,)),
            per_chip,
            per_chip,
            per_chip,
            pltpu.SemaphoreType.DMA((chips + 1,)),
            per_chip,
        ]
        + [halves] * 8
        + [pltpu.SemaphoreType.DMA((chips + 1, 2)), halves]
        + ([] if steps // 2 >= chips else [pltpu.VMEM((chips, tokens, part), BF16)]),
        compiler_params=pltpu.CompilerParams(
            collective_id=ident, has_side_effects=True, vmem_limit_bytes=VMEM_MOST
        ),
        name="moe_turn",
    )(x, g, routes, *operands, gate_w, up_w, *downs)


def rope_tables(length, head_dim):
    half_dim = head_dim // 2
    frequency = rope_base ** (-(2.0 * jnp.arange(half_dim, dtype=F32)) / head_dim)
    angles = jnp.arange(length, dtype=F32)[:, None] * frequency[None, :]
    cosine, sine = jnp.cos(angles), jnp.sin(angles)
    return jnp.concatenate([cosine, cosine], axis=1), jnp.concatenate([-sine, sine], axis=1)


def shards(
    inputs,
    cotangent,
    norm_first,
    norm_second,
    query_gain,
    key_gain,
    w_query,
    w_key,
    w_value,
    w_out,
    w_router,
    w_gate,
    w_up,
    w_down,
    adapter_a,
    adapter_b,
    adapter_router,
    routes,
    prefix,
    adapter_index,
):
    seq_len, width_part = inputs.shape
    col_count = lax.axis_size("col")
    row_count = lax.axis_size("row")
    col_index = lax.axis_index("col")
    row_index = lax.axis_index("row")
    chips = col_count // 2
    full_width = width_part * col_count
    head_width = w_query.shape[1]
    local_experts = w_gate.shape[0]
    expert_total = w_router.shape[1]
    feature_start = col_index * width_part
    head_start = col_index * head_width
    own_rows = seq_len // col_count
    row_start = col_index * own_rows
    score_scale = HD ** (-0.5)
    reach = seq_len // 2
    lanes = 128

    def columns(array, axis_num):
        return lax.dynamic_slice_in_dim(array, feature_start, width_part, axis_num)

    def head_cols(array, axis_num=1):
        return lax.dynamic_slice_in_dim(array, head_start, head_width, axis_num)

    def held_rows(array):
        return lax.dynamic_slice_in_dim(array, row_start, own_rows, 0)

    def col_sum(pair, ident):
        return jnp.sum(small_gather(pair, col_count, ident), axis=0)

    full_gate = lax.all_gather(w_gate, "row", axis=2, tiled=True)
    full_up = lax.all_gather(w_up, "row", axis=2, tiled=True)
    across = row_count == 4 and local_experts == 2
    down_shares = w_down.reshape(SHARES, -1, full_width)
    riders = (cotangent, down_shares) if across else (cotangent,)
    adapter_slot = adapter_index[0]
    chosen_a = lax.dynamic_index_in_dim(adapter_a, adapter_slot, 1, keepdims=False).swapaxes(1, 2)
    chosen_b = lax.dynamic_index_in_dim(adapter_b, adapter_slot, 1, keepdims=False)
    chosen_router = lax.dynamic_index_in_dim(adapter_router, adapter_slot, 0, keepdims=False)
    rank = chosen_a.shape[1]
    a_three = chosen_a[:3].reshape(3 * rank, full_width)
    b_three = head_cols(chosen_b[:3].reshape(3 * rank, full_width))
    blank = jnp.zeros((rank, head_width), BF16)
    b_cols = jnp.concatenate(
        [
            jnp.concatenate([b_three[m * rank : (m + 1) * rank] if n == m else blank for n in range(3)], axis=0)
            for m in range(3)
        ],
        axis=1,
    )
    a_out = head_cols(chosen_a[3])
    out_map = (w_out.astype(F32) + tn(a_out, chosen_b[3])).astype(BF16)
    out_wide = jnp.concatenate([out_map, a_out.T, jnp.zeros((head_width, lanes - rank), BF16)], axis=1)
    router_rows = jnp.pad(w_router.T, ((0, lanes - expert_total), (0, 0)))
    router_up = jnp.pad(chosen_router, ((0, 0), (0, lanes - expert_total)))
    gains = jnp.stack([head_cols(query_gain, 0), head_cols(key_gain, 0)])
    tables = rope_tables(seq_len, HD)
    gain_first, gain_second = norm_first[None], norm_second[None]

    full_inputs, *down_first = line_gather(inputs, chips, 1, 0, rider=down_shares if across else None)
    proj, mid, inv_first, squares = project(
        full_inputs, gain_first, (w_query, w_key, w_value), a_three, b_cols
    )
    inv = lax.rsqrt(col_sum(squares, 1) / full_width + norm_eps).T
    part_out, attended, rot_query, rot_key, value_rows, log_totals = attend(
        prefix, proj, inv, gains, tables, out_wide, reach, score_scale
    )
    wide = full_width + lanes
    row_shape = jax.ShapeDtypeStruct
    normed_two, hidden_rows, mid_out, mid_router, probs, full_cot, *down_second = line_turn(
        part_out,
        (held_rows(full_inputs), gain_second, chosen_a[4], router_rows, router_up),
        wide,
        (
            row_shape((own_rows, full_width), F32),
            row_shape((own_rows, lanes), BF16),
            row_shape((own_rows, rank), BF16),
            row_shape((own_rows, lanes), F32),
        ),
        functools.partial(turn_forward, full_width, expert_total),
        lambda kept, operands, results: None,
        chips,
        2,
        riders,
    )
    if across:
        downs = (w_down,) + tuple(
            others.reshape(3, -1, full_width) for others in down_first + down_second
        )
    else:
        downs = (lax.all_gather(w_down, "row", axis=1, tiled=True),)

    layer_out, grad_attn, late, router_late = moe_turn(
        normed_two,
        full_cot,
        routes,
        (
            hidden_rows,
            gain_second,
            chosen_a[4],
            router_rows,
            router_up,
            probs,
            mid_router,
            mid_out,
        ),
        expert_total,
        full_gate,
        full_up,
        downs,
        (row_shape((2 * rank, full_width), F32), row_shape((rank, lanes), F32)),
        chips,
        7,
    )
    layer_out = layer_out.astype(BF16)

    held_adapters = adapter_a.shape[1] // row_count
    grad_inputs, grad_a, grad_b, grad_router = back(
        prefix,
        adapter_index,
        (
            grad_attn,
            out_map,
            chosen_b[3],
            attended,
            rot_query,
            rot_key,
            value_rows,
            log_totals,
            proj,
            gains,
            *tables,
            inv,
            b_cols,
            a_three,
            full_inputs,
            inv_first,
            gain_first,
            mid,
            late,
            router_late,
        ),
        (w_query, w_key, w_value),
        reach,
        score_scale,
        chips,
        row_count,
        held_adapters,
        12,
    )
    grad_a = grad_a.swapaxes(2, 3)
    grad_router = grad_router[:, :, :expert_total]
    return (layer_out, grad_inputs, grad_a, grad_b, grad_router)


def solution(mesh):
    placed = (
        P("row", "col"),
        P("row", "col"),
        P(),
        P(),
        P(),
        P(),
        P(None, "col"),
        P(None, "col"),
        P(None, "col"),
        P("col", None),
        P(),
        P("col", None, "row"),
        P("col", None, "row"),
        P("col", "row", None),
        P(),
        P(),
        P(),
        P("row", None),
        P("row"),
        P("row"),
    )
    return jax.shard_map(
        shards,
        mesh=mesh,
        in_specs=placed,
        out_specs=(
            P("row", "col"),
            P("row", "col"),
            P(None, "row", "col", None),
            P(None, "row", None, "col"),
            P("row", None, None),
        ),
        check_vma=False,
    )
```
